32 devices in a mesh: row: 8 (over z, y), col: 4 (over x, core).
Axes of the slice: x: 2, y: 2, z: 4, core: 2. Of those that a mesh axis runs over, the one named last changes fastest.
Arguments:
- tokens: bfloat16 [6272, 2048], P('row', 'col'), may hold values from -6 to 6
- first_gain: float32 [1024], P('col'), may hold values from 0.1 to 1.9
- first_shift: float32 [1024], P('col'), may hold values from -1.5 to 1.5
- inward_weight: bfloat16 [1024, 3, 1024], P('row', None, 'col'), may hold values from -0.25 to 0.25
- attention_bias: float32 [2, 1024], P(None, 'col'), may hold values from -2.5 to 2.5
- output_weight: bfloat16 [1024, 1024], P('col', 'row'), may hold values from -2 to 2
- output_bias: float32 [1024], P('col'), may hold values from -2.5 to 2.5
- second_gain: float32 [1024], P('col'), may hold values from 0.1 to 1.9
- second_shift: float32 [1024], P('col'), may hold values from -1.5 to 1.5
- expand_weight: bfloat16 [1024, 4096], P('row', 'col'), may hold values from -0.1875 to 0.1875
- expand_bias: float32 [4096], P('col'), may hold values from -2.5 to 2.5
- reduce_weight: bfloat16 [4096, 1024], P('col', 'row'), may hold values from -0.125 to 0.125
- reduce_bias: float32 [1024], P('col'), may hold values from -2.5 to 2.5
- cotangent: bfloat16 [6272, 2048], P('row', 'col'), may hold values from -6 to 6
Outputs:
- layer_output: bfloat16 [6272, 2048], P('row', 'col')
- tokens_grad: float32 [6272, 2048], P('row', 'col')
- first_gain_grad: float32 [1024], P('col')
- first_shift_grad: float32 [1024], P('col')
- inward_grad: float32 [1024, 3, 1024], P('row', None, 'col')
- attention_bias_grad: float32 [2, 1024], P(None, 'col')
- output_grad: float32 [1024, 1024], P('col', 'row')
- output_bias_grad: float32 [1024], P('col')
- second_gain_grad: float32 [1024], P('col')
- second_shift_grad: float32 [1024], P('col')
- expand_grad: float32 [1024, 4096], P('row', 'col')
- expand_bias_grad: float32 [4096], P('col')
- reduce_grad: float32 [4096, 1024], P('col', 'row')
- reduce_bias_grad: float32 [1024], P('col')
The draws below stay inside these ranges and needn't reach their ends.
All inputs are finite; a program needn't handle non-finite values.
Results may differ from the reference program's by a relative error of at most 0.015.
The reference program's roundings to bfloat16 on the way count: a program that leaves them out, or rounds other values in their place, can miss the bound.
Values may be sent and summed in bfloat16 or wider, within the bound.
A program may use at most 192 MiB of HBM per device.

```python
import jax
import jax.numpy as jnp
from jax import lax

D = 1024
HEADS = 16
FF = 4096
HEAD_DIM = 64
SEQ = 1568
TOKENS = 12544
N_COL = 4


def levels(rng, shape, cuts, smallest, largest):
    loudness = 1.0
    for position, blocks in cuts:
        draws = jax.random.uniform(jax.random.fold_in(jax.random.fold_in(rng, 6), position), (blocks,), jnp.float32, smallest / len(cuts), largest / len(cuts))
        loudness = loudness * jnp.repeat(jnp.exp(draws), shape[position] // blocks).reshape((-1,) + (1,) * (len(shape) - 1 - position))
    return loudness


def normal_values(own_key, shape, scale, bound, split=(), dtype=jnp.bfloat16):
    drawn = scale * jax.random.normal(own_key, shape, jnp.float32)
    if split:
        drawn = drawn * levels(own_key, shape, split, -0.22, 0.18)
    return jnp.clip(drawn, -bound, bound).astype(dtype)


def setup_inputs(seed: int = 0) -> dict:
    seeds = jax.random.split(jax.random.key(seed), 15)
    tokens = normal_values(seeds[0], (TOKENS // 2, 2 * D), 1.0, 6.0, ((0, 8), (1, 4)))
    first_gain = jnp.clip(1.0 + 0.18 * jax.random.normal(seeds[1], (D,), jnp.float32), 0.1, 1.9)
    first_shift = normal_values(seeds[2], (D,), 0.3, 1.5, ((0, 4),), jnp.float32)
    inward_weight = normal_values(seeds[3], (D, 3, D), (D // 2) ** -0.5, 0.25, ((0, 8), (2, 4)))
    attention_bias = normal_values(seeds[4], (2, D), 0.5, 2.5, ((1, 4),), jnp.float32)
    output_weight = normal_values(seeds[5], (D, D), (max(D // 128, 1)) ** -0.5, 2.0, ((0, 4), (1, 8)))
    output_bias = normal_values(seeds[6], (D,), 0.5, 2.5, ((0, 4),), jnp.float32)
    second_gain = jnp.clip(1.0 + 0.18 * jax.random.normal(seeds[7], (D,), jnp.float32), 0.1, 1.9)
    second_shift = normal_values(seeds[8], (D,), 0.3, 1.5, ((0, 4),), jnp.float32)
    expand_weight = normal_values(seeds[9], (D, FF), D ** -0.5, 0.1875, ((0, 8), (1, 4)))
    expand_bias = normal_values(seeds[10], (FF,), 0.5, 2.5, ((0, 4),), jnp.float32)
    reduce_weight = normal_values(seeds[11], (FF, D), (FF // 2) ** -0.5, 0.125, ((0, 4), (1, 8)))
    reduce_bias = normal_values(seeds[12], (D,), 0.5, 2.5, ((0, 4),), jnp.float32)
    cotangent = normal_values(seeds[13], (TOKENS // 2, 2 * D), 1.0, 6.0, ((0, 8), (1, 4)))
    return dict(tokens=tokens, first_gain=first_gain, first_shift=first_shift, inward_weight=inward_weight, attention_bias=attention_bias, output_weight=output_weight, output_bias=output_bias, second_gain=second_gain, second_shift=second_shift, expand_weight=expand_weight, expand_bias=expand_bias, reduce_weight=reduce_weight, reduce_bias=reduce_bias, cotangent=cotangent)


EPSILON = 1e-06
HIGHEST = lax.Precision.HIGHEST

@jax.custom_vjp
def low(v):
    return lax.optimization_barrier(v.astype(jnp.bfloat16)).astype(jnp.float32)

@jax.custom_vjp
def low_back(v):
    return v

def low_keep(v):
    return (low(v), None)

def low_pass(kept, grad):
    return (grad,)

def back_keep(v):
    return (v, None)

def back_low(kept, grad):
    return (low(grad),)
low.defvjp(low_keep, low_pass)
low_back.defvjp(back_keep, back_low)

def unpack_rows(packed):
    return packed.reshape(packed.shape[0], N_COL, 2, D // N_COL).transpose(0, 2, 1, 3).reshape(-1, D)

def pack_rows(plain):
    return plain.reshape(-1, 2, N_COL, D // N_COL).transpose(0, 2, 1, 3).reshape(-1, 2 * D)

def layer_norm(values, gain, shift):
    average = lax.optimization_barrier(jnp.mean(values, axis=-1, keepdims=True))
    centred = values - average
    spread = lax.optimization_barrier(jnp.mean(centred * centred, axis=-1, keepdims=True))
    return centred * lax.rsqrt(spread + EPSILON) * gain + shift

def attend(clip_parts):
    queries, key_rows, value_rows = clip_parts
    scores = jnp.einsum('qhd,khd->hqk', queries, key_rows, precision=HIGHEST) * HEAD_DIM ** (-0.5)
    scores = low_back(scores)
    prob_low = low(jax.nn.softmax(scores, axis=-1))
    return jnp.einsum('hqk,khd->qhd', prob_low, value_rows, precision=HIGHEST)

def forward(tokens, first_gain, first_shift, inward_weight, attention_bias, output_weight, output_bias, second_gain, second_shift, expand_weight, expand_bias, reduce_weight, reduce_bias):
    normed_one = low(layer_norm(tokens, first_gain, first_shift))
    projected = jnp.einsum('td,dje->tje', normed_one, inward_weight, precision=HIGHEST)
    queries = low_back(low(projected[:, 0] + attention_bias[0]))
    key_rows = low_back(low(projected[:, 1]))
    value_rows = low_back(low(projected[:, 2] + attention_bias[1]))
    clip_shape = (-1, SEQ, HEADS, HEAD_DIM)
    mixed_rows = lax.map(jax.checkpoint(attend), (queries.reshape(clip_shape), key_rows.reshape(clip_shape), value_rows.reshape(clip_shape)))
    mixed_rows = low_back(low(mixed_rows.reshape(tokens.shape)))
    hidden_state = tokens + low_back(jnp.dot(mixed_rows, output_weight, precision=HIGHEST) + output_bias)
    normed_two = low(layer_norm(hidden_state, second_gain, second_shift))
    expanded = low_back(jnp.dot(normed_two, expand_weight, precision=HIGHEST) + expand_bias)
    activated = low(jax.nn.gelu(expanded, approximate=False))
    return hidden_state + low_back(jnp.dot(activated, reduce_weight, precision=HIGHEST) + reduce_bias)

def reference(tokens, first_gain, first_shift, inward_weight, attention_bias, output_weight, output_bias, second_gain, second_shift, expand_weight, expand_bias, reduce_weight, reduce_bias, cotangent):
    floats = (unpack_rows(tokens.astype(jnp.float32)), first_gain.astype(jnp.float32), first_shift.astype(jnp.float32), inward_weight.astype(jnp.float32), attention_bias.astype(jnp.float32), output_weight.astype(jnp.float32), output_bias.astype(jnp.float32), second_gain.astype(jnp.float32), second_shift.astype(jnp.float32), expand_weight.astype(jnp.float32), expand_bias.astype(jnp.float32), reduce_weight.astype(jnp.float32), reduce_bias.astype(jnp.float32))
    result, pullback = jax.vjp(forward, *floats)
    grads = pullback(unpack_rows(cotangent.astype(jnp.float32)))
    return (pack_rows(result).astype(jnp.bfloat16), pack_rows(grads[0]), grads[1], grads[2], grads[3], grads[4], grads[5], grads[6], grads[7], grads[8], grads[9], grads[10], grads[11], grads[12])
```

```python
import functools
import jax
import jax.numpy as jnp
from jax import lax
from jax.experimental import pallas as pl
from jax.experimental.pallas import tpu as pltpu
from jax.sharding import PartitionSpec as P

HEAD_DIM = 64
SEQ = 1568
EPSILON = 1e-06
CHUNKS = 7
F32 = jnp.float32
BF16 = jnp.bfloat16
MESH = pl.DeviceIdType.MESH
LOG2E = 1.4426950408889634
NT_DIMS = (((1,), (1,)), ((), ()))
TN_DIMS = (((0,), (0,)), ((), ()))


def remote(src, dst, send, recv, row, col):
    return pltpu.make_async_remote_copy(
        src_ref=src, dst_ref=dst, send_sem=send, recv_sem=recv,
        device_id=(row, col), device_id_type=MESH,
    )


def aligned(index, size):
    return pl.ds(pl.multiple_of(index * size, size), size)


def row_norm(values):
    mean = jnp.mean(values, axis=1, keepdims=True)
    centred = values - mean
    inverse = lax.rsqrt(jnp.mean(centred * centred, axis=1, keepdims=True) + EPSILON)
    return centred * inverse, mean, inverse


def weight_blocks(ref, kind, row):
    if kind == "rows":
        return ref.at[aligned(row, 128), :]
    return ref.at[:, aligned(row, 128)]


WEIGHT_KINDS = ("rows", "cols", "rows", "cols")


def forward_kernel(
    tok, cot, vec, attn_bias, exp_bias, win_s, wo_s, we_s, wr_s,
    tok_o, cot_o, q_o, qt_o, k_o, kt_o, v_o, mixf_o, lse_o, hid_o, unit_o, inv_o,
    norm_o, act_o, slope_o, win_o, wo_o, we_o, wr_o, vec_o, one_o, stat_o,
    tok_all, cot_all, norm_one, q, qt, k, kt, v, vt, mixed, mixf, lse, hid, unit, inv, norm_two, act, slope,
    win, wo, we, wr, vecs, stat, scores, sb, rb, xb, xr,
    local_sem, wz_send, wz_recv, wy_send, wy_recv, vec_send, vec_recv,
    tx_send, tx_recv, tc_send, tc_recv, cx_send, cx_recv, cc_send, cc_recv,
    h1_send, h1_recv, h2_send, h2_recv, h3_send, h3_recv,
):
    r, c = lax.axis_index("row"), lax.axis_index("col")
    z, y = r // 2, r % 2
    xx, core = c // 2, c % 2
    c_x, c_core, c_far = (c + 2) % 4, c + 1 - 2 * core, (c + 2) % 4 + 1 - 2 * core
    r_y = r + 1 - 2 * y
    z_peers = [((z + step) % 4) * 2 + y for step in (1, 2, 3)]
    half = tok.shape[0] // CHUNKS
    chunk = 2 * half
    width = vec.shape[1]
    scale = LOG2E * HEAD_DIM ** (-0.5)

    barrier = pltpu.get_barrier_semaphore()
    for col in (c_x, c_core, c_far):
        pl.semaphore_signal(barrier, inc=1, device_id=(r, col), device_id_type=MESH)
    for row in (r_y, *z_peers):
        pl.semaphore_signal(barrier, inc=1, device_id=(row, c), device_id_type=MESH)

    own = aligned(c, width)
    for i in range(CHUNKS):
        for s in range(2):
            rows = pl.ds(i * half, half)
            tok_all[i, s * half : (s + 1) * half, own] = tok[rows, s * width : (s + 1) * width]
            cot_all[i, s * half : (s + 1) * half, own] = cot[rows, s * width : (s + 1) * width]
    vecs[:, own] = vec[...]
    shards = (win_s, wo_s, we_s, wr_s)
    fulls = (win, wo, we, wr)
    for w in range(4):
        weight_blocks(fulls[w], WEIGHT_KINDS[w], r)[...] = shards[w][...]
    pl.semaphore_wait(barrier, 7)

    def z_send(w, step):
        block = weight_blocks(fulls[w], WEIGHT_KINDS[w], r)
        return remote(shards[w], block, wz_send.at[w, step], wz_recv.at[w, step], z_peers[step], c)

    def z_arrival(w, step):
        source = ((z + 4 - (step + 1)) % 4) * 2 + y
        block = weight_blocks(fulls[w], WEIGHT_KINDS[w], source)
        return remote(block, block, wz_send.at[w, step], wz_recv.at[w, step], source, c), source

    def y_send(w, slot, row):
        block = weight_blocks(fulls[w], WEIGHT_KINDS[w], row)
        return remote(block, block, wy_send.at[w, slot], wy_recv.at[w, slot], r_y, c)

    def start_weight(w):
        for step in range(3):
            z_send(w, step).start()
        y_send(w, 3, r).start()

    def forward_weight(w):
        for step in (0, 2, 1):
            arrival, source = z_arrival(w, step)
            arrival.wait_recv()
            y_send(w, step, source).start()

    def finish_weight(w):
        for step in range(3):
            z_send(w, step).wait_send()
            source = ((z + 4 - (step + 1)) % 4) * 2 + y
            y_send(w, step, source).wait_send()
            pair = source + 1 - 2 * y
            y_send(w, step, pair).wait_recv()
        y_send(w, 3, r).wait_send()
        y_send(w, 3, r_y).wait_recv()

    def x_copy(ref, send, recv, i, col):
        block = ref.at[i, :, aligned(col, width)]
        return remote(block, block, send.at[i], recv.at[i], r, c_x)

    def core_copy(ref, send, recv, i, slot, col):
        block = ref.at[i, :, aligned(col, width)]
        return remote(block, block, send.at[i, slot], recv.at[i, slot], r, c_core)

    def vec_copy(slot, target, col):
        block = vecs.at[:, aligned(col, width)]
        return remote(block, block, vec_send.at[slot], vec_recv.at[slot], r, target)

    for i in range(CHUNKS):
        x_copy(tok_all, tx_send, tx_recv, i, c).start()
        core_copy(tok_all, tc_send, tc_recv, i, 0, c).start()
    for slot, target in enumerate((c_x, c_core, c_far)):
        vec_copy(slot, target, c).start()
    start_weight(0)
    start_weight(1)
    for slot, target in enumerate((c_x, c_core, c_far)):
        vec_copy(slot, target, c).wait_send()
        vec_copy(slot, target, target).wait_recv()

    def keep(index, i, src, dst):
        return pltpu.make_async_copy(src, dst, local_sem.at[index, i])

    def kept(i, stage):
        if stage == 0:
            pairs = ((tok_all, tok_o), (q, q_o), (qt, qt_o), (k, k_o), (kt, kt_o), (v, v_o), (norm_one, one_o), (stat, stat_o))
            base = 0
        elif stage == 1:
            pairs = ((mixf, mixf_o), (lse, lse_o))
            base = 8
        elif stage == 2:
            pairs = ((unit, unit_o), (inv, inv_o), (norm_two, norm_o), (act, act_o), (slope, slope_o))
            base = 10
        else:
            pairs = ((cot_all, cot_o),)
            base = 15
        return [keep(base + n, i, a.at[i], b.at[i]) for n, (a, b) in enumerate(pairs)]

    def keep_hid(i):
        return keep(16, i, hid.at[i, :, own], hid_o.at[i])

    lane_ids = lax.broadcasted_iota(jnp.int32, (chunk // 7, 128), 1)

    @pl.loop(0, CHUNKS)
    def _(i):
        x_copy(tok_all, tx_send, tx_recv, i, c_x).wait_recv()
        core_copy(tok_all, tc_send, tc_recv, i, 1, c_x).start()
        core_copy(tok_all, tc_send, tc_recv, i, 0, c_core).wait_recv()
        core_copy(tok_all, tc_send, tc_recv, i, 1, c_far).wait_recv()
        for part in range(7):
            rows = pl.ds(part * (chunk // 7), chunk // 7)
            units, mean, inverse = row_norm(tok_all[i, rows, :].astype(F32))
            stat[i, rows, :] = jnp.where(lane_ids < 64, mean, inverse)
            norm_one[i, rows, :] = (units * vecs[0:1, :] + vecs[1:2, :]).astype(BF16)

    forward_weight(0)
    start_weight(2)
    forward_weight(1)
    finish_weight(0)

    @pl.loop(0, CHUNKS)
    def _(i):
        part = jnp.dot(norm_one[i], win[:, 0:width], preferred_element_type=F32)
        part = (part + attn_bias[0:1, :]).astype(BF16)
        q[i] = part
        qt[i] = part.T
        part = jnp.dot(norm_one[i], win[:, width : 2 * width], preferred_element_type=F32).astype(BF16)
        k[i] = part
        kt[i] = part.T
        part = jnp.dot(norm_one[i], win[:, 2 * width : 3 * width], preferred_element_type=F32)
        part = (part + attn_bias[1:2, :]).astype(BF16)
        v[i] = part
        vt[i] = part.T
        for copy in kept(i, 0):
            copy.start()

    finish_weight(1)

    def attend(i):
        row_ids = lax.broadcasted_iota(jnp.int32, (128, chunk), 0)

        @pl.loop(0, width // 128)
        def _(pair):
            lanes = aligned(pair, 128)
            peaks = []
            for h in range(2):
                query = qt[i, lanes, :]
                query = jnp.where(row_ids // HEAD_DIM == h, query, jnp.zeros_like(query))
                peak = jnp.full((1, chunk), -jnp.inf, F32)
                for j in range(CHUNKS):
                    block = jnp.dot(k[j, :, lanes], query, preferred_element_type=F32)
                    scores[h, j] = block
                    peak = jnp.maximum(peak, jnp.max(block, axis=0, keepdims=True))
                peaks.append(peak * scale)
            outs = []
            for h in range(2):
                total = jnp.zeros((1, chunk), F32)
                acc = jnp.zeros((HEAD_DIM, chunk), F32)
                rows = pl.ds(pl.multiple_of(pair * 128 + h * HEAD_DIM, HEAD_DIM), HEAD_DIM)
                for j in range(CHUNKS):
                    weights = jnp.exp2(scores[h, j] * scale - peaks[h])
                    total = total + jnp.sum(weights, axis=0, keepdims=True)
                    acc = acc + jnp.dot(vt[j, rows, :], weights.astype(BF16), preferred_element_type=F32)
                outs.append(acc / total)
                lse[i, pl.ds(pair * 2 + h, 1), :] = peaks[h] + jnp.log2(total)
            out = jnp.concatenate(outs, axis=0).T
            mixf[i, :, lanes] = out
            mixed[i, :, lanes] = out.astype(BF16)

    def h1(i):
        slot = i % 2
        return remote(sb.at[slot, 1 - core], rb.at[i], h1_send.at[i], h1_recv.at[i], r, c_core)

    def h2(i):
        return remote(xb.at[i % 2], xr.at[i], h2_send.at[i], h2_recv.at[i], r, c_x)

    def h3(i, x, side):
        block = hid.at[i, :, aligned(x * 2 + side, width)]
        return remote(block, block, h3_send.at[i, x], h3_recv.at[i, x], r, c_core)

    @pl.loop(0, CHUNKS + 2)
    def _(i):
        @pl.when(i < CHUNKS)
        def _():
            x_copy(cot_all, cx_send, cx_recv, i, c).start()
            core_copy(cot_all, cc_send, cc_recv, i, 0, c).start()
            attend(i)
            for copy in kept(i, 1):
                copy.start()
            partial = jnp.dot(mixed[i], wo[...], preferred_element_type=F32)
            for x in range(2):
                for side in range(2):
                    block = x * 2 + side
                    sb[i % 2, side, x] = partial[:, block * width : (block + 1) * width].astype(BF16)
            h1(i).start()

        @pl.when(i == 1)
        def _():
            forward_weight(2)
            start_weight(3)

        @pl.when(i == 2)
        def _():
            finish_weight(2)

        @pl.when(i == 5)
        def _():
            forward_weight(3)

        @pl.when(i >= 2)
        def _():
            t = i - 2
            for x in range(2):
                h3(t, x, core).wait_send()
                h3(t, x, 1 - core).wait_recv()
            for part in range(7):
                rows = pl.ds(part * (chunk // 7), chunk // 7)
                units, _, inverse = row_norm(hid[t, rows, :])
                unit[t, rows, :] = units.astype(BF16)
                inv[t, rows, :] = jnp.broadcast_to(inverse, (chunk // 7, 128))
                norm_two[t, rows, :] = (units * vecs[3:4, :] + vecs[4:5, :]).astype(BF16)
            for n in range(we.shape[1] // 256):
                lanes = slice(n * 256, (n + 1) * 256)
                expanded = jnp.dot(norm_two[t], we[:, lanes], preferred_element_type=F32) + exp_bias[:, lanes]
                gate = 0.5 + 0.5 * lax.erf(expanded * (0.5 ** 0.5))
                act[t, :, lanes] = (expanded * gate).astype(BF16)
                bell = jnp.exp2(expanded * expanded * (-0.5 * LOG2E)) * 0.3989422804014327
                slope[t, :, lanes] = (gate + expanded * bell).astype(BF16)
            for copy in kept(t, 2):
                copy.start()
            keep_hid(t).start()

        @pl.when(i < CHUNKS)
        def _():
            h1(i).wait()
            for x in range(2):
                xb[i % 2, x] = (sb[i % 2, core, x].astype(F32) + rb[i, x].astype(F32)).astype(BF16)
            h2(i).start()

        @pl.when((i >= 1) & (i <= CHUNKS))
        def _():
            t = i - 1
            x_copy(cot_all, cx_send, cx_recv, t, c_x).wait_recv()
            core_copy(cot_all, cc_send, cc_recv, t, 1, c_x).start()
            h2(t).wait()
            for x in range(2):
                lanes = aligned(x * 2 + core, width)
                total = xb[t % 2, x].astype(F32) + xr[t, x].astype(F32)
                hid[t, :, lanes] = tok_all[t, :, lanes].astype(F32) + total + vecs[2:3, lanes]
            for x in range(2):
                h3(t, x, core).start()

    @pl.loop(0, CHUNKS)
    def _(i):
        x_copy(tok_all, tx_send, tx_recv, i, c).wait_send()
        x_copy(cot_all, cx_send, cx_recv, i, c).wait_send()
        core_copy(tok_all, tc_send, tc_recv, i, 0, c).wait_send()
        core_copy(tok_all, tc_send, tc_recv, i, 1, c_x).wait_send()
        core_copy(cot_all, cc_send, cc_recv, i, 0, c).wait_send()
        core_copy(cot_all, cc_send, cc_recv, i, 1, c_x).wait_send()
        core_copy(cot_all, cc_send, cc_recv, i, 0, c_core).wait_recv()
        core_copy(cot_all, cc_send, cc_recv, i, 1, c_far).wait_recv()
        for copy in kept(i, 3):
            copy.start()

    finish_weight(3)
    last = [
        keep(17, n, a, b)
        for n, (a, b) in enumerate(((win, win_o), (wo, wo_o), (we, we_o), (wr, wr_o), (vecs, vec_o)))
    ]
    for copy in last:
        copy.start()

    @pl.loop(0, CHUNKS)
    def _(i):
        for stage in range(4):
            for copy in kept(i, stage):
                copy.wait()
        keep_hid(i).wait()

    for copy in last:
        copy.wait()


def forward_call(tok, cot, vec, attn_bias, exp_bias, win_s, wo_s, we_s, wr_s):
    pairs, width = tok.shape[0], vec.shape[1]
    chunk = 2 * pairs // CHUNKS
    full = 4 * width
    hidden = we_s.shape[1]
    n = CHUNKS

    def sd(shape, dtype):
        return jax.ShapeDtypeStruct(shape, dtype)

    outs = [
        sd((n, chunk, full), BF16),
        sd((n, chunk, full), BF16),
        sd((n, chunk, width), BF16),
        sd((n, width, chunk), BF16),
        sd((n, chunk, width), BF16),
        sd((n, width, chunk), BF16),
        sd((n, chunk, width), BF16),
        sd((n, chunk, width), F32),
        sd((n, 8, chunk), F32),
        sd((n, chunk, width), F32),
        sd((n, chunk, full), BF16),
        sd((n, chunk, 128), F32),
        sd((n, chunk, full), BF16),
        sd((n, chunk, hidden), BF16),
        sd((n, chunk, hidden), BF16),
        sd((full, 3 * width), BF16),
        sd((width, full), BF16),
        sd((full, hidden), BF16),
        sd((hidden, full), BF16),
        sd((8, full), F32),
        sd((n, chunk, full), BF16),
        sd((n, chunk, 128), F32),
    ]
    vm = pltpu.VMEM
    dma = pltpu.SemaphoreType.DMA
    scratch = [
        vm((n, chunk, full), BF16), vm((n, chunk, full), BF16), vm((n, chunk, full), BF16),
        vm((n, chunk, width), BF16), vm((n, width, chunk), BF16),
        vm((n, chunk, width), BF16), vm((n, width, chunk), BF16),
        vm((n, chunk, width), BF16), vm((n, width, chunk), BF16),
        vm((n, chunk, width), BF16), vm((n, chunk, width), F32), vm((n, 8, chunk), F32),
        vm((n, chunk, full), F32), vm((n, chunk, full), BF16), vm((n, chunk, 128), F32),
        vm((n, chunk, full), BF16), vm((n, chunk, hidden), BF16), vm((n, chunk, hidden), BF16),
        vm((full, 3 * width), BF16), vm((width, full), BF16), vm((full, hidden), BF16), vm((hidden, full), BF16),
        vm((8, full), F32), vm((n, chunk, 128), F32),
        vm((2, n, chunk, chunk), F32),
        vm((2, 2, 2, chunk, width), BF16), vm((n, 2, chunk, width), BF16),
        vm((2, 2, chunk, width), BF16), vm((n, 2, chunk, width), BF16),
        dma((18, n)), dma((4, 3)), dma((4, 3)), dma((4, 4)), dma((4, 4)), dma((3,)), dma((3,)),
        dma((n,)), dma((n,)), dma((n, 2)), dma((n, 2)), dma((n,)), dma((n,)), dma((n, 2)), dma((n, 2)),
        dma((n,)), dma((n,)), dma((n,)), dma((n,)), dma((n, 2)), dma((n, 2)),
    ]
    return pl.pallas_call(
        forward_kernel,
        out_shape=outs,
        in_specs=[pl.BlockSpec(memory_space=pltpu.VMEM)] * 9,
        out_specs=[pl.BlockSpec(memory_space=pl.ANY)] * len(outs),
        scratch_shapes=scratch,
        compiler_params=pltpu.CompilerParams(
            collective_id=0, has_side_effects=True, vmem_limit_bytes=63 << 20
        ),
    )(tok, cot, vec, attn_bias, exp_bias, win_s, wo_s, we_s, wr_s)


GRAD_KINDS = ("rows", "cols", "rows", "cols")


def backward_kernel(
    tok_h, cot_h, q_h, qt_h, k_h, kt_h, v_h, mixf_h, lse_h, hid_h, unit_h, inv_h,
    normed_h, act_h, slope_h, win_h, wo_h, we_h, wr_h, vec_h, one_h, stat_h,
    out_o, tg_o, sums_o, gin_o, gout_o, gexp_o, gred_o,
    cot, q, qt, k, kt, v, mixf, lse, hid, unit, inv, normed, act, slope, win, wo, we, wr, vecs, stat,
    grad, dq, dk, dv, tg, out, sb_g, sb_o, rb_g, xr_g, rb_o, xr_o, xr_1, st, st_in,
    col_sums, hid_sums, packet, packets,
    ys_in, ys_out, ys_exp, ys_red, oh_in, oh_out, oh_exp, oh_red,
    yr_in, yr_out, yr_exp, yr_red, zr_in, zr_out, zr_exp, zr_red,
    gin, gout, gexp, gred,
    load_sem, store_sem, hid_sem, gy_send, gy_recv, gz_send, gz_recv,
    h1g_send, h1g_recv, h2g_send, h2g_recv, h3g_send, h3g_recv,
    h1o_send, h1o_recv, h2o_send, h2o_recv, h1t_send, h1t_recv, h2t_send, h2t_recv,
    st_send, st_recv, pk_send, pk_recv,
):
    r, c = lax.axis_index("row"), lax.axis_index("col")
    z, y = r // 2, r % 2
    xx, core = c // 2, c % 2
    c_x, c_core, c_far = (c + 2) % 4, c + 1 - 2 * core, (c + 2) % 4 + 1 - 2 * core
    r_y = r + 1 - 2 * y
    tok, one = act, normed
    chunk = q.shape[0] // CHUNKS
    half = chunk // 2
    width = q.shape[1]
    full = cot.shape[1]
    scale = LOG2E * HEAD_DIM ** (-0.5)
    own = aligned(c, width)
    others = [(r + step) % 8 for step in range(1, 8)]

    barrier = pltpu.get_barrier_semaphore()
    for col in (c_x, c_core, c_far):
        pl.semaphore_signal(barrier, inc=1, device_id=(r, col), device_id_type=MESH)
    for row in others:
        pl.semaphore_signal(barrier, inc=1, device_id=(row, c), device_id_type=MESH)

    loads = {}
    order = (
        ("wr", wr_h, wr), ("cot", cot_h, cot), ("slope", slope_h, slope), ("we", we_h, we), ("act", act_h, act),
        ("vec", vec_h, vecs), ("unit", unit_h, unit), ("inv", inv_h, inv), ("wo", wo_h, wo),
        ("normed", normed_h, normed), ("mixf", mixf_h, mixf), ("lse", lse_h, lse), ("qt", qt_h, qt), ("q", q_h, q),
        ("k", k_h, k), ("v", v_h, v), ("kt", kt_h, kt), ("win", win_h, win), ("stat", stat_h, stat),
        ("tok", tok_h, tok), ("one", one_h, one),
    )
    for n, (name, src, dst) in enumerate(order):
        loads[name] = pltpu.make_async_copy(src, dst, load_sem.at[n])
    late = ("tok", "one")
    for name, _, _ in order:
        if name not in late:
            loads[name].start()
    dk[...] = jnp.zeros_like(dk)
    dv[...] = jnp.zeros_like(dv)
    col_sums[...] = jnp.zeros_like(col_sums)
    hid_sums[...] = jnp.zeros_like(hid_sums)
    pl.semaphore_wait(barrier, 10)

    def rows_of(i):
        return pl.ds(pl.multiple_of(i * chunk, chunk), chunk)

    def h1(sb, rb, send, recv, i):
        return remote(sb.at[i % 2, 1 - core], rb.at[i], send.at[i], recv.at[i], r, c_core)

    def fill(sb, i, partial):
        for x in range(2):
            for side in range(2):
                block = x * 2 + side
                sb[i % 2, side, x] = partial[:, block * width : (block + 1) * width].astype(BF16)

    def merge(sb, rb, i):
        for x in range(2):
            rb[i, x] = (sb[i % 2, core, x].astype(F32) + rb[i, x].astype(F32)).astype(BF16)

    def h1g(i):
        return h1(sb_g, rb_g, h1g_send, h1g_recv, i)

    def h1o(i):
        return h1(sb_o, rb_o, h1o_send, h1o_recv, i)

    def h1t(i):
        return h1(sb_g, rb_g, h1t_send, h1t_recv, i)

    def h2g(i):
        return remote(rb_g.at[i], xr_g.at[i], h2g_send.at[i], h2g_recv.at[i], r, c_x)

    def h2o(i):
        return remote(rb_o.at[i, 1 - xx], xr_o.at[i], h2o_send.at[i], h2o_recv.at[i], r, c_x)

    def h2t(i):
        return remote(rb_g.at[i, 1 - xx], xr_1.at[i], h2t_send.at[i], h2t_recv.at[i], r, c_x)

    def h3g(i, x, side):
        block = grad.at[i % 4, :, aligned(x * 2 + side, width)]
        return remote(block, block, h3g_send.at[i, x], h3g_recv.at[i, x], r, c_core)

    def spread_grad(i):
        h2g(i).wait()
        for x in range(2):
            grad[i % 4, :, aligned(x * 2 + core, width)] = rb_g[i, x].astype(F32) + xr_g[i, x].astype(F32)
        for x in range(2):
            h3g(i, x, core).start()

    ys = (ys_in, ys_out, ys_exp, ys_red)
    oh = (oh_in, oh_out, oh_exp, oh_red)
    yr = (yr_in, yr_out, yr_exp, yr_red)
    zr = (zr_in, zr_out, zr_exp, zr_red)

    def gy(w, s):
        return remote(ys[w].at[s], yr[w].at[s], gy_send.at[w, s], gy_recv.at[w, s], r_y, c)

    def gz(w, s):
        target = ((z + 1 + s) % 4) * 2 + y
        return remote(oh[w].at[s], zr[w].at[s], gz_send.at[w, s], gz_recv.at[w, s], target, c)

    def grad_block(w, s, left, right):
        zt = (z + 1 + s) % 4
        lanes = aligned(zt, 256)
        if GRAD_KINDS[w] == "rows":
            block = lax.dot_general(left[:, lanes], right, TN_DIMS, preferred_element_type=F32).astype(BF16)
            low, high = block[0:128, :], block[128:256, :]
        else:
            block = lax.dot_general(left, right[:, lanes], TN_DIMS, preferred_element_type=F32).astype(BF16)
            low, high = block[:, 0:128], block[:, 128:256]

        @pl.when(y == 0)
        def _():
            oh[w][s] = low
            ys[w][s] = high

        @pl.when(y == 1)
        def _():
            oh[w][s] = high
            ys[w][s] = low

        gy(w, s).start()

    def pass_on(w, s):
        gy(w, s).wait()
        oh[w][s] = (oh[w][s].astype(F32) + yr[w][s].astype(F32)).astype(BF16)
        gz(w, s).start()

    def finish_grad(w, dst):
        gy(w, 3).wait()
        total = oh[w][3].astype(F32) + yr[w][3].astype(F32)
        for s in range(3):
            gz(w, s).wait()
            total = total + zr[w][s].astype(F32)
        dst[...] = total

    loads["wr"].wait()
    loads["cot"].wait()
    loads["slope"].wait()
    loads["we"].wait()
    loads["act"].wait()

    @pl.loop(0, CHUNKS + 1)
    def _(i):
        @pl.when(i < CHUNKS)
        def _():
            rows = rows_of(i)
            for n in range(slope.shape[1] // 256):
                lanes = slice(n * 256, (n + 1) * 256)
                grad_act = lax.dot_general(cot[rows, :], wr[lanes, :], NT_DIMS, preferred_element_type=F32)
                low = (slope[rows, lanes].astype(F32) * grad_act).astype(BF16)
                slope[rows, lanes] = low
                hid_sums[0:1, lanes] += jnp.sum(low.astype(F32), axis=0, keepdims=True)
            fill(sb_g, i, lax.dot_general(slope[rows, :], we[...], NT_DIMS, preferred_element_type=F32))
            h1g(i).start()

        @pl.when(i >= 1)
        def _():
            h1o(i - 1).wait()
            merge(sb_o, rb_o, i - 1)

        @pl.when(i < CHUNKS)
        def _():
            rows = rows_of(i)
            fill(sb_o, i, jnp.dot(act[rows, :], wr[...], preferred_element_type=F32))
            h1o(i).start()
            h1g(i).wait()
            merge(sb_g, rb_g, i)
            h2g(i).start()
            col_sums[0:1, :] += jnp.sum(cot[rows, :].astype(F32), axis=0, keepdims=True)

    loads["normed"].wait()
    for s in range(3):
        grad_block(3, s, act[...], cot)
    spread_grad(0)
    for s in range(3):
        grad_block(2, s, normed, slope[...])
    spread_grad(1)
    grad_block(3, 3, act[...], cot)
    grad_block(2, 3, normed, slope[...])
    for name in late:
        loads[name].start()
    for name in ("unit", "inv", "vec", "wo", "mixf", "lse", "qt", "q", "k", "v", "kt", "win", "stat"):
        loads[name].wait()

    def hid_load(i):
        return pltpu.make_async_copy(hid_h.at[rows_of(i), :], hid.at[i % 2], hid_sem.at[i])

    def out_store(i, s):
        return pltpu.make_async_copy(
            out.at[i % 2, s], out_o.at[pl.ds(pl.multiple_of(i * half, half), half), pl.ds(s * width, width)],
            store_sem.at[0, i, s],
        )

    def tg_store(i, s):
        return pltpu.make_async_copy(
            tg.at[i, s], tg_o.at[pl.ds(pl.multiple_of(i * half, half), half), pl.ds(s * width, width)],
            store_sem.at[1, i, s],
        )

    def attend_back(i):
        rows = rows_of(i)
        go = lax.dot_general(unit[rows, :], wo[...], NT_DIMS, preferred_element_type=F32).astype(BF16)
        inner = (go.astype(F32) * mixf[rows, :]).T
        go_t = go.T
        row_ids = lax.broadcasted_iota(jnp.int32, (128, chunk), 0)
        lane_ids = lax.broadcasted_iota(jnp.int32, (chunk, 128), 1)
        for pair in range(width // 128):
            lanes = slice(pair * 128, (pair + 1) * 128)
            queries, grads, query_rows, grad_rows, deltas, logs = [], [], [], [], [], []
            for h in range(2):
                pick = row_ids // HEAD_DIM == h
                value = qt[i, lanes, :]
                queries.append(jnp.where(pick, value, jnp.zeros_like(value)))
                value = go_t[lanes, :]
                grads.append(jnp.where(pick, value, jnp.zeros_like(value)))
                pick = lane_ids // HEAD_DIM == h
                value = q[rows, lanes]
                query_rows.append(jnp.where(pick, value, jnp.zeros_like(value)))
                value = go[:, lanes]
                grad_rows.append(jnp.where(pick, value, jnp.zeros_like(value)))
                first = pair * 128 + h * HEAD_DIM
                deltas.append(jnp.sum(inner[first : first + HEAD_DIM, :], axis=0, keepdims=True))
                logs.append(lse[i, pair * 2 + h : pair * 2 + h + 1, :])

            def step(j, query_grads):
                keys = rows_of(j)
                key_block = k[keys, lanes]
                value_block = v[keys, lanes]
                key_sum = dk[keys, lanes]
                value_sum = dv[keys, lanes]
                results = []
                for h in range(2):
                    block = jnp.dot(key_block, queries[h], preferred_element_type=F32)
                    probs = jnp.exp2(block * scale - logs[h])
                    grad_probs = jnp.dot(value_block, grads[h], preferred_element_type=F32)
                    grad_scores = (probs * (grad_probs - deltas[h])).astype(BF16)
                    value_sum = value_sum + jnp.dot(probs.astype(BF16), grad_rows[h], preferred_element_type=F32)
                    key_sum = key_sum + jnp.dot(grad_scores, query_rows[h], preferred_element_type=F32)
                    first = pair * 128 + h * HEAD_DIM
                    results.append(
                        query_grads[h]
                        + jnp.dot(kt[j, first : first + HEAD_DIM, :], grad_scores, preferred_element_type=F32)
                    )
                dk[keys, lanes] = key_sum
                dv[keys, lanes] = value_sum
                return tuple(results)

            empty = jnp.zeros((HEAD_DIM, chunk), F32)
            parts = lax.fori_loop(0, CHUNKS, step, (empty, empty))
            query_grad = (jnp.concatenate(parts, axis=0).T * HEAD_DIM ** (-0.5)).astype(BF16)
            dq[rows, lanes] = query_grad

    def finish_out(i):
        h2o(i).wait()
        hid_load(i).wait()
        total = rb_o[i, xx].astype(F32) + xr_o[i].astype(F32)
        value = (hid[i % 2] + total + vecs[5:6, own]).astype(BF16)
        for s in range(2):
            out[i % 2, s] = value[s * half : (s + 1) * half, :]
        for s in range(2):
            out_store(i, s).start()

    @pl.loop(0, CHUNKS)
    def _(i):
        h2o(i).start()
        hid_load(i).start()
        for x in range(2):
            h3g(i, x, core).wait_send()
            h3g(i, x, 1 - core).wait_recv()
        step_rows = chunk // 7
        for part in range(7):
            rows = pl.ds(pl.multiple_of(i * chunk + part * step_rows, step_rows), step_rows)
            span = slice(part * step_rows, (part + 1) * step_rows)
            incoming = grad[i % 4, span, :]
            units = unit[rows, :].astype(F32)
            scaled = incoming * vecs[3:4, :]
            plain = jnp.mean(scaled, axis=1, keepdims=True)
            cross = jnp.mean(scaled * units, axis=1, keepdims=True)
            total = cot[rows, :].astype(F32) + inv[rows, 0:1] * (scaled - plain - units * cross)
            low = total.astype(BF16)
            col_sums[1:2, :] += jnp.sum(incoming * units, axis=0, keepdims=True)
            col_sums[2:3, :] += jnp.sum(incoming, axis=0, keepdims=True)
            col_sums[3:4, :] += jnp.sum(low.astype(F32), axis=0, keepdims=True)
            unit[rows, :] = low
            grad[i % 4, span, :] = total
        for s in range(2):
            tg[i, s] = grad[i % 4, s * half : (s + 1) * half, own]
        attend_back(i)

        @pl.when(i + 2 < CHUNKS)
        def _():
            spread_grad(i + 2)

        for s in range(3):
            @pl.when(i == s)
            def _():
                pass_on(3, s)

            @pl.when(i == s + 3)
            def _():
                pass_on(2, s)

        @pl.when(i >= 1)
        def _():
            @pl.when(i >= 3)
            def _():
                for s in range(2):
                    out_store(i - 3, s).wait()
            finish_out(i - 1)

    for s in range(2):
        out_store(CHUNKS - 3, s).wait()
    finish_out(CHUNKS - 1)

    for i in range(CHUNKS):
        rows = pl.ds(i * chunk, chunk)
        k[rows, :] = (dk[rows, :] * HEAD_DIM ** (-0.5)).astype(BF16)
        low = dv[rows, :].astype(BF16)
        v[rows, :] = low
        col_sums[4:5, 0:width] += jnp.sum(dq[rows, :].astype(F32), axis=0, keepdims=True)
        col_sums[5:6, 0:width] += jnp.sum(low.astype(F32), axis=0, keepdims=True)
    for name in late:
        loads[name].wait()

    def inward_block(s):
        zt = (z + 1 + s) % 4
        left = one[:, aligned(zt, 256)]
        for n, right in enumerate((dq, k, v)):
            lanes = slice(n * width, (n + 1) * width)
            block = lax.dot_general(left, right[...], TN_DIMS, preferred_element_type=F32).astype(BF16)

            @pl.when(y == 0)
            def _():
                oh_in[s, :, lanes] = block[0:128, :]
                ys_in[s, :, lanes] = block[128:256, :]

            @pl.when(y == 1)
            def _():
                oh_in[s, :, lanes] = block[128:256, :]
                ys_in[s, :, lanes] = block[0:128, :]

        gy(0, s).start()

    for s in range(3):
        inward_block(s)

    def stat_copy(i, slot, target):
        return remote(st.at[i], st_in.at[i, slot], st_send.at[i, slot], st_recv.at[i, slot], r, target)

    lane_ids = lax.broadcasted_iota(jnp.int32, (chunk, 128), 1)
    gain = vecs[0:1, :]

    @pl.loop(0, CHUNKS + 2)
    def _(i):
        @pl.when(i < CHUNKS)
        def _():
            rows = rows_of(i)
            partial = lax.dot_general(dq[rows, :], win[:, 0:width], NT_DIMS, preferred_element_type=F32)
            partial = partial + lax.dot_general(
                k[rows, :], win[:, width : 2 * width], NT_DIMS, preferred_element_type=F32
            )
            partial = partial + lax.dot_general(
                v[rows, :], win[:, 2 * width : 3 * width], NT_DIMS, preferred_element_type=F32
            )
            fill(sb_g, i, partial)
            h1t(i).start()
            units = (tok[rows, :].astype(F32) - stat[rows, 0:1]) * stat[rows, 64:65]
            scaled = partial * gain
            plain = jnp.sum(scaled, axis=1, keepdims=True)
            cross = jnp.sum(scaled * units, axis=1, keepdims=True)
            both = jnp.where(lane_ids == 0, plain, jnp.where(lane_ids == 1, cross, 0.0))
            st[i] = both.T[0:8, :]
            for slot, target in enumerate((c_x, c_core, c_far)):
                stat_copy(i, slot, target).start()
            h1t(i).wait()
            merge(sb_g, rb_g, i)
            h2t(i).start()

        for s in range(3):
            @pl.when(i == s + 1)
            def _():
                pass_on(0, s)

        @pl.when(i == 4)
        def _():
            for s in range(3):
                grad_block(1, s, mixf[...].astype(BF16), unit)

        @pl.when(i == 5)
        def _():
            inward_block(3)
            grad_block(1, 3, mixf[...].astype(BF16), unit)

        @pl.when(i == 6)
        def _():
            for s in range(3):
                pass_on(1, s)

        @pl.when(i >= 2)
        def _():
            t = i - 2
            rows = rows_of(t)
            h2t(t).wait()
            total = st[t]
            for slot, target in enumerate((c_x, c_core, c_far)):
                stat_copy(t, slot, target).wait()
                total = total + st_in[t, slot]
            columns = jnp.concatenate([total, jnp.zeros((120, chunk), F32)], axis=0).T
            plain = columns[:, 0:1] / full
            cross = columns[:, 1:2] / full
            incoming = rb_g[t, xx].astype(F32) + xr_1[t].astype(F32)
            inverse = stat[rows, 64:65]
            units = (tok[rows, own].astype(F32) - stat[rows, 0:1]) * inverse
            back = inverse * (incoming * vecs[0:1, own] - plain - units * cross)
            for s in range(2):
                tg[t, s] = tg[t, s] + back[s * half : (s + 1) * half, :]
            for s in range(2):
                tg_store(t, s).start()
            col_sums[6:7, 0:width] += jnp.sum(incoming * units, axis=0, keepdims=True)
            col_sums[7:8, 0:width] += jnp.sum(incoming, axis=0, keepdims=True)

    packet[0:1, :] = col_sums[6:7, 0:width]
    packet[1:2, :] = col_sums[7:8, 0:width]
    packet[2:4, :] = col_sums[4:6, 0:width]
    packet[4:5, :] = col_sums[3:4, own]
    packet[5:7, :] = col_sums[1:3, own]
    packet[7:8, :] = col_sums[0:1, own]
    for n in range(4):
        packet[8 + n : 9 + n, :] = hid_sums[0:1, n * width : (n + 1) * width]

    def packet_copy(step):
        return remote(packet, packets.at[step], pk_send.at[step], pk_recv.at[step], others[step], c)

    for step in range(7):
        packet_copy(step).start()
    finish_grad(3, gred)
    finish_grad(2, gexp)
    finish_grad(0, gin)
    finish_grad(1, gout)
    stores = [
        pltpu.make_async_copy(src, dst, store_sem.at[2, n, 0])
        for n, (src, dst) in enumerate(((gin, gin_o), (gout, gout_o), (gexp, gexp_o), (gred, gred_o)))
    ]
    for copy in stores:
        copy.start()
    total = packet[...]
    for step in range(7):
        packet_copy(step).wait()
        total = total + packets[step]
    packet[...] = total
    copy = pltpu.make_async_copy(packet, sums_o, store_sem.at[2, 4, 0])
    copy.start()
    copy.wait()
    for copy in stores:
        copy.wait()
    for i in range(CHUNKS - 2, CHUNKS):
        for s in range(2):
            out_store(i, s).wait()

    @pl.loop(0, CHUNKS)
    def _(i):
        for s in range(2):
            tg_store(i, s).wait()


def backward_call(*arrays):
    (tok, cot, q, qt, k, kt, v, mixf, lse, hid, unit, inv, normed, act, slope, win, wo, we, wr, vec, one, stat) = arrays
    rows, width = q.shape
    full, hidden = we.shape
    n, chunk = CHUNKS, rows // CHUNKS
    half = chunk // 2
    pairs = rows // 2

    def sd(shape, dtype):
        return jax.ShapeDtypeStruct(shape, dtype)

    outs = [
        sd((pairs, 2 * width), BF16), sd((pairs, 2 * width), F32), sd((16, width), F32),
        sd((128, 3 * width), F32), sd((width, 128), F32), sd((128, hidden), F32), sd((hidden, 128), F32),
    ]
    vm = pltpu.VMEM
    dma = pltpu.SemaphoreType.DMA

    def shapes(lead):
        return [
            vm((lead, 128, 3 * width), BF16), vm((lead, width, 128), BF16),
            vm((lead, 128, hidden), BF16), vm((lead, hidden, 128), BF16),
        ]

    def like(array):
        return vm(array.shape, array.dtype)

    scratch = [
        like(cot), like(q), like(qt), like(k), like(kt), like(v), like(mixf), like(lse),
        vm((2, chunk, width), F32),
        like(unit), like(inv), like(normed), like(act), like(slope),
        like(win), like(wo), like(we), like(wr), like(vec), like(stat),
        vm((4, chunk, full), F32), vm((rows, width), BF16), vm((rows, width), F32), vm((rows, width), F32),
        vm((n, 2, half, width), F32), vm((2, 2, half, width), BF16),
        vm((2, 2, 2, chunk, width), BF16), vm((2, 2, 2, chunk, width), BF16),
        vm((n, 2, chunk, width), BF16), vm((n, 2, chunk, width), BF16),
        vm((n, 2, chunk, width), BF16), vm((n, chunk, width), BF16), vm((n, chunk, width), BF16),
        vm((n, 8, chunk), F32), vm((n, 3, 8, chunk), F32),
        vm((8, full), F32), vm((8, hidden), F32), vm((16, width), F32), vm((7, 16, width), F32),
        *shapes(4), *shapes(4), *shapes(4), *shapes(3),
        vm((128, 3 * width), F32), vm((width, 128), F32), vm((128, hidden), F32), vm((hidden, 128), F32),
        dma((21,)), dma((3, n, 2)), dma((n,)), dma((4, 4)), dma((4, 4)), dma((4, 3)), dma((4, 3)),
        dma((n,)), dma((n,)), dma((n,)), dma((n,)), dma((n, 2)), dma((n, 2)),
        dma((n,)), dma((n,)), dma((n,)), dma((n,)), dma((n,)), dma((n,)), dma((n,)), dma((n,)),
        dma((n, 3)), dma((n, 3)), dma((7,)), dma((7,)),
    ]
    return pl.pallas_call(
        backward_kernel,
        out_shape=outs,
        in_specs=[pl.BlockSpec(memory_space=pl.ANY)] * len(arrays),
        out_specs=[pl.BlockSpec(memory_space=pl.ANY)] * len(outs),
        scratch_shapes=scratch,
        compiler_params=pltpu.CompilerParams(
            collective_id=1, has_side_effects=True, vmem_limit_bytes=63 << 20
        ),
    )(*arrays)


CONTRACT_ROWS = (((0,), (0,)), ((), ()))
CONTRACT_COLS = (((1,), (1,)), ((), ()))


def norm_forward(values, gain, shift, full_width):
    row_total = lax.psum(jnp.sum(values, axis=1), "col")
    centred = values - (row_total / full_width)[:, None]
    row_square = lax.psum(jnp.sum(centred * centred, axis=1), "col")
    inverse = lax.rsqrt(row_square / full_width + EPSILON)
    unit_rows = centred * inverse[:, None]
    return (unit_rows, inverse, unit_rows * gain + shift)


def norm_backward(incoming, unit_rows, inverse, gain, full_width):
    scaled = incoming * gain
    plain_sum, cross_sum = lax.psum(
        (jnp.sum(scaled, axis=1), jnp.sum(scaled * unit_rows, axis=1)), "col"
    )
    result = inverse[:, None] * (
        scaled - (plain_sum / full_width)[:, None] - unit_rows * (cross_sum / full_width)[:, None]
    )
    return (result, jnp.sum(incoming * unit_rows, axis=0), jnp.sum(incoming, axis=0))


def spread_features(values):
    return lax.all_gather(values, "col", axis=1, tiled=True)


def sum_partials(values):
    return lax.psum_scatter(values, "col", scatter_dimension=1, tiled=True)


def spread_grads(values):
    return lax.all_gather(values, "col", axis=1, tiled=True)


def sum_grad_partials(values):
    return lax.psum_scatter(values, "col", scatter_dimension=1, tiled=True)


def fetch_weights(inward_weight, output_weight, expand_weight, reduce_weight):
    return (
        lax.all_gather(inward_weight, "row", axis=0, tiled=True),
        lax.all_gather(output_weight, "row", axis=1, tiled=True),
        lax.all_gather(expand_weight, "row", axis=0, tiled=True),
        lax.all_gather(reduce_weight, "row", axis=1, tiled=True),
    )


def attend_clip(queries, key_rows, value_rows, score_scale):
    seq_len = queries.shape[0]
    blocks = queries.reshape((2, seq_len // 2) + queries.shape[1:])

    def one_block(query_part):
        scores = (
            jnp.einsum("qhd,khd->hqk", query_part, key_rows, preferred_element_type=jnp.float32)
            * score_scale
        )
        row_peak = jnp.max(scores, axis=-1, keepdims=True)
        exponent = jnp.exp(scores - row_peak)
        row_sum = jnp.sum(exponent, axis=-1, keepdims=True)
        prob_low = (exponent / row_sum).astype(jnp.bfloat16)
        mixed_rows = jnp.einsum(
            "hqk,khd->qhd", prob_low, value_rows, preferred_element_type=jnp.float32
        )
        return (mixed_rows, (row_peak + jnp.log(row_sum))[..., 0])

    mixed_rows, logsum = lax.map(one_block, blocks)
    return (mixed_rows.reshape(queries.shape), logsum)


def attend_clip_back(queries, key_rows, value_rows, logsum, grad_out, score_scale):
    seq_len = queries.shape[0]
    block_shape = (2, seq_len // 2) + queries.shape[1:]

    def step_block(carry, pieces):
        key_acc, value_acc = carry
        query_part, grad_part, log_part = pieces
        scores = (
            jnp.einsum("qhd,khd->hqk", query_part, key_rows, preferred_element_type=jnp.float32)
            * score_scale
        )
        probs = jnp.exp(scores - log_part[..., None])
        grad_probs = jnp.einsum(
            "qhd,khd->hqk", grad_part, value_rows, preferred_element_type=jnp.float32
        )
        inner_sum = jnp.sum(probs * grad_probs, axis=-1, keepdims=True)
        grad_scores = (probs * (grad_probs - inner_sum)).astype(jnp.bfloat16)
        query_grad = (
            jnp.einsum("hqk,khd->qhd", grad_scores, key_rows, preferred_element_type=jnp.float32)
            * score_scale
        )
        key_acc = key_acc + jnp.einsum(
            "hqk,qhd->khd", grad_scores, query_part, preferred_element_type=jnp.float32
        )
        value_acc = value_acc + jnp.einsum(
            "hqk,qhd->khd",
            probs.astype(jnp.bfloat16),
            grad_part,
            preferred_element_type=jnp.float32,
        )
        return ((key_acc, value_acc), query_grad)

    zero_acc = jnp.zeros(key_rows.shape, jnp.float32)
    (key_acc, value_acc), query_grads = lax.scan(
        step_block,
        (zero_acc, zero_acc),
        (queries.reshape(block_shape), grad_out.reshape(block_shape), logsum),
    )
    return (query_grads.reshape(queries.shape), key_acc * score_scale, value_acc)


def forward_pass(
    tokens,
    first_gain,
    first_shift,
    attention_bias,
    output_bias,
    second_gain,
    second_shift,
    expand_bias,
    reduce_bias,
    gathered,
):
    inward_all, output_rows, expand_all, reduce_rows = gathered
    full_width = inward_all.shape[0]
    local_width = inward_all.shape[2]
    row_count = tokens.shape[0]
    clip_shape = (row_count // SEQ, SEQ, local_width // HEAD_DIM, HEAD_DIM)
    score_scale = HEAD_DIM ** (-0.5)
    source = tokens.astype(jnp.float32)
    unit_one, inverse_one, normed_one = norm_forward(source, first_gain, first_shift, full_width)
    normed_all = spread_features(normed_one.astype(jnp.bfloat16))
    projected = jnp.dot(
        normed_all,
        inward_all.reshape(full_width, 3 * local_width),
        preferred_element_type=jnp.float32,
    )
    projected = projected.reshape(row_count, 3, local_width)
    queries = (projected[:, 0] + attention_bias[0]).astype(jnp.bfloat16)
    key_rows = projected[:, 1].astype(jnp.bfloat16)
    value_rows = (projected[:, 2] + attention_bias[1]).astype(jnp.bfloat16)
    mixed_rows, logsum = lax.map(
        lambda clip_parts: attend_clip(clip_parts[0], clip_parts[1], clip_parts[2], score_scale),
        (queries.reshape(clip_shape), key_rows.reshape(clip_shape), value_rows.reshape(clip_shape)),
    )
    mixed_low = mixed_rows.reshape(row_count, local_width).astype(jnp.bfloat16)
    hidden_state = (
        source
        + sum_partials(jnp.dot(mixed_low, output_rows, preferred_element_type=jnp.float32))
        + output_bias
    )
    unit_two, inverse_two, normed_two = norm_forward(
        hidden_state, second_gain, second_shift, full_width
    )
    normed_all_two = spread_features(normed_two.astype(jnp.bfloat16))
    expanded = jnp.dot(normed_all_two, expand_all, preferred_element_type=jnp.float32) + expand_bias
    activated = jax.nn.gelu(expanded, approximate=False).astype(jnp.bfloat16)
    output_value = (
        hidden_state
        + sum_partials(jnp.dot(activated, reduce_rows, preferred_element_type=jnp.float32))
        + reduce_bias
    )
    saved_state = (
        unit_one,
        inverse_one,
        normed_all,
        queries,
        key_rows,
        value_rows,
        logsum,
        mixed_low,
        unit_two,
        inverse_two,
        normed_all_two,
        expanded,
        activated,
    )
    return (output_value, saved_state)


def plain_device(
    tokens,
    first_gain,
    first_shift,
    inward_weight,
    attention_bias,
    output_weight,
    output_bias,
    second_gain,
    second_shift,
    expand_weight,
    expand_bias,
    reduce_weight,
    reduce_bias,
    cotangent,
):
    packed_width = tokens.shape[1]
    tokens = tokens.reshape(-1, packed_width // 2)
    cotangent = cotangent.reshape(-1, packed_width // 2)
    gathered = fetch_weights(inward_weight, output_weight, expand_weight, reduce_weight)
    output_value, saved_state = forward_pass(
        tokens,
        first_gain,
        first_shift,
        attention_bias,
        output_bias,
        second_gain,
        second_shift,
        expand_bias,
        reduce_bias,
        gathered,
    )
    gathered = fetch_weights(inward_weight, output_weight, expand_weight, reduce_weight)
    unused_value, saved_state = forward_pass(
        tokens,
        first_gain,
        first_shift,
        attention_bias,
        output_bias,
        second_gain,
        second_shift,
        expand_bias,
        reduce_bias,
        gathered,
    )
    inward_all, output_rows, expand_all, reduce_rows = gathered
    (
        unit_one,
        inverse_one,
        normed_all,
        queries,
        key_rows,
        value_rows,
        logsum,
        mixed_low,
        unit_two,
        inverse_two,
        normed_all_two,
        expanded,
        activated,
    ) = saved_state
    full_width = inward_all.shape[0]
    local_width = inward_all.shape[2]
    row_count = tokens.shape[0]
    clip_shape = (row_count // SEQ, SEQ, local_width // HEAD_DIM, HEAD_DIM)
    score_scale = HEAD_DIM ** (-0.5)
    grad_rows = cotangent.astype(jnp.float32)
    grad_all = spread_grads(cotangent)
    grad_act = lax.dot_general(
        grad_all, reduce_rows, CONTRACT_COLS, preferred_element_type=jnp.float32
    )
    reduce_grad = lax.dot_general(
        activated, grad_all, CONTRACT_ROWS, preferred_element_type=jnp.float32
    )
    reduce_bias_grad = jnp.sum(grad_rows, axis=0)
    gelu_value, gelu_back = jax.vjp(
        lambda inner_value: jax.nn.gelu(inner_value, approximate=False), expanded
    )
    grad_expanded = gelu_back(grad_act)[0].astype(jnp.bfloat16)
    expand_grad = lax.dot_general(
        normed_all_two, grad_expanded, CONTRACT_ROWS, preferred_element_type=jnp.float32
    )
    expand_bias_grad = jnp.sum(grad_expanded.astype(jnp.float32), axis=0)
    grad_normed_two = sum_grad_partials(
        lax.dot_general(
            grad_expanded, expand_all, CONTRACT_COLS, preferred_element_type=jnp.float32
        )
    )
    back_two, second_gain_grad, second_shift_grad = norm_backward(
        grad_normed_two, unit_two, inverse_two, second_gain, full_width
    )
    grad_hidden = grad_rows + back_two
    grad_hidden_low = grad_hidden.astype(jnp.bfloat16)
    grad_hidden_all = spread_grads(grad_hidden_low)
    output_grad = lax.dot_general(
        mixed_low, grad_hidden_all, CONTRACT_ROWS, preferred_element_type=jnp.float32
    )
    output_bias_grad = jnp.sum(grad_hidden_low.astype(jnp.float32), axis=0)
    grad_mixed = lax.dot_general(
        grad_hidden_all, output_rows, CONTRACT_COLS, preferred_element_type=jnp.float32
    ).astype(jnp.bfloat16)
    query_grads, key_grads, value_grads = lax.map(
        lambda clip_parts: attend_clip_back(
            clip_parts[0], clip_parts[1], clip_parts[2], clip_parts[3], clip_parts[4], score_scale
        ),
        (
            queries.reshape(clip_shape),
            key_rows.reshape(clip_shape),
            value_rows.reshape(clip_shape),
            logsum,
            grad_mixed.reshape(clip_shape),
        ),
    )
    stacked = jnp.stack(
        [
            query_grads.reshape(row_count, local_width),
            key_grads.reshape(row_count, local_width),
            value_grads.reshape(row_count, local_width),
        ],
        axis=1,
    ).astype(jnp.bfloat16)
    attention_bias_grad = jnp.stack(
        [
            jnp.sum(stacked[:, 0].astype(jnp.float32), axis=0),
            jnp.sum(stacked[:, 2].astype(jnp.float32), axis=0),
        ]
    )
    flat_grads = stacked.reshape(row_count, 3 * local_width)
    inward_grad = lax.dot_general(
        normed_all, flat_grads, CONTRACT_ROWS, preferred_element_type=jnp.float32
    ).reshape(full_width, 3, local_width)
    grad_normed_one = sum_grad_partials(
        lax.dot_general(
            flat_grads,
            inward_all.reshape(full_width, 3 * local_width),
            CONTRACT_COLS,
            preferred_element_type=jnp.float32,
        )
    )
    back_one, first_gain_grad, first_shift_grad = norm_backward(
        grad_normed_one, unit_one, inverse_one, first_gain, full_width
    )
    tokens_grad = grad_hidden + back_one
    inward_grad, output_grad, expand_grad, reduce_grad = (
        lax.psum_scatter(
            inward_grad.astype(jnp.bfloat16), "row", scatter_dimension=0, tiled=True
        ).astype(jnp.float32),
        lax.psum_scatter(
            output_grad.astype(jnp.bfloat16), "row", scatter_dimension=1, tiled=True
        ).astype(jnp.float32),
        lax.psum_scatter(
            expand_grad.astype(jnp.bfloat16), "row", scatter_dimension=0, tiled=True
        ).astype(jnp.float32),
        lax.psum_scatter(
            reduce_grad.astype(jnp.bfloat16), "row", scatter_dimension=1, tiled=True
        ).astype(jnp.float32),
    )
    (
        first_gain_grad,
        first_shift_grad,
        attention_bias_grad,
        output_bias_grad,
        second_gain_grad,
        second_shift_grad,
        expand_bias_grad,
        reduce_bias_grad,
    ) = lax.psum(
        (
            first_gain_grad,
            first_shift_grad,
            attention_bias_grad,
            output_bias_grad,
            second_gain_grad,
            second_shift_grad,
            expand_bias_grad,
            reduce_bias_grad,
        ),
        "row",
    )
    return (
        output_value.astype(jnp.bfloat16).reshape(-1, packed_width),
        tokens_grad.reshape(-1, packed_width),
        first_gain_grad,
        first_shift_grad,
        inward_grad,
        attention_bias_grad,
        output_grad,
        output_bias_grad,
        second_gain_grad,
        second_shift_grad,
        expand_grad,
        expand_bias_grad,
        reduce_grad,
        reduce_bias_grad,
    )


def fused_device(
    tokens,
    first_gain,
    first_shift,
    inward_weight,
    attention_bias,
    output_weight,
    output_bias,
    second_gain,
    second_shift,
    expand_weight,
    expand_bias,
    reduce_weight,
    reduce_bias,
    cotangent,
):
    empty = jnp.zeros_like(first_gain)
    vectors = jnp.stack(
        [first_gain, first_shift, output_bias, second_gain, second_shift, reduce_bias, empty, empty]
    )
    kept = forward_call(
        tokens,
        cotangent,
        vectors,
        attention_bias,
        expand_bias[None],
        inward_weight.reshape(inward_weight.shape[0], -1),
        output_weight,
        expand_weight,
        reduce_weight,
    )
    (tok, cot, q, qt, k, kt, v, mixf, lse, hid, unit, inv, normed, act, slope, win, wo, we, wr, vec, one, stat) = kept

    def flat(array):
        return array.reshape(-1, array.shape[-1])

    outs = backward_call(
        flat(tok), flat(cot), flat(q), qt, flat(k), kt, flat(v), flat(mixf), lse, flat(hid), flat(unit), flat(inv),
        flat(normed), flat(act), flat(slope), win, wo, we, wr, vec, flat(one), flat(stat),
    )
    layer_output, tokens_grad, sums, inward_grad, output_grad, expand_grad, reduce_grad = outs
    return (
        layer_output,
        tokens_grad,
        sums[0],
        sums[1],
        inward_grad.reshape(inward_weight.shape),
        sums[2:4],
        output_grad,
        sums[4],
        sums[5],
        sums[6],
        expand_grad,
        sums[8:12].reshape(-1),
        reduce_grad,
        sums[7],
    )


def per_device(rows, cols, *arrays):
    tokens, inward_weight, expand_weight = arrays[0], arrays[3], arrays[9]
    fits = (
        (rows, cols) == (8, 4)
        and tokens.shape == (SEQ // 2, 512)
        and inward_weight.shape == (128, 3, 256)
        and expand_weight.shape == (128, 1024)
    )
    return fused_device(*arrays) if fits else plain_device(*arrays)


def solution(mesh):
    in_specs = (
        P("row", "col"),
        P("col"),
        P("col"),
        P("row", None, "col"),
        P(None, "col"),
        P("col", "row"),
        P("col"),
        P("col"),
        P("col"),
        P("row", "col"),
        P("col"),
        P("col", "row"),
        P("col"),
        P("row", "col"),
    )
    out_specs = (
        P("row", "col"),
        P("row", "col"),
        P("col"),
        P("col"),
        P("row", None, "col"),
        P(None, "col"),
        P("col", "row"),
        P("col"),
        P("col"),
        P("col"),
        P("row", "col"),
        P("col"),
        P("col", "row"),
        P("col"),
    )
    return jax.shard_map(
        functools.partial(per_device, mesh.shape["row"], mesh.shape["col"]),
        mesh=mesh, in_specs=in_specs, out_specs=out_specs, check_vma=False
    )
```

```python
import functools
import jax
import jax.numpy as jnp
from jax import lax
from jax.experimental import pallas as pl
from jax.experimental.pallas import tpu as pltpu
from jax.sharding import PartitionSpec as P

HEAD_DIM = 64
SEQ = 1568
EPSILON = 1e-06
CHUNKS = 7
EARLY = 3
F32 = jnp.float32
BF16 = jnp.bfloat16
MESH = pl.DeviceIdType.MESH
LOG2E = 1.4426950408889634
NT_DIMS = (((1,), (1,)), ((), ()))
TN_DIMS = (((0,), (0,)), ((), ()))


def remote(src, dst, send, recv, row, col):
    return pltpu.make_async_remote_copy(
        src_ref=src, dst_ref=dst, send_sem=send, recv_sem=recv,
        device_id=(row, col), device_id_type=MESH,
    )


def aligned(index, size):
    return pl.ds(pl.multiple_of(index * size, size), size)


def row_norm(values):
    mean = jnp.mean(values, axis=1, keepdims=True)
    centred = values - mean
    inverse = lax.rsqrt(jnp.mean(centred * centred, axis=1, keepdims=True) + EPSILON)
    return centred * inverse, mean, inverse


def weight_blocks(ref, kind, row):
    if kind == "three":
        return ref.at[:, aligned(row, 128), :]
    if kind == "rows":
        return ref.at[aligned(row, 128), :]
    return ref.at[:, aligned(row, 128)]


WEIGHT_KINDS = ("three", "cols", "rows", "cols")


def forward_kernel(
    tok, cot, g_one, s_one, b_out, g_two, s_two, b_red, attn_bias, exp_bias, win_s, wo_s, we_s, wr_s,
    tok_o, cot_o, q_o, qt_o, k_o, kt_o, v_o, mixf_o, lse_o, hid_o, unit_o, inv_o,
    norm_o, act_o, slope_o, win_o, wo_o, we_o, wr_o, vec_o, one_o, stat_o,
    tok_all, cot_all, norm_one, q, qt, k, kt, v, vt, mixed, mixf, lse, hid, unit, inv, norm_two, act, slope,
    win, wo, we, wr, vecs, stat, scores, sb, rb, xr,
    local_sem, shard_sem, tok_sem, cot_sem, wz_send, wz_recv, wy_send, wy_recv, vec_send, vec_recv,
    tx_send, tx_recv, tc_send, tc_recv, tp_send, tp_recv, cx_send, cx_recv, cc_send, cc_recv, cp_send, cp_recv,
    h1_send, h1_recv, h2_send, h2_recv, h3_send, h3_recv,
):
    r, c = lax.axis_index("row"), lax.axis_index("col")
    z, y = r // 2, r % 2
    xx, core = c // 2, c % 2
    c_x, c_core, c_far = (c + 2) % 4, c + 1 - 2 * core, (c + 2) % 4 + 1 - 2 * core
    r_y = r + 1 - 2 * y
    half = tok.shape[0] // CHUNKS
    chunk = 2 * half
    width = g_one.shape[1]
    scale = LOG2E * HEAD_DIM ** (-0.5)

    barrier = pltpu.get_barrier_semaphore()
    for col in (c_x, c_core, c_far):
        pl.semaphore_signal(barrier, inc=1, device_id=(r, col), device_id_type=MESH)
    pl.semaphore_signal(barrier, inc=1, device_id=(r_y, c), device_id_type=MESH)

    @pl.when(z >= 1)
    def _():
        pl.semaphore_signal(barrier, inc=1, device_id=(r - 2, c), device_id_type=MESH)

    @pl.when(z <= 2)
    def _():
        pl.semaphore_signal(barrier, inc=1, device_id=(r + 2, c), device_id_type=MESH)


    own = aligned(c, width)
    shards = (win_s, wo_s, we_s, wr_s)
    fulls = (win, wo, we, wr)
    shard_loads = [
        pltpu.make_async_copy(shards[w], weight_blocks(fulls[w], WEIGHT_KINDS[w], r), shard_sem.at[w])
        for w in range(4)
    ]
    for copy in shard_loads:
        copy.start()

    def half_source(ref, i, s):
        return ref.at[pl.ds(pl.multiple_of(i * half, half), half), pl.ds(s * width, width)]

    def half_load(ref, full_ref, sem, i, s):
        return pltpu.make_async_copy(
            half_source(ref, i, s), full_ref.at[i, pl.ds(s * half, half), own], sem.at[i, s]
        )

    for i in range(CHUNKS):
        for s in range(2):
            half_load(tok, tok_all, tok_sem, i, s).start()
            if i < EARLY:
                half_load(cot, cot_all, cot_sem, i, s).start()
    for n, vector in enumerate((g_one, s_one, b_out, g_two, s_two, b_red, b_red, b_red)):
        vecs[n : n + 1, own] = vector[...]
    pl.semaphore_wait(barrier, 4 + jnp.where(z >= 1, 1, 0) + jnp.where(z <= 2, 1, 0))

    def weight_ref(w, zb, side):
        return weight_blocks(fulls[w], WEIGHT_KINDS[w], zb * 2 + side)

    def line_copy(w, up, hop):
        zb = z - hop if up else z + hop
        block = weight_ref(w, zb, y)
        target = (z + 1 if up else z - 1) * 2 + y
        return remote(shards[w] if hop == 0 else block, block, wz_send.at[w, up, hop], wz_recv.at[w, up, hop], target, c)

    def line_sends(up, hop):
        return (z >= hop) & (z <= 2) if up else (z <= 3 - hop) & (z >= 1)

    def line_receives(up, hop):
        return z >= hop + 1 if up else z <= 2 - hop

    def y_copy(w, zb, side):
        block = weight_ref(w, zb, side)
        return remote(block, block, wy_send.at[w, zb], wy_recv.at[w, zb], r_y, c)

    def start_weight(w):
        for up in (0, 1):
            @pl.when(line_sends(up, 0))
            def _():
                line_copy(w, up, 0).start()

    def own_to_y(w):
        return remote(shards[w], weight_ref(w, z, y), wy_send.at[w, z], wy_recv.at[w, z], r_y, c)

    def forward_weight(w, hop):
        for up in (0, 1):
            @pl.when(line_receives(up, hop))
            def _():
                zb = z - 1 - hop if up else z + 1 + hop
                block = weight_ref(w, zb, y)
                remote(block, block, wz_send.at[w, up, hop], wz_recv.at[w, up, hop], r_y, c).wait_recv()
                y_copy(w, zb, y).start()

            if hop < 2:
                @pl.when(line_receives(up, hop) & line_sends(up, hop + 1))
                def _():
                    line_copy(w, up, hop + 1).start()

    def finish_weight(w):
        for up in (0, 1):
            for hop in range(3):
                @pl.when(line_sends(up, hop))
                def _():
                    line_copy(w, up, hop).wait_send()
        for zb in range(4):
            y_copy(w, zb, y).wait_send()
            y_copy(w, zb, 1 - y).wait_recv()

    def vec_copy(slot, target, col):
        block = vecs.at[:, aligned(col, width)]
        return remote(block, block, vec_send.at[slot], vec_recv.at[slot], r, target)

    def half_x(ref, full_ref, send, recv, i, s, col):
        block = full_ref.at[i, pl.ds(s * half, half), aligned(col, width)]
        return remote(half_source(ref, i, s), block, send.at[i, s], recv.at[i, s], r, c_x)

    def half_core(ref, full_ref, send, recv, i, s, col):
        block = full_ref.at[i, pl.ds(s * half, half), aligned(col, width)]
        return remote(half_source(ref, i, s), block, send.at[i, s], recv.at[i, s], r, c_core)

    def tok_x(i, s, col):
        return half_x(tok, tok_all, tx_send, tx_recv, i, s, col)

    def tok_core(i, s, col):
        return half_core(tok, tok_all, tc_send, tc_recv, i, s, col)

    def cot_x(i, s, col):
        return half_x(cot, cot_all, cx_send, cx_recv, i, s, col)

    def cot_core(i, s, col):
        return half_core(cot, cot_all, cc_send, cc_recv, i, s, col)

    def pass_core(full_ref, send, recv, i, col):
        block = full_ref.at[i, :, aligned(col, width)]
        return remote(block, block, send.at[i], recv.at[i], r, c_core)

    def tok_pass(i, col):
        return pass_core(tok_all, tp_send, tp_recv, i, col)

    def cot_pass(i, col):
        return pass_core(cot_all, cp_send, cp_recv, i, col)

    def send_cot(i):
        for s in range(2):
            cot_x(i, s, c).start()
            cot_core(i, s, c).start()

    def send_tok(i):
        for s in range(2):
            tok_x(i, s, c).start()
            tok_core(i, s, c).start()

    start_weight(0)
    own_to_y(0).start()
    send_tok(0)
    send_tok(1)
    for slot, target in enumerate((c_x, c_core, c_far)):
        vec_copy(slot, target, c).start()

    def keep(index, i, src, dst):
        return pltpu.make_async_copy(src, dst, local_sem.at[index, i])

    def kept(i, stage):
        if stage == 0:
            pairs = ((tok_all, tok_o), (q, q_o), (qt, qt_o), (k, k_o), (kt, kt_o), (v, v_o), (norm_one, one_o), (stat, stat_o))
            base = 0
        elif stage == 1:
            pairs = ((mixf, mixf_o), (lse, lse_o))
            base = 8
        elif stage == 2:
            pairs = ((unit, unit_o), (inv, inv_o), (norm_two, norm_o), (act, act_o), (slope, slope_o))
            base = 10
        else:
            pairs = ((cot_all, cot_o),)
            base = 15
        return [keep(base + n, i, a.at[i], b.at[i]) for n, (a, b) in enumerate(pairs)]

    def keep_hid(i):
        return keep(16, i, hid.at[i, :, own], hid_o.at[i])

    lane_ids = lax.broadcasted_iota(jnp.int32, (chunk // 7, 128), 1)

    def first_norm(i):
        for s in range(2):
            half_load(tok, tok_all, tok_sem, i, s).wait()
            tok_core(i, s, c_core).wait_recv()
        tok_pass(i, c_far).wait_recv()
        for part in range(7):
            rows = pl.ds(part * (chunk // 7), chunk // 7)
            units, mean, inverse = row_norm(tok_all[i, rows, :].astype(F32))
            stat[i, rows, :] = jnp.where(lane_ids < 64, mean, inverse)
            norm_one[i, rows, :] = (units * vecs[0:1, :] + vecs[1:2, :]).astype(BF16)

    @pl.loop(0, CHUNKS // 2 + 1)
    def _(g):
        @pl.loop(2 * g, jnp.minimum(2 * g + 2, CHUNKS))
        def _(i):
            for s in range(2):
                tok_x(i, s, c_x).wait_recv()

            @pl.when(i + 2 < CHUNKS)
            def _():
                send_tok(i + 2)

            @pl.when(i == CHUNKS - 2)
            def _():
                send_cot(0)

            tok_pass(i, c_x).start()

        @pl.when(g == 0)
        def _():
            for slot, target in enumerate((c_x, c_core, c_far)):
                vec_copy(slot, target, c).wait_send()
                vec_copy(slot, target, target).wait_recv()

        for hop in range(3):
            @pl.when(g == hop)
            def _():
                forward_weight(0, hop)

        @pl.when(g == 2)
        def _():
            start_weight(1)
            start_weight(2)

        @pl.loop(2 * g, jnp.minimum(2 * g + 2, CHUNKS))
        def _(i):
            first_norm(i)

    send_cot(1)
    send_cot(2)
    forward_weight(1, 0)
    for w in range(4):
        shard_loads[w].wait()
    finish_weight(0)
    own_to_y(1).start()
    own_to_y(2).start()
    forward_weight(1, 1)

    @pl.loop(0, CHUNKS)
    def _(i):
        part = jnp.dot(norm_one[i], win[0], preferred_element_type=F32)
        part = (part + attn_bias[0:1, :]).astype(BF16)
        q[i] = part
        qt[i] = part.T
        part = jnp.dot(norm_one[i], win[1], preferred_element_type=F32).astype(BF16)
        k[i] = part
        kt[i] = part.T
        part = jnp.dot(norm_one[i], win[2], preferred_element_type=F32)
        part = (part + attn_bias[1:2, :]).astype(BF16)
        v[i] = part
        vt[i] = part.T
        for copy in kept(i, 0):
            copy.start()

        @pl.when(i == 2)
        def _():
            forward_weight(1, 2)

        @pl.when(i == 4)
        def _():
            forward_weight(2, 0)

    finish_weight(1)

    def attend(i):
        row_ids = lax.broadcasted_iota(jnp.int32, (128, chunk), 0)

        @pl.loop(0, width // 128)
        def _(pair):
            lanes = aligned(pair, 128)
            peaks = []
            for h in range(2):
                query = qt[i, lanes, :]
                query = jnp.where(row_ids // HEAD_DIM == h, query, jnp.zeros_like(query))
                peak = jnp.full((1, chunk), -jnp.inf, F32)
                for j in range(CHUNKS):
                    block = jnp.dot(k[j, :, lanes], query, preferred_element_type=F32)
                    scores[h, j] = block
                    peak = jnp.maximum(peak, jnp.max(block, axis=0, keepdims=True))
                peaks.append(peak * scale)
            outs = []
            for h in range(2):
                total = jnp.zeros((1, chunk), F32)
                acc = jnp.zeros((HEAD_DIM, chunk), F32)
                rows = pl.ds(pl.multiple_of(pair * 128 + h * HEAD_DIM, HEAD_DIM), HEAD_DIM)
                for j in range(CHUNKS):
                    weights = jnp.exp2(scores[h, j] * scale - peaks[h])
                    total = total + jnp.sum(weights, axis=0, keepdims=True)
                    acc = acc + jnp.dot(vt[j, rows, :], weights.astype(BF16), preferred_element_type=F32)
                outs.append(acc / total)
                lse[i, pl.ds(pair * 2 + h, 1), :] = peaks[h] + jnp.log2(total)
            out = jnp.concatenate(outs, axis=0).T
            mixf[i, :, lanes] = out
            mixed[i, :, lanes] = out.astype(BF16)

    def h1(i):
        slot = i % 2
        return remote(sb.at[slot, 1 - core], rb.at[i], h1_send.at[i], h1_recv.at[i], r, c_core)

    def h2(i):
        return remote(rb.at[i], xr.at[i], h2_send.at[i], h2_recv.at[i], r, c_x)

    def h3(i, x, side):
        block = hid.at[i, :, aligned(x * 2 + side, width)]
        return remote(block, block, h3_send.at[i, x], h3_recv.at[i, x], r, c_core)

    def expand(t):
        for x in range(2):
            h3(t, x, core).wait_send()
            h3(t, x, 1 - core).wait_recv()
        for part in range(7):
            rows = pl.ds(part * (chunk // 7), chunk // 7)
            units, _, inverse = row_norm(hid[t, rows, :])
            unit[t, rows, :] = units.astype(BF16)
            inv[t, rows, :] = jnp.broadcast_to(inverse, (chunk // 7, 128))
            norm_two[t, rows, :] = (units * vecs[3:4, :] + vecs[4:5, :]).astype(BF16)
        for n in range(we.shape[1] // 256):
            lanes = slice(n * 256, (n + 1) * 256)
            expanded = jnp.dot(norm_two[t], we[:, lanes], preferred_element_type=F32) + exp_bias[:, lanes]
            gate = 0.5 + 0.5 * lax.erf(expanded * (0.5 ** 0.5))
            act[t, :, lanes] = (expanded * gate).astype(BF16)
            bell = jnp.exp2(expanded * expanded * (-0.5 * LOG2E)) * 0.3989422804014327
            slope[t, :, lanes] = (gate + expanded * bell).astype(BF16)
        for copy in kept(t, 2):
            copy.start()
        keep_hid(t).start()

    def spread_hidden(t):
        h2(t).wait()
        for x in range(2):
            lanes = aligned(x * 2 + core, width)
            total = rb[t, x].astype(F32) + xr[t, x].astype(F32)
            hid[t, :, lanes] = tok_all[t, :, lanes].astype(F32) + total + vecs[2:3, lanes]
        for x in range(2):
            h3(t, x, core).start()

    @pl.loop(0, CHUNKS)
    def _(i):
        attend(i)
        for copy in kept(i, 1):
            copy.start()
        partial = jnp.dot(mixed[i], wo[...], preferred_element_type=F32)
        for x in range(2):
            for side in range(2):
                block = x * 2 + side
                sb[i % 2, side, x] = partial[:, block * width : (block + 1) * width].astype(BF16)
        h1(i).start()

        @pl.when(i == 0)
        def _():
            forward_weight(2, 1)

        @pl.when(i == 1)
        def _():
            forward_weight(2, 2)
            start_weight(3)

        @pl.when(i == 2)
        def _():
            own_to_y(3).start()
            forward_weight(3, 0)

        @pl.when(i == 3)
        def _():
            forward_weight(3, 1)

        @pl.when(i == 4)
        def _():
            forward_weight(3, 2)

        @pl.when((i >= 1) & (i <= EARLY))
        def _():
            for s in range(2):
                cot_x(i - 1, s, c_x).wait_recv()
                half_load(cot, cot_all, cot_sem, i - 1, s).wait()
            cot_pass(i - 1, c_x).start()

        h1(i).wait()
        for x in range(2):
            rb[i, x] = (sb[i % 2, core, x].astype(F32) + rb[i, x].astype(F32)).astype(BF16)
        h2(i).start()

        @pl.when(i >= 1)
        def _():
            spread_hidden(i - 1)

        @pl.when(i == 5)
        def _():
            finish_weight(2)

        @pl.loop(jnp.maximum(2 * (i - 5), 0), jnp.maximum(2 * (i - 4), 0))
        def _(t):
            expand(t)

    @pl.loop(4, CHUNKS)
    def _(t):
        @pl.when(t == CHUNKS - 1)
        def _():
            spread_hidden(CHUNKS - 1)

        expand(t)

    @pl.loop(0, EARLY)
    def _(i):
        for s in range(2):
            cot_x(i, s, c).wait_send()
            cot_core(i, s, c).wait_send()
            cot_core(i, s, c_core).wait_recv()
        cot_pass(i, c_x).wait_send()
        cot_pass(i, c_far).wait_recv()
        for copy in kept(i, 3):
            copy.start()

    @pl.loop(0, CHUNKS)
    def _(i):
        for s in range(2):
            tok_x(i, s, c).wait_send()
            tok_core(i, s, c).wait_send()
        tok_pass(i, c_x).wait_send()

    finish_weight(3)
    last = [
        keep(17, n, a, b)
        for n, (a, b) in enumerate(((win, win_o), (wo, wo_o), (we, we_o), (wr, wr_o), (vecs, vec_o)))
    ]
    for copy in last:
        copy.start()

    @pl.loop(0, CHUNKS)
    def _(i):
        for stage in range(3):
            for copy in kept(i, stage):
                copy.wait()
        keep_hid(i).wait()

        @pl.when(i < EARLY)
        def _():
            for copy in kept(i, 3):
                copy.wait()

    for copy in last:
        copy.wait()


def forward_call(*arrays):
    tok, we_s = arrays[0], arrays[-2]
    pairs, width = tok.shape[0], tok.shape[1] // 2
    chunk = 2 * pairs // CHUNKS
    full = 4 * width
    hidden = we_s.shape[1]
    n = CHUNKS

    def sd(shape, dtype):
        return jax.ShapeDtypeStruct(shape, dtype)

    outs = [
        sd((n, chunk, full), BF16),
        sd((EARLY, chunk, full), BF16),
        sd((n, chunk, width), BF16),
        sd((n, width, chunk), BF16),
        sd((n, chunk, width), BF16),
        sd((n, width, chunk), BF16),
        sd((n, chunk, width), BF16),
        sd((n, chunk, width), F32),
        sd((n, 8, chunk), F32),
        sd((n, chunk, width), F32),
        sd((n, chunk, full), BF16),
        sd((n, chunk, 128), F32),
        sd((n, chunk, full), BF16),
        sd((n, chunk, hidden), BF16),
        sd((n, chunk, hidden), BF16),
        sd((3, full, width), BF16),
        sd((width, full), BF16),
        sd((full, hidden), BF16),
        sd((hidden, full), BF16),
        sd((8, full), F32),
        sd((n, chunk, full), BF16),
        sd((n, chunk, 128), F32),
    ]
    vm = pltpu.VMEM
    dma = pltpu.SemaphoreType.DMA
    scratch = [
        vm((n, chunk, full), BF16), vm((EARLY, chunk, full), BF16), vm((n, chunk, full), BF16),
        vm((n, chunk, width), BF16), vm((n, width, chunk), BF16),
        vm((n, chunk, width), BF16), vm((n, width, chunk), BF16),
        vm((n, chunk, width), BF16), vm((n, width, chunk), BF16),
        vm((n, chunk, width), BF16), vm((n, chunk, width), F32), vm((n, 8, chunk), F32),
        vm((n, chunk, full), F32), vm((n, chunk, full), BF16), vm((n, chunk, 128), F32),
        vm((n, chunk, full), BF16), vm((n, chunk, hidden), BF16), vm((n, chunk, hidden), BF16),
        vm((3, full, width), BF16), vm((width, full), BF16), vm((full, hidden), BF16), vm((hidden, full), BF16),
        vm((8, full), F32), vm((n, chunk, 128), F32),
        vm((2, n, chunk, chunk), F32),
        vm((2, 2, 2, chunk, width), BF16), vm((n, 2, chunk, width), BF16),
        vm((n, 2, chunk, width), BF16),
        dma((18, n)), dma((4,)), dma((n, 2)), dma((EARLY, 2)), dma((4, 2, 3)), dma((4, 2, 3)), dma((4, 4)), dma((4, 4)), dma((3,)), dma((3,)),
        dma((n, 2)), dma((n, 2)), dma((n, 2)), dma((n, 2)), dma((n,)), dma((n,)),
        dma((EARLY, 2)), dma((EARLY, 2)), dma((EARLY, 2)), dma((EARLY, 2)), dma((EARLY,)), dma((EARLY,)),
        dma((n,)), dma((n,)), dma((n,)), dma((n,)), dma((n, 2)), dma((n, 2)),
    ]
    return pl.pallas_call(
        forward_kernel,
        out_shape=outs,
        in_specs=[pl.BlockSpec(memory_space=pl.ANY if n in (0, 1, 10, 11, 12, 13) else pltpu.VMEM) for n in range(len(arrays))],
        out_specs=[pl.BlockSpec(memory_space=pl.ANY)] * len(outs),
        scratch_shapes=scratch,
        compiler_params=pltpu.CompilerParams(
            collective_id=0, has_side_effects=True, vmem_limit_bytes=63 << 20
        ),
    )(*arrays)


GRAD_KINDS = ("three", "cols", "rows", "cols")


def backward_kernel(
    tok_h, cot_h, cot_in, q_h, qt_h, k_h, kt_h, v_h, mixf_h, lse_h, hid_h, unit_h, inv_h,
    normed_h, act_h, slope_h, win_h, wo_h, we_h, wr_h, vec_h, one_h, stat_h,
    out_o, tg_o, sums_o, gin_o, gout_o, gexp_o, gred_o,
    cot, q, qt, k, kt, v, mixf, lse, hid, unit, inv, normed, act, slope, win, wo, we, wr, vecs, stat,
    grad, dq, dk, dv, tg, out, sb_g, sb_o, rb_g, xr_g, rb_o, xr_o, xr_1, st, st_in,
    col_sums, hid_sums, packet, packets,
    ys_in, ys_out, ys_exp, ys_red, oh_in, oh_out, oh_exp, oh_red,
    yr_in, yr_out, yr_exp, yr_red, zr_in, zr_out, zr_exp, zr_red,
    gin, gout, gexp, gred,
    load_sem, store_sem, hid_sem, cot_sem, cx_send, cx_recv, cc_send, cc_recv, cp_send, cp_recv, gy_send, gy_recv, gz_send, gz_recv,
    h1g_send, h1g_recv, h2g_send, h2g_recv, h3g_send, h3g_recv,
    h1o_send, h1o_recv, h2o_send, h2o_recv, h1t_send, h1t_recv, h2t_send, h2t_recv,
    st_send, st_recv, pk_send, pk_recv,
):
    r, c = lax.axis_index("row"), lax.axis_index("col")
    z, y = r // 2, r % 2
    xx, core = c // 2, c % 2
    c_x, c_core, c_far = (c + 2) % 4, c + 1 - 2 * core, (c + 2) % 4 + 1 - 2 * core
    r_y = r + 1 - 2 * y
    tok, one = act, normed
    chunk = q.shape[0] // CHUNKS
    half = chunk // 2
    width = q.shape[1]
    full = cot.shape[1]
    scale = LOG2E * HEAD_DIM ** (-0.5)
    own = aligned(c, width)
    others = [(r + step) % 8 for step in range(1, 8)]

    barrier = pltpu.get_barrier_semaphore()
    for col in (c_x, c_core, c_far):
        pl.semaphore_signal(barrier, inc=1, device_id=(r, col), device_id_type=MESH)
    for row in others:
        pl.semaphore_signal(barrier, inc=1, device_id=(row, c), device_id_type=MESH)

    loads = {}
    order = (
        ("wr", wr_h, wr), ("cot", cot_h, cot.at[pl.ds(0, EARLY * chunk), :]), ("slope", slope_h, slope), ("we", we_h, we), ("act", act_h, act),
        ("vec", vec_h, vecs), ("unit", unit_h, unit), ("inv", inv_h, inv), ("wo", wo_h, wo),
        ("normed", normed_h, normed), ("mixf", mixf_h, mixf), ("lse", lse_h, lse), ("qt", qt_h, qt), ("q", q_h, q),
        ("k", k_h, k), ("v", v_h, v), ("kt", kt_h, kt), ("win", win_h, win), ("stat", stat_h, stat),
        ("tok", tok_h, tok), ("one", one_h, one),
    )
    for n, (name, src, dst) in enumerate(order):
        loads[name] = pltpu.make_async_copy(src, dst, load_sem.at[n])
    late = ("tok", "one")
    for name, _, _ in order:
        if name not in late:
            loads[name].start()
    def cot_source(i, s):
        return cot_in.at[pl.ds(pl.multiple_of(i * half, half), half), pl.ds(s * width, width)]

    def cot_block(i, s, col):
        return cot.at[pl.ds(pl.multiple_of(i * chunk + s * half, half), half), aligned(col, width)]

    def cot_load(i, s):
        return pltpu.make_async_copy(cot_source(i, s), cot_block(i, s, c), cot_sem.at[i, s])

    for i in range(EARLY, CHUNKS):
        for s in range(2):
            cot_load(i, s).start()
    dk[...] = jnp.zeros_like(dk)
    dv[...] = jnp.zeros_like(dv)
    col_sums[...] = jnp.zeros_like(col_sums)
    hid_sums[...] = jnp.zeros_like(hid_sums)
    pl.semaphore_wait(barrier, 10)

    def rows_of(i):
        return pl.ds(pl.multiple_of(i * chunk, chunk), chunk)

    def cot_x(i, s, col):
        return remote(cot_source(i, s), cot_block(i, s, col), cx_send.at[i, s], cx_recv.at[i, s], r, c_x)

    def cot_core(i, s, col):
        return remote(cot_source(i, s), cot_block(i, s, col), cc_send.at[i, s], cc_recv.at[i, s], r, c_core)

    def cot_pass(i, col):
        block = cot.at[rows_of(i), aligned(col, width)]
        return remote(block, block, cp_send.at[i], cp_recv.at[i], r, c_core)

    def send_cot(i):
        for s in range(2):
            cot_x(i, s, c).start()
            cot_core(i, s, c).start()

    def pass_cot(i):
        for s in range(2):
            cot_x(i, s, c_x).wait_recv()
        cot_pass(i, c_x).start()

    def finish_cot(i):
        for s in range(2):
            cot_load(i, s).wait()
            cot_x(i, s, c).wait_send()
            cot_core(i, s, c).wait_send()
            cot_core(i, s, c_core).wait_recv()
        cot_pass(i, c_x).wait_send()
        cot_pass(i, c_far).wait_recv()

    send_cot(EARLY)
    send_cot(EARLY + 1)

    def h1(sb, rb, send, recv, i):
        return remote(sb.at[i % 2, 1 - core], rb.at[i], send.at[i], recv.at[i], r, c_core)

    def fill(sb, i, partial):
        for x in range(2):
            for side in range(2):
                block = x * 2 + side
                sb[i % 2, side, x] = partial[:, block * width : (block + 1) * width].astype(BF16)

    def merge(sb, rb, i):
        for x in range(2):
            rb[i, x] = (sb[i % 2, core, x].astype(F32) + rb[i, x].astype(F32)).astype(BF16)

    def h1g(i):
        return h1(sb_g, rb_g, h1g_send, h1g_recv, i)

    def h1o(i):
        return h1(sb_o, rb_o, h1o_send, h1o_recv, i)

    def h1t(i):
        return h1(sb_g, rb_g, h1t_send, h1t_recv, i)

    def h2g(i):
        return remote(rb_g.at[i], xr_g.at[i], h2g_send.at[i], h2g_recv.at[i], r, c_x)

    def h2o(i):
        return remote(rb_o.at[i, 1 - xx], xr_o.at[i], h2o_send.at[i], h2o_recv.at[i], r, c_x)

    def h2t(i):
        return remote(rb_g.at[i, 1 - xx], xr_1.at[i], h2t_send.at[i], h2t_recv.at[i], r, c_x)

    def h3g(i, x, side):
        block = grad.at[i % 4, :, aligned(x * 2 + side, width)]
        return remote(block, block, h3g_send.at[i, x], h3g_recv.at[i, x], r, c_core)

    def spread_grad(i):
        h2g(i).wait()
        if isinstance(i, int):
            h2g(i + 2).start()
        else:
            @pl.when(i + 2 < CHUNKS)
            def _():
                h2g(i + 2).start()

        for x in range(2):
            grad[i % 4, :, aligned(x * 2 + core, width)] = rb_g[i, x].astype(F32) + xr_g[i, x].astype(F32)
        for x in range(2):
            h3g(i, x, core).start()

    ys = (ys_in, ys_out, ys_exp, ys_red)
    oh = (oh_in, oh_out, oh_exp, oh_red)
    yr = (yr_in, yr_out, yr_exp, yr_red)
    zr = (zr_in, zr_out, zr_exp, zr_red)

    def gy(w, s):
        return remote(ys[w].at[s], yr[w].at[s], gy_send.at[w, s], gy_recv.at[w, s], r_y, c)

    def gz(w, s):
        target = ((z + 1 + s) % 4) * 2 + y
        return remote(oh[w].at[s], zr[w].at[s], gz_send.at[w, s], gz_recv.at[w, s], target, c)

    def grad_block(w, s, left, right):
        zt = (z + 1 + s) % 4
        lanes = aligned(zt, 256)
        if GRAD_KINDS[w] == "rows":
            block = lax.dot_general(left[:, lanes], right, TN_DIMS, preferred_element_type=F32).astype(BF16)
            low, high = block[0:128, :], block[128:256, :]
        else:
            block = lax.dot_general(left, right[:, lanes], TN_DIMS, preferred_element_type=F32).astype(BF16)
            low, high = block[:, 0:128], block[:, 128:256]

        @pl.when(y == 0)
        def _():
            oh[w][s] = low
            ys[w][s] = high

        @pl.when(y == 1)
        def _():
            oh[w][s] = high
            ys[w][s] = low

    def pass_on(w, s):
        gy(w, s).wait()
        oh[w][s] = (oh[w][s].astype(F32) + yr[w][s].astype(F32)).astype(BF16)
        gz(w, s).start()

    def finish_grad(w, dst):
        gy(w, 3).wait()
        total = oh[w][3].astype(F32) + yr[w][3].astype(F32)
        for s in range(3):
            gz(w, s).wait()
            total = total + zr[w][s].astype(F32)
        dst[...] = total

    loads["wr"].wait()
    loads["cot"].wait()
    loads["slope"].wait()
    loads["we"].wait()
    loads["act"].wait()

    @pl.loop(0, CHUNKS)
    def _(i):
        @pl.when(i >= EARLY)
        def _():
            finish_cot(i)

        rows = rows_of(i)
        for n in range(slope.shape[1] // 256):
            lanes = slice(n * 256, (n + 1) * 256)
            grad_act = lax.dot_general(cot[rows, :], wr[lanes, :], NT_DIMS, preferred_element_type=F32)
            low = (slope[rows, lanes].astype(F32) * grad_act).astype(BF16)
            slope[rows, lanes] = low
            hid_sums[0:1, lanes] += jnp.sum(low.astype(F32), axis=0, keepdims=True)
        fill(sb_g, i, lax.dot_general(slope[rows, :], we[...], NT_DIMS, preferred_element_type=F32))
        h1g(i).start()

        @pl.when(i >= 1)
        def _():
            h1o(i - 1).wait()
            merge(sb_o, rb_o, i - 1)

        fill(sb_o, i, jnp.dot(act[rows, :], wr[...], preferred_element_type=F32))
        h1o(i).start()
        h1g(i).wait()
        merge(sb_g, rb_g, i)

        @pl.when((i >= 1) & (i + 2 < CHUNKS))
        def _():
            pass_cot(i + 2)

            @pl.when(i + 4 < CHUNKS)
            def _():
                send_cot(i + 4)

        @pl.when((i == 3) | (i == 4))
        def _():
            h2g(i - 3).start()

        col_sums[0:1, :] += jnp.sum(cot[rows, :].astype(F32), axis=0, keepdims=True)

    h1o(CHUNKS - 1).wait()
    merge(sb_o, rb_o, CHUNKS - 1)
    loads["normed"].wait()
    for s in range(3):
        grad_block(3, s, act[...], cot)
        if s < 2:
            gy(3, s).start()
    spread_grad(0)
    for s in range(3):
        grad_block(2, s, normed, slope[...])
    pass_on(3, 0)
    gy(3, 2).start()
    spread_grad(1)
    grad_block(3, 3, act[...], cot)
    grad_block(2, 3, normed, slope[...])
    for name in late:
        loads[name].start()
    for name in ("unit", "inv", "vec", "wo", "mixf", "lse", "qt", "q", "k", "v", "kt", "win", "stat"):
        loads[name].wait()

    def hid_load(i):
        return pltpu.make_async_copy(hid_h.at[rows_of(i), :], hid.at[i % 2], hid_sem.at[i])

    def out_store(i, s):
        return pltpu.make_async_copy(
            out.at[i % 2, s], out_o.at[pl.ds(pl.multiple_of(i * half, half), half), pl.ds(s * width, width)],
            store_sem.at[0, i, s],
        )

    def tg_store(i, s):
        return pltpu.make_async_copy(
            tg.at[i, s], tg_o.at[pl.ds(pl.multiple_of(i * half, half), half), pl.ds(s * width, width)],
            store_sem.at[1, i, s],
        )

    def attend_back(i):
        rows = rows_of(i)
        go = lax.dot_general(unit[rows, :], wo[...], NT_DIMS, preferred_element_type=F32).astype(BF16)
        inner = (go.astype(F32) * mixf[rows, :]).T
        go_t = go.T
        row_ids = lax.broadcasted_iota(jnp.int32, (128, chunk), 0)
        lane_ids = lax.broadcasted_iota(jnp.int32, (chunk, 128), 1)
        heads = width // HEAD_DIM
        queries, grads, query_rows, grad_rows, deltas, logs = [], [], [], [], [], []
        for h in range(heads):
            lanes = slice(h // 2 * 128, h // 2 * 128 + 128)
            pick = row_ids // HEAD_DIM == h % 2
            value = qt[i, lanes, :]
            queries.append(jnp.where(pick, value, jnp.zeros_like(value)))
            value = go_t[lanes, :]
            grads.append(jnp.where(pick, value, jnp.zeros_like(value)))
            pick = lane_ids // HEAD_DIM == h % 2
            value = q[rows, lanes]
            query_rows.append(jnp.where(pick, value, jnp.zeros_like(value)))
            value = go[:, lanes]
            grad_rows.append(jnp.where(pick, value, jnp.zeros_like(value)))
            deltas.append(jnp.sum(inner[h * HEAD_DIM : (h + 1) * HEAD_DIM, :], axis=0, keepdims=True))
            logs.append(lse[i, h : h + 1, :])

        parts = [jnp.zeros((HEAD_DIM, chunk), F32)] * heads
        for j in range(CHUNKS):
            keys = pl.ds(j * chunk, chunk)
            probs, grad_scores = [], []
            for h in range(heads):
                lanes = slice(h // 2 * 128, h // 2 * 128 + 128)
                block = jnp.dot(k[keys, lanes], queries[h], preferred_element_type=F32)
                grad_probs = jnp.dot(v[keys, lanes], grads[h], preferred_element_type=F32)
                prob = jnp.exp2(block * scale - logs[h])
                probs.append(prob.astype(BF16))
                grad_scores.append((prob * (grad_probs - deltas[h])).astype(BF16))
            for pair in range(heads // 2):
                lanes = slice(pair * 128, pair * 128 + 128)
                h = 2 * pair
                dv[keys, lanes] += jnp.dot(
                    probs[h], grad_rows[h], preferred_element_type=F32
                ) + jnp.dot(probs[h + 1], grad_rows[h + 1], preferred_element_type=F32)
                dk[keys, lanes] += jnp.dot(
                    grad_scores[h], query_rows[h], preferred_element_type=F32
                ) + jnp.dot(grad_scores[h + 1], query_rows[h + 1], preferred_element_type=F32)
            for h in range(heads):
                rows_h = slice(h * HEAD_DIM, (h + 1) * HEAD_DIM)
                parts[h] = parts[h] + jnp.dot(kt[j, rows_h, :], grad_scores[h], preferred_element_type=F32)
        dq[rows, :] = (jnp.concatenate(parts, axis=0).T * HEAD_DIM ** (-0.5)).astype(BF16)

    def finish_out(i):
        h2o(i).wait()
        hid_load(i).wait()
        total = rb_o[i, xx].astype(F32) + xr_o[i].astype(F32)
        value = (hid[i % 2] + total + vecs[5:6, own]).astype(BF16)
        for s in range(2):
            out[i % 2, s] = value[s * half : (s + 1) * half, :]
        for s in range(2):
            out_store(i, s).start()

    @pl.loop(0, CHUNKS)
    def _(i):
        hid_load(i).start()
        for x in range(2):
            h3g(i, x, core).wait_send()
            h3g(i, x, 1 - core).wait_recv()
        step_rows = chunk // 7
        for part in range(7):
            rows = pl.ds(pl.multiple_of(i * chunk + part * step_rows, step_rows), step_rows)
            span = slice(part * step_rows, (part + 1) * step_rows)
            incoming = grad[i % 4, span, :]
            units = unit[rows, :].astype(F32)
            scaled = incoming * vecs[3:4, :]
            plain = jnp.mean(scaled, axis=1, keepdims=True)
            cross = jnp.mean(scaled * units, axis=1, keepdims=True)
            total = cot[rows, :].astype(F32) + inv[rows, 0:1] * (scaled - plain - units * cross)
            low = total.astype(BF16)
            col_sums[1:2, :] += jnp.sum(incoming * units, axis=0, keepdims=True)
            col_sums[2:3, :] += jnp.sum(incoming, axis=0, keepdims=True)
            col_sums[3:4, :] += jnp.sum(low.astype(F32), axis=0, keepdims=True)
            unit[rows, :] = low
            grad[i % 4, span, :] = total
        for s in range(2):
            tg[i, s] = grad[i % 4, s * half : (s + 1) * half, own]
        h2o(i).start()
        attend_back(i)

        @pl.when(i + 2 < CHUNKS)
        def _():
            spread_grad(i + 2)

        queue = ((3, 0), (3, 1), (3, 2), (2, 0), (2, 1), (2, 2), (3, 3), (2, 3))
        for at in range(5):
            @pl.when(i == at)
            def _():
                pass_on(*queue[at + 1])
                gy(*queue[at + 3]).start()

        @pl.when(i >= 1)
        def _():
            @pl.when(i >= 3)
            def _():
                for s in range(2):
                    out_store(i - 3, s).wait()
            finish_out(i - 1)

    for s in range(2):
        out_store(CHUNKS - 3, s).wait()
    finish_out(CHUNKS - 1)

    for i in range(CHUNKS):
        rows = pl.ds(i * chunk, chunk)
        k[rows, :] = (dk[rows, :] * HEAD_DIM ** (-0.5)).astype(BF16)
        low = dv[rows, :].astype(BF16)
        v[rows, :] = low
        col_sums[4:5, 0:width] += jnp.sum(dq[rows, :].astype(F32), axis=0, keepdims=True)
        col_sums[5:6, 0:width] += jnp.sum(low.astype(F32), axis=0, keepdims=True)
    for name in late:
        loads[name].wait()

    def inward_block(s):
        zt = (z + 1 + s) % 4
        left = one[:, aligned(zt, 256)]
        for n, right in enumerate((dq, k, v)):
            block = lax.dot_general(left, right[...], TN_DIMS, preferred_element_type=F32).astype(BF16)

            @pl.when(y == 0)
            def _():
                oh_in[s, n] = block[0:128, :]
                ys_in[s, n] = block[128:256, :]

            @pl.when(y == 1)
            def _():
                oh_in[s, n] = block[128:256, :]
                ys_in[s, n] = block[0:128, :]

        gy(0, s).start()

    for s in range(3):
        inward_block(s)

    def stat_copy(i, slot, target):
        return remote(st.at[i], st_in.at[i, slot], st_send.at[i, slot], st_recv.at[i, slot], r, target)

    lane_ids = lax.broadcasted_iota(jnp.int32, (chunk, 128), 1)
    gain = vecs[0:1, :]

    @pl.loop(0, CHUNKS + 2)
    def _(i):
        @pl.when(i < CHUNKS)
        def _():
            rows = rows_of(i)
            partial = lax.dot_general(dq[rows, :], win[0], NT_DIMS, preferred_element_type=F32)
            partial = partial + lax.dot_general(
                k[rows, :], win[1], NT_DIMS, preferred_element_type=F32
            )
            partial = partial + lax.dot_general(
                v[rows, :], win[2], NT_DIMS, preferred_element_type=F32
            )
            fill(sb_g, i, partial)
            h1t(i).start()
            units = (tok[rows, :].astype(F32) - stat[rows, 0:1]) * stat[rows, 64:65]
            scaled = partial * gain
            plain = jnp.sum(scaled, axis=1, keepdims=True)
            cross = jnp.sum(scaled * units, axis=1, keepdims=True)
            both = jnp.where(lane_ids == 0, plain, jnp.where(lane_ids == 1, cross, 0.0))
            st[i] = both.T[0:8, :]
            for slot, target in enumerate((c_x, c_core, c_far)):
                stat_copy(i, slot, target).start()
            h1t(i).wait()
            merge(sb_g, rb_g, i)
            h2t(i).start()

        for s in range(3):
            @pl.when(i == s + 1)
            def _():
                pass_on(0, s)

        @pl.when(i == 4)
        def _():
            for s in range(3):
                grad_block(1, s, mixf[...].astype(BF16), unit)
                gy(1, s).start()

        @pl.when(i == 5)
        def _():
            inward_block(3)
            grad_block(1, 3, mixf[...].astype(BF16), unit)
            gy(1, 3).start()

        @pl.when(i == 6)
        def _():
            for s in range(3):
                pass_on(1, s)

        @pl.when(i >= 2)
        def _():
            t = i - 2
            rows = rows_of(t)
            h2t(t).wait()
            total = st[t]
            for slot, target in enumerate((c_x, c_core, c_far)):
                stat_copy(t, slot, target).wait()
                total = total + st_in[t, slot]
            columns = jnp.concatenate([total, jnp.zeros((120, chunk), F32)], axis=0).T
            plain = columns[:, 0:1] / full
            cross = columns[:, 1:2] / full
            incoming = rb_g[t, xx].astype(F32) + xr_1[t].astype(F32)
            inverse = stat[rows, 64:65]
            units = (tok[rows, own].astype(F32) - stat[rows, 0:1]) * inverse
            back = inverse * (incoming * vecs[0:1, own] - plain - units * cross)
            for s in range(2):
                tg[t, s] = tg[t, s] + back[s * half : (s + 1) * half, :]
            for s in range(2):
                tg_store(t, s).start()
            col_sums[6:7, 0:width] += jnp.sum(incoming * units, axis=0, keepdims=True)
            col_sums[7:8, 0:width] += jnp.sum(incoming, axis=0, keepdims=True)

    packet[0:1, :] = col_sums[6:7, 0:width]
    packet[1:2, :] = col_sums[7:8, 0:width]
    packet[2:4, :] = col_sums[4:6, 0:width]
    packet[4:5, :] = col_sums[3:4, own]
    packet[5:7, :] = col_sums[1:3, own]
    packet[7:8, :] = col_sums[0:1, own]
    for n in range(4):
        packet[8 + n : 9 + n, :] = hid_sums[0:1, n * width : (n + 1) * width]

    def packet_copy(step):
        return remote(packet, packets.at[step], pk_send.at[step], pk_recv.at[step], others[step], c)

    for step in range(7):
        packet_copy(step).start()
    finish_grad(3, gred)
    finish_grad(2, gexp)
    finish_grad(0, gin)
    finish_grad(1, gout)
    stores = [
        pltpu.make_async_copy(src, dst, store_sem.at[2, n, 0])
        for n, (src, dst) in enumerate(((gin, gin_o), (gout, gout_o), (gexp, gexp_o), (gred, gred_o)))
    ]
    for copy in stores:
        copy.start()
    total = packet[...]
    for step in range(7):
        packet_copy(step).wait()
        total = total + packets[step]
    packet[...] = total
    copy = pltpu.make_async_copy(packet, sums_o, store_sem.at[2, 4, 0])
    copy.start()
    copy.wait()
    for copy in stores:
        copy.wait()
    for i in range(CHUNKS - 2, CHUNKS):
        for s in range(2):
            out_store(i, s).wait()

    @pl.loop(0, CHUNKS)
    def _(i):
        for s in range(2):
            tg_store(i, s).wait()


def backward_call(*arrays):
    (tok, cot, cot_in, q, qt, k, kt, v, mixf, lse, hid, unit, inv, normed, act, slope, win, wo, we, wr, vec, one, stat) = arrays
    rows, width = q.shape
    full, hidden = we.shape
    n, chunk = CHUNKS, rows // CHUNKS
    half = chunk // 2
    pairs = rows // 2

    def sd(shape, dtype):
        return jax.ShapeDtypeStruct(shape, dtype)

    outs = [
        sd((pairs, 2 * width), BF16), sd((pairs, 2 * width), F32), sd((16, width), F32),
        sd((3, 128, width), F32), sd((width, 128), F32), sd((128, hidden), F32), sd((hidden, 128), F32),
    ]
    vm = pltpu.VMEM
    dma = pltpu.SemaphoreType.DMA

    def shapes(lead):
        return [
            vm((lead, 3, 128, width), BF16), vm((lead, width, 128), BF16),
            vm((lead, 128, hidden), BF16), vm((lead, hidden, 128), BF16),
        ]

    def like(array):
        return vm(array.shape, array.dtype)

    scratch = [
        vm((rows, full), BF16), like(q), like(qt), like(k), like(kt), like(v), like(mixf), like(lse),
        vm((2, chunk, width), F32),
        like(unit), like(inv), like(normed), like(act), like(slope),
        like(win), like(wo), like(we), like(wr), like(vec), like(stat),
        vm((4, chunk, full), F32), vm((rows, width), BF16), vm((rows, width), F32), vm((rows, width), F32),
        vm((n, 2, half, width), F32), vm((2, 2, half, width), BF16),
        vm((2, 2, 2, chunk, width), BF16), vm((2, 2, 2, chunk, width), BF16),
        vm((n, 2, chunk, width), BF16), vm((n, 2, chunk, width), BF16),
        vm((n, 2, chunk, width), BF16), vm((n, chunk, width), BF16), vm((n, chunk, width), BF16),
        vm((n, 8, chunk), F32), vm((n, 3, 8, chunk), F32),
        vm((8, full), F32), vm((8, hidden), F32), vm((16, width), F32), vm((7, 16, width), F32),
        *shapes(4), *shapes(4), *shapes(4), *shapes(3),
        vm((3, 128, width), F32), vm((width, 128), F32), vm((128, hidden), F32), vm((hidden, 128), F32),
        dma((21,)), dma((3, n, 2)), dma((n,)), dma((n, 2)), dma((n, 2)), dma((n, 2)), dma((n, 2)), dma((n, 2)), dma((n,)), dma((n,)),
        dma((4, 4)), dma((4, 4)), dma((4, 3)), dma((4, 3)),
        dma((n,)), dma((n,)), dma((n,)), dma((n,)), dma((n, 2)), dma((n, 2)),
        dma((n,)), dma((n,)), dma((n,)), dma((n,)), dma((n,)), dma((n,)), dma((n,)), dma((n,)),
        dma((n, 3)), dma((n, 3)), dma((7,)), dma((7,)),
    ]
    return pl.pallas_call(
        backward_kernel,
        out_shape=outs,
        in_specs=[pl.BlockSpec(memory_space=pl.ANY)] * len(arrays),
        out_specs=[pl.BlockSpec(memory_space=pl.ANY)] * len(outs),
        scratch_shapes=scratch,
        compiler_params=pltpu.CompilerParams(
            collective_id=1, has_side_effects=True, vmem_limit_bytes=63 << 20
        ),
    )(*arrays)


def finish_kernel(out_i, tg_i, sums_i, gin_i, gout_i, gexp_i, gred_i, *refs):
    outs, vector_o, buffers = refs[:6], refs[6:14], refs[14:20]
    load_sem, store_sem = refs[20:]
    ins = (out_i, tg_i, gin_i, gout_i, gexp_i, gred_i)
    loads = [pltpu.make_async_copy(a, b, load_sem.at[n]) for n, (a, b) in enumerate(zip(ins, buffers))]
    stores = [pltpu.make_async_copy(a, b, store_sem.at[n]) for n, (a, b) in enumerate(zip(buffers, outs))]
    order = (0, 2, 3, 4, 5, 1)
    for n in order:
        loads[n].start()
    first_gain, first_shift, attn, b_out, g_two, s_two, b_red, b_exp = vector_o
    first_gain[...] = sums_i[0:1, :]
    first_shift[...] = sums_i[1:2, :]
    attn[...] = sums_i[2:4, :]
    b_out[...] = sums_i[4:5, :]
    g_two[...] = sums_i[5:6, :]
    s_two[...] = sums_i[6:7, :]
    b_red[...] = sums_i[7:8, :]
    for n in range(4):
        width = sums_i.shape[1]
        b_exp[:, n * width : (n + 1) * width] = sums_i[8 + n : 9 + n, :]
    for n in order:
        loads[n].wait()
        stores[n].start()
    for n in order:
        stores[n].wait()


def finish_call(out, tg, sums, gin, gout, gexp, gred):
    width = sums.shape[1]
    big = [jax.ShapeDtypeStruct(a.shape, a.dtype) for a in (out, tg, gin, gout, gexp, gred)]
    small = [jax.ShapeDtypeStruct((n, m), F32) for n, m in ((1, width),) * 2 + ((2, width),) + ((1, width),) * 4 + ((1, 4 * width),)]
    hbm, vm = pl.BlockSpec(memory_space=pl.ANY), pl.BlockSpec(memory_space=pltpu.VMEM)
    return pl.pallas_call(
        finish_kernel,
        out_shape=big + small,
        in_specs=[hbm, hbm, vm, hbm, hbm, hbm, hbm],
        out_specs=[hbm] * 6 + [vm] * 8,
        scratch_shapes=[pltpu.VMEM(a.shape, a.dtype) for a in big] + [pltpu.SemaphoreType.DMA((6,))] * 2,
    )(out, tg, sums, gin, gout, gexp, gred)


CONTRACT_ROWS = (((0,), (0,)), ((), ()))
CONTRACT_COLS = (((1,), (1,)), ((), ()))


def norm_forward(values, gain, shift, full_width):
    row_total = lax.psum(jnp.sum(values, axis=1), "col")
    centred = values - (row_total / full_width)[:, None]
    row_square = lax.psum(jnp.sum(centred * centred, axis=1), "col")
    inverse = lax.rsqrt(row_square / full_width + EPSILON)
    unit_rows = centred * inverse[:, None]
    return (unit_rows, inverse, unit_rows * gain + shift)


def norm_backward(incoming, unit_rows, inverse, gain, full_width):
    scaled = incoming * gain
    plain_sum, cross_sum = lax.psum(
        (jnp.sum(scaled, axis=1), jnp.sum(scaled * unit_rows, axis=1)), "col"
    )
    result = inverse[:, None] * (
        scaled - (plain_sum / full_width)[:, None] - unit_rows * (cross_sum / full_width)[:, None]
    )
    return (result, jnp.sum(incoming * unit_rows, axis=0), jnp.sum(incoming, axis=0))


def spread_features(values):
    return lax.all_gather(values, "col", axis=1, tiled=True)


def sum_partials(values):
    return lax.psum_scatter(values, "col", scatter_dimension=1, tiled=True)


def spread_grads(values):
    return lax.all_gather(values, "col", axis=1, tiled=True)


def sum_grad_partials(values):
    return lax.psum_scatter(values, "col", scatter_dimension=1, tiled=True)


def fetch_weights(inward_weight, output_weight, expand_weight, reduce_weight):
    return (
        lax.all_gather(inward_weight, "row", axis=0, tiled=True),
        lax.all_gather(output_weight, "row", axis=1, tiled=True),
        lax.all_gather(expand_weight, "row", axis=0, tiled=True),
        lax.all_gather(reduce_weight, "row", axis=1, tiled=True),
    )


def attend_clip(queries, key_rows, value_rows, score_scale):
    seq_len = queries.shape[0]
    blocks = queries.reshape((2, seq_len // 2) + queries.shape[1:])

    def one_block(query_part):
        scores = (
            jnp.einsum("qhd,khd->hqk", query_part, key_rows, preferred_element_type=jnp.float32)
            * score_scale
        )
        row_peak = jnp.max(scores, axis=-1, keepdims=True)
        exponent = jnp.exp(scores - row_peak)
        row_sum = jnp.sum(exponent, axis=-1, keepdims=True)
        prob_low = (exponent / row_sum).astype(jnp.bfloat16)
        mixed_rows = jnp.einsum(
            "hqk,khd->qhd", prob_low, value_rows, preferred_element_type=jnp.float32
        )
        return (mixed_rows, (row_peak + jnp.log(row_sum))[..., 0])

    mixed_rows, logsum = lax.map(one_block, blocks)
    return (mixed_rows.reshape(queries.shape), logsum)


def attend_clip_back(queries, key_rows, value_rows, logsum, grad_out, score_scale):
    seq_len = queries.shape[0]
    block_shape = (2, seq_len // 2) + queries.shape[1:]

    def step_block(carry, pieces):
        key_acc, value_acc = carry
        query_part, grad_part, log_part = pieces
        scores = (
            jnp.einsum("qhd,khd->hqk", query_part, key_rows, preferred_element_type=jnp.float32)
            * score_scale
        )
        probs = jnp.exp(scores - log_part[..., None])
        grad_probs = jnp.einsum(
            "qhd,khd->hqk", grad_part, value_rows, preferred_element_type=jnp.float32
        )
        inner_sum = jnp.sum(probs * grad_probs, axis=-1, keepdims=True)
        grad_scores = (probs * (grad_probs - inner_sum)).astype(jnp.bfloat16)
        query_grad = (
            jnp.einsum("hqk,khd->qhd", grad_scores, key_rows, preferred_element_type=jnp.float32)
            * score_scale
        )
        key_acc = key_acc + jnp.einsum(
            "hqk,qhd->khd", grad_scores, query_part, preferred_element_type=jnp.float32
        )
        value_acc = value_acc + jnp.einsum(
            "hqk,qhd->khd",
            probs.astype(jnp.bfloat16),
            grad_part,
            preferred_element_type=jnp.float32,
        )
        return ((key_acc, value_acc), query_grad)

    zero_acc = jnp.zeros(key_rows.shape, jnp.float32)
    (key_acc, value_acc), query_grads = lax.scan(
        step_block,
        (zero_acc, zero_acc),
        (queries.reshape(block_shape), grad_out.reshape(block_shape), logsum),
    )
    return (query_grads.reshape(queries.shape), key_acc * score_scale, value_acc)


def forward_pass(
    tokens,
    first_gain,
    first_shift,
    attention_bias,
    output_bias,
    second_gain,
    second_shift,
    expand_bias,
    reduce_bias,
    gathered,
):
    inward_all, output_rows, expand_all, reduce_rows = gathered
    full_width = inward_all.shape[0]
    local_width = inward_all.shape[2]
    row_count = tokens.shape[0]
    clip_shape = (row_count // SEQ, SEQ, local_width // HEAD_DIM, HEAD_DIM)
    score_scale = HEAD_DIM ** (-0.5)
    source = tokens.astype(jnp.float32)
    unit_one, inverse_one, normed_one = norm_forward(source, first_gain, first_shift, full_width)
    normed_all = spread_features(normed_one.astype(jnp.bfloat16))
    projected = jnp.dot(
        normed_all,
        inward_all.reshape(full_width, 3 * local_width),
        preferred_element_type=jnp.float32,
    )
    projected = projected.reshape(row_count, 3, local_width)
    queries = (projected[:, 0] + attention_bias[0]).astype(jnp.bfloat16)
    key_rows = projected[:, 1].astype(jnp.bfloat16)
    value_rows = (projected[:, 2] + attention_bias[1]).astype(jnp.bfloat16)
    mixed_rows, logsum = lax.map(
        lambda clip_parts: attend_clip(clip_parts[0], clip_parts[1], clip_parts[2], score_scale),
        (queries.reshape(clip_shape), key_rows.reshape(clip_shape), value_rows.reshape(clip_shape)),
    )
    mixed_low = mixed_rows.reshape(row_count, local_width).astype(jnp.bfloat16)
    hidden_state = (
        source
        + sum_partials(jnp.dot(mixed_low, output_rows, preferred_element_type=jnp.float32))
        + output_bias
    )
    unit_two, inverse_two, normed_two = norm_forward(
        hidden_state, second_gain, second_shift, full_width
    )
    normed_all_two = spread_features(normed_two.astype(jnp.bfloat16))
    expanded = jnp.dot(normed_all_two, expand_all, preferred_element_type=jnp.float32) + expand_bias
    activated = jax.nn.gelu(expanded, approximate=False).astype(jnp.bfloat16)
    output_value = (
        hidden_state
        + sum_partials(jnp.dot(activated, reduce_rows, preferred_element_type=jnp.float32))
        + reduce_bias
    )
    saved_state = (
        unit_one,
        inverse_one,
        normed_all,
        queries,
        key_rows,
        value_rows,
        logsum,
        mixed_low,
        unit_two,
        inverse_two,
        normed_all_two,
        expanded,
        activated,
    )
    return (output_value, saved_state)


def plain_device(
    tokens,
    first_gain,
    first_shift,
    inward_weight,
    attention_bias,
    output_weight,
    output_bias,
    second_gain,
    second_shift,
    expand_weight,
    expand_bias,
    reduce_weight,
    reduce_bias,
    cotangent,
):
    packed_width = tokens.shape[1]
    tokens = tokens.reshape(-1, packed_width // 2)
    cotangent = cotangent.reshape(-1, packed_width // 2)
    gathered = fetch_weights(inward_weight, output_weight, expand_weight, reduce_weight)
    output_value, saved_state = forward_pass(
        tokens,
        first_gain,
        first_shift,
        attention_bias,
        output_bias,
        second_gain,
        second_shift,
        expand_bias,
        reduce_bias,
        gathered,
    )
    gathered = fetch_weights(inward_weight, output_weight, expand_weight, reduce_weight)
    unused_value, saved_state = forward_pass(
        tokens,
        first_gain,
        first_shift,
        attention_bias,
        output_bias,
        second_gain,
        second_shift,
        expand_bias,
        reduce_bias,
        gathered,
    )
    inward_all, output_rows, expand_all, reduce_rows = gathered
    (
        unit_one,
        inverse_one,
        normed_all,
        queries,
        key_rows,
        value_rows,
        logsum,
        mixed_low,
        unit_two,
        inverse_two,
        normed_all_two,
        expanded,
        activated,
    ) = saved_state
    full_width = inward_all.shape[0]
    local_width = inward_all.shape[2]
    row_count = tokens.shape[0]
    clip_shape = (row_count // SEQ, SEQ, local_width // HEAD_DIM, HEAD_DIM)
    score_scale = HEAD_DIM ** (-0.5)
    grad_rows = cotangent.astype(jnp.float32)
    grad_all = spread_grads(cotangent)
    grad_act = lax.dot_general(
        grad_all, reduce_rows, CONTRACT_COLS, preferred_element_type=jnp.float32
    )
    reduce_grad = lax.dot_general(
        activated, grad_all, CONTRACT_ROWS, preferred_element_type=jnp.float32
    )
    reduce_bias_grad = jnp.sum(grad_rows, axis=0)
    gelu_value, gelu_back = jax.vjp(
        lambda inner_value: jax.nn.gelu(inner_value, approximate=False), expanded
    )
    grad_expanded = gelu_back(grad_act)[0].astype(jnp.bfloat16)
    expand_grad = lax.dot_general(
        normed_all_two, grad_expanded, CONTRACT_ROWS, preferred_element_type=jnp.float32
    )
    expand_bias_grad = jnp.sum(grad_expanded.astype(jnp.float32), axis=0)
    grad_normed_two = sum_grad_partials(
        lax.dot_general(
            grad_expanded, expand_all, CONTRACT_COLS, preferred_element_type=jnp.float32
        )
    )
    back_two, second_gain_grad, second_shift_grad = norm_backward(
        grad_normed_two, unit_two, inverse_two, second_gain, full_width
    )
    grad_hidden = grad_rows + back_two
    grad_hidden_low = grad_hidden.astype(jnp.bfloat16)
    grad_hidden_all = spread_grads(grad_hidden_low)
    output_grad = lax.dot_general(
        mixed_low, grad_hidden_all, CONTRACT_ROWS, preferred_element_type=jnp.float32
    )
    output_bias_grad = jnp.sum(grad_hidden_low.astype(jnp.float32), axis=0)
    grad_mixed = lax.dot_general(
        grad_hidden_all, output_rows, CONTRACT_COLS, preferred_element_type=jnp.float32
    ).astype(jnp.bfloat16)
    query_grads, key_grads, value_grads = lax.map(
        lambda clip_parts: attend_clip_back(
            clip_parts[0], clip_parts[1], clip_parts[2], clip_parts[3], clip_parts[4], score_scale
        ),
        (
            queries.reshape(clip_shape),
            key_rows.reshape(clip_shape),
            value_rows.reshape(clip_shape),
            logsum,
            grad_mixed.reshape(clip_shape),
        ),
    )
    stacked = jnp.stack(
        [
            query_grads.reshape(row_count, local_width),
            key_grads.reshape(row_count, local_width),
            value_grads.reshape(row_count, local_width),
        ],
        axis=1,
    ).astype(jnp.bfloat16)
    attention_bias_grad = jnp.stack(
        [
            jnp.sum(stacked[:, 0].astype(jnp.float32), axis=0),
            jnp.sum(stacked[:, 2].astype(jnp.float32), axis=0),
        ]
    )
    flat_grads = stacked.reshape(row_count, 3 * local_width)
    inward_grad = lax.dot_general(
        normed_all, flat_grads, CONTRACT_ROWS, preferred_element_type=jnp.float32
    ).reshape(full_width, 3, local_width)
    grad_normed_one = sum_grad_partials(
        lax.dot_general(
            flat_grads,
            inward_all.reshape(full_width, 3 * local_width),
            CONTRACT_COLS,
            preferred_element_type=jnp.float32,
        )
    )
    back_one, first_gain_grad, first_shift_grad = norm_backward(
        grad_normed_one, unit_one, inverse_one, first_gain, full_width
    )
    tokens_grad = grad_hidden + back_one
    inward_grad, output_grad, expand_grad, reduce_grad = (
        lax.psum_scatter(
            inward_grad.astype(jnp.bfloat16), "row", scatter_dimension=0, tiled=True
        ).astype(jnp.float32),
        lax.psum_scatter(
            output_grad.astype(jnp.bfloat16), "row", scatter_dimension=1, tiled=True
        ).astype(jnp.float32),
        lax.psum_scatter(
            expand_grad.astype(jnp.bfloat16), "row", scatter_dimension=0, tiled=True
        ).astype(jnp.float32),
        lax.psum_scatter(
            reduce_grad.astype(jnp.bfloat16), "row", scatter_dimension=1, tiled=True
        ).astype(jnp.float32),
    )
    (
        first_gain_grad,
        first_shift_grad,
        attention_bias_grad,
        output_bias_grad,
        second_gain_grad,
        second_shift_grad,
        expand_bias_grad,
        reduce_bias_grad,
    ) = lax.psum(
        (
            first_gain_grad,
            first_shift_grad,
            attention_bias_grad,
            output_bias_grad,
            second_gain_grad,
            second_shift_grad,
            expand_bias_grad,
            reduce_bias_grad,
        ),
        "row",
    )
    return (
        output_value.astype(jnp.bfloat16).reshape(-1, packed_width),
        tokens_grad.reshape(-1, packed_width),
        first_gain_grad,
        first_shift_grad,
        inward_grad,
        attention_bias_grad,
        output_grad,
        output_bias_grad,
        second_gain_grad,
        second_shift_grad,
        expand_grad,
        expand_bias_grad,
        reduce_grad,
        reduce_bias_grad,
    )


def fused_device(
    tokens,
    first_gain,
    first_shift,
    inward_weight,
    attention_bias,
    output_weight,
    output_bias,
    second_gain,
    second_shift,
    expand_weight,
    expand_bias,
    reduce_weight,
    reduce_bias,
    cotangent,
):
    kept = forward_call(
        tokens,
        cotangent,
        first_gain[None],
        first_shift[None],
        output_bias[None],
        second_gain[None],
        second_shift[None],
        reduce_bias[None],
        attention_bias,
        expand_bias[None],
        inward_weight.transpose(1, 0, 2),
        output_weight,
        expand_weight,
        reduce_weight,
    )
    (tok, cot, q, qt, k, kt, v, mixf, lse, hid, unit, inv, normed, act, slope, win, wo, we, wr, vec, one, stat) = kept

    def flat(array):
        return array.reshape(-1, array.shape[-1])

    outs = backward_call(
        flat(tok), flat(cot), cotangent, flat(q), qt, flat(k), kt, flat(v), flat(mixf), lse, flat(hid), flat(unit),
        flat(inv), flat(normed), flat(act), flat(slope), win, wo, we, wr, vec, flat(one), flat(stat),
    )
    outs = finish_call(*outs)
    layer_output, tokens_grad, inward_grad, output_grad, expand_grad, reduce_grad = outs[:6]
    first_gain_grad, first_shift_grad, attention_grad, out_grad, gain_grad, shift_grad, red_grad, exp_grad = outs[6:]
    return (
        layer_output,
        tokens_grad,
        first_gain_grad[0],
        first_shift_grad[0],
        inward_grad.transpose(1, 0, 2),
        attention_grad,
        output_grad,
        out_grad[0],
        gain_grad[0],
        shift_grad[0],
        expand_grad,
        exp_grad[0],
        reduce_grad,
        red_grad[0],
    )


def per_device(rows, cols, *arrays):
    tokens, inward_weight, expand_weight = arrays[0], arrays[3], arrays[9]
    fits = (
        (rows, cols) == (8, 4)
        and tokens.shape == (SEQ // 2, 512)
        and inward_weight.shape == (128, 3, 256)
        and expand_weight.shape == (128, 1024)
    )
    return fused_device(*arrays) if fits else plain_device(*arrays)


def solution(mesh):
    in_specs = (
        P("row", "col"),
        P("col"),
        P("col"),
        P("row", None, "col"),
        P(None, "col"),
        P("col", "row"),
        P("col"),
        P("col"),
        P("col"),
        P("row", "col"),
        P("col"),
        P("col", "row"),
        P("col"),
        P("row", "col"),
    )
    out_specs = (
        P("row", "col"),
        P("row", "col"),
        P("col"),
        P("col"),
        P("row", None, "col"),
        P(None, "col"),
        P("col", "row"),
        P("col"),
        P("col"),
        P("col"),
        P("row", "col"),
        P("col"),
        P("col", "row"),
        P("col"),
    )
    return jax.shard_map(
        functools.partial(per_device, mesh.shape["row"], mesh.shape["col"]),
        mesh=mesh, in_specs=in_specs, out_specs=out_specs, check_vma=False
    )
```

```python
import functools
import jax
import jax.numpy as jnp
from jax import lax
from jax.experimental import pallas as pl
from jax.experimental.pallas import tpu as pltpu
from jax.sharding import PartitionSpec as P

HEAD_DIM = 64
SEQ = 1568
EPSILON = 1e-06
CHUNKS = 7
WINDOW = 2
F32 = jnp.float32
BF16 = jnp.bfloat16
MESH = pl.DeviceIdType.MESH
LOG2E = 1.4426950408889634
NT_DIMS = (((1,), (1,)), ((), ()))
TN_DIMS = (((0,), (0,)), ((), ()))


def remote(src, dst, send, recv, row, col):
    return pltpu.make_async_remote_copy(
        src_ref=src, dst_ref=dst, send_sem=send, recv_sem=recv,
        device_id=(row, col), device_id_type=MESH,
    )


def aligned(index, size):
    return pl.ds(pl.multiple_of(index * size, size), size)


def row_norm(values):
    mean = jnp.mean(values, axis=1, keepdims=True)
    centred = values - mean
    inverse = lax.rsqrt(jnp.mean(centred * centred, axis=1, keepdims=True) + EPSILON)
    return centred * inverse, mean, inverse


def weight_blocks(ref, kind, row):
    if kind == "three":
        return ref.at[:, aligned(row, 128), :]
    if kind == "rows":
        return ref.at[aligned(row, 128), :]
    return ref.at[:, aligned(row, 128)]


WEIGHT_KINDS = ("three", "cols", "rows", "cols")


def forward_kernel(
    tok, cot, g_one, s_one, b_out, g_two, s_two, b_red, attn_bias, exp_bias, win_s, wo_s, we_s, wr_s,
    tok_o, cot_o, q_o, qt_o, k_o, kt_o, v_o, mixf_o, lse_o, hid_o, unit_o, inv_o,
    norm_o, act_o, slope_o, win_o, wo_o, we_o, wr_o, vec_o, one_o, stat_o,
    tok_all, cot_all, norm_one, q, qt, k, kt, v, vt, mixed, mixf, lse, hid, unit, inv, norm_two, act, slope,
    win, wo, we, wr, vecs, stat, scores,
    local_sem, shard_sem, tok_sem, cot_sem, wz_send, wz_recv, wy_send, wy_recv, vec_send, vec_recv,
    tx_send, tx_recv, tc_send, tc_recv, tp_send, tp_recv, cx_send, cx_recv, cc_send, cc_recv, cp_send, cp_recv,
    wx_send, wx_recv, wc_send, wc_recv, mx_send, mx_recv, mc_send, mc_recv,
):
    r, c = lax.axis_index("row"), lax.axis_index("col")
    z, y = r // 2, r % 2
    xx, core = c // 2, c % 2
    c_x, c_core, c_far = (c + 2) % 4, c + 1 - 2 * core, (c + 2) % 4 + 1 - 2 * core
    r_y = r + 1 - 2 * y
    half = tok.shape[0] // CHUNKS
    chunk = 2 * half
    width = g_one.shape[1]
    scale = LOG2E * HEAD_DIM ** (-0.5)

    barrier = pltpu.get_barrier_semaphore()
    for col in (c_x, c_core, c_far):
        pl.semaphore_signal(barrier, inc=1, device_id=(r, col), device_id_type=MESH)
    pl.semaphore_signal(barrier, inc=1, device_id=(r_y, c), device_id_type=MESH)

    @pl.when(z >= 1)
    def _():
        pl.semaphore_signal(barrier, inc=1, device_id=(r - 2, c), device_id_type=MESH)

    @pl.when(z <= 2)
    def _():
        pl.semaphore_signal(barrier, inc=1, device_id=(r + 2, c), device_id_type=MESH)


    own = aligned(c, width)
    shards = (win_s, wo_s, we_s, wr_s)
    fulls = (win, wo, we, wr)
    shard_loads = [
        pltpu.make_async_copy(
            shards[w],
            wo.at[aligned(core * 2 + xx, width), aligned(r, 128)] if w == 1
            else weight_blocks(fulls[w], WEIGHT_KINDS[w], r),
            shard_sem.at[w],
        )
        for w in range(4)
    ]
    for copy in shard_loads:
        copy.start()

    def half_source(ref, i, s):
        return ref.at[pl.ds(pl.multiple_of(i * half, half), half), pl.ds(s * width, width)]

    def half_load(ref, full_ref, sem, i, s):
        return pltpu.make_async_copy(
            half_source(ref, i, s), full_ref.at[i, pl.ds(s * half, half), own], sem.at[i, s]
        )

    for i in range(CHUNKS):
        for s in range(2):
            half_load(tok, tok_all, tok_sem, i, s).start()
            half_load(cot, cot_all, cot_sem, i, s).start()
    for n, vector in enumerate((g_one, s_one, b_out, g_two, s_two, b_red, b_red, b_red)):
        vecs[n : n + 1, own] = vector[...]
    pl.semaphore_wait(barrier, 4 + jnp.where(z >= 1, 1, 0) + jnp.where(z <= 2, 1, 0))

    slab = core * 2 + xx

    def out_piece(x, row):
        return wo.at[aligned(core * 2 + x, width), aligned(row, 128)]

    def out_x():
        return remote(wo_s, out_piece(xx, r), wx_send.at[0], wx_recv.at[0], r, c_x)

    def out_y(row):
        block = wo.at[aligned(core, 2 * width), aligned(row, 128)]
        return remote(block, block, wy_send.at[1, 0], wy_recv.at[1, 0], r_y, c)

    def out_core(side):
        block = wo.at[aligned(side, 2 * width), :]
        return remote(block, block, wc_send.at[0], wc_recv.at[0], r, c_core)

    def weight_ref(w, zb, side):
        if w == 1:
            return wo.at[aligned(core, 2 * width), aligned(zb, 256)]
        return weight_blocks(fulls[w], WEIGHT_KINDS[w], zb * 2 + side)

    def line_copy(w, up, hop):
        zb = z - hop if up else z + hop
        block = weight_ref(w, zb, y)
        target = (z + 1 if up else z - 1) * 2 + y
        source = shards[w] if hop == 0 and w != 1 else block
        return remote(source, block, wz_send.at[w, up, hop], wz_recv.at[w, up, hop], target, c)

    def line_sends(up, hop):
        return (z >= hop) & (z <= 2) if up else (z <= 3 - hop) & (z >= 1)

    def line_receives(up, hop):
        return z >= hop + 1 if up else z <= 2 - hop

    def y_copy(w, zb, side):
        block = weight_ref(w, zb, side)
        return remote(block, block, wy_send.at[w, zb], wy_recv.at[w, zb], r_y, c)

    def start_weight(w):
        for up in (0, 1):
            @pl.when(line_sends(up, 0))
            def _():
                line_copy(w, up, 0).start()

    def own_to_y(w):
        return remote(shards[w], weight_ref(w, z, y), wy_send.at[w, z], wy_recv.at[w, z], r_y, c)

    def forward_weight(w, hop):
        for up in (0, 1):
            @pl.when(line_receives(up, hop))
            def _():
                zb = z - 1 - hop if up else z + 1 + hop
                block = weight_ref(w, zb, y)
                remote(block, block, wz_send.at[w, up, hop], wz_recv.at[w, up, hop], r_y, c).wait_recv()
                if w != 1:
                    y_copy(w, zb, y).start()

            if hop < 2:
                @pl.when(line_receives(up, hop) & line_sends(up, hop + 1))
                def _():
                    line_copy(w, up, hop + 1).start()

    def finish_weight(w):
        for up in (0, 1):
            for hop in range(3):
                @pl.when(line_sends(up, hop))
                def _():
                    line_copy(w, up, hop).wait_send()
        if w != 1:
            for zb in range(4):
                y_copy(w, zb, y).wait_send()
                y_copy(w, zb, 1 - y).wait_recv()

    def vec_copy(slot, target, col):
        block = vecs.at[:, aligned(col, width)]
        return remote(block, block, vec_send.at[slot], vec_recv.at[slot], r, target)

    def half_x(ref, full_ref, send, recv, i, s, col):
        block = full_ref.at[i, pl.ds(s * half, half), aligned(col, width)]
        return remote(half_source(ref, i, s), block, send.at[i, s], recv.at[i, s], r, c_x)

    def half_core(ref, full_ref, send, recv, i, s, col):
        block = full_ref.at[i, pl.ds(s * half, half), aligned(col, width)]
        return remote(half_source(ref, i, s), block, send.at[i, s], recv.at[i, s], r, c_core)

    def tok_x(i, s, col):
        return half_x(tok, tok_all, tx_send, tx_recv, i, s, col)

    def tok_core(i, s, col):
        return half_core(tok, tok_all, tc_send, tc_recv, i, s, col)

    def cot_x(i, s, col):
        return half_x(cot, cot_all, cx_send, cx_recv, i, s, col)

    def cot_core(i, s, col):
        return half_core(cot, cot_all, cc_send, cc_recv, i, s, col)

    def pass_core(full_ref, send, recv, i, col):
        block = full_ref.at[i, :, aligned(col, width)]
        return remote(block, block, send.at[i], recv.at[i], r, c_core)

    def tok_pass(i, col):
        return pass_core(tok_all, tp_send, tp_recv, i, col)

    def cot_pass(i, col):
        return pass_core(cot_all, cp_send, cp_recv, i, col)

    def send_cot(i):
        for s in range(2):
            cot_x(i, s, c).start()
            cot_core(i, s, c).start()

    def send_tok(i):
        for s in range(2):
            tok_x(i, s, c).start()
            tok_core(i, s, c).start()

    start_weight(0)
    own_to_y(0).start()
    for i in range(WINDOW):
        send_tok(i)
    out_x().start()
    for slot, target in enumerate((c_x, c_core, c_far)):
        vec_copy(slot, target, c).start()

    def keep(index, i, src, dst):
        return pltpu.make_async_copy(src, dst, local_sem.at[index, i])

    def kept(i, stage):
        if stage == 0:
            pairs = ((tok_all, tok_o), (q, q_o), (qt, qt_o), (k, k_o), (kt, kt_o), (v, v_o), (norm_one, one_o), (stat, stat_o))
            base = 0
        elif stage == 1:
            pairs = ((mixf, mixf_o), (lse, lse_o))
            base = 8
        elif stage == 2:
            pairs = ((unit, unit_o), (inv, inv_o), (norm_two, norm_o), (act, act_o), (slope, slope_o))
            base = 10
        else:
            pairs = ((cot_all, cot_o),)
            base = 15
        return [keep(base + n, i, a.at[i], b.at[i]) for n, (a, b) in enumerate(pairs)]

    def keep_hid(i):
        return keep(16, i, hid.at[i % 2, :, own], hid_o.at[i])

    lane_ids = lax.broadcasted_iota(jnp.int32, (chunk // 7, 128), 1)

    def first_norm(i):
        for s in range(2):
            half_load(tok, tok_all, tok_sem, i, s).wait()
            tok_core(i, s, c_core).wait_recv()
        tok_pass(i, c_far).wait_recv()
        for part in range(7):
            rows = pl.ds(part * (chunk // 7), chunk // 7)
            units, mean, inverse = row_norm(tok_all[i, rows, :].astype(F32))
            stat[i, rows, :] = jnp.where(lane_ids < 64, mean, inverse)
            norm_one[i, rows, :] = (units * vecs[0:1, :] + vecs[1:2, :]).astype(BF16)

    @pl.loop(0, CHUNKS // 2 + 1)
    def _(g):
        @pl.loop(2 * g, jnp.minimum(2 * g + 2, CHUNKS))
        def _(i):
            for s in range(2):
                tok_x(i, s, c_x).wait_recv()

            @pl.when(i + WINDOW < CHUNKS)
            def _():
                send_tok(i + WINDOW)

            tok_pass(i, c_x).start()

        @pl.when(g == 0)
        def _():
            for slot, target in enumerate((c_x, c_core, c_far)):
                vec_copy(slot, target, c).wait_send()
                vec_copy(slot, target, target).wait_recv()

        for hop in range(3):
            @pl.when(g == hop)
            def _():
                forward_weight(0, hop)

        @pl.when(g == 0)
        def _():
            shard_loads[1].wait()
            out_x().wait()
            out_y(r).start()
            start_weight(2)

        @pl.when(g == 3)
        def _():
            out_y(r).wait_send()
            out_y(r_y).wait_recv()
            start_weight(1)

        @pl.loop(2 * g, jnp.minimum(2 * g + 2, CHUNKS))
        def _(i):
            first_norm(i)

    send_cot(0)
    for w in (0, 2, 3):
        shard_loads[w].wait()
    finish_weight(0)

    @pl.loop(0, CHUNKS)
    def _(i):
        part = jnp.dot(norm_one[i], win[0], preferred_element_type=F32)
        part = (part + attn_bias[0:1, :]).astype(BF16)
        q[i] = part
        qt[i] = part.T
        part = jnp.dot(norm_one[i], win[1], preferred_element_type=F32).astype(BF16)
        k[i] = part
        kt[i] = part.T
        part = jnp.dot(norm_one[i], win[2], preferred_element_type=F32)
        part = (part + attn_bias[1:2, :]).astype(BF16)
        v[i] = part
        vt[i] = part.T
        for copy in kept(i, 0):
            copy.start()

        @pl.when(i == 2)
        def _():
            own_to_y(2).start()
            forward_weight(2, 0)

        @pl.when(i == 5)
        def _():
            send_cot(1)

        @pl.when(i == 6)
        def _():
            own_to_y(3).start()


    def attend(i):
        row_ids = lax.broadcasted_iota(jnp.int32, (128, chunk), 0)

        @pl.loop(0, width // 128)
        def _(pair):
            lanes = aligned(pair, 128)
            peaks = []
            for h in range(2):
                query = qt[i, lanes, :]
                query = jnp.where(row_ids // HEAD_DIM == h, query, jnp.zeros_like(query))
                peak = jnp.full((1, chunk), -jnp.inf, F32)
                for j in range(CHUNKS):
                    block = jnp.dot(k[j, :, lanes], query, preferred_element_type=F32)
                    scores[h, j] = block
                    peak = jnp.maximum(peak, jnp.max(block, axis=0, keepdims=True))
                peaks.append(peak * scale)
            outs = []
            for h in range(2):
                total = jnp.zeros((1, chunk), F32)
                acc = jnp.zeros((HEAD_DIM, chunk), F32)
                rows = pl.ds(pl.multiple_of(pair * 128 + h * HEAD_DIM, HEAD_DIM), HEAD_DIM)
                for j in range(CHUNKS):
                    weights = jnp.exp2(scores[h, j] * scale - peaks[h])
                    total = total + jnp.sum(weights, axis=0, keepdims=True)
                    acc = acc + jnp.dot(vt[j, rows, :], weights.astype(BF16), preferred_element_type=F32)
                outs.append(acc / total)
                lse[i, pl.ds(pair * 2 + h, 1), :] = peaks[h] + jnp.log2(total)
            out = jnp.concatenate(outs, axis=0).T
            mixf[i, :, lanes] = out
            mixed[i, :, aligned(slab * 2 + pair, 128)] = out.astype(BF16)

    def mixed_block(i, order):
        return mixed.at[i, :, aligned(order, width)]

    def mixed_x(i, order):
        block = mixed_block(i, order)
        return remote(block, block, mx_send.at[i], mx_recv.at[i], r, c_x)

    def mixed_core(i, slot, order):
        block = mixed_block(i, order)
        return remote(block, block, mc_send.at[i, slot], mc_recv.at[i, slot], r, c_core)

    def expand(t):
        mixed_core(t, 0, (1 - core) * 2 + xx).wait_recv()
        mixed_core(t, 1, (1 - core) * 2 + 1 - xx).wait_recv()

        @pl.when(t >= 2)
        def _():
            keep_hid(t - 2).wait()

        hid[t % 2] = tok_all[t].astype(F32) + (
            jnp.dot(mixed[t], wo[...], preferred_element_type=F32) + vecs[2:3, :]
        )
        for part in range(7):
            rows = pl.ds(part * (chunk // 7), chunk // 7)
            units, _, inverse = row_norm(hid[t % 2, rows, :])
            unit[t, rows, :] = units.astype(BF16)
            inv[t, rows, :] = jnp.broadcast_to(inverse, (chunk // 7, 128))
            norm_two[t, rows, :] = (units * vecs[3:4, :] + vecs[4:5, :]).astype(BF16)
        for n in range(we.shape[1] // 256):
            lanes = slice(n * 256, (n + 1) * 256)
            expanded = jnp.dot(norm_two[t], we[:, lanes], preferred_element_type=F32) + exp_bias[:, lanes]
            gate = 0.5 + 0.5 * lax.erf(expanded * (0.5 ** 0.5))
            act[t, :, lanes] = (expanded * gate).astype(BF16)
            bell = jnp.exp2(expanded * expanded * (-0.5 * LOG2E)) * 0.3989422804014327
            slope[t, :, lanes] = (gate + expanded * bell).astype(BF16)
        for copy in kept(t, 2):
            copy.start()
        keep_hid(t).start()

    def pass_mixed(t):
        mixed_x(t, core * 2 + 1 - xx).wait_recv()
        mixed_core(t, 1, core * 2 + 1 - xx).start()

    def pass_on_cot(t):
        for s in range(2):
            cot_x(t, s, c_x).wait_recv()
            half_load(cot, cot_all, cot_sem, t, s).wait()
        cot_pass(t, c_x).start()

    @pl.loop(0, CHUNKS)
    def _(i):
        attend(i)
        mixed_x(i, slab).start()
        mixed_core(i, 0, slab).start()
        for copy in kept(i, 1):
            copy.start()

        @pl.when(i == 0)
        def _():
            forward_weight(1, 0)

        @pl.when(i == 1)
        def _():
            forward_weight(2, 1)

        @pl.when(i == 3)
        def _():
            start_weight(3)
            forward_weight(1, 1)

        @pl.when(i == 5)
        def _():
            forward_weight(2, 2)

        @pl.when(i == 6)
        def _():
            forward_weight(3, 0)

        @pl.when(i >= 1)
        def _():
            pass_mixed(i - 1)

    pass_mixed(CHUNKS - 1)
    forward_weight(1, 2)
    finish_weight(1)
    out_core(core).start()
    send_cot(2)
    pass_on_cot(0)
    pass_on_cot(1)
    out_core(core).wait_send()
    out_core(1 - core).wait_recv()
    finish_weight(2)

    @pl.loop(0, CHUNKS)
    def _(t):
        expand(t)

        @pl.when(t == 0)
        def _():
            send_cot(3)
            forward_weight(3, 1)

        @pl.when(t == 1)
        def _():
            for n in range(4, CHUNKS):
                send_cot(n)

        @pl.when(t == 3)
        def _():
            forward_weight(3, 2)

        @pl.when(t >= 2)
        def _():
            pass_on_cot(t)

    @pl.loop(0, CHUNKS)
    def _(i):
        mixed_x(i, slab).wait_send()
        mixed_core(i, 0, slab).wait_send()
        mixed_core(i, 1, core * 2 + 1 - xx).wait_send()
        for s in range(2):
            cot_x(i, s, c).wait_send()
            cot_core(i, s, c).wait_send()
            cot_core(i, s, c_core).wait_recv()
        cot_pass(i, c_x).wait_send()
        cot_pass(i, c_far).wait_recv()
        for copy in kept(i, 3):
            copy.start()

    @pl.loop(0, CHUNKS)
    def _(i):
        for s in range(2):
            tok_x(i, s, c).wait_send()
            tok_core(i, s, c).wait_send()
        tok_pass(i, c_x).wait_send()

    finish_weight(3)
    last = [
        keep(17, n, a, b)
        for n, (a, b) in enumerate(((win, win_o), (wo.at[aligned(slab, width), :], wo_o), (we, we_o), (wr, wr_o), (vecs, vec_o)))
    ]
    for copy in last:
        copy.start()

    @pl.loop(0, CHUNKS)
    def _(i):
        for stage in range(4):
            for copy in kept(i, stage):
                copy.wait()

    for t in (CHUNKS - 2, CHUNKS - 1):
        keep_hid(t).wait()

    for copy in last:
        copy.wait()


def forward_call(*arrays):
    tok, we_s = arrays[0], arrays[-2]
    pairs, width = tok.shape[0], tok.shape[1] // 2
    chunk = 2 * pairs // CHUNKS
    full = 4 * width
    hidden = we_s.shape[1]
    n = CHUNKS

    def sd(shape, dtype):
        return jax.ShapeDtypeStruct(shape, dtype)

    outs = [
        sd((n, chunk, full), BF16),
        sd((n, chunk, full), BF16),
        sd((n, chunk, width), BF16),
        sd((n, width, chunk), BF16),
        sd((n, chunk, width), BF16),
        sd((n, width, chunk), BF16),
        sd((n, chunk, width), BF16),
        sd((n, chunk, width), F32),
        sd((n, 8, chunk), F32),
        sd((n, chunk, width), F32),
        sd((n, chunk, full), BF16),
        sd((n, chunk, 128), F32),
        sd((n, chunk, full), BF16),
        sd((n, chunk, hidden), BF16),
        sd((n, chunk, hidden), BF16),
        sd((3, full, width), BF16),
        sd((width, full), BF16),
        sd((full, hidden), BF16),
        sd((hidden, full), BF16),
        sd((8, full), F32),
        sd((n, chunk, full), BF16),
        sd((n, chunk, 128), F32),
    ]
    vm = pltpu.VMEM
    dma = pltpu.SemaphoreType.DMA
    scratch = [
        vm((n, chunk, full), BF16), vm((n, chunk, full), BF16), vm((n, chunk, full), BF16),
        vm((n, chunk, width), BF16), vm((n, width, chunk), BF16),
        vm((n, chunk, width), BF16), vm((n, width, chunk), BF16),
        vm((n, chunk, width), BF16), vm((n, width, chunk), BF16),
        vm((n, chunk, full), BF16), vm((n, chunk, width), F32), vm((n, 8, chunk), F32),
        vm((2, chunk, full), F32), vm((n, chunk, full), BF16), vm((n, chunk, 128), F32),
        vm((n, chunk, full), BF16), vm((n, chunk, hidden), BF16), vm((n, chunk, hidden), BF16),
        vm((3, full, width), BF16), vm((full, full), BF16), vm((full, hidden), BF16), vm((hidden, full), BF16),
        vm((8, full), F32), vm((n, chunk, 128), F32),
        vm((2, n, chunk, chunk), F32),
        dma((18, n)), dma((4,)), dma((n, 2)), dma((n, 2)), dma((4, 2, 3)), dma((4, 2, 3)), dma((4, 4)), dma((4, 4)), dma((3,)), dma((3,)),
        dma((n, 2)), dma((n, 2)), dma((n, 2)), dma((n, 2)), dma((n,)), dma((n,)),
        dma((n, 2)), dma((n, 2)), dma((n, 2)), dma((n, 2)), dma((n,)), dma((n,)),
        dma((1,)), dma((1,)), dma((1,)), dma((1,)), dma((n,)), dma((n,)), dma((n, 2)), dma((n, 2)),
    ]
    return pl.pallas_call(
        forward_kernel,
        out_shape=outs,
        in_specs=[pl.BlockSpec(memory_space=pl.ANY if n in (0, 1, 10, 11, 12, 13) else pltpu.VMEM) for n in range(len(arrays))],
        out_specs=[pl.BlockSpec(memory_space=pl.ANY)] * len(outs),
        scratch_shapes=scratch,
        compiler_params=pltpu.CompilerParams(
            collective_id=0, has_side_effects=True, vmem_limit_bytes=63 << 20
        ),
    )(*arrays)


GRAD_KINDS = ("three", "cols", "rows", "cols")


def backward_kernel(
    tok_h, cot_h, q_h, qt_h, k_h, kt_h, v_h, mixf_h, lse_h, hid_h, unit_h, inv_h,
    normed_h, act_h, slope_h, win_h, wo_h, we_h, wr_h, vec_h, one_h, stat_h,
    out_o, tg_o, sums_o, gin_o, gout_o, gexp_o, gred_o,
    cot, q, qt, k, kt, v, mixf, lse, hid, unit, inv, normed, act, slope, win, wo, we, wr, vecs,
    grad, flat, dk, dv, tg, out, sb_g, sb_o, rb_g, xr_g, rb_o, xr_o, xr_1, st, st_in,
    col_sums, packet, packets,
    ys_in, ys_out, ys_exp, ys_red, oh_in, oh_out, oh_exp, oh_red,
    yr_in, yr_out, yr_exp, yr_red, zr_in, zr_out, zr_exp, zr_red,
    gin, gout, gexp, gred,
    load_sem, store_sem, hid_sem, gy_send, gy_recv, gz_send, gz_recv,
    h1g_send, h1g_recv, h2g_send, h2g_recv, h3g_send, h3g_recv,
    h1o_send, h1o_recv, h2o_send, h2o_recv, h1t_send, h1t_recv, h2t_send, h2t_recv,
    st_send, st_recv, pk_send, pk_recv,
):
    r, c = lax.axis_index("row"), lax.axis_index("col")
    z, y = r // 2, r % 2
    xx, core = c // 2, c % 2
    c_x, c_core, c_far = (c + 2) % 4, c + 1 - 2 * core, (c + 2) % 4 + 1 - 2 * core
    r_y = r + 1 - 2 * y
    tok, one, stat = act, normed, inv
    chunk = q.shape[0] // CHUNKS
    half = chunk // 2
    width = q.shape[1]
    full = cot.shape[1]
    scale = LOG2E * HEAD_DIM ** (-0.5)
    own = aligned(c, width)
    others = [(r + step) % 8 for step in range(1, 8)]

    barrier = pltpu.get_barrier_semaphore()
    for col in (c_x, c_core, c_far):
        pl.semaphore_signal(barrier, inc=1, device_id=(r, col), device_id_type=MESH)
    for row in others:
        pl.semaphore_signal(barrier, inc=1, device_id=(row, c), device_id_type=MESH)

    loads = {}
    order = (
        ("wr", wr_h, wr), ("cot", cot_h, cot), ("slope", slope_h, slope), ("we", we_h, we), ("act", act_h, act),
        ("vec", vec_h, vecs), ("unit", unit_h, unit), ("inv", inv_h, inv), ("wo", wo_h, wo),
        ("normed", normed_h, normed), ("mixf", mixf_h, mixf), ("lse", lse_h, lse), ("qt", qt_h, qt), ("q", q_h, q),
        ("k", k_h, k), ("v", v_h, v), ("kt", kt_h, kt), ("stat", stat_h, stat),
        ("tok", tok_h, tok), ("one", one_h, one),
    )
    for n, (name, src, dst) in enumerate(order):
        loads[name] = pltpu.make_async_copy(src, dst, load_sem.at[n])
    for n in range(3):
        loads["win" + str(n)] = pltpu.make_async_copy(
            win_h.at[n], win.at[:, pl.ds(n * width, width)], load_sem.at[len(order) + n]
        )
    late = ("tok", "one", "stat", "win0", "win1", "win2")
    for name in loads:
        if name not in late:
            loads[name].start()
    dk[...] = jnp.zeros_like(dk)
    dv[...] = jnp.zeros_like(dv)
    col_sums[...] = jnp.zeros_like(col_sums)
    pl.semaphore_wait(barrier, 10)

    def rows_of(i):
        return pl.ds(pl.multiple_of(i * chunk, chunk), chunk)

    def h1(sb, rb, send, recv, i):
        return remote(sb.at[i % 2, 1 - core], rb.at[i], send.at[i], recv.at[i], r, c_core)

    def fill(sb, i, partial):
        for x in range(2):
            for side in range(2):
                block = x * 2 + side
                sb[i % 2, side, x] = partial[:, block * width : (block + 1) * width].astype(BF16)

    def merge(sb, rb, i):
        for x in range(2):
            rb[i, x] = (sb[i % 2, core, x].astype(F32) + rb[i, x].astype(F32)).astype(BF16)

    def h1g(i):
        return h1(sb_g, rb_g, h1g_send, h1g_recv, i)

    def h1o(i):
        return h1(sb_o, rb_o, h1o_send, h1o_recv, i)

    def h1t(i):
        return h1(sb_g, rb_g, h1t_send, h1t_recv, i)

    def h2g(i):
        return remote(rb_g.at[i], xr_g.at[i], h2g_send.at[i], h2g_recv.at[i], r, c_x)

    def h2o(i):
        return remote(rb_o.at[i, 1 - xx], xr_o.at[i], h2o_send.at[i], h2o_recv.at[i], r, c_x)

    def h2t(i):
        return remote(rb_g.at[i, 1 - xx], xr_1.at[i], h2t_send.at[i], h2t_recv.at[i], r, c_x)

    def h3g(i, x, side):
        block = grad.at[i % 4, :, aligned(x * 2 + side, width)]
        return remote(block, block, h3g_send.at[i, x], h3g_recv.at[i, x], r, c_core)

    def spread_grad(i):
        h2g(i).wait()
        if isinstance(i, int):
            h2g(i + 4).start()
        else:
            @pl.when(i + 4 < CHUNKS)
            def _():
                h2g(i + 4).start()

        for x in range(2):
            grad[i % 4, :, aligned(x * 2 + core, width)] = rb_g[i, x].astype(F32) + xr_g[i, x].astype(F32)
        for x in range(2):
            h3g(i, x, core).start()

    def column_sums(values):
        ones = jnp.ones((8, values.shape[0]), BF16)
        return jnp.dot(ones, values, preferred_element_type=F32)[0:1, :]

    ys = (ys_in, ys_out, ys_exp, ys_red)
    oh = (oh_in, oh_out, oh_exp, oh_red)
    yr = (yr_in, yr_out, yr_exp, yr_red)
    zr = (zr_in, zr_out, zr_exp, zr_red)

    def gy(w, s):
        return remote(ys[w].at[s], yr[w].at[s], gy_send.at[w, s], gy_recv.at[w, s], r_y, c)

    def gz(w, s):
        target = ((z + 1 + s) % 4) * 2 + y
        return remote(oh[w].at[s], zr[w].at[s], gz_send.at[w, s], gz_recv.at[w, s], target, c)

    def grad_block(w, s, left, right):
        zt = (z + 1 + s) % 4
        lanes = aligned(zt, 256)
        if GRAD_KINDS[w] == "rows":
            block = lax.dot_general(left[:, lanes], right, TN_DIMS, preferred_element_type=F32).astype(BF16)
            low, high = block[0:128, :], block[128:256, :]
        else:
            block = lax.dot_general(left, right[:, lanes], TN_DIMS, preferred_element_type=F32).astype(BF16)
            low, high = block[:, 0:128], block[:, 128:256]

        @pl.when(y == 0)
        def _():
            oh[w][s] = low
            ys[w][s] = high

        @pl.when(y == 1)
        def _():
            oh[w][s] = high
            ys[w][s] = low

    def pass_on(w, s):
        gy(w, s).wait()
        oh[w][s] = (oh[w][s].astype(F32) + yr[w][s].astype(F32)).astype(BF16)
        gz(w, s).start()

    def finish_grad(w, dst):
        gy(w, 3).wait()
        total = oh[w][3].astype(F32) + yr[w][3].astype(F32)
        for s in range(3):
            gz(w, s).wait()
            total = total + zr[w][s].astype(F32)
        dst[...] = total

    for name in ("wr", "cot", "slope", "we", "act"):
        loads[name].wait()

    @pl.loop(0, CHUNKS + 1)
    def _(i):
        @pl.when(i < CHUNKS)
        def _():
            rows = rows_of(i)
            for n in range(slope.shape[1] // 256):
                lanes = slice(n * 256, (n + 1) * 256)
                grad_act = lax.dot_general(cot[rows, :], wr[lanes, :], NT_DIMS, preferred_element_type=F32)
                low = (slope[rows, lanes].astype(F32) * grad_act).astype(BF16)
                slope[rows, lanes] = low
            fill(sb_g, i, lax.dot_general(slope[rows, :], we[...], NT_DIMS, preferred_element_type=F32))
            h1g(i).start()

        @pl.when(i >= 1)
        def _():
            h1o(i - 1).wait()
            merge(sb_o, rb_o, i - 1)
            h1g(i - 1).wait()
            merge(sb_g, rb_g, i - 1)

        for at, n in ((1, 0), (2, 1), (4, 2), (6, 3)):
            @pl.when(i == at)
            def _():
                h2g(n).start()

        @pl.when(i == 3)
        def _():
            grad_block(3, 0, act[...], cot)
            gy(3, 0).start()

        @pl.when(i == 5)
        def _():
            grad_block(3, 1, act[...], cot)
            gy(3, 1).start()

        @pl.when(i < CHUNKS)
        def _():
            fill(sb_o, i, jnp.dot(act[rows_of(i), :], wr[...], preferred_element_type=F32))
            h1o(i).start()

    for n in range(4):
        packet[8 + n : 9 + n, :] = column_sums(slope[:, n * width : (n + 1) * width])
    loads["normed"].wait()
    spread_grad(0)
    pass_on(3, 0)
    grad_block(3, 2, act[...], cot)
    gy(3, 2).start()
    grad_block(3, 3, act[...], cot)
    spread_grad(1)
    grad_block(2, 0, normed, slope[...])
    pass_on(3, 1)
    gy(2, 0).start()
    for s in range(1, 4):
        grad_block(2, s, normed, slope[...])
    for name in late:
        if name != "stat":
            loads[name].start()
    for name in ("unit", "inv", "vec", "wo", "mixf", "lse", "qt", "q", "k", "v", "kt"):
        loads[name].wait()

    def hid_load(i):
        return pltpu.make_async_copy(hid_h.at[rows_of(i), :], hid.at[i % 2], hid_sem.at[i])

    def out_store(i, s):
        return pltpu.make_async_copy(
            out.at[i % 2, s], out_o.at[pl.ds(pl.multiple_of(i * half, half), half), pl.ds(s * width, width)],
            store_sem.at[0, i, s],
        )

    def tg_store(i, s):
        return pltpu.make_async_copy(
            tg.at[i, s], tg_o.at[pl.ds(pl.multiple_of(i * half, half), half), pl.ds(s * width, width)],
            store_sem.at[1, i, s],
        )

    def attend_back(i):
        rows = rows_of(i)
        go = lax.dot_general(unit[rows, :], wo[...], NT_DIMS, preferred_element_type=F32).astype(BF16)
        inner = (go.astype(F32) * mixf[rows, :]).T
        go_t = go.T
        row_ids = lax.broadcasted_iota(jnp.int32, (128, chunk), 0)
        lane_ids = lax.broadcasted_iota(jnp.int32, (chunk, 128), 1)
        heads = width // HEAD_DIM
        queries, grads, query_rows, grad_rows, deltas, logs = [], [], [], [], [], []
        for h in range(heads):
            lanes = slice(h // 2 * 128, h // 2 * 128 + 128)
            pick = row_ids // HEAD_DIM == h % 2
            value = qt[i, lanes, :]
            queries.append(jnp.where(pick, value, jnp.zeros_like(value)))
            value = go_t[lanes, :]
            grads.append(jnp.where(pick, value, jnp.zeros_like(value)))
            pick = lane_ids // HEAD_DIM == h % 2
            value = q[rows, lanes]
            query_rows.append(jnp.where(pick, value, jnp.zeros_like(value)))
            value = go[:, lanes]
            grad_rows.append(jnp.where(pick, value, jnp.zeros_like(value)))
            deltas.append(jnp.sum(inner[h * HEAD_DIM : (h + 1) * HEAD_DIM, :], axis=0, keepdims=True))
            logs.append(lse[i, h : h + 1, :])

        parts = [jnp.zeros((HEAD_DIM, chunk), F32)] * heads
        for j in range(CHUNKS):
            keys = pl.ds(j * chunk, chunk)
            probs, grad_scores = [], []
            for h in range(heads):
                lanes = slice(h // 2 * 128, h // 2 * 128 + 128)
                block = jnp.dot(k[keys, lanes], queries[h], preferred_element_type=F32)
                grad_probs = jnp.dot(v[keys, lanes], grads[h], preferred_element_type=F32)
                prob = jnp.exp2(block * scale - logs[h])
                probs.append(prob.astype(BF16))
                grad_scores.append((prob * (grad_probs - deltas[h])).astype(BF16))
            for pair in range(heads // 2):
                lanes = slice(pair * 128, pair * 128 + 128)
                h = 2 * pair
                dv[keys, lanes] += jnp.dot(
                    probs[h], grad_rows[h], preferred_element_type=F32
                ) + jnp.dot(probs[h + 1], grad_rows[h + 1], preferred_element_type=F32)
                dk[keys, lanes] += jnp.dot(
                    grad_scores[h], query_rows[h], preferred_element_type=F32
                ) + jnp.dot(grad_scores[h + 1], query_rows[h + 1], preferred_element_type=F32)
            for h in range(heads):
                rows_h = slice(h * HEAD_DIM, (h + 1) * HEAD_DIM)
                parts[h] = parts[h] + jnp.dot(kt[j, rows_h, :], grad_scores[h], preferred_element_type=F32)
        flat[rows, 0:width] = (jnp.concatenate(parts, axis=0).T * HEAD_DIM ** (-0.5)).astype(BF16)

    def finish_out(i):
        @pl.when(i >= 2)
        def _():
            for s in range(2):
                out_store(i - 2, s).wait()

        hid_load(i).start()
        h2o(i).wait()
        hid_load(i).wait()
        total = rb_o[i, xx].astype(F32) + xr_o[i].astype(F32)
        value = (hid[i % 2] + total + vecs[5:6, own]).astype(BF16)
        for s in range(2):
            out[i % 2, s] = value[s * half : (s + 1) * half, :]
        for s in range(2):
            out_store(i, s).start()

    def second_norm_back(i):
        for x in range(2):
            h3g(i, x, core).wait_send()
            h3g(i, x, 1 - core).wait_recv()
        step_rows = chunk // 7
        for part in range(7):
            rows = pl.ds(pl.multiple_of(i * chunk + part * step_rows, step_rows), step_rows)
            span = slice(part * step_rows, (part + 1) * step_rows)
            incoming = grad[i % 4, span, :]
            units = unit[rows, :].astype(F32)
            scaled = incoming * vecs[3:4, :]
            plain = jnp.mean(scaled, axis=1, keepdims=True)
            cross = jnp.mean(scaled * units, axis=1, keepdims=True)
            total = cot[rows, :].astype(F32) + inv[rows, 0:1] * (scaled - plain - units * cross)
            mine = grad[i % 4, span, own]
            col_sums[1:2, 0:width] += jnp.sum(mine * unit[rows, own].astype(F32), axis=0, keepdims=True)
            col_sums[2:3, 0:width] += jnp.sum(mine, axis=0, keepdims=True)
            unit[rows, :] = total.astype(BF16)
            grad[i % 4, span, :] = total
        for s in range(2):
            tg[i, s] = grad[i % 4, s * half : (s + 1) * half, own]

    @pl.loop(-1, CHUNKS)
    def _(i):
        @pl.when(i + 1 < CHUNKS)
        def _():
            second_norm_back(i + 1)

        @pl.when((i >= 0) & (i + 2 < CHUNKS))
        def _():
            spread_grad(i + 2)

        @pl.when(i == CHUNKS - 2)
        def _():
            for s in range(4):
                grad_block(1, s, mixf[...].astype(BF16), unit)
                gy(1, s).start()

        @pl.when(i == CHUNKS - 1)
        def _():
            loads["stat"].start()

        @pl.when(i >= 0)
        def _():
            attend_back(i)

        @pl.when(i == -1)
        def _():
            pass_on(3, 2)
            gy(2, 1).start()

        @pl.when(i == 0)
        def _():
            pass_on(2, 0)
            gy(2, 2).start()

        @pl.when(i == 1)
        def _():
            pass_on(2, 1)
            gy(3, 3).start()

        @pl.when(i == 2)
        def _():
            pass_on(2, 2)
            gy(2, 3).start()

        @pl.when(i == CHUNKS - 2)
        def _():
            finish_grad(3, gred)

        @pl.when(i == CHUNKS - 1)
        def _():
            for s in range(3):
                pass_on(1, s)

        @pl.when(i >= 3)
        def _():
            @pl.loop(2 * (i - 3), jnp.minimum(2 * (i - 3) + 2, CHUNKS))
            def _(n):
                h2o(n).start()

        @pl.when(i >= 5)
        def _():
            @pl.loop(2 * (i - 5), 2 * (i - 5) + 2)
            def _(n):
                finish_out(n)

    for i in range(CHUNKS):
        rows = pl.ds(i * chunk, chunk)
        flat[rows, width : 2 * width] = (dk[rows, :] * HEAD_DIM ** (-0.5)).astype(BF16)
        flat[rows, 2 * width : 3 * width] = dv[rows, :].astype(BF16)
    for name in late:
        loads[name].wait()

    def inward_block(s):
        zt = (z + 1 + s) % 4
        left = one[:, aligned(zt, 256)]
        block = lax.dot_general(left, flat[...], TN_DIMS, preferred_element_type=F32).astype(BF16)
        for n in range(3):
            lanes = slice(n * width, (n + 1) * width)

            @pl.when(y == 0)
            def _():
                oh_in[s, n] = block[0:128, lanes]
                ys_in[s, n] = block[128:256, lanes]

            @pl.when(y == 1)
            def _():
                oh_in[s, n] = block[128:256, lanes]
                ys_in[s, n] = block[0:128, lanes]

        gy(0, s).start()

    def stat_copy(i, slot, target):
        return remote(st.at[i], st_in.at[i, slot], st_send.at[i, slot], st_recv.at[i, slot], r, target)

    lane_ids = lax.broadcasted_iota(jnp.int32, (chunk, 128), 1)
    gain = vecs[0:1, :]

    @pl.loop(0, CHUNKS + 3)
    def _(i):
        for s in range(4):
            @pl.when(i == s)
            def _():
                inward_block(s)

        @pl.when(i < CHUNKS)
        def _():
            rows = rows_of(i)
            partial = lax.dot_general(flat[rows, :], win[...], NT_DIMS, preferred_element_type=F32)
            fill(sb_g, i, partial)
            h1t(i).start()
            units = (tok[rows, :].astype(F32) - stat[rows, 0:1]) * stat[rows, 64:65]
            scaled = partial * gain
            plain = jnp.sum(scaled, axis=1, keepdims=True)
            cross = jnp.sum(scaled * units, axis=1, keepdims=True)
            both = jnp.where(lane_ids == 0, plain, jnp.where(lane_ids == 1, cross, 0.0))
            st[i] = both.T[0:8, :]
            for slot, target in enumerate((c_x, c_core, c_far)):
                stat_copy(i, slot, target).start()

        @pl.when((i >= 4) & (i <= 6))
        def _():
            finish_out(i)

        @pl.when((i >= 1) & (i <= CHUNKS))
        def _():
            h1t(i - 1).wait()
            merge(sb_g, rb_g, i - 1)
            h2t(i - 1).start()

        for s in range(3):
            @pl.when(i == s + 2)
            def _():
                pass_on(0, s)

        @pl.when(i == 5)
        def _():
            packet[7:8, :] = column_sums(cot[:, own])
            packet[4:5, :] = column_sums(unit[:, own])

        @pl.when(i == 6)
        def _():
            packet[2:3, :] = column_sums(flat[:, 0:width])
            packet[3:4, :] = column_sums(flat[:, 2 * width : 3 * width])
            finish_grad(2, gexp)

        @pl.when(i == 7)
        def _():
            finish_grad(1, gout)

        @pl.when(i >= 3)
        def _():
            t = i - 3
            rows = rows_of(t)
            h2t(t).wait()
            total = st[t]
            for slot, target in enumerate((c_x, c_core, c_far)):
                stat_copy(t, slot, target).wait()
                total = total + st_in[t, slot]
            columns = jnp.concatenate([total, jnp.zeros((120, chunk), F32)], axis=0).T
            plain = columns[:, 0:1] / full
            cross = columns[:, 1:2] / full
            incoming = rb_g[t, xx].astype(F32) + xr_1[t].astype(F32)
            inverse = stat[rows, 64:65]
            units = (tok[rows, own].astype(F32) - stat[rows, 0:1]) * inverse
            back = inverse * (incoming * vecs[0:1, own] - plain - units * cross)
            for s in range(2):
                tg[t, s] = tg[t, s] + back[s * half : (s + 1) * half, :]
            for s in range(2):
                tg_store(t, s).start()
            col_sums[6:7, 0:width] += jnp.sum(incoming * units, axis=0, keepdims=True)
            col_sums[7:8, 0:width] += jnp.sum(incoming, axis=0, keepdims=True)

    packet[0:1, :] = col_sums[6:7, 0:width]
    packet[1:2, :] = col_sums[7:8, 0:width]
    packet[5:7, :] = col_sums[1:3, 0:width]

    def packet_copy(step):
        return remote(packet, packets.at[step], pk_send.at[step], pk_recv.at[step], others[step], c)

    for step in range(7):
        packet_copy(step).start()
    finish_grad(0, gin)
    stores = [
        pltpu.make_async_copy(src, dst, store_sem.at[2, n, 0])
        for n, (src, dst) in enumerate(((gin, gin_o), (gout, gout_o), (gexp, gexp_o), (gred, gred_o)))
    ]
    for copy in stores:
        copy.start()
    total = packet[...]
    for step in range(7):
        packet_copy(step).wait()
        total = total + packets[step]
    packet[...] = total
    copy = pltpu.make_async_copy(packet, sums_o, store_sem.at[2, 4, 0])
    copy.start()
    copy.wait()
    for copy in stores:
        copy.wait()
    for i in range(CHUNKS - 2, CHUNKS):
        for s in range(2):
            out_store(i, s).wait()

    @pl.loop(0, CHUNKS)
    def _(i):
        for s in range(2):
            tg_store(i, s).wait()


def backward_call(*arrays):
    (tok, cot, q, qt, k, kt, v, mixf, lse, hid, unit, inv, normed, act, slope, win, wo, we, wr, vec, one, stat) = arrays
    rows, width = q.shape
    full, hidden = we.shape
    n, chunk = CHUNKS, rows // CHUNKS
    half = chunk // 2
    pairs = rows // 2

    def sd(shape, dtype):
        return jax.ShapeDtypeStruct(shape, dtype)

    outs = [
        sd((pairs, 2 * width), BF16), sd((pairs, 2 * width), F32), sd((16, width), F32),
        sd((3, 128, width), F32), sd((width, 128), F32), sd((128, hidden), F32), sd((hidden, 128), F32),
    ]
    vm = pltpu.VMEM
    dma = pltpu.SemaphoreType.DMA

    def shapes(lead):
        return [
            vm((lead, 3, 128, width), BF16), vm((lead, width, 128), BF16),
            vm((lead, 128, hidden), BF16), vm((lead, hidden, 128), BF16),
        ]

    def like(array):
        return vm(array.shape, array.dtype)

    scratch = [
        vm((rows, full), BF16), like(q), like(qt), like(k), like(kt), like(v), like(mixf), like(lse),
        vm((2, chunk, width), F32),
        like(unit), like(inv), like(normed), like(act), like(slope),
        vm((full, 3 * width), BF16), like(wo), like(we), like(wr), like(vec),
        vm((4, chunk, full), F32), vm((rows, 3 * width), BF16), vm((rows, width), F32), vm((rows, width), F32),
        vm((n, 2, half, width), F32), vm((2, 2, half, width), BF16),
        vm((2, 2, 2, chunk, width), BF16), vm((2, 2, 2, chunk, width), BF16),
        vm((n, 2, chunk, width), BF16), vm((n, 2, chunk, width), BF16),
        vm((n, 2, chunk, width), BF16), vm((n, chunk, width), BF16), vm((n, chunk, width), BF16),
        vm((n, 8, chunk), F32), vm((n, 3, 8, chunk), F32),
        vm((8, full), F32), vm((16, width), F32), vm((7, 16, width), F32),
        *shapes(4), *shapes(4), *shapes(4), *shapes(3),
        vm((3, 128, width), F32), vm((width, 128), F32), vm((128, hidden), F32), vm((hidden, 128), F32),
        dma((23,)), dma((3, n, 2)), dma((n,)), dma((4, 4)), dma((4, 4)), dma((4, 3)), dma((4, 3)),
        dma((n,)), dma((n,)), dma((n,)), dma((n,)), dma((n, 2)), dma((n, 2)),
        dma((n,)), dma((n,)), dma((n,)), dma((n,)), dma((n,)), dma((n,)), dma((n,)), dma((n,)),
        dma((n, 3)), dma((n, 3)), dma((7,)), dma((7,)),
    ]
    return pl.pallas_call(
        backward_kernel,
        out_shape=outs,
        in_specs=[pl.BlockSpec(memory_space=pl.ANY)] * len(arrays),
        out_specs=[pl.BlockSpec(memory_space=pl.ANY)] * len(outs),
        scratch_shapes=scratch,
        compiler_params=pltpu.CompilerParams(
            collective_id=1, has_side_effects=True, vmem_limit_bytes=63 << 20
        ),
    )(*arrays)


def finish_kernel(out_i, tg_i, sums_i, gin_i, gout_i, gexp_i, gred_i, *refs):
    outs, vector_o, buffers = refs[:6], refs[6:14], refs[14:20]
    load_sem, store_sem = refs[20:]
    ins = (out_i, tg_i, gin_i, gout_i, gexp_i, gred_i)
    loads = [pltpu.make_async_copy(a, b, load_sem.at[n]) for n, (a, b) in enumerate(zip(ins, buffers))]
    stores = [pltpu.make_async_copy(a, b, store_sem.at[n]) for n, (a, b) in enumerate(zip(buffers, outs))]
    order = (0, 2, 3, 4, 5, 1)
    for n in order:
        loads[n].start()
    first_gain, first_shift, attn, b_out, g_two, s_two, b_red, b_exp = vector_o
    first_gain[...] = sums_i[0:1, :]
    first_shift[...] = sums_i[1:2, :]
    attn[...] = sums_i[2:4, :]
    b_out[...] = sums_i[4:5, :]
    g_two[...] = sums_i[5:6, :]
    s_two[...] = sums_i[6:7, :]
    b_red[...] = sums_i[7:8, :]
    for n in range(4):
        width = sums_i.shape[1]
        b_exp[:, n * width : (n + 1) * width] = sums_i[8 + n : 9 + n, :]
    for n in order:
        loads[n].wait()
        stores[n].start()
    for n in order:
        stores[n].wait()


def finish_call(out, tg, sums, gin, gout, gexp, gred):
    width = sums.shape[1]
    big = [jax.ShapeDtypeStruct(a.shape, a.dtype) for a in (out, tg, gin, gout, gexp, gred)]
    small = [jax.ShapeDtypeStruct((n, m), F32) for n, m in ((1, width),) * 2 + ((2, width),) + ((1, width),) * 4 + ((1, 4 * width),)]
    hbm, vm = pl.BlockSpec(memory_space=pl.ANY), pl.BlockSpec(memory_space=pltpu.VMEM)
    return pl.pallas_call(
        finish_kernel,
        out_shape=big + small,
        in_specs=[hbm, hbm, vm, hbm, hbm, hbm, hbm],
        out_specs=[hbm] * 6 + [vm] * 8,
        scratch_shapes=[pltpu.VMEM(a.shape, a.dtype) for a in big] + [pltpu.SemaphoreType.DMA((6,))] * 2,
    )(out, tg, sums, gin, gout, gexp, gred)


CONTRACT_ROWS = (((0,), (0,)), ((), ()))
CONTRACT_COLS = (((1,), (1,)), ((), ()))


def norm_forward(values, gain, shift, full_width):
    row_total = lax.psum(jnp.sum(values, axis=1), "col")
    centred = values - (row_total / full_width)[:, None]
    row_square = lax.psum(jnp.sum(centred * centred, axis=1), "col")
    inverse = lax.rsqrt(row_square / full_width + EPSILON)
    unit_rows = centred * inverse[:, None]
    return (unit_rows, inverse, unit_rows * gain + shift)


def norm_backward(incoming, unit_rows, inverse, gain, full_width):
    scaled = incoming * gain
    plain_sum, cross_sum = lax.psum(
        (jnp.sum(scaled, axis=1), jnp.sum(scaled * unit_rows, axis=1)), "col"
    )
    result = inverse[:, None] * (
        scaled - (plain_sum / full_width)[:, None] - unit_rows * (cross_sum / full_width)[:, None]
    )
    return (result, jnp.sum(incoming * unit_rows, axis=0), jnp.sum(incoming, axis=0))


def spread_features(values):
    return lax.all_gather(values, "col", axis=1, tiled=True)


def sum_partials(values):
    return lax.psum_scatter(values, "col", scatter_dimension=1, tiled=True)


def spread_grads(values):
    return lax.all_gather(values, "col", axis=1, tiled=True)


def sum_grad_partials(values):
    return lax.psum_scatter(values, "col", scatter_dimension=1, tiled=True)


def fetch_weights(inward_weight, output_weight, expand_weight, reduce_weight):
    return (
        lax.all_gather(inward_weight, "row", axis=0, tiled=True),
        lax.all_gather(output_weight, "row", axis=1, tiled=True),
        lax.all_gather(expand_weight, "row", axis=0, tiled=True),
        lax.all_gather(reduce_weight, "row", axis=1, tiled=True),
    )


def attend_clip(queries, key_rows, value_rows, score_scale):
    seq_len = queries.shape[0]
    blocks = queries.reshape((2, seq_len // 2) + queries.shape[1:])

    def one_block(query_part):
        scores = (
            jnp.einsum("qhd,khd->hqk", query_part, key_rows, preferred_element_type=jnp.float32)
            * score_scale
        )
        row_peak = jnp.max(scores, axis=-1, keepdims=True)
        exponent = jnp.exp(scores - row_peak)
        row_sum = jnp.sum(exponent, axis=-1, keepdims=True)
        prob_low = (exponent / row_sum).astype(jnp.bfloat16)
        mixed_rows = jnp.einsum(
            "hqk,khd->qhd", prob_low, value_rows, preferred_element_type=jnp.float32
        )
        return (mixed_rows, (row_peak + jnp.log(row_sum))[..., 0])

    mixed_rows, logsum = lax.map(one_block, blocks)
    return (mixed_rows.reshape(queries.shape), logsum)


def attend_clip_back(queries, key_rows, value_rows, logsum, grad_out, score_scale):
    seq_len = queries.shape[0]
    block_shape = (2, seq_len // 2) + queries.shape[1:]

    def step_block(carry, pieces):
        key_acc, value_acc = carry
        query_part, grad_part, log_part = pieces
        scores = (
            jnp.einsum("qhd,khd->hqk", query_part, key_rows, preferred_element_type=jnp.float32)
            * score_scale
        )
        probs = jnp.exp(scores - log_part[..., None])
        grad_probs = jnp.einsum(
            "qhd,khd->hqk", grad_part, value_rows, preferred_element_type=jnp.float32
        )
        inner_sum = jnp.sum(probs * grad_probs, axis=-1, keepdims=True)
        grad_scores = (probs * (grad_probs - inner_sum)).astype(jnp.bfloat16)
        query_grad = (
            jnp.einsum("hqk,khd->qhd", grad_scores, key_rows, preferred_element_type=jnp.float32)
            * score_scale
        )
        key_acc = key_acc + jnp.einsum(
            "hqk,qhd->khd", grad_scores, query_part, preferred_element_type=jnp.float32
        )
        value_acc = value_acc + jnp.einsum(
            "hqk,qhd->khd",
            probs.astype(jnp.bfloat16),
            grad_part,
            preferred_element_type=jnp.float32,
        )
        return ((key_acc, value_acc), query_grad)

    zero_acc = jnp.zeros(key_rows.shape, jnp.float32)
    (key_acc, value_acc), query_grads = lax.scan(
        step_block,
        (zero_acc, zero_acc),
        (queries.reshape(block_shape), grad_out.reshape(block_shape), logsum),
    )
    return (query_grads.reshape(queries.shape), key_acc * score_scale, value_acc)


def forward_pass(
    tokens,
    first_gain,
    first_shift,
    attention_bias,
    output_bias,
    second_gain,
    second_shift,
    expand_bias,
    reduce_bias,
    gathered,
):
    inward_all, output_rows, expand_all, reduce_rows = gathered
    full_width = inward_all.shape[0]
    local_width = inward_all.shape[2]
    row_count = tokens.shape[0]
    clip_shape = (row_count // SEQ, SEQ, local_width // HEAD_DIM, HEAD_DIM)
    score_scale = HEAD_DIM ** (-0.5)
    source = tokens.astype(jnp.float32)
    unit_one, inverse_one, normed_one = norm_forward(source, first_gain, first_shift, full_width)
    normed_all = spread_features(normed_one.astype(jnp.bfloat16))
    projected = jnp.dot(
        normed_all,
        inward_all.reshape(full_width, 3 * local_width),
        preferred_element_type=jnp.float32,
    )
    projected = projected.reshape(row_count, 3, local_width)
    queries = (projected[:, 0] + attention_bias[0]).astype(jnp.bfloat16)
    key_rows = projected[:, 1].astype(jnp.bfloat16)
    value_rows = (projected[:, 2] + attention_bias[1]).astype(jnp.bfloat16)
    mixed_rows, logsum = lax.map(
        lambda clip_parts: attend_clip(clip_parts[0], clip_parts[1], clip_parts[2], score_scale),
        (queries.reshape(clip_shape), key_rows.reshape(clip_shape), value_rows.reshape(clip_shape)),
    )
    mixed_low = mixed_rows.reshape(row_count, local_width).astype(jnp.bfloat16)
    hidden_state = (
        source
        + sum_partials(jnp.dot(mixed_low, output_rows, preferred_element_type=jnp.float32))
        + output_bias
    )
    unit_two, inverse_two, normed_two = norm_forward(
        hidden_state, second_gain, second_shift, full_width
    )
    normed_all_two = spread_features(normed_two.astype(jnp.bfloat16))
    expanded = jnp.dot(normed_all_two, expand_all, preferred_element_type=jnp.float32) + expand_bias
    activated = jax.nn.gelu(expanded, approximate=False).astype(jnp.bfloat16)
    output_value = (
        hidden_state
        + sum_partials(jnp.dot(activated, reduce_rows, preferred_element_type=jnp.float32))
        + reduce_bias
    )
    saved_state = (
        unit_one,
        inverse_one,
        normed_all,
        queries,
        key_rows,
        value_rows,
        logsum,
        mixed_low,
        unit_two,
        inverse_two,
        normed_all_two,
        expanded,
        activated,
    )
    return (output_value, saved_state)


def plain_device(
    tokens,
    first_gain,
    first_shift,
    inward_weight,
    attention_bias,
    output_weight,
    output_bias,
    second_gain,
    second_shift,
    expand_weight,
    expand_bias,
    reduce_weight,
    reduce_bias,
    cotangent,
):
    packed_width = tokens.shape[1]
    tokens = tokens.reshape(-1, packed_width // 2)
    cotangent = cotangent.reshape(-1, packed_width // 2)
    gathered = fetch_weights(inward_weight, output_weight, expand_weight, reduce_weight)
    output_value, saved_state = forward_pass(
        tokens,
        first_gain,
        first_shift,
        attention_bias,
        output_bias,
        second_gain,
        second_shift,
        expand_bias,
        reduce_bias,
        gathered,
    )
    gathered = fetch_weights(inward_weight, output_weight, expand_weight, reduce_weight)
    unused_value, saved_state = forward_pass(
        tokens,
        first_gain,
        first_shift,
        attention_bias,
        output_bias,
        second_gain,
        second_shift,
        expand_bias,
        reduce_bias,
        gathered,
    )
    inward_all, output_rows, expand_all, reduce_rows = gathered
    (
        unit_one,
        inverse_one,
        normed_all,
        queries,
        key_rows,
        value_rows,
        logsum,
        mixed_low,
        unit_two,
        inverse_two,
        normed_all_two,
        expanded,
        activated,
    ) = saved_state
    full_width = inward_all.shape[0]
    local_width = inward_all.shape[2]
    row_count = tokens.shape[0]
    clip_shape = (row_count // SEQ, SEQ, local_width // HEAD_DIM, HEAD_DIM)
    score_scale = HEAD_DIM ** (-0.5)
    grad_rows = cotangent.astype(jnp.float32)
    grad_all = spread_grads(cotangent)
    grad_act = lax.dot_general(
        grad_all, reduce_rows, CONTRACT_COLS, preferred_element_type=jnp.float32
    )
    reduce_grad = lax.dot_general(
        activated, grad_all, CONTRACT_ROWS, preferred_element_type=jnp.float32
    )
    reduce_bias_grad = jnp.sum(grad_rows, axis=0)
    gelu_value, gelu_back = jax.vjp(
        lambda inner_value: jax.nn.gelu(inner_value, approximate=False), expanded
    )
    grad_expanded = gelu_back(grad_act)[0].astype(jnp.bfloat16)
    expand_grad = lax.dot_general(
        normed_all_two, grad_expanded, CONTRACT_ROWS, preferred_element_type=jnp.float32
    )
    expand_bias_grad = jnp.sum(grad_expanded.astype(jnp.float32), axis=0)
    grad_normed_two = sum_grad_partials(
        lax.dot_general(
            grad_expanded, expand_all, CONTRACT_COLS, preferred_element_type=jnp.float32
        )
    )
    back_two, second_gain_grad, second_shift_grad = norm_backward(
        grad_normed_two, unit_two, inverse_two, second_gain, full_width
    )
    grad_hidden = grad_rows + back_two
    grad_hidden_low = grad_hidden.astype(jnp.bfloat16)
    grad_hidden_all = spread_grads(grad_hidden_low)
    output_grad = lax.dot_general(
        mixed_low, grad_hidden_all, CONTRACT_ROWS, preferred_element_type=jnp.float32
    )
    output_bias_grad = jnp.sum(grad_hidden_low.astype(jnp.float32), axis=0)
    grad_mixed = lax.dot_general(
        grad_hidden_all, output_rows, CONTRACT_COLS, preferred_element_type=jnp.float32
    ).astype(jnp.bfloat16)
    query_grads, key_grads, value_grads = lax.map(
        lambda clip_parts: attend_clip_back(
            clip_parts[0], clip_parts[1], clip_parts[2], clip_parts[3], clip_parts[4], score_scale
        ),
        (
            queries.reshape(clip_shape),
            key_rows.reshape(clip_shape),
            value_rows.reshape(clip_shape),
            logsum,
            grad_mixed.reshape(clip_shape),
        ),
    )
    stacked = jnp.stack(
        [
            query_grads.reshape(row_count, local_width),
            key_grads.reshape(row_count, local_width),
            value_grads.reshape(row_count, local_width),
        ],
        axis=1,
    ).astype(jnp.bfloat16)
    attention_bias_grad = jnp.stack(
        [
            jnp.sum(stacked[:, 0].astype(jnp.float32), axis=0),
            jnp.sum(stacked[:, 2].astype(jnp.float32), axis=0),
        ]
    )
    flat_grads = stacked.reshape(row_count, 3 * local_width)
    inward_grad = lax.dot_general(
        normed_all, flat_grads, CONTRACT_ROWS, preferred_element_type=jnp.float32
    ).reshape(full_width, 3, local_width)
    grad_normed_one = sum_grad_partials(
        lax.dot_general(
            flat_grads,
            inward_all.reshape(full_width, 3 * local_width),
            CONTRACT_COLS,
            preferred_element_type=jnp.float32,
        )
    )
    back_one, first_gain_grad, first_shift_grad = norm_backward(
        grad_normed_one, unit_one, inverse_one, first_gain, full_width
    )
    tokens_grad = grad_hidden + back_one
    inward_grad, output_grad, expand_grad, reduce_grad = (
        lax.psum_scatter(
            inward_grad.astype(jnp.bfloat16), "row", scatter_dimension=0, tiled=True
        ).astype(jnp.float32),
        lax.psum_scatter(
            output_grad.astype(jnp.bfloat16), "row", scatter_dimension=1, tiled=True
        ).astype(jnp.float32),
        lax.psum_scatter(
            expand_grad.astype(jnp.bfloat16), "row", scatter_dimension=0, tiled=True
        ).astype(jnp.float32),
        lax.psum_scatter(
            reduce_grad.astype(jnp.bfloat16), "row", scatter_dimension=1, tiled=True
        ).astype(jnp.float32),
    )
    (
        first_gain_grad,
        first_shift_grad,
        attention_bias_grad,
        output_bias_grad,
        second_gain_grad,
        second_shift_grad,
        expand_bias_grad,
        reduce_bias_grad,
    ) = lax.psum(
        (
            first_gain_grad,
            first_shift_grad,
            attention_bias_grad,
            output_bias_grad,
            second_gain_grad,
            second_shift_grad,
            expand_bias_grad,
            reduce_bias_grad,
        ),
        "row",
    )
    return (
        output_value.astype(jnp.bfloat16).reshape(-1, packed_width),
        tokens_grad.reshape(-1, packed_width),
        first_gain_grad,
        first_shift_grad,
        inward_grad,
        attention_bias_grad,
        output_grad,
        output_bias_grad,
        second_gain_grad,
        second_shift_grad,
        expand_grad,
        expand_bias_grad,
        reduce_grad,
        reduce_bias_grad,
    )


def fused_device(
    tokens,
    first_gain,
    first_shift,
    inward_weight,
    attention_bias,
    output_weight,
    output_bias,
    second_gain,
    second_shift,
    expand_weight,
    expand_bias,
    reduce_weight,
    reduce_bias,
    cotangent,
):
    kept = forward_call(
        tokens,
        cotangent,
        first_gain[None],
        first_shift[None],
        output_bias[None],
        second_gain[None],
        second_shift[None],
        reduce_bias[None],
        attention_bias,
        expand_bias[None],
        inward_weight.transpose(1, 0, 2),
        output_weight,
        expand_weight,
        reduce_weight,
    )
    (tok, cot, q, qt, k, kt, v, mixf, lse, hid, unit, inv, normed, act, slope, win, wo, we, wr, vec, one, stat) = kept

    def flat(array):
        return array.reshape(-1, array.shape[-1])

    outs = backward_call(
        flat(tok), flat(cot), flat(q), qt, flat(k), kt, flat(v), flat(mixf), lse, flat(hid), flat(unit),
        flat(inv), flat(normed), flat(act), flat(slope), win, wo, we, wr, vec, flat(one), flat(stat),
    )
    outs = finish_call(*outs)
    layer_output, tokens_grad, inward_grad, output_grad, expand_grad, reduce_grad = outs[:6]
    first_gain_grad, first_shift_grad, attention_grad, out_grad, gain_grad, shift_grad, red_grad, exp_grad = outs[6:]
    return (
        layer_output,
        tokens_grad,
        first_gain_grad[0],
        first_shift_grad[0],
        inward_grad.transpose(1, 0, 2),
        attention_grad,
        output_grad,
        out_grad[0],
        gain_grad[0],
        shift_grad[0],
        expand_grad,
        exp_grad[0],
        reduce_grad,
        red_grad[0],
    )


def per_device(rows, cols, *arrays):
    tokens, inward_weight, expand_weight = arrays[0], arrays[3], arrays[9]
    fits = (
        (rows, cols) == (8, 4)
        and tokens.shape == (SEQ // 2, 512)
        and inward_weight.shape == (128, 3, 256)
        and expand_weight.shape == (128, 1024)
    )
    return fused_device(*arrays) if fits else plain_device(*arrays)


def solution(mesh):
    in_specs = (
        P("row", "col"),
        P("col"),
        P("col"),
        P("row", None, "col"),
        P(None, "col"),
        P("col", "row"),
        P("col"),
        P("col"),
        P("col"),
        P("row", "col"),
        P("col"),
        P("col", "row"),
        P("col"),
        P("row", "col"),
    )
    out_specs = (
        P("row", "col"),
        P("row", "col"),
        P("col"),
        P("col"),
        P("row", None, "col"),
        P(None, "col"),
        P("col", "row"),
        P("col"),
        P("col"),
        P("col"),
        P("row", "col"),
        P("col"),
        P("col", "row"),
        P("col"),
    )
    return jax.shard_map(
        functools.partial(per_device, mesh.shape["row"], mesh.shape["col"]),
        mesh=mesh, in_specs=in_specs, out_specs=out_specs, check_vma=False
    )
```

```python
import functools
import jax
import jax.numpy as jnp
from jax import lax
from jax.experimental import pallas as pl
from jax.experimental.pallas import tpu as pltpu
from jax.sharding import PartitionSpec as P

HEAD_DIM = 64
SEQ = 1568
EPSILON = 1e-06
CHUNKS = 7
WINDOW = 2
F32 = jnp.float32
BF16 = jnp.bfloat16
MESH = pl.DeviceIdType.MESH
LOG2E = 1.4426950408889634
NT_DIMS = (((1,), (1,)), ((), ()))
TN_DIMS = (((0,), (0,)), ((), ()))


def remote(src, dst, send, recv, row, col):
    return pltpu.make_async_remote_copy(
        src_ref=src, dst_ref=dst, send_sem=send, recv_sem=recv,
        device_id=(row, col), device_id_type=MESH,
    )


def aligned(index, size):
    return pl.ds(pl.multiple_of(index * size, size), size)


def row_norm(values):
    mean = jnp.mean(values, axis=1, keepdims=True)
    centred = values - mean
    inverse = lax.rsqrt(jnp.mean(centred * centred, axis=1, keepdims=True) + EPSILON)
    return centred * inverse, mean, inverse


def weight_blocks(ref, kind, row):
    if kind == "three":
        return ref.at[:, aligned(row, 128), :]
    if kind == "rows":
        return ref.at[aligned(row, 128), :]
    return ref.at[:, aligned(row, 128)]


WEIGHT_KINDS = ("three", "cols", "rows", "cols")


def forward_kernel(
    tok, cot, g_one, s_one, b_out, g_two, s_two, b_red, attn_bias, exp_bias, win_s, wo_s, we_s, wr_s,
    tok_o, cot_o, q_o, qt_o, k_o, kt_o, v_o, mixf_o, lse_o, hid_o, unit_o, inv_o,
    norm_o, act_o, slope_o, win_o, wo_o, we_o, wr_o, vec_o, one_o, stat_o,
    tok_all, cot_all, norm_one, q, qt, k, kt, v, vt, mixed, mixf, lse, hid, unit, inv, norm_two, act, slope,
    win, wo, we, wr, vecs, stat, scores,
    local_sem, shard_sem, tok_sem, cot_sem, wz_send, wz_recv, wy_send, wy_recv, vec_send, vec_recv,
    tx_send, tx_recv, tc_send, tc_recv, tp_send, tp_recv, cx_send, cx_recv, cc_send, cc_recv, cp_send, cp_recv,
    wx_send, wx_recv, wc_send, wc_recv, mx_send, mx_recv, mc_send, mc_recv,
):
    r, c = lax.axis_index("row"), lax.axis_index("col")
    z, y = r // 2, r % 2
    xx, core = c // 2, c % 2
    c_x, c_core, c_far = (c + 2) % 4, c + 1 - 2 * core, (c + 2) % 4 + 1 - 2 * core
    r_y = r + 1 - 2 * y
    half = tok.shape[0] // CHUNKS
    chunk = 2 * half
    width = g_one.shape[1]
    scale = LOG2E * HEAD_DIM ** (-0.5)

    barrier = pltpu.get_barrier_semaphore()
    for col in (c_x, c_core, c_far):
        pl.semaphore_signal(barrier, inc=1, device_id=(r, col), device_id_type=MESH)
    pl.semaphore_signal(barrier, inc=1, device_id=(r_y, c), device_id_type=MESH)

    @pl.when(z >= 1)
    def _():
        pl.semaphore_signal(barrier, inc=1, device_id=(r - 2, c), device_id_type=MESH)

    @pl.when(z <= 2)
    def _():
        pl.semaphore_signal(barrier, inc=1, device_id=(r + 2, c), device_id_type=MESH)


    own = aligned(c, width)
    shards = (win_s, wo_s, we_s, wr_s)
    fulls = (win, wo, we, wr)
    shard_loads = [
        pltpu.make_async_copy(
            shards[w],
            wo.at[aligned(core * 2 + xx, width), aligned(r, 128)] if w == 1
            else weight_blocks(fulls[w], WEIGHT_KINDS[w], r),
            shard_sem.at[w],
        )
        for w in range(4)
    ]
    for copy in shard_loads:
        copy.start()

    def half_source(ref, i, s):
        return ref.at[pl.ds(pl.multiple_of(i * half, half), half), pl.ds(s * width, width)]

    def half_load(ref, full_ref, sem, i, s):
        return pltpu.make_async_copy(
            half_source(ref, i, s), full_ref.at[i, pl.ds(s * half, half), own], sem.at[i, s]
        )

    for i in range(CHUNKS):
        for s in range(2):
            half_load(tok, tok_all, tok_sem, i, s).start()
            half_load(cot, cot_all, cot_sem, i, s).start()
    for n, vector in enumerate((g_one, s_one, b_out, g_two, s_two, b_red, b_red, b_red)):
        vecs[n : n + 1, own] = vector[...]
    pl.semaphore_wait(barrier, 4 + jnp.where(z >= 1, 1, 0) + jnp.where(z <= 2, 1, 0))

    slab = core * 2 + xx

    def out_x(order):
        block = wo.at[aligned(order, width), :]
        return remote(block, block, wx_send.at[0], wx_recv.at[0], r, c_x)

    def out_core(side):
        block = wo.at[aligned(side, 2 * width), :]
        return remote(block, block, wc_send.at[0], wc_recv.at[0], r, c_core)

    def weight_ref(w, zb, side):
        if w == 1:
            return wo.at[aligned(slab, width), aligned(zb * 2 + side, 128)]
        return weight_blocks(fulls[w], WEIGHT_KINDS[w], zb * 2 + side)

    def line_copy(w, up, hop):
        zb = z - hop if up else z + hop
        block = weight_ref(w, zb, y)
        target = (z + 1 if up else z - 1) * 2 + y
        source = shards[w] if hop == 0 else block
        return remote(source, block, wz_send.at[w, up, hop], wz_recv.at[w, up, hop], target, c)

    def line_sends(up, hop):
        return (z >= hop) & (z <= 2) if up else (z <= 3 - hop) & (z >= 1)

    def line_receives(up, hop):
        return z >= hop + 1 if up else z <= 2 - hop

    def y_copy(w, zb, side):
        block = weight_ref(w, zb, side)
        return remote(block, block, wy_send.at[w, zb], wy_recv.at[w, zb], r_y, c)

    def start_weight(w):
        for up in (0, 1):
            @pl.when(line_sends(up, 0))
            def _():
                line_copy(w, up, 0).start()

    def own_to_y(w):
        return remote(shards[w], weight_ref(w, z, y), wy_send.at[w, z], wy_recv.at[w, z], r_y, c)

    def forward_weight(w, hop):
        for up in (0, 1):
            @pl.when(line_receives(up, hop))
            def _():
                zb = z - 1 - hop if up else z + 1 + hop
                block = weight_ref(w, zb, y)
                remote(block, block, wz_send.at[w, up, hop], wz_recv.at[w, up, hop], r_y, c).wait_recv()
                y_copy(w, zb, y).start()

            if hop < 2:
                @pl.when(line_receives(up, hop) & line_sends(up, hop + 1))
                def _():
                    line_copy(w, up, hop + 1).start()

    def finish_weight(w):
        for up in (0, 1):
            for hop in range(3):
                @pl.when(line_sends(up, hop))
                def _():
                    line_copy(w, up, hop).wait_send()
        for zb in range(4):
            y_copy(w, zb, y).wait_send()
            y_copy(w, zb, 1 - y).wait_recv()

    def vec_copy(slot, target, col):
        block = vecs.at[:, aligned(col, width)]
        return remote(block, block, vec_send.at[slot], vec_recv.at[slot], r, target)

    def half_x(ref, full_ref, send, recv, i, s, col):
        block = full_ref.at[i, pl.ds(s * half, half), aligned(col, width)]
        return remote(half_source(ref, i, s), block, send.at[i, s], recv.at[i, s], r, c_x)

    def half_core(ref, full_ref, send, recv, i, s, col):
        block = full_ref.at[i, pl.ds(s * half, half), aligned(col, width)]
        return remote(half_source(ref, i, s), block, send.at[i, s], recv.at[i, s], r, c_core)

    def tok_x(i, s, col):
        return half_x(tok, tok_all, tx_send, tx_recv, i, s, col)

    def tok_core(i, s, col):
        return half_core(tok, tok_all, tc_send, tc_recv, i, s, col)

    def cot_x(i, s, col):
        return half_x(cot, cot_all, cx_send, cx_recv, i, s, col)

    def cot_core(i, s, col):
        return half_core(cot, cot_all, cc_send, cc_recv, i, s, col)

    def pass_core(full_ref, send, recv, i, col):
        block = full_ref.at[i, :, aligned(col, width)]
        return remote(block, block, send.at[i], recv.at[i], r, c_core)

    def tok_pass(i, col):
        return pass_core(tok_all, tp_send, tp_recv, i, col)

    def cot_pass(i, col):
        return pass_core(cot_all, cp_send, cp_recv, i, col)

    def send_cot(i):
        for s in range(2):
            cot_x(i, s, c).start()
            cot_core(i, s, c).start()

    def send_tok(i):
        for s in range(2):
            tok_x(i, s, c).start()
            tok_core(i, s, c).start()

    start_weight(0)
    own_to_y(0).start()
    for i in range(WINDOW):
        send_tok(i)
    for slot, target in enumerate((c_x, c_core, c_far)):
        vec_copy(slot, target, c).start()

    def keep(index, i, src, dst):
        return pltpu.make_async_copy(src, dst, local_sem.at[index, i])

    def kept(i, stage):
        if stage == 0:
            pairs = ((tok_all, tok_o), (q, q_o), (qt, qt_o), (k, k_o), (kt, kt_o), (v, v_o), (norm_one, one_o), (stat, stat_o))
            base = 0
        elif stage == 1:
            pairs = ((mixf, mixf_o), (lse, lse_o))
            base = 8
        elif stage == 2:
            pairs = ((unit, unit_o), (inv, inv_o), (norm_two, norm_o))
            base = 10
        elif stage == 4:
            pairs = ((act, act_o), (slope, slope_o))
            base = 13
        else:
            pairs = ((cot_all, cot_o),)
            base = 15
        return [keep(base + n, i, a.at[i], b.at[i]) for n, (a, b) in enumerate(pairs)]

    last = [
        keep(17, n, a, b)
        for n, (a, b) in enumerate(
            ((win, win_o), (wo.at[aligned(slab, width), :], wo_o), (we, we_o), (wr, wr_o), (vecs, vec_o))
        )
    ]

    def keep_hid(i):
        return keep(16, i, hid.at[i % 2, :, own], hid_o.at[i])

    lane_ids = lax.broadcasted_iota(jnp.int32, (chunk // 7, 128), 1)

    def first_norm(i):
        for s in range(2):
            half_load(tok, tok_all, tok_sem, i, s).wait()
            tok_core(i, s, c_core).wait_recv()
        tok_pass(i, c_far).wait_recv()
        for part in range(7):
            rows = pl.ds(part * (chunk // 7), chunk // 7)
            units, mean, inverse = row_norm(tok_all[i, rows, :].astype(F32))
            stat[i, rows, :] = jnp.where(lane_ids < 64, mean, inverse)
            norm_one[i, rows, :] = (units * vecs[0:1, :] + vecs[1:2, :]).astype(BF16)

    @pl.loop(0, CHUNKS // 2 + 1)
    def _(g):
        @pl.loop(2 * g, jnp.minimum(2 * g + 2, CHUNKS))
        def _(i):
            for s in range(2):
                tok_x(i, s, c_x).wait_recv()

            @pl.when(i + WINDOW < CHUNKS)
            def _():
                send_tok(i + WINDOW)

            tok_pass(i, c_x).start()

        @pl.when(g == 0)
        def _():
            for slot, target in enumerate((c_x, c_core, c_far)):
                vec_copy(slot, target, c).wait_send()
                vec_copy(slot, target, target).wait_recv()

        for hop in range(3):
            @pl.when(g == hop)
            def _():
                forward_weight(0, hop)

        @pl.when(g == 0)
        def _():
            start_weight(1)
            own_to_y(1).start()

        @pl.when(g == 1)
        def _():
            forward_weight(1, 0)

        @pl.when(g == 3)
        def _():
            start_weight(2)
            forward_weight(1, 1)
            send_cot(0)
            send_cot(1)

        @pl.loop(2 * g, jnp.minimum(2 * g + 2, CHUNKS))
        def _(i):
            first_norm(i)

    for w in range(4):
        shard_loads[w].wait()
    own_to_y(3).start()
    forward_weight(1, 2)
    finish_weight(0)
    last[0].start()
    last[4].start()

    @pl.loop(0, CHUNKS)
    def _(i):
        part = jnp.dot(norm_one[i], win[0], preferred_element_type=F32)
        part = (part + attn_bias[0:1, :]).astype(BF16)
        q[i] = part
        qt[i] = part.T
        part = jnp.dot(norm_one[i], win[1], preferred_element_type=F32).astype(BF16)
        k[i] = part
        kt[i] = part.T
        part = jnp.dot(norm_one[i], win[2], preferred_element_type=F32)
        part = (part + attn_bias[1:2, :]).astype(BF16)
        v[i] = part
        vt[i] = part.T
        for copy in kept(i, 0):
            copy.start()

        @pl.when(i == 0)
        def _():
            own_to_y(2).start()
            finish_weight(1)
            out_x(slab).start()

        @pl.when(i == 4)
        def _():
            forward_weight(2, 0)

        @pl.when(i == 6)
        def _():
            forward_weight(2, 1)

    def attend(i):
        row_ids = lax.broadcasted_iota(jnp.int32, (128, chunk), 0)
        heads = width // HEAD_DIM

        def score(h):
            lanes = slice(h // 2 * 128, h // 2 * 128 + 128)
            query = qt[i, lanes, :]
            query = jnp.where(row_ids // HEAD_DIM == h % 2, query, jnp.zeros_like(query))
            peak = jnp.full((1, chunk), -jnp.inf, F32)
            for j in range(CHUNKS):
                block = jnp.dot(k[j, :, lanes], query, preferred_element_type=F32)
                scores[h % 2, j] = block
                peak = jnp.maximum(peak, jnp.max(block, axis=0, keepdims=True))
            return peak * scale

        def mix(h, peak):
            total = jnp.zeros((1, chunk), F32)
            acc = jnp.zeros((HEAD_DIM, chunk), F32)
            for j in range(CHUNKS):
                weights = jnp.exp2(scores[h % 2, j] * scale - peak)
                total = total + jnp.sum(weights, axis=0, keepdims=True)
                rows = slice(h * HEAD_DIM, (h + 1) * HEAD_DIM)
                acc = acc + jnp.dot(vt[j, rows, :], weights.astype(BF16), preferred_element_type=F32)
            lse[i, h : h + 1, :] = peak + jnp.log2(total)
            return acc / total

        outs = []
        peak = score(0)
        for h in range(heads):
            following = score(h + 1) if h + 1 < heads else None
            outs.append(mix(h, peak))
            peak = following
        out = jnp.concatenate(outs, axis=0).T
        mixf[i] = out
        mixed[i, :, aligned(slab, width)] = out.astype(BF16)

    def mixed_block(i, order):
        return mixed.at[i, :, aligned(order, width)]

    def mixed_x(i, order):
        block = mixed_block(i, order)
        return remote(block, block, mx_send.at[i], mx_recv.at[i], r, c_x)

    def mixed_core(i, slot, order):
        block = mixed_block(i, order)
        return remote(block, block, mc_send.at[i, slot], mc_recv.at[i, slot], r, c_core)

    def second_norm(t):
        mixed_core(t, 0, (1 - core) * 2 + xx).wait_recv()
        mixed_core(t, 1, (1 - core) * 2 + 1 - xx).wait_recv()

        @pl.when(t >= 2)
        def _():
            keep_hid(t - 2).wait()

        hid[t % 2] = tok_all[t].astype(F32) + (
            jnp.dot(mixed[t], wo[...], preferred_element_type=F32) + vecs[2:3, :]
        )
        for part in range(7):
            rows = pl.ds(part * (chunk // 7), chunk // 7)
            units, _, inverse = row_norm(hid[t % 2, rows, :])
            unit[t, rows, :] = units.astype(BF16)
            inv[t, rows, :] = jnp.broadcast_to(inverse, (chunk // 7, 128))
            norm_two[t, rows, :] = (units * vecs[3:4, :] + vecs[4:5, :]).astype(BF16)
        for copy in kept(t, 2):
            copy.start()
        keep_hid(t).start()

    def expand(t):
        for n in range(we.shape[1] // 256):
            lanes = slice(n * 256, (n + 1) * 256)
            expanded = jnp.dot(norm_two[t], we[:, lanes], preferred_element_type=F32) + exp_bias[:, lanes]
            gate = 0.5 + 0.5 * lax.erf(expanded * (0.5 ** 0.5))
            act[t, :, lanes] = (expanded * gate).astype(BF16)
            bell = jnp.exp2(expanded * expanded * (-0.5 * LOG2E)) * 0.3989422804014327
            slope[t, :, lanes] = (gate + expanded * bell).astype(BF16)
        for copy in kept(t, 4):
            copy.start()

    def pass_mixed(t):
        mixed_x(t, core * 2 + 1 - xx).wait_recv()
        mixed_core(t, 1, core * 2 + 1 - xx).start()

    def pass_on_cot(t):
        for s in range(2):
            cot_x(t, s, c_x).wait_recv()
            half_load(cot, cot_all, cot_sem, t, s).wait()
        cot_pass(t, c_x).start()

    @pl.loop(0, CHUNKS)
    def _(i):
        attend(i)
        mixed_x(i, slab).start()
        mixed_core(i, 0, slab).start()
        for copy in kept(i, 1):
            copy.start()

        @pl.when(i == 0)
        def _():
            start_weight(3)

        @pl.when(i == 2)
        def _():
            forward_weight(2, 2)

        @pl.when(i == 3)
        def _():
            out_x(slab).wait_send()
            out_x(core * 2 + 1 - xx).wait_recv()
            out_core(core).start()

        @pl.when(i == 4)
        def _():
            forward_weight(3, 0)
            send_cot(2)
            pass_mixed(0)
            pass_mixed(1)
            out_core(core).wait_send()
            out_core(1 - core).wait_recv()

        @pl.when(i == 6)
        def _():
            forward_weight(3, 1)
            send_cot(3)

        @pl.when(i >= 5)
        def _():
            @pl.loop(2 * (i - 5), i - 3)
            def _(t):
                second_norm(t)

        @pl.when(i == 5)
        def _():
            pass_mixed(2)

    finish_weight(2)
    last[1].start()
    last[2].start()

    @pl.loop(0, CHUNKS)
    def _(t):
        expand(t)

        @pl.when(t == 0)
        def _():
            send_cot(4)

        @pl.when(t == 1)
        def _():
            send_cot(5)
            send_cot(6)

        @pl.when(t == 3)
        def _():
            forward_weight(3, 2)

        @pl.when((t >= 2) & (t <= 5))
        def _():
            second_norm(t + 1)

        @pl.when((t >= 1) & (t <= 4))
        def _():
            pass_mixed(t + 2)

        @pl.when(t >= 3)
        def _():
            pass_on_cot(t - 3)

    for n in range(4, CHUNKS):
        pass_on_cot(n)

    @pl.loop(0, CHUNKS)
    def _(i):
        mixed_x(i, slab).wait_send()
        mixed_core(i, 0, slab).wait_send()
        mixed_core(i, 1, core * 2 + 1 - xx).wait_send()
        for s in range(2):
            cot_x(i, s, c).wait_send()
            cot_core(i, s, c).wait_send()
            cot_core(i, s, c_core).wait_recv()
        cot_pass(i, c_x).wait_send()
        cot_pass(i, c_far).wait_recv()
        for copy in kept(i, 3):
            copy.start()

    @pl.loop(0, CHUNKS)
    def _(i):
        for s in range(2):
            tok_x(i, s, c).wait_send()
            tok_core(i, s, c).wait_send()
        tok_pass(i, c_x).wait_send()

    finish_weight(3)
    last[3].start()

    @pl.loop(0, CHUNKS)
    def _(i):
        for stage in range(5):
            for copy in kept(i, stage):
                copy.wait()

    for t in (CHUNKS - 2, CHUNKS - 1):
        keep_hid(t).wait()

    for copy in last:
        copy.wait()


def forward_call(*arrays):
    tok, we_s = arrays[0], arrays[-2]
    pairs, width = tok.shape[0], tok.shape[1] // 2
    chunk = 2 * pairs // CHUNKS
    full = 4 * width
    hidden = we_s.shape[1]
    n = CHUNKS

    def sd(shape, dtype):
        return jax.ShapeDtypeStruct(shape, dtype)

    outs = [
        sd((n, chunk, full), BF16),
        sd((n, chunk, full), BF16),
        sd((n, chunk, width), BF16),
        sd((n, width, chunk), BF16),
        sd((n, chunk, width), BF16),
        sd((n, width, chunk), BF16),
        sd((n, chunk, width), BF16),
        sd((n, chunk, width), F32),
        sd((n, 8, chunk), F32),
        sd((n, chunk, width), F32),
        sd((n, chunk, full), BF16),
        sd((n, chunk, 128), F32),
        sd((n, chunk, full), BF16),
        sd((n, chunk, hidden), BF16),
        sd((n, chunk, hidden), BF16),
        sd((3, full, width), BF16),
        sd((width, full), BF16),
        sd((full, hidden), BF16),
        sd((hidden, full), BF16),
        sd((8, full), F32),
        sd((n, chunk, full), BF16),
        sd((n, chunk, 128), F32),
    ]
    vm = pltpu.VMEM
    dma = pltpu.SemaphoreType.DMA
    scratch = [
        vm((n, chunk, full), BF16), vm((n, chunk, full), BF16), vm((n, chunk, full), BF16),
        vm((n, chunk, width), BF16), vm((n, width, chunk), BF16),
        vm((n, chunk, width), BF16), vm((n, width, chunk), BF16),
        vm((n, chunk, width), BF16), vm((n, width, chunk), BF16),
        vm((n, chunk, full), BF16), vm((n, chunk, width), F32), vm((n, 8, chunk), F32),
        vm((2, chunk, full), F32), vm((n, chunk, full), BF16), vm((n, chunk, 128), F32),
        vm((n, chunk, full), BF16), vm((n, chunk, hidden), BF16), vm((n, chunk, hidden), BF16),
        vm((3, full, width), BF16), vm((full, full), BF16), vm((full, hidden), BF16), vm((hidden, full), BF16),
        vm((8, full), F32), vm((n, chunk, 128), F32),
        vm((2, n, chunk, chunk), F32),
        dma((18, n)), dma((4,)), dma((n, 2)), dma((n, 2)), dma((4, 2, 3)), dma((4, 2, 3)), dma((4, 4)), dma((4, 4)), dma((3,)), dma((3,)),
        dma((n, 2)), dma((n, 2)), dma((n, 2)), dma((n, 2)), dma((n,)), dma((n,)),
        dma((n, 2)), dma((n, 2)), dma((n, 2)), dma((n, 2)), dma((n,)), dma((n,)),
        dma((1,)), dma((1,)), dma((1,)), dma((1,)), dma((n,)), dma((n,)), dma((n, 2)), dma((n, 2)),
    ]
    return pl.pallas_call(
        forward_kernel,
        out_shape=outs,
        in_specs=[pl.BlockSpec(memory_space=pl.ANY if n in (0, 1, 10, 11, 12, 13) else pltpu.VMEM) for n in range(len(arrays))],
        out_specs=[pl.BlockSpec(memory_space=pl.ANY)] * len(outs),
        scratch_shapes=scratch,
        compiler_params=pltpu.CompilerParams(
            collective_id=0, has_side_effects=True, vmem_limit_bytes=63 << 20
        ),
    )(*arrays)


GRAD_KINDS = ("three", "cols", "rows", "cols")


def backward_kernel(
    tok_h, cot_h, q_h, qt_h, k_h, kt_h, v_h, mixf_h, lse_h, hid_h, unit_h, inv_h,
    normed_h, act_h, slope_h, win_h, wo_h, we_h, wr_h, vec_h, one_h, stat_h,
    out_o, tg_o, sums_o, gin_o, gout_o, gexp_o, gred_o,
    cot, q, qt, k, kt, v, mixf, lse, hid, unit, inv, normed, act, slope, win, wo, we, wr, vecs,
    grad, flat, dk, dv, tg, out, sb_g, sb_o, rb_g, xr_g, rb_o, xr_o, xr_1, st, st_in,
    col_sums, packet, packets,
    ys_in, ys_out, ys_exp, ys_red, oh_in, oh_out, oh_exp, oh_red,
    yr_in, yr_out, yr_exp, yr_red, zr_in, zr_out, zr_exp, zr_red,
    gin, gout, gexp, gred,
    load_sem, chunk_sem, store_sem, hid_sem, gy_send, gy_recv, gz_send, gz_recv,
    h1g_send, h1g_recv, h2g_send, h2g_recv, h3g_send, h3g_recv,
    h1o_send, h1o_recv, h2o_send, h2o_recv, h1t_send, h1t_recv, h2t_send, h2t_recv,
    st_send, st_recv, pk_send, pk_recv,
):
    r, c = lax.axis_index("row"), lax.axis_index("col")
    z, y = r // 2, r % 2
    xx, core = c // 2, c % 2
    c_x, c_core, c_far = (c + 2) % 4, c + 1 - 2 * core, (c + 2) % 4 + 1 - 2 * core
    r_y = r + 1 - 2 * y
    tok, one, stat = act, normed, inv
    chunk = q.shape[0] // CHUNKS
    half = chunk // 2
    width = q.shape[1]
    full = cot.shape[1]
    scale = LOG2E * HEAD_DIM ** (-0.5)
    own = aligned(c, width)
    others = [(r + step) % 8 for step in range(1, 8)]

    barrier = pltpu.get_barrier_semaphore()
    for col in (c_x, c_core, c_far):
        pl.semaphore_signal(barrier, inc=1, device_id=(r, col), device_id_type=MESH)
    for row in others:
        pl.semaphore_signal(barrier, inc=1, device_id=(row, c), device_id_type=MESH)

    def rows_of(i):
        return pl.ds(pl.multiple_of(i * chunk, chunk), chunk)

    loads = {}
    order = (
        ("wr", wr_h, wr), ("we", we_h, we),
        ("vec", vec_h, vecs), ("unit", unit_h, unit), ("inv", inv_h, inv), ("wo", wo_h, wo),
        ("normed", normed_h, normed), ("mixf", mixf_h, mixf), ("lse", lse_h, lse), ("qt", qt_h, qt), ("q", q_h, q),
        ("k", k_h, k), ("v", v_h, v), ("kt", kt_h, kt), ("stat", stat_h, stat),
        ("tok", tok_h, tok), ("one", one_h, one),
    )
    for n, (name, src, dst) in enumerate(order):
        loads[name] = pltpu.make_async_copy(src, dst, load_sem.at[n])
    for n in range(3):
        loads["win" + str(n)] = pltpu.make_async_copy(
            win_h.at[n], win.at[:, pl.ds(n * width, width)], load_sem.at[len(order) + n]
        )
    def chunk_loads(i):
        rows = rows_of(i)
        return [
            pltpu.make_async_copy(a.at[rows, :], b.at[rows, :], chunk_sem.at[n, i])
            for n, (a, b) in enumerate(((cot_h, cot), (slope_h, slope), (act_h, act)))
        ]

    loads["wr"].start()
    loads["we"].start()
    for i in range(CHUNKS):
        for copy in chunk_loads(i):
            copy.start()
    late = ("wr", "we", "tok", "one", "stat", "win0", "win1", "win2")
    for name in loads:
        if name not in late:
            loads[name].start()
    dk[...] = jnp.zeros_like(dk)
    dv[...] = jnp.zeros_like(dv)
    col_sums[...] = jnp.zeros_like(col_sums)
    pl.semaphore_wait(barrier, 10)

    def h1(sb, rb, send, recv, i):
        return remote(sb.at[i % 2, 1 - core], rb.at[i], send.at[i], recv.at[i], r, c_core)

    def fill(sb, i, partial):
        for x in range(2):
            for side in range(2):
                block = x * 2 + side
                sb[i % 2, side, x] = partial[:, block * width : (block + 1) * width].astype(BF16)

    def merge(sb, rb, i):
        for x in range(2):
            rb[i, x] = (sb[i % 2, core, x].astype(F32) + rb[i, x].astype(F32)).astype(BF16)

    def h1g(i):
        return h1(sb_g, rb_g, h1g_send, h1g_recv, i)

    def h1o(i):
        return h1(sb_o, rb_o, h1o_send, h1o_recv, i)

    def h1t(i):
        return h1(sb_g, rb_g, h1t_send, h1t_recv, i)

    def h2g(i):
        return remote(rb_g.at[i], xr_g.at[i], h2g_send.at[i], h2g_recv.at[i], r, c_x)

    def h2o(i):
        return remote(rb_o.at[i, 1 - xx], xr_o.at[i], h2o_send.at[i], h2o_recv.at[i], r, c_x)

    def h2t(i):
        return remote(rb_g.at[i, 1 - xx], xr_1.at[i], h2t_send.at[i], h2t_recv.at[i], r, c_x)

    def h3g(i, x, side):
        block = grad.at[i % 4, :, aligned(x * 2 + side, width)]
        return remote(block, block, h3g_send.at[i, x], h3g_recv.at[i, x], r, c_core)

    def spread_grad(i):
        h2g(i).wait()
        if isinstance(i, int):
            h2g(i + 4).start()
        else:
            @pl.when(i + 4 < CHUNKS)
            def _():
                h2g(i + 4).start()

        for x in range(2):
            grad[i % 4, :, aligned(x * 2 + core, width)] = rb_g[i, x].astype(F32) + xr_g[i, x].astype(F32)
        for x in range(2):
            h3g(i, x, core).start()

    def column_sums(values):
        ones = jnp.ones((8, values.shape[0]), BF16)
        return jnp.dot(ones, values, preferred_element_type=F32)[0:1, :]

    ys = (ys_in, ys_out, ys_exp, ys_red)
    oh = (oh_in, oh_out, oh_exp, oh_red)
    yr = (yr_in, yr_out, yr_exp, yr_red)
    zr = (zr_in, zr_out, zr_exp, zr_red)

    def gy(w, s):
        return remote(ys[w].at[s], yr[w].at[s], gy_send.at[w, s], gy_recv.at[w, s], r_y, c)

    def gz(w, s):
        target = ((z + 1 + s) % 4) * 2 + y
        return remote(oh[w].at[s], zr[w].at[s], gz_send.at[w, s], gz_recv.at[w, s], target, c)

    def grad_block(w, s, left, right):
        zt = (z + 1 + s) % 4
        lanes = aligned(zt, 256)
        if GRAD_KINDS[w] == "rows":
            block = lax.dot_general(left[:, lanes], right, TN_DIMS, preferred_element_type=F32).astype(BF16)
            low, high = block[0:128, :], block[128:256, :]
        else:
            block = lax.dot_general(left, right[:, lanes], TN_DIMS, preferred_element_type=F32).astype(BF16)
            low, high = block[:, 0:128], block[:, 128:256]

        @pl.when(y == 0)
        def _():
            oh[w][s] = low
            ys[w][s] = high

        @pl.when(y == 1)
        def _():
            oh[w][s] = high
            ys[w][s] = low

    def pass_on(w, s):
        gy(w, s).wait()
        oh[w][s] = (oh[w][s].astype(F32) + yr[w][s].astype(F32)).astype(BF16)
        gz(w, s).start()

    def finish_grad(w, dst):
        gy(w, 3).wait()
        total = oh[w][3].astype(F32) + yr[w][3].astype(F32)
        for s in range(3):
            gz(w, s).wait()
            total = total + zr[w][s].astype(F32)
        dst[...] = total

    loads["wr"].wait()
    loads["we"].wait()

    @pl.loop(0, CHUNKS + 1)
    def _(i):
        @pl.when(i < CHUNKS)
        def _():
            @pl.when(i < 3)
            def _():
                for copy in chunk_loads(i):
                    copy.wait()

            @pl.when(i == 3)
            def _():
                for n in range(3, CHUNKS):
                    for copy in chunk_loads(n):
                        copy.wait()

            rows = rows_of(i)
            for n in range(slope.shape[1] // 256):
                lanes = slice(n * 256, (n + 1) * 256)
                grad_act = lax.dot_general(cot[rows, :], wr[lanes, :], NT_DIMS, preferred_element_type=F32)
                low = (slope[rows, lanes].astype(F32) * grad_act).astype(BF16)
                slope[rows, lanes] = low
            fill(sb_g, i, lax.dot_general(slope[rows, :], we[...], NT_DIMS, preferred_element_type=F32))
            h1g(i).start()

        @pl.when(i >= 1)
        def _():
            h1o(i - 1).wait()
            merge(sb_o, rb_o, i - 1)
            h1g(i - 1).wait()
            merge(sb_g, rb_g, i - 1)

        for at, n in ((1, 0), (2, 1), (4, 2), (6, 3)):
            @pl.when(i == at)
            def _():
                h2g(n).start()

        @pl.when(i == 3)
        def _():
            grad_block(3, 0, act[...], cot)
            gy(3, 0).start()

        @pl.when(i == 5)
        def _():
            grad_block(3, 1, act[...], cot)
            gy(3, 1).start()

        @pl.when(i < CHUNKS)
        def _():
            fill(sb_o, i, jnp.dot(act[rows_of(i), :], wr[...], preferred_element_type=F32))
            h1o(i).start()

    for n in range(4):
        packet[8 + n : 9 + n, :] = column_sums(slope[:, n * width : (n + 1) * width])
    loads["normed"].wait()
    spread_grad(0)
    pass_on(3, 0)
    grad_block(3, 2, act[...], cot)
    gy(3, 2).start()
    grad_block(3, 3, act[...], cot)
    spread_grad(1)
    grad_block(2, 0, normed, slope[...])
    pass_on(3, 1)
    gy(2, 0).start()
    for s in range(1, 4):
        grad_block(2, s, normed, slope[...])
    for name in late[2:]:
        if name != "stat":
            loads[name].start()
    for name in ("unit", "inv", "vec", "wo", "mixf", "lse", "qt", "q", "k", "v", "kt"):
        loads[name].wait()

    def hid_load(i):
        return pltpu.make_async_copy(hid_h.at[rows_of(i), :], hid, hid_sem.at[i])

    def out_store(i, s):
        return pltpu.make_async_copy(
            out.at[i % 2, s], out_o.at[pl.ds(pl.multiple_of(i * half, half), half), pl.ds(s * width, width)],
            store_sem.at[0, i, s],
        )

    def tg_store(i, s):
        return pltpu.make_async_copy(
            tg.at[i, s], tg_o.at[pl.ds(pl.multiple_of(i * half, half), half), pl.ds(s * width, width)],
            store_sem.at[1, i, s],
        )

    def attend_back(i):
        rows = rows_of(i)
        go = lax.dot_general(unit[rows, :], wo[...], NT_DIMS, preferred_element_type=F32).astype(BF16)
        inner = (go.astype(F32) * mixf[rows, :]).T
        go_t = go.T
        row_ids = lax.broadcasted_iota(jnp.int32, (128, chunk), 0)
        lane_ids = lax.broadcasted_iota(jnp.int32, (chunk, 128), 1)
        heads = width // HEAD_DIM
        queries, grads, query_rows, grad_rows, deltas, logs = [], [], [], [], [], []
        for h in range(heads):
            lanes = slice(h // 2 * 128, h // 2 * 128 + 128)
            pick = row_ids // HEAD_DIM == h % 2
            value = qt[i, lanes, :]
            queries.append(jnp.where(pick, value, jnp.zeros_like(value)))
            value = go_t[lanes, :]
            grads.append(jnp.where(pick, value, jnp.zeros_like(value)))
            pick = lane_ids // HEAD_DIM == h % 2
            value = q[rows, lanes]
            query_rows.append(jnp.where(pick, value, jnp.zeros_like(value)))
            value = go[:, lanes]
            grad_rows.append(jnp.where(pick, value, jnp.zeros_like(value)))
            deltas.append(jnp.sum(inner[h * HEAD_DIM : (h + 1) * HEAD_DIM, :], axis=0, keepdims=True))
            logs.append(lse[i, h : h + 1, :])

        parts = [jnp.zeros((HEAD_DIM, chunk), F32)] * heads
        for j in range(CHUNKS):
            keys = pl.ds(j * chunk, chunk)
            probs, grad_scores = [], []
            for h in range(heads):
                lanes = slice(h // 2 * 128, h // 2 * 128 + 128)
                block = jnp.dot(k[keys, lanes], queries[h], preferred_element_type=F32)
                grad_probs = jnp.dot(v[keys, lanes], grads[h], preferred_element_type=F32)
                prob = jnp.exp2(block * scale - logs[h])
                probs.append(prob.astype(BF16))
                grad_scores.append((prob * (grad_probs - deltas[h])).astype(BF16))
            for pair in range(heads // 2):
                lanes = slice(pair * 128, pair * 128 + 128)
                h = 2 * pair
                dv[keys, lanes] += jnp.dot(
                    probs[h], grad_rows[h], preferred_element_type=F32
                ) + jnp.dot(probs[h + 1], grad_rows[h + 1], preferred_element_type=F32)
                dk[keys, lanes] += jnp.dot(
                    grad_scores[h], query_rows[h], preferred_element_type=F32
                ) + jnp.dot(grad_scores[h + 1], query_rows[h + 1], preferred_element_type=F32)
            for h in range(heads):
                rows_h = slice(h * HEAD_DIM, (h + 1) * HEAD_DIM)
                parts[h] = parts[h] + jnp.dot(kt[j, rows_h, :], grad_scores[h], preferred_element_type=F32)
        flat[rows, 0:width] = (jnp.concatenate(parts, axis=0).T * HEAD_DIM ** (-0.5)).astype(BF16)

    def finish_out(i):
        @pl.when(i >= 2)
        def _():
            for s in range(2):
                out_store(i - 2, s).wait()

        hid_load(i).start()
        h2o(i).wait()
        hid_load(i).wait()
        total = rb_o[i, xx].astype(F32) + xr_o[i].astype(F32)
        value = (hid[...] + total + vecs[5:6, own]).astype(BF16)
        for s in range(2):
            out[i % 2, s] = value[s * half : (s + 1) * half, :]
        for s in range(2):
            out_store(i, s).start()

    def second_norm_back(i):
        for x in range(2):
            h3g(i, x, core).wait_send()
            h3g(i, x, 1 - core).wait_recv()
        step_rows = chunk // 7
        for part in range(7):
            rows = pl.ds(pl.multiple_of(i * chunk + part * step_rows, step_rows), step_rows)
            span = slice(part * step_rows, (part + 1) * step_rows)
            incoming = grad[i % 4, span, :]
            units = unit[rows, :].astype(F32)
            scaled = incoming * vecs[3:4, :]
            plain = jnp.mean(scaled, axis=1, keepdims=True)
            cross = jnp.mean(scaled * units, axis=1, keepdims=True)
            total = cot[rows, :].astype(F32) + inv[rows, 0:1] * (scaled - plain - units * cross)
            mine = grad[i % 4, span, own]
            col_sums[1:2, 0:width] += jnp.sum(mine * unit[rows, own].astype(F32), axis=0, keepdims=True)
            col_sums[2:3, 0:width] += jnp.sum(mine, axis=0, keepdims=True)
            unit[rows, :] = total.astype(BF16)
            grad[i % 4, span, :] = total
        for s in range(2):
            tg[i, s] = grad[i % 4, s * half : (s + 1) * half, own]

    @pl.loop(-1, CHUNKS)
    def _(i):
        @pl.when(i + 1 < CHUNKS)
        def _():
            second_norm_back(i + 1)

        @pl.when((i >= 0) & (i + 2 < CHUNKS))
        def _():
            spread_grad(i + 2)

        @pl.when(i == CHUNKS - 2)
        def _():
            for s in range(4):
                grad_block(1, s, mixf[...].astype(BF16), unit)
                gy(1, s).start()

        @pl.when(i == CHUNKS - 1)
        def _():
            loads["stat"].start()

        @pl.when(i >= 0)
        def _():
            attend_back(i)

        @pl.when(i == -1)
        def _():
            pass_on(3, 2)
            gy(2, 1).start()

        @pl.when(i == 0)
        def _():
            pass_on(2, 0)
            gy(2, 2).start()

        @pl.when(i == 1)
        def _():
            pass_on(2, 1)
            gy(3, 3).start()

        @pl.when(i == 2)
        def _():
            pass_on(2, 2)
            gy(2, 3).start()

        @pl.when(i == CHUNKS - 2)
        def _():
            finish_grad(3, gred)

        @pl.when(i == CHUNKS - 1)
        def _():
            for s in range(3):
                pass_on(1, s)

        @pl.when(i >= 3)
        def _():
            @pl.loop(2 * (i - 3), jnp.minimum(2 * (i - 3) + 2, CHUNKS))
            def _(n):
                h2o(n).start()

        @pl.when(i >= 5)
        def _():
            @pl.loop(2 * (i - 5), 2 * (i - 5) + 2)
            def _(n):
                finish_out(n)

    for i in range(CHUNKS):
        rows = pl.ds(i * chunk, chunk)
        flat[rows, width : 2 * width] = (dk[rows, :] * HEAD_DIM ** (-0.5)).astype(BF16)
        flat[rows, 2 * width : 3 * width] = dv[rows, :].astype(BF16)
    for name in late[2:]:
        loads[name].wait()

    def inward_block(s):
        zt = (z + 1 + s) % 4
        left = one[:, aligned(zt, 256)]
        block = lax.dot_general(left, flat[...], TN_DIMS, preferred_element_type=F32).astype(BF16)
        for n in range(3):
            lanes = slice(n * width, (n + 1) * width)

            @pl.when(y == 0)
            def _():
                oh_in[s, n] = block[0:128, lanes]
                ys_in[s, n] = block[128:256, lanes]

            @pl.when(y == 1)
            def _():
                oh_in[s, n] = block[128:256, lanes]
                ys_in[s, n] = block[0:128, lanes]

        gy(0, s).start()

    def stat_copy(i, slot, target):
        return remote(st.at[i], st_in.at[i, slot], st_send.at[i, slot], st_recv.at[i, slot], r, target)

    lane_ids = lax.broadcasted_iota(jnp.int32, (chunk, 128), 1)
    gain = vecs[0:1, :]

    @pl.loop(0, CHUNKS + 3)
    def _(i):
        for s in range(4):
            @pl.when(i == s)
            def _():
                inward_block(s)

        @pl.when(i < CHUNKS)
        def _():
            rows = rows_of(i)
            partial = lax.dot_general(flat[rows, :], win[...], NT_DIMS, preferred_element_type=F32)
            fill(sb_g, i, partial)
            h1t(i).start()
            units = (tok[rows, :].astype(F32) - stat[rows, 0:1]) * stat[rows, 64:65]
            scaled = partial * gain
            plain = jnp.sum(scaled, axis=1, keepdims=True)
            cross = jnp.sum(scaled * units, axis=1, keepdims=True)
            both = jnp.where(lane_ids == 0, plain, jnp.where(lane_ids == 1, cross, 0.0))
            st[i] = both.T[0:8, :]
            for slot, target in enumerate((c_x, c_core, c_far)):
                stat_copy(i, slot, target).start()

        @pl.when((i >= 4) & (i <= 6))
        def _():
            finish_out(i)

        @pl.when((i >= 1) & (i <= CHUNKS))
        def _():
            h1t(i - 1).wait()
            merge(sb_g, rb_g, i - 1)
            h2t(i - 1).start()

        for s in range(3):
            @pl.when(i == s + 2)
            def _():
                pass_on(0, s)

        @pl.when(i == 5)
        def _():
            packet[7:8, :] = column_sums(cot[:, own])
            packet[4:5, :] = column_sums(unit[:, own])

        @pl.when(i == 6)
        def _():
            packet[2:3, :] = column_sums(flat[:, 0:width])
            packet[3:4, :] = column_sums(flat[:, 2 * width : 3 * width])
            finish_grad(2, gexp)

        @pl.when(i == 7)
        def _():
            finish_grad(1, gout)

        @pl.when(i >= 3)
        def _():
            t = i - 3
            rows = rows_of(t)
            h2t(t).wait()
            total = st[t]
            for slot, target in enumerate((c_x, c_core, c_far)):
                stat_copy(t, slot, target).wait()
                total = total + st_in[t, slot]
            columns = jnp.concatenate([total, jnp.zeros((120, chunk), F32)], axis=0).T
            plain = columns[:, 0:1] / full
            cross = columns[:, 1:2] / full
            incoming = rb_g[t, xx].astype(F32) + xr_1[t].astype(F32)
            inverse = stat[rows, 64:65]
            units = (tok[rows, own].astype(F32) - stat[rows, 0:1]) * inverse
            back = inverse * (incoming * vecs[0:1, own] - plain - units * cross)
            for s in range(2):
                tg[t, s] = tg[t, s] + back[s * half : (s + 1) * half, :]
            for s in range(2):
                tg_store(t, s).start()
            col_sums[6:7, 0:width] += jnp.sum(incoming * units, axis=0, keepdims=True)
            col_sums[7:8, 0:width] += jnp.sum(incoming, axis=0, keepdims=True)

    packet[0:1, :] = col_sums[6:7, 0:width]
    packet[1:2, :] = col_sums[7:8, 0:width]
    packet[5:7, :] = col_sums[1:3, 0:width]

    def packet_copy(step):
        return remote(packet, packets.at[step], pk_send.at[step], pk_recv.at[step], others[step], c)

    for step in range(7):
        packet_copy(step).start()
    finish_grad(0, gin)
    stores = [
        pltpu.make_async_copy(src, dst, store_sem.at[2, n, 0])
        for n, (src, dst) in enumerate(((gin, gin_o), (gout, gout_o), (gexp, gexp_o), (gred, gred_o)))
    ]
    for copy in stores:
        copy.start()
    total = packet[...]
    for step in range(7):
        packet_copy(step).wait()
        total = total + packets[step]
    packet[...] = total
    copy = pltpu.make_async_copy(packet, sums_o, store_sem.at[2, 4, 0])
    copy.start()
    copy.wait()
    for copy in stores:
        copy.wait()
    for i in range(CHUNKS - 2, CHUNKS):
        for s in range(2):
            out_store(i, s).wait()

    @pl.loop(0, CHUNKS)
    def _(i):
        for s in range(2):
            tg_store(i, s).wait()


def backward_call(*arrays):
    (tok, cot, q, qt, k, kt, v, mixf, lse, hid, unit, inv, normed, act, slope, win, wo, we, wr, vec, one, stat) = arrays
    rows, width = q.shape
    full, hidden = we.shape
    n, chunk = CHUNKS, rows // CHUNKS
    half = chunk // 2
    pairs = rows // 2

    def sd(shape, dtype):
        return jax.ShapeDtypeStruct(shape, dtype)

    outs = [
        sd((pairs, 2 * width), BF16), sd((pairs, 2 * width), F32), sd((16, width), F32),
        sd((3, 128, width), F32), sd((width, 128), F32), sd((128, hidden), F32), sd((hidden, 128), F32),
    ]
    vm = pltpu.VMEM
    dma = pltpu.SemaphoreType.DMA

    def shapes(lead):
        return [
            vm((lead, 3, 128, width), BF16), vm((lead, width, 128), BF16),
            vm((lead, 128, hidden), BF16), vm((lead, hidden, 128), BF16),
        ]

    def like(array):
        return vm(array.shape, array.dtype)

    scratch = [
        vm((rows, full), BF16), like(q), like(qt), like(k), like(kt), like(v), like(mixf), like(lse),
        vm((chunk, width), F32),
        like(unit), like(inv), like(normed), like(act), like(slope),
        vm((full, 3 * width), BF16), like(wo), like(we), like(wr), like(vec),
        vm((4, chunk, full), F32), vm((rows, 3 * width), BF16), vm((rows, width), F32), vm((rows, width), F32),
        vm((n, 2, half, width), F32), vm((2, 2, half, width), BF16),
        vm((2, 2, 2, chunk, width), BF16), vm((2, 2, 2, chunk, width), BF16),
        vm((n, 2, chunk, width), BF16), vm((n, 2, chunk, width), BF16),
        vm((n, 2, chunk, width), BF16), vm((n, chunk, width), BF16), vm((n, chunk, width), BF16),
        vm((n, 8, chunk), F32), vm((n, 3, 8, chunk), F32),
        vm((8, full), F32), vm((16, width), F32), vm((7, 16, width), F32),
        *shapes(4), *shapes(4), *shapes(4), *shapes(3),
        vm((3, 128, width), F32), vm((width, 128), F32), vm((128, hidden), F32), vm((hidden, 128), F32),
        dma((23,)), dma((3, n)), dma((3, n, 2)), dma((n,)), dma((4, 4)), dma((4, 4)), dma((4, 3)), dma((4, 3)),
        dma((n,)), dma((n,)), dma((n,)), dma((n,)), dma((n, 2)), dma((n, 2)),
        dma((n,)), dma((n,)), dma((n,)), dma((n,)), dma((n,)), dma((n,)), dma((n,)), dma((n,)),
        dma((n, 3)), dma((n, 3)), dma((7,)), dma((7,)),
    ]
    return pl.pallas_call(
        backward_kernel,
        out_shape=outs,
        in_specs=[pl.BlockSpec(memory_space=pl.ANY)] * len(arrays),
        out_specs=[pl.BlockSpec(memory_space=pl.ANY)] * len(outs),
        scratch_shapes=scratch,
        compiler_params=pltpu.CompilerParams(
            collective_id=1, has_side_effects=True, vmem_limit_bytes=63 << 20
        ),
    )(*arrays)


def finish_kernel(out_i, tg_i, sums_i, gin_i, gout_i, gexp_i, gred_i, *refs):
    outs, vector_o, buffers = refs[:6], refs[6:14], refs[14:20]
    load_sem, store_sem = refs[20:]
    ins = (out_i, tg_i, gin_i, gout_i, gexp_i, gred_i)
    loads = [pltpu.make_async_copy(a, b, load_sem.at[n]) for n, (a, b) in enumerate(zip(ins, buffers))]
    stores = [pltpu.make_async_copy(a, b, store_sem.at[n]) for n, (a, b) in enumerate(zip(buffers, outs))]
    order = (0, 2, 3, 4, 5, 1)
    for n in order:
        loads[n].start()
    first_gain, first_shift, attn, b_out, g_two, s_two, b_red, b_exp = vector_o
    first_gain[...] = sums_i[0:1, :]
    first_shift[...] = sums_i[1:2, :]
    attn[...] = sums_i[2:4, :]
    b_out[...] = sums_i[4:5, :]
    g_two[...] = sums_i[5:6, :]
    s_two[...] = sums_i[6:7, :]
    b_red[...] = sums_i[7:8, :]
    for n in range(4):
        width = sums_i.shape[1]
        b_exp[:, n * width : (n + 1) * width] = sums_i[8 + n : 9 + n, :]
    for n in order:
        loads[n].wait()
        stores[n].start()
    for n in order:
        stores[n].wait()


def finish_call(out, tg, sums, gin, gout, gexp, gred):
    width = sums.shape[1]
    big = [jax.ShapeDtypeStruct(a.shape, a.dtype) for a in (out, tg, gin, gout, gexp, gred)]
    small = [jax.ShapeDtypeStruct((n, m), F32) for n, m in ((1, width),) * 2 + ((2, width),) + ((1, width),) * 4 + ((1, 4 * width),)]
    hbm, vm = pl.BlockSpec(memory_space=pl.ANY), pl.BlockSpec(memory_space=pltpu.VMEM)
    return pl.pallas_call(
        finish_kernel,
        out_shape=big + small,
        in_specs=[hbm, hbm, vm, hbm, hbm, hbm, hbm],
        out_specs=[hbm] * 6 + [vm] * 8,
        scratch_shapes=[pltpu.VMEM(a.shape, a.dtype) for a in big] + [pltpu.SemaphoreType.DMA((6,))] * 2,
    )(out, tg, sums, gin, gout, gexp, gred)


CONTRACT_ROWS = (((0,), (0,)), ((), ()))
CONTRACT_COLS = (((1,), (1,)), ((), ()))


def norm_forward(values, gain, shift, full_width):
    row_total = lax.psum(jnp.sum(values, axis=1), "col")
    centred = values - (row_total / full_width)[:, None]
    row_square = lax.psum(jnp.sum(centred * centred, axis=1), "col")
    inverse = lax.rsqrt(row_square / full_width + EPSILON)
    unit_rows = centred * inverse[:, None]
    return (unit_rows, inverse, unit_rows * gain + shift)


def norm_backward(incoming, unit_rows, inverse, gain, full_width):
    scaled = incoming * gain
    plain_sum, cross_sum = lax.psum(
        (jnp.sum(scaled, axis=1), jnp.sum(scaled * unit_rows, axis=1)), "col"
    )
    result = inverse[:, None] * (
        scaled - (plain_sum / full_width)[:, None] - unit_rows * (cross_sum / full_width)[:, None]
    )
    return (result, jnp.sum(incoming * unit_rows, axis=0), jnp.sum(incoming, axis=0))


def spread_features(values):
    return lax.all_gather(values, "col", axis=1, tiled=True)


def sum_partials(values):
    return lax.psum_scatter(values, "col", scatter_dimension=1, tiled=True)


def spread_grads(values):
    return lax.all_gather(values, "col", axis=1, tiled=True)


def sum_grad_partials(values):
    return lax.psum_scatter(values, "col", scatter_dimension=1, tiled=True)


def fetch_weights(inward_weight, output_weight, expand_weight, reduce_weight):
    return (
        lax.all_gather(inward_weight, "row", axis=0, tiled=True),
        lax.all_gather(output_weight, "row", axis=1, tiled=True),
        lax.all_gather(expand_weight, "row", axis=0, tiled=True),
        lax.all_gather(reduce_weight, "row", axis=1, tiled=True),
    )


def attend_clip(queries, key_rows, value_rows, score_scale):
    seq_len = queries.shape[0]
    blocks = queries.reshape((2, seq_len // 2) + queries.shape[1:])

    def one_block(query_part):
        scores = (
            jnp.einsum("qhd,khd->hqk", query_part, key_rows, preferred_element_type=jnp.float32)
            * score_scale
        )
        row_peak = jnp.max(scores, axis=-1, keepdims=True)
        exponent = jnp.exp(scores - row_peak)
        row_sum = jnp.sum(exponent, axis=-1, keepdims=True)
        prob_low = (exponent / row_sum).astype(jnp.bfloat16)
        mixed_rows = jnp.einsum(
            "hqk,khd->qhd", prob_low, value_rows, preferred_element_type=jnp.float32
        )
        return (mixed_rows, (row_peak + jnp.log(row_sum))[..., 0])

    mixed_rows, logsum = lax.map(one_block, blocks)
    return (mixed_rows.reshape(queries.shape), logsum)


def attend_clip_back(queries, key_rows, value_rows, logsum, grad_out, score_scale):
    seq_len = queries.shape[0]
    block_shape = (2, seq_len // 2) + queries.shape[1:]

    def step_block(carry, pieces):
        key_acc, value_acc = carry
        query_part, grad_part, log_part = pieces
        scores = (
            jnp.einsum("qhd,khd->hqk", query_part, key_rows, preferred_element_type=jnp.float32)
            * score_scale
        )
        probs = jnp.exp(scores - log_part[..., None])
        grad_probs = jnp.einsum(
            "qhd,khd->hqk", grad_part, value_rows, preferred_element_type=jnp.float32
        )
        inner_sum = jnp.sum(probs * grad_probs, axis=-1, keepdims=True)
        grad_scores = (probs * (grad_probs - inner_sum)).astype(jnp.bfloat16)
        query_grad = (
            jnp.einsum("hqk,khd->qhd", grad_scores, key_rows, preferred_element_type=jnp.float32)
            * score_scale
        )
        key_acc = key_acc + jnp.einsum(
            "hqk,qhd->khd", grad_scores, query_part, preferred_element_type=jnp.float32
        )
        value_acc = value_acc + jnp.einsum(
            "hqk,qhd->khd",
            probs.astype(jnp.bfloat16),
            grad_part,
            preferred_element_type=jnp.float32,
        )
        return ((key_acc, value_acc), query_grad)

    zero_acc = jnp.zeros(key_rows.shape, jnp.float32)
    (key_acc, value_acc), query_grads = lax.scan(
        step_block,
        (zero_acc, zero_acc),
        (queries.reshape(block_shape), grad_out.reshape(block_shape), logsum),
    )
    return (query_grads.reshape(queries.shape), key_acc * score_scale, value_acc)


def forward_pass(
    tokens,
    first_gain,
    first_shift,
    attention_bias,
    output_bias,
    second_gain,
    second_shift,
    expand_bias,
    reduce_bias,
    gathered,
):
    inward_all, output_rows, expand_all, reduce_rows = gathered
    full_width = inward_all.shape[0]
    local_width = inward_all.shape[2]
    row_count = tokens.shape[0]
    clip_shape = (row_count // SEQ, SEQ, local_width // HEAD_DIM, HEAD_DIM)
    score_scale = HEAD_DIM ** (-0.5)
    source = tokens.astype(jnp.float32)
    unit_one, inverse_one, normed_one = norm_forward(source, first_gain, first_shift, full_width)
    normed_all = spread_features(normed_one.astype(jnp.bfloat16))
    projected = jnp.dot(
        normed_all,
        inward_all.reshape(full_width, 3 * local_width),
        preferred_element_type=jnp.float32,
    )
    projected = projected.reshape(row_count, 3, local_width)
    queries = (projected[:, 0] + attention_bias[0]).astype(jnp.bfloat16)
    key_rows = projected[:, 1].astype(jnp.bfloat16)
    value_rows = (projected[:, 2] + attention_bias[1]).astype(jnp.bfloat16)
    mixed_rows, logsum = lax.map(
        lambda clip_parts: attend_clip(clip_parts[0], clip_parts[1], clip_parts[2], score_scale),
        (queries.reshape(clip_shape), key_rows.reshape(clip_shape), value_rows.reshape(clip_shape)),
    )
    mixed_low = mixed_rows.reshape(row_count, local_width).astype(jnp.bfloat16)
    hidden_state = (
        source
        + sum_partials(jnp.dot(mixed_low, output_rows, preferred_element_type=jnp.float32))
        + output_bias
    )
    unit_two, inverse_two, normed_two = norm_forward(
        hidden_state, second_gain, second_shift, full_width
    )
    normed_all_two = spread_features(normed_two.astype(jnp.bfloat16))
    expanded = jnp.dot(normed_all_two, expand_all, preferred_element_type=jnp.float32) + expand_bias
    activated = jax.nn.gelu(expanded, approximate=False).astype(jnp.bfloat16)
    output_value = (
        hidden_state
        + sum_partials(jnp.dot(activated, reduce_rows, preferred_element_type=jnp.float32))
        + reduce_bias
    )
    saved_state = (
        unit_one,
        inverse_one,
        normed_all,
        queries,
        key_rows,
        value_rows,
        logsum,
        mixed_low,
        unit_two,
        inverse_two,
        normed_all_two,
        expanded,
        activated,
    )
    return (output_value, saved_state)


def plain_device(
    tokens,
    first_gain,
    first_shift,
    inward_weight,
    attention_bias,
    output_weight,
    output_bias,
    second_gain,
    second_shift,
    expand_weight,
    expand_bias,
    reduce_weight,
    reduce_bias,
    cotangent,
):
    packed_width = tokens.shape[1]
    tokens = tokens.reshape(-1, packed_width // 2)
    cotangent = cotangent.reshape(-1, packed_width // 2)
    gathered = fetch_weights(inward_weight, output_weight, expand_weight, reduce_weight)
    output_value, saved_state = forward_pass(
        tokens,
        first_gain,
        first_shift,
        attention_bias,
        output_bias,
        second_gain,
        second_shift,
        expand_bias,
        reduce_bias,
        gathered,
    )
    gathered = fetch_weights(inward_weight, output_weight, expand_weight, reduce_weight)
    unused_value, saved_state = forward_pass(
        tokens,
        first_gain,
        first_shift,
        attention_bias,
        output_bias,
        second_gain,
        second_shift,
        expand_bias,
        reduce_bias,
        gathered,
    )
    inward_all, output_rows, expand_all, reduce_rows = gathered
    (
        unit_one,
        inverse_one,
        normed_all,
        queries,
        key_rows,
        value_rows,
        logsum,
        mixed_low,
        unit_two,
        inverse_two,
        normed_all_two,
        expanded,
        activated,
    ) = saved_state
    full_width = inward_all.shape[0]
    local_width = inward_all.shape[2]
    row_count = tokens.shape[0]
    clip_shape = (row_count // SEQ, SEQ, local_width // HEAD_DIM, HEAD_DIM)
    score_scale = HEAD_DIM ** (-0.5)
    grad_rows = cotangent.astype(jnp.float32)
    grad_all = spread_grads(cotangent)
    grad_act = lax.dot_general(
        grad_all, reduce_rows, CONTRACT_COLS, preferred_element_type=jnp.float32
    )
    reduce_grad = lax.dot_general(
        activated, grad_all, CONTRACT_ROWS, preferred_element_type=jnp.float32
    )
    reduce_bias_grad = jnp.sum(grad_rows, axis=0)
    gelu_value, gelu_back = jax.vjp(
        lambda inner_value: jax.nn.gelu(inner_value, approximate=False), expanded
    )
    grad_expanded = gelu_back(grad_act)[0].astype(jnp.bfloat16)
    expand_grad = lax.dot_general(
        normed_all_two, grad_expanded, CONTRACT_ROWS, preferred_element_type=jnp.float32
    )
    expand_bias_grad = jnp.sum(grad_expanded.astype(jnp.float32), axis=0)
    grad_normed_two = sum_grad_partials(
        lax.dot_general(
            grad_expanded, expand_all, CONTRACT_COLS, preferred_element_type=jnp.float32
        )
    )
    back_two, second_gain_grad, second_shift_grad = norm_backward(
        grad_normed_two, unit_two, inverse_two, second_gain, full_width
    )
    grad_hidden = grad_rows + back_two
    grad_hidden_low = grad_hidden.astype(jnp.bfloat16)
    grad_hidden_all = spread_grads(grad_hidden_low)
    output_grad = lax.dot_general(
        mixed_low, grad_hidden_all, CONTRACT_ROWS, preferred_element_type=jnp.float32
    )
    output_bias_grad = jnp.sum(grad_hidden_low.astype(jnp.float32), axis=0)
    grad_mixed = lax.dot_general(
        grad_hidden_all, output_rows, CONTRACT_COLS, preferred_element_type=jnp.float32
    ).astype(jnp.bfloat16)
    query_grads, key_grads, value_grads = lax.map(
        lambda clip_parts: attend_clip_back(
            clip_parts[0], clip_parts[1], clip_parts[2], clip_parts[3], clip_parts[4], score_scale
        ),
        (
            queries.reshape(clip_shape),
            key_rows.reshape(clip_shape),
            value_rows.reshape(clip_shape),
            logsum,
            grad_mixed.reshape(clip_shape),
        ),
    )
    stacked = jnp.stack(
        [
            query_grads.reshape(row_count, local_width),
            key_grads.reshape(row_count, local_width),
            value_grads.reshape(row_count, local_width),
        ],
        axis=1,
    ).astype(jnp.bfloat16)
    attention_bias_grad = jnp.stack(
        [
            jnp.sum(stacked[:, 0].astype(jnp.float32), axis=0),
            jnp.sum(stacked[:, 2].astype(jnp.float32), axis=0),
        ]
    )
    flat_grads = stacked.reshape(row_count, 3 * local_width)
    inward_grad = lax.dot_general(
        normed_all, flat_grads, CONTRACT_ROWS, preferred_element_type=jnp.float32
    ).reshape(full_width, 3, local_width)
    grad_normed_one = sum_grad_partials(
        lax.dot_general(
            flat_grads,
            inward_all.reshape(full_width, 3 * local_width),
            CONTRACT_COLS,
            preferred_element_type=jnp.float32,
        )
    )
    back_one, first_gain_grad, first_shift_grad = norm_backward(
        grad_normed_one, unit_one, inverse_one, first_gain, full_width
    )
    tokens_grad = grad_hidden + back_one
    inward_grad, output_grad, expand_grad, reduce_grad = (
        lax.psum_scatter(
            inward_grad.astype(jnp.bfloat16), "row", scatter_dimension=0, tiled=True
        ).astype(jnp.float32),
        lax.psum_scatter(
            output_grad.astype(jnp.bfloat16), "row", scatter_dimension=1, tiled=True
        ).astype(jnp.float32),
        lax.psum_scatter(
            expand_grad.astype(jnp.bfloat16), "row", scatter_dimension=0, tiled=True
        ).astype(jnp.float32),
        lax.psum_scatter(
            reduce_grad.astype(jnp.bfloat16), "row", scatter_dimension=1, tiled=True
        ).astype(jnp.float32),
    )
    (
        first_gain_grad,
        first_shift_grad,
        attention_bias_grad,
        output_bias_grad,
        second_gain_grad,
        second_shift_grad,
        expand_bias_grad,
        reduce_bias_grad,
    ) = lax.psum(
        (
            first_gain_grad,
            first_shift_grad,
            attention_bias_grad,
            output_bias_grad,
            second_gain_grad,
            second_shift_grad,
            expand_bias_grad,
            reduce_bias_grad,
        ),
        "row",
    )
    return (
        output_value.astype(jnp.bfloat16).reshape(-1, packed_width),
        tokens_grad.reshape(-1, packed_width),
        first_gain_grad,
        first_shift_grad,
        inward_grad,
        attention_bias_grad,
        output_grad,
        output_bias_grad,
        second_gain_grad,
        second_shift_grad,
        expand_grad,
        expand_bias_grad,
        reduce_grad,
        reduce_bias_grad,
    )


def fused_device(
    tokens,
    first_gain,
    first_shift,
    inward_weight,
    attention_bias,
    output_weight,
    output_bias,
    second_gain,
    second_shift,
    expand_weight,
    expand_bias,
    reduce_weight,
    reduce_bias,
    cotangent,
):
    kept = forward_call(
        tokens,
        cotangent,
        first_gain[None],
        first_shift[None],
        output_bias[None],
        second_gain[None],
        second_shift[None],
        reduce_bias[None],
        attention_bias,
        expand_bias[None],
        inward_weight.transpose(1, 0, 2),
        output_weight,
        expand_weight,
        reduce_weight,
    )
    (tok, cot, q, qt, k, kt, v, mixf, lse, hid, unit, inv, normed, act, slope, win, wo, we, wr, vec, one, stat) = kept

    def flat(array):
        return array.reshape(-1, array.shape[-1])

    outs = backward_call(
        flat(tok), flat(cot), flat(q), qt, flat(k), kt, flat(v), flat(mixf), lse, flat(hid), flat(unit),
        flat(inv), flat(normed), flat(act), flat(slope), win, wo, we, wr, vec, flat(one), flat(stat),
    )
    outs = finish_call(*outs)
    layer_output, tokens_grad, inward_grad, output_grad, expand_grad, reduce_grad = outs[:6]
    first_gain_grad, first_shift_grad, attention_grad, out_grad, gain_grad, shift_grad, red_grad, exp_grad = outs[6:]
    return (
        layer_output,
        tokens_grad,
        first_gain_grad[0],
        first_shift_grad[0],
        inward_grad.transpose(1, 0, 2),
        attention_grad,
        output_grad,
        out_grad[0],
        gain_grad[0],
        shift_grad[0],
        expand_grad,
        exp_grad[0],
        reduce_grad,
        red_grad[0],
    )


def per_device(rows, cols, *arrays):
    tokens, inward_weight, expand_weight = arrays[0], arrays[3], arrays[9]
    fits = (
        (rows, cols) == (8, 4)
        and tokens.shape == (SEQ // 2, 512)
        and inward_weight.shape == (128, 3, 256)
        and expand_weight.shape == (128, 1024)
    )
    return fused_device(*arrays) if fits else plain_device(*arrays)


def solution(mesh):
    in_specs = (
        P("row", "col"),
        P("col"),
        P("col"),
        P("row", None, "col"),
        P(None, "col"),
        P("col", "row"),
        P("col"),
        P("col"),
        P("col"),
        P("row", "col"),
        P("col"),
        P("col", "row"),
        P("col"),
        P("row", "col"),
    )
    out_specs = (
        P("row", "col"),
        P("row", "col"),
        P("col"),
        P("col"),
        P("row", None, "col"),
        P(None, "col"),
        P("col", "row"),
        P("col"),
        P("col"),
        P("col"),
        P("row", "col"),
        P("col"),
        P("col", "row"),
        P("col"),
    )
    return jax.shard_map(
        functools.partial(per_device, mesh.shape["row"], mesh.shape["col"]),
        mesh=mesh, in_specs=in_specs, out_specs=out_specs, check_vma=False
    )
```

```python
import functools
import jax
import jax.numpy as jnp
from jax import lax
from jax.experimental import pallas as pl
from jax.experimental.pallas import tpu as pltpu
from jax.sharding import PartitionSpec as P

HEAD_DIM = 64
SEQ = 1568
EPSILON = 1e-06
CHUNKS = 7
WINDOW = 2
F32 = jnp.float32
BF16 = jnp.bfloat16
MESH = pl.DeviceIdType.MESH
LOG2E = 1.4426950408889634
NT_DIMS = (((1,), (1,)), ((), ()))
TN_DIMS = (((0,), (0,)), ((), ()))


def remote(src, dst, send, recv, row, col):
    return pltpu.make_async_remote_copy(
        src_ref=src, dst_ref=dst, send_sem=send, recv_sem=recv,
        device_id=(row, col), device_id_type=MESH,
    )


def aligned(index, size):
    return pl.ds(pl.multiple_of(index * size, size), size)


def row_norm(values):
    mean = jnp.mean(values, axis=1, keepdims=True)
    centred = values - mean
    inverse = lax.rsqrt(jnp.mean(centred * centred, axis=1, keepdims=True) + EPSILON)
    return centred * inverse, mean, inverse


def weight_blocks(ref, kind, row):
    if kind == "three":
        return ref.at[:, aligned(row, 128), :]
    if kind == "rows":
        return ref.at[aligned(row, 128), :]
    return ref.at[:, aligned(row, 128)]


WEIGHT_KINDS = ("three", "cols", "rows", "cols")


def forward_kernel(
    tok, cot, g_one, s_one, b_out, g_two, s_two, b_red, attn_bias, exp_bias, win_s, wo_s, we_s, wr_s,
    tok_o, cot_o, q_o, qt_o, k_o, kt_o, v_o, mixf_o, lse_o, hid_o, unit_o, inv_o,
    norm_o, act_o, slope_o, win_o, wo_o, we_o, wr_o, vec_o, one_o, stat_o,
    tok_all, cot_all, norm_one, q, qt, k, kt, v, vt, mixed, mixf, lse, hid, unit, inv, norm_two, act, slope,
    win, wo, we, wr, vecs, stat, scores,
    local_sem, shard_sem, tok_sem, cot_sem, wz_send, wz_recv, wy_send, wy_recv, vec_send, vec_recv,
    tx_send, tx_recv, tc_send, tc_recv, tp_send, tp_recv, cx_send, cx_recv, cc_send, cc_recv, cp_send, cp_recv,
    wx_send, wx_recv, wc_send, wc_recv, mx_send, mx_recv, mc_send, mc_recv,
):
    r, c = lax.axis_index("row"), lax.axis_index("col")
    z, y = r // 2, r % 2
    xx, core = c // 2, c % 2
    c_x, c_core, c_far = (c + 2) % 4, c + 1 - 2 * core, (c + 2) % 4 + 1 - 2 * core
    r_y = r + 1 - 2 * y
    half = tok.shape[0] // CHUNKS
    chunk = 2 * half
    width = g_one.shape[1]
    scale = LOG2E * HEAD_DIM ** (-0.5)

    barrier = pltpu.get_barrier_semaphore()
    for col in (c_x, c_core, c_far):
        pl.semaphore_signal(barrier, inc=1, device_id=(r, col), device_id_type=MESH)
    pl.semaphore_signal(barrier, inc=1, device_id=(r_y, c), device_id_type=MESH)

    @pl.when(z >= 1)
    def _():
        pl.semaphore_signal(barrier, inc=1, device_id=(r - 2, c), device_id_type=MESH)

    @pl.when(z <= 2)
    def _():
        pl.semaphore_signal(barrier, inc=1, device_id=(r + 2, c), device_id_type=MESH)


    own = aligned(c, width)
    shards = (win_s, wo_s, we_s, wr_s)
    fulls = (win, wo, we, wr)
    shard_loads = [
        pltpu.make_async_copy(
            shards[w],
            wo.at[aligned(core * 2 + xx, width), aligned(r, 128)] if w == 1
            else weight_blocks(fulls[w], WEIGHT_KINDS[w], r),
            shard_sem.at[w],
        )
        for w in range(4)
    ]
    for copy in shard_loads:
        copy.start()

    def half_source(ref, i, s):
        return ref.at[pl.ds(pl.multiple_of(i * half, half), half), pl.ds(s * width, width)]

    def half_load(ref, full_ref, sem, i, s):
        return pltpu.make_async_copy(
            half_source(ref, i, s), full_ref.at[i, pl.ds(s * half, half), own], sem.at[i, s]
        )

    for i in range(CHUNKS):
        for s in range(2):
            half_load(tok, tok_all, tok_sem, i, s).start()
            half_load(cot, cot_all, cot_sem, i, s).start()
    for n, vector in enumerate((g_one, s_one, b_out, g_two, s_two, b_red, b_red, b_red)):
        vecs[n : n + 1, own] = vector[...]
    pl.semaphore_wait(barrier, 4 + jnp.where(z >= 1, 1, 0) + jnp.where(z <= 2, 1, 0))

    slab = core * 2 + xx

    def out_x(order):
        block = wo.at[aligned(order, width), :]
        return remote(block, block, wx_send.at[0], wx_recv.at[0], r, c_x)

    def out_core(side):
        block = wo.at[aligned(side, 2 * width), :]
        return remote(block, block, wc_send.at[0], wc_recv.at[0], r, c_core)

    def weight_ref(w, zb, side):
        if w == 1:
            return wo.at[aligned(slab, width), aligned(zb * 2 + side, 128)]
        return weight_blocks(fulls[w], WEIGHT_KINDS[w], zb * 2 + side)

    def line_copy(w, up, hop):
        zb = z - hop if up else z + hop
        block = weight_ref(w, zb, y)
        target = (z + 1 if up else z - 1) * 2 + y
        source = shards[w] if hop == 0 else block
        return remote(source, block, wz_send.at[w, up, hop], wz_recv.at[w, up, hop], target, c)

    def line_sends(up, hop):
        return (z >= hop) & (z <= 2) if up else (z <= 3 - hop) & (z >= 1)

    def line_receives(up, hop):
        return z >= hop + 1 if up else z <= 2 - hop

    def y_copy(w, zb, side):
        block = weight_ref(w, zb, side)
        return remote(block, block, wy_send.at[w, zb], wy_recv.at[w, zb], r_y, c)

    def start_weight(w):
        for up in (0, 1):
            @pl.when(line_sends(up, 0))
            def _():
                line_copy(w, up, 0).start()

    def own_to_y(w):
        return remote(shards[w], weight_ref(w, z, y), wy_send.at[w, z], wy_recv.at[w, z], r_y, c)

    def forward_weight(w, hop):
        for up in (0, 1):
            @pl.when(line_receives(up, hop))
            def _():
                zb = z - 1 - hop if up else z + 1 + hop
                block = weight_ref(w, zb, y)
                remote(block, block, wz_send.at[w, up, hop], wz_recv.at[w, up, hop], r_y, c).wait_recv()
                y_copy(w, zb, y).start()

            if hop < 2:
                @pl.when(line_receives(up, hop) & line_sends(up, hop + 1))
                def _():
                    line_copy(w, up, hop + 1).start()

    def finish_weight(w):
        for up in (0, 1):
            for hop in range(3):
                @pl.when(line_sends(up, hop))
                def _():
                    line_copy(w, up, hop).wait_send()
        for zb in range(4):
            y_copy(w, zb, y).wait_send()
            y_copy(w, zb, 1 - y).wait_recv()

    def vec_copy(slot, target, col):
        block = vecs.at[:, aligned(col, width)]
        return remote(block, block, vec_send.at[slot], vec_recv.at[slot], r, target)

    def half_x(ref, full_ref, send, recv, i, s, col):
        block = full_ref.at[i, pl.ds(s * half, half), aligned(col, width)]
        return remote(half_source(ref, i, s), block, send.at[i, s], recv.at[i, s], r, c_x)

    def half_core(ref, full_ref, send, recv, i, s, col):
        block = full_ref.at[i, pl.ds(s * half, half), aligned(col, width)]
        return remote(half_source(ref, i, s), block, send.at[i, s], recv.at[i, s], r, c_core)

    def tok_x(i, s, col):
        return half_x(tok, tok_all, tx_send, tx_recv, i, s, col)

    def tok_core(i, s, col):
        return half_core(tok, tok_all, tc_send, tc_recv, i, s, col)

    def cot_x(i, s, col):
        return half_x(cot, cot_all, cx_send, cx_recv, i, s, col)

    def cot_core(i, s, col):
        return half_core(cot, cot_all, cc_send, cc_recv, i, s, col)

    def pass_core(full_ref, send, recv, i, col):
        block = full_ref.at[i, :, aligned(col, width)]
        return remote(block, block, send.at[i], recv.at[i], r, c_core)

    def tok_pass(i, col):
        return pass_core(tok_all, tp_send, tp_recv, i, col)

    def cot_pass(i, col):
        return pass_core(cot_all, cp_send, cp_recv, i, col)

    def send_cot(i):
        for s in range(2):
            cot_x(i, s, c).start()
            cot_core(i, s, c).start()

    def send_tok(i):
        for s in range(2):
            tok_x(i, s, c).start()
            tok_core(i, s, c).start()

    start_weight(0)
    own_to_y(0).start()
    for i in range(WINDOW):
        send_tok(i)
    for slot, target in enumerate((c_x, c_core, c_far)):
        vec_copy(slot, target, c).start()

    def keep(index, i, src, dst):
        return pltpu.make_async_copy(src, dst, local_sem.at[index, i])

    def kept(i, stage):
        if stage == 0:
            pairs = ((tok_all, tok_o), (q, q_o), (qt, qt_o), (k, k_o), (kt, kt_o), (v, v_o), (norm_one, one_o), (stat, stat_o))
            base = 0
        elif stage == 1:
            pairs = ((mixf, mixf_o), (lse, lse_o))
            base = 8
        elif stage == 2:
            pairs = ((unit, unit_o), (inv, inv_o), (norm_two, norm_o))
            base = 10
        elif stage == 4:
            pairs = ((act, act_o), (slope, slope_o))
            base = 13
        else:
            pairs = ((cot_all, cot_o),)
            base = 15
        return [keep(base + n, i, a.at[i], b.at[i]) for n, (a, b) in enumerate(pairs)]

    last = [
        keep(17, n, a, b)
        for n, (a, b) in enumerate(
            ((win, win_o), (wo.at[aligned(slab, width), :], wo_o), (we, we_o), (wr, wr_o), (vecs, vec_o))
        )
    ]

    def keep_hid(i):
        return keep(16, i, hid.at[i % 2, :, own], hid_o.at[i])

    lane_ids = lax.broadcasted_iota(jnp.int32, (chunk // 7, 128), 1)

    def first_norm(i):
        for s in range(2):
            half_load(tok, tok_all, tok_sem, i, s).wait()
            tok_core(i, s, c_core).wait_recv()
        tok_pass(i, c_far).wait_recv()
        for part in range(7):
            rows = pl.ds(part * (chunk // 7), chunk // 7)
            units, mean, inverse = row_norm(tok_all[i, rows, :].astype(F32))
            stat[i, rows, :] = jnp.where(lane_ids < 64, mean, inverse)
            norm_one[i, rows, :] = (units * vecs[0:1, :] + vecs[1:2, :]).astype(BF16)

    @pl.loop(0, CHUNKS // 2 + 1)
    def _(g):
        @pl.loop(2 * g, jnp.minimum(2 * g + 2, CHUNKS))
        def _(i):
            for s in range(2):
                tok_x(i, s, c_x).wait_recv()

            @pl.when(i + WINDOW < CHUNKS)
            def _():
                send_tok(i + WINDOW)

            tok_pass(i, c_x).start()

        @pl.when(g == 0)
        def _():
            for slot, target in enumerate((c_x, c_core, c_far)):
                vec_copy(slot, target, c).wait_send()
                vec_copy(slot, target, target).wait_recv()

        for hop in range(3):
            @pl.when(g == hop)
            def _():
                forward_weight(0, hop)

        @pl.when(g == 0)
        def _():
            start_weight(1)
            own_to_y(1).start()

        @pl.when(g == 1)
        def _():
            forward_weight(1, 0)

        @pl.when(g == 3)
        def _():
            start_weight(2)
            forward_weight(1, 1)
            send_cot(0)
            send_cot(1)

        @pl.loop(2 * g, jnp.minimum(2 * g + 2, CHUNKS))
        def _(i):
            first_norm(i)

    for w in range(4):
        shard_loads[w].wait()
    own_to_y(3).start()
    forward_weight(1, 2)
    finish_weight(0)
    last[0].start()
    last[4].start()

    @pl.loop(0, CHUNKS)
    def _(i):
        part = jnp.dot(norm_one[i], win[0], preferred_element_type=F32)
        part = (part + attn_bias[0:1, :]).astype(BF16)
        q[i] = part
        qt[i] = part.T
        part = jnp.dot(norm_one[i], win[1], preferred_element_type=F32).astype(BF16)
        k[i] = part
        kt[i] = part.T
        part = jnp.dot(norm_one[i], win[2], preferred_element_type=F32)
        part = (part + attn_bias[1:2, :]).astype(BF16)
        v[i] = part
        vt[i] = part.T
        for copy in kept(i, 0):
            copy.start()

        @pl.when(i == 0)
        def _():
            own_to_y(2).start()
            finish_weight(1)
            out_x(slab).start()

        @pl.when(i == 4)
        def _():
            forward_weight(2, 0)

        @pl.when(i == 6)
        def _():
            forward_weight(2, 1)

    def attend(i):
        row_ids = lax.broadcasted_iota(jnp.int32, (128, chunk), 0)
        heads = width // HEAD_DIM

        def score(h):
            lanes = slice(h // 2 * 128, h // 2 * 128 + 128)
            query = qt[i, lanes, :]
            query = jnp.where(row_ids // HEAD_DIM == h % 2, query, jnp.zeros_like(query))
            peak = jnp.full((1, chunk), -jnp.inf, F32)
            for j in range(CHUNKS):
                block = jnp.dot(k[j, :, lanes], query, preferred_element_type=F32)
                scores[h % 2, j] = block
                peak = jnp.maximum(peak, jnp.max(block, axis=0, keepdims=True))
            return peak * scale

        def mix(h, peak):
            total = jnp.zeros((1, chunk), F32)
            acc = jnp.zeros((HEAD_DIM, chunk), F32)
            for j in range(CHUNKS):
                weights = jnp.exp2(scores[h % 2, j] * scale - peak)
                total = total + jnp.sum(weights, axis=0, keepdims=True)
                rows = slice(h * HEAD_DIM, (h + 1) * HEAD_DIM)
                acc = acc + jnp.dot(vt[j, rows, :], weights.astype(BF16), preferred_element_type=F32)
            lse[i, h : h + 1, :] = peak + jnp.log2(total)
            return acc / total

        outs = []
        peak = score(0)
        for h in range(heads):
            following = score(h + 1) if h + 1 < heads else None
            outs.append(mix(h, peak))
            peak = following
        out = jnp.concatenate(outs, axis=0).T
        mixf[i] = out
        mixed[i, :, aligned(slab, width)] = out.astype(BF16)

    def mixed_block(i, order):
        return mixed.at[i, :, aligned(order, width)]

    def mixed_x(i, order):
        block = mixed_block(i, order)
        return remote(block, block, mx_send.at[i], mx_recv.at[i], r, c_x)

    def mixed_core(i, slot, order):
        block = mixed_block(i, order)
        return remote(block, block, mc_send.at[i, slot], mc_recv.at[i, slot], r, c_core)

    def second_norm(t):
        mixed_core(t, 0, (1 - core) * 2 + xx).wait_recv()
        mixed_core(t, 1, (1 - core) * 2 + 1 - xx).wait_recv()

        @pl.when(t >= 2)
        def _():
            keep_hid(t - 2).wait()

        hid[t % 2] = tok_all[t].astype(F32) + (
            jnp.dot(mixed[t], wo[...], preferred_element_type=F32) + vecs[2:3, :]
        )
        for part in range(7):
            rows = pl.ds(part * (chunk // 7), chunk // 7)
            units, _, inverse = row_norm(hid[t % 2, rows, :])
            unit[t, rows, :] = units.astype(BF16)
            inv[t, rows, :] = jnp.broadcast_to(inverse, (chunk // 7, 128))
            norm_two[t, rows, :] = (units * vecs[3:4, :] + vecs[4:5, :]).astype(BF16)
        for copy in kept(t, 2):
            copy.start()
        keep_hid(t).start()

    def expand(t):
        for n in range(we.shape[1] // 256):
            lanes = slice(n * 256, (n + 1) * 256)
            expanded = jnp.dot(norm_two[t], we[:, lanes], preferred_element_type=F32) + exp_bias[:, lanes]
            gate = 0.5 + 0.5 * lax.erf(expanded * (0.5 ** 0.5))
            act[t, :, lanes] = (expanded * gate).astype(BF16)
            bell = jnp.exp2(expanded * expanded * (-0.5 * LOG2E)) * 0.3989422804014327
            slope[t, :, lanes] = (gate + expanded * bell).astype(BF16)
        for copy in kept(t, 4):
            copy.start()

    def pass_mixed(t):
        mixed_x(t, core * 2 + 1 - xx).wait_recv()
        mixed_core(t, 1, core * 2 + 1 - xx).start()

    def pass_on_cot(t):
        for s in range(2):
            cot_x(t, s, c_x).wait_recv()
            half_load(cot, cot_all, cot_sem, t, s).wait()
        cot_pass(t, c_x).start()

    @pl.loop(0, CHUNKS)
    def _(i):
        attend(i)
        mixed_x(i, slab).start()
        mixed_core(i, 0, slab).start()
        for copy in kept(i, 1):
            copy.start()

        @pl.when(i == 0)
        def _():
            start_weight(3)

        @pl.when(i == 2)
        def _():
            forward_weight(2, 2)

        @pl.when(i == 3)
        def _():
            out_x(slab).wait_send()
            out_x(core * 2 + 1 - xx).wait_recv()
            out_core(core).start()

        @pl.when(i == 4)
        def _():
            forward_weight(3, 0)
            send_cot(2)
            pass_mixed(0)
            pass_mixed(1)
            out_core(core).wait_send()
            out_core(1 - core).wait_recv()

        @pl.when(i == 6)
        def _():
            forward_weight(3, 1)
            send_cot(3)

        @pl.when(i >= 5)
        def _():
            @pl.loop(2 * (i - 5), i - 3)
            def _(t):
                second_norm(t)

        @pl.when(i == 5)
        def _():
            pass_mixed(2)

    finish_weight(2)
    last[1].start()
    last[2].start()

    @pl.loop(0, CHUNKS)
    def _(t):
        expand(t)

        @pl.when(t == 0)
        def _():
            send_cot(4)

        @pl.when(t == 1)
        def _():
            send_cot(5)
            send_cot(6)

        @pl.when(t == 3)
        def _():
            forward_weight(3, 2)

        @pl.when((t >= 2) & (t <= 5))
        def _():
            second_norm(t + 1)

        @pl.when((t >= 1) & (t <= 4))
        def _():
            pass_mixed(t + 2)

        @pl.when(t >= 3)
        def _():
            pass_on_cot(t - 3)

    for n in range(4, CHUNKS):
        pass_on_cot(n)

    @pl.loop(0, CHUNKS)
    def _(i):
        mixed_x(i, slab).wait_send()
        mixed_core(i, 0, slab).wait_send()
        mixed_core(i, 1, core * 2 + 1 - xx).wait_send()
        for s in range(2):
            cot_x(i, s, c).wait_send()
            cot_core(i, s, c).wait_send()
            cot_core(i, s, c_core).wait_recv()
        cot_pass(i, c_x).wait_send()
        cot_pass(i, c_far).wait_recv()
        for copy in kept(i, 3):
            copy.start()

    @pl.loop(0, CHUNKS)
    def _(i):
        for s in range(2):
            tok_x(i, s, c).wait_send()
            tok_core(i, s, c).wait_send()
        tok_pass(i, c_x).wait_send()

    finish_weight(3)
    last[3].start()

    @pl.loop(0, CHUNKS)
    def _(i):
        for stage in range(5):
            for copy in kept(i, stage):
                copy.wait()

    for t in (CHUNKS - 2, CHUNKS - 1):
        keep_hid(t).wait()

    for copy in last:
        copy.wait()


def forward_call(*arrays):
    tok, we_s = arrays[0], arrays[-2]
    pairs, width = tok.shape[0], tok.shape[1] // 2
    chunk = 2 * pairs // CHUNKS
    full = 4 * width
    hidden = we_s.shape[1]
    n = CHUNKS

    def sd(shape, dtype):
        return jax.ShapeDtypeStruct(shape, dtype)

    outs = [
        sd((n, chunk, full), BF16),
        sd((n, chunk, full), BF16),
        sd((n, chunk, width), BF16),
        sd((n, width, chunk), BF16),
        sd((n, chunk, width), BF16),
        sd((n, width, chunk), BF16),
        sd((n, chunk, width), BF16),
        sd((n, chunk, width), F32),
        sd((n, 8, chunk), F32),
        sd((n, chunk, width), F32),
        sd((n, chunk, full), BF16),
        sd((n, chunk, 128), F32),
        sd((n, chunk, full), BF16),
        sd((n, chunk, hidden), BF16),
        sd((n, chunk, hidden), BF16),
        sd((3, full, width), BF16),
        sd((width, full), BF16),
        sd((full, hidden), BF16),
        sd((hidden, full), BF16),
        sd((8, full), F32),
        sd((n, chunk, full), BF16),
        sd((n, chunk, 128), F32),
    ]
    vm = pltpu.VMEM
    dma = pltpu.SemaphoreType.DMA
    scratch = [
        vm((n, chunk, full), BF16), vm((n, chunk, full), BF16), vm((n, chunk, full), BF16),
        vm((n, chunk, width), BF16), vm((n, width, chunk), BF16),
        vm((n, chunk, width), BF16), vm((n, width, chunk), BF16),
        vm((n, chunk, width), BF16), vm((n, width, chunk), BF16),
        vm((n, chunk, full), BF16), vm((n, chunk, width), F32), vm((n, 8, chunk), F32),
        vm((2, chunk, full), F32), vm((n, chunk, full), BF16), vm((n, chunk, 128), F32),
        vm((n, chunk, full), BF16), vm((n, chunk, hidden), BF16), vm((n, chunk, hidden), BF16),
        vm((3, full, width), BF16), vm((full, full), BF16), vm((full, hidden), BF16), vm((hidden, full), BF16),
        vm((8, full), F32), vm((n, chunk, 128), F32),
        vm((2, n, chunk, chunk), F32),
        dma((18, n)), dma((4,)), dma((n, 2)), dma((n, 2)), dma((4, 2, 3)), dma((4, 2, 3)), dma((4, 4)), dma((4, 4)), dma((3,)), dma((3,)),
        dma((n, 2)), dma((n, 2)), dma((n, 2)), dma((n, 2)), dma((n,)), dma((n,)),
        dma((n, 2)), dma((n, 2)), dma((n, 2)), dma((n, 2)), dma((n,)), dma((n,)),
        dma((1,)), dma((1,)), dma((1,)), dma((1,)), dma((n,)), dma((n,)), dma((n, 2)), dma((n, 2)),
    ]
    return pl.pallas_call(
        forward_kernel,
        out_shape=outs,
        in_specs=[pl.BlockSpec(memory_space=pl.ANY if n in (0, 1, 10, 11, 12, 13) else pltpu.VMEM) for n in range(len(arrays))],
        out_specs=[pl.BlockSpec(memory_space=pl.ANY)] * len(outs),
        scratch_shapes=scratch,
        compiler_params=pltpu.CompilerParams(
            collective_id=0, has_side_effects=True, vmem_limit_bytes=63 << 20
        ),
    )(*arrays)


GRAD_KINDS = ("three", "cols", "rows", "cols")


def backward_kernel(
    tok_h, cot_h, q_h, qt_h, k_h, kt_h, v_h, mixf_h, lse_h, hid_h, unit_h, inv_h,
    normed_h, act_h, slope_h, win_h, wo_h, we_h, wr_h, vec_h, one_h, stat_h,
    out_o, tg_o, sums_o, gin_o, gout_o, gexp_o, gred_o,
    cot, q, qt, k, kt, v, mixf, lse, hid, unit, inv, normed, act, slope, win, wo, we, wr, vecs,
    grad, flat, dk, dv, tg, out, sb_g, sb_o, rb_g, xr_g, rb_o, xr_o, xr_1, st, st_in,
    col_sums, packet, packets,
    ys_in, ys_out, ys_exp, ys_red, oh_in, oh_out, oh_exp, oh_red,
    yr_in, yr_out, yr_exp, yr_red, zr_in, zr_out, zr_exp, zr_red,
    gin, gout, gexp, gred,
    load_sem, chunk_sem, store_sem, hid_sem, gy_send, gy_recv, gz_send, gz_recv,
    h1g_send, h1g_recv, h2g_send, h2g_recv, h3g_send, h3g_recv,
    h1o_send, h1o_recv, h2o_send, h2o_recv, h1t_send, h1t_recv, h2t_send, h2t_recv,
    st_send, st_recv, pk_send, pk_recv,
):
    r, c = lax.axis_index("row"), lax.axis_index("col")
    z, y = r // 2, r % 2
    xx, core = c // 2, c % 2
    c_x, c_core, c_far = (c + 2) % 4, c + 1 - 2 * core, (c + 2) % 4 + 1 - 2 * core
    r_y = r + 1 - 2 * y
    tok, one, stat = act, normed, inv
    chunk = q.shape[0] // CHUNKS
    half = chunk // 2
    width = q.shape[1]
    full = cot.shape[1]
    scale = LOG2E * HEAD_DIM ** (-0.5)
    own = aligned(c, width)
    others = [(r + step) % 8 for step in range(1, 8)]

    barrier = pltpu.get_barrier_semaphore()
    for col in (c_x, c_core, c_far):
        pl.semaphore_signal(barrier, inc=1, device_id=(r, col), device_id_type=MESH)
    for row in others:
        pl.semaphore_signal(barrier, inc=1, device_id=(row, c), device_id_type=MESH)

    def rows_of(i):
        return pl.ds(pl.multiple_of(i * chunk, chunk), chunk)

    loads = {}
    order = (
        ("wr", wr_h, wr), ("we", we_h, we),
        ("vec", vec_h, vecs), ("unit", unit_h, unit), ("inv", inv_h, inv), ("wo", wo_h, wo),
        ("normed", normed_h, normed), ("mixf", mixf_h, mixf), ("lse", lse_h, lse), ("qt", qt_h, qt), ("q", q_h, q),
        ("k", k_h, k), ("v", v_h, v), ("kt", kt_h, kt), ("stat", stat_h, stat),
        ("tok", tok_h, tok), ("one", one_h, one),
    )
    for n, (name, src, dst) in enumerate(order):
        loads[name] = pltpu.make_async_copy(src, dst, load_sem.at[n])
    for n in range(3):
        loads["win" + str(n)] = pltpu.make_async_copy(
            win_h.at[n], win.at[:, pl.ds(n * width, width)], load_sem.at[len(order) + n]
        )
    def chunk_loads(i):
        rows = rows_of(i)
        return [
            pltpu.make_async_copy(a.at[rows, :], b.at[rows, :], chunk_sem.at[n, i])
            for n, (a, b) in enumerate(((cot_h, cot), (slope_h, slope), (act_h, act)))
        ]

    loads["wr"].start()
    loads["we"].start()
    for i in range(CHUNKS):
        for copy in chunk_loads(i):
            copy.start()
    late = ("wr", "we", "tok", "one", "stat", "win0", "win1", "win2")
    for name in loads:
        if name not in late:
            loads[name].start()
    dk[...] = jnp.zeros_like(dk)
    dv[...] = jnp.zeros_like(dv)
    col_sums[...] = jnp.zeros_like(col_sums)
    pl.semaphore_wait(barrier, 10)

    def h1(sb, rb, send, recv, i):
        return remote(sb.at[i % 2, 1 - core], rb.at[i], send.at[i], recv.at[i], r, c_core)

    def fill(sb, i, partial):
        for x in range(2):
            for side in range(2):
                block = x * 2 + side
                sb[i % 2, side, x] = partial[:, block * width : (block + 1) * width].astype(BF16)

    def merge(sb, rb, i):
        for x in range(2):
            rb[i, x] = (sb[i % 2, core, x].astype(F32) + rb[i, x].astype(F32)).astype(BF16)

    def h1g(i):
        return h1(sb_g, rb_g, h1g_send, h1g_recv, i)

    def h1o(i):
        return h1(sb_o, rb_o, h1o_send, h1o_recv, i)

    def h1t(i):
        return h1(sb_g, rb_g, h1t_send, h1t_recv, i)

    def h2g(i):
        return remote(rb_g.at[i], xr_g.at[i], h2g_send.at[i], h2g_recv.at[i], r, c_x)

    def h2o(i):
        return remote(rb_o.at[i, 1 - xx], xr_o.at[i], h2o_send.at[i], h2o_recv.at[i], r, c_x)

    def h2t(i):
        return remote(rb_g.at[i, 1 - xx], xr_1.at[i], h2t_send.at[i], h2t_recv.at[i], r, c_x)

    def h3g(i, x, side):
        block = grad.at[i % 4, :, aligned(x * 2 + side, width)]
        return remote(block, block, h3g_send.at[i, x], h3g_recv.at[i, x], r, c_core)

    def spread_grad(i):
        h2g(i).wait()
        if isinstance(i, int):
            h2g(i + 4).start()
        else:
            @pl.when(i + 4 < CHUNKS)
            def _():
                h2g(i + 4).start()

        for x in range(2):
            grad[i % 4, :, aligned(x * 2 + core, width)] = rb_g[i, x].astype(F32) + xr_g[i, x].astype(F32)
        for x in range(2):
            h3g(i, x, core).start()

    def column_sums(values):
        ones = jnp.ones((8, values.shape[0]), BF16)
        return jnp.dot(ones, values, preferred_element_type=F32)[0:1, :]

    ys = (ys_in, ys_out, ys_exp, ys_red)
    oh = (oh_in, oh_out, oh_exp, oh_red)
    yr = (yr_in, yr_out, yr_exp, yr_red)
    zr = (zr_in, zr_out, zr_exp, zr_red)

    def gy(w, s):
        return remote(ys[w].at[s], yr[w].at[s], gy_send.at[w, s], gy_recv.at[w, s], r_y, c)

    def gz(w, s):
        target = ((z + 1 + s) % 4) * 2 + y
        return remote(oh[w].at[s], zr[w].at[s], gz_send.at[w, s], gz_recv.at[w, s], target, c)

    def grad_block(w, s, left, right):
        zt = (z + 1 + s) % 4
        lanes = aligned(zt, 256)
        if GRAD_KINDS[w] == "rows":
            block = lax.dot_general(left[:, lanes], right, TN_DIMS, preferred_element_type=F32).astype(BF16)
            low, high = block[0:128, :], block[128:256, :]
        else:
            block = lax.dot_general(left, right[:, lanes], TN_DIMS, preferred_element_type=F32).astype(BF16)
            low, high = block[:, 0:128], block[:, 128:256]

        @pl.when(y == 0)
        def _():
            oh[w][s] = low
            ys[w][s] = high

        @pl.when(y == 1)
        def _():
            oh[w][s] = high
            ys[w][s] = low

    def pass_on(w, s):
        gy(w, s).wait()
        oh[w][s] = (oh[w][s].astype(F32) + yr[w][s].astype(F32)).astype(BF16)
        gz(w, s).start()

    def finish_grad(w, dst):
        gy(w, 3).wait()
        total = oh[w][3].astype(F32) + yr[w][3].astype(F32)
        for s in range(3):
            gz(w, s).wait()
            total = total + zr[w][s].astype(F32)
        dst[...] = total

    loads["wr"].wait()
    loads["we"].wait()

    @pl.loop(0, CHUNKS + 1)
    def _(i):
        @pl.when(i < CHUNKS)
        def _():
            @pl.when(i < 3)
            def _():
                for copy in chunk_loads(i):
                    copy.wait()

            @pl.when(i == 3)
            def _():
                for n in range(3, CHUNKS):
                    for copy in chunk_loads(n):
                        copy.wait()

            rows = rows_of(i)
            for n in range(slope.shape[1] // 256):
                lanes = slice(n * 256, (n + 1) * 256)
                grad_act = lax.dot_general(cot[rows, :], wr[lanes, :], NT_DIMS, preferred_element_type=F32)
                low = (slope[rows, lanes].astype(F32) * grad_act).astype(BF16)
                slope[rows, lanes] = low
            fill(sb_g, i, lax.dot_general(slope[rows, :], we[...], NT_DIMS, preferred_element_type=F32))
            h1g(i).start()

        @pl.when(i >= 1)
        def _():
            h1o(i - 1).wait()
            merge(sb_o, rb_o, i - 1)
            h1g(i - 1).wait()
            merge(sb_g, rb_g, i - 1)

        for at, n in ((1, 0), (2, 1), (4, 2), (6, 3)):
            @pl.when(i == at)
            def _():
                h2g(n).start()

        @pl.when(i == 3)
        def _():
            grad_block(3, 0, act[...], cot)
            gy(3, 0).start()

        @pl.when(i == 5)
        def _():
            grad_block(3, 1, act[...], cot)
            gy(3, 1).start()

        @pl.when(i < CHUNKS)
        def _():
            fill(sb_o, i, jnp.dot(act[rows_of(i), :], wr[...], preferred_element_type=F32))
            h1o(i).start()

    for n in range(4):
        packet[8 + n : 9 + n, :] = column_sums(slope[:, n * width : (n + 1) * width])
    loads["normed"].wait()
    spread_grad(0)
    pass_on(3, 0)
    grad_block(3, 2, act[...], cot)
    gy(3, 2).start()
    grad_block(3, 3, act[...], cot)
    spread_grad(1)
    grad_block(2, 0, normed, slope[...])
    pass_on(3, 1)
    gy(2, 0).start()
    for s in range(1, 4):
        grad_block(2, s, normed, slope[...])
    for name in late[2:]:
        if name != "stat":
            loads[name].start()
    for name in ("unit", "inv", "vec", "wo", "mixf", "lse", "qt", "q", "k", "v", "kt"):
        loads[name].wait()

    def hid_load(i):
        return pltpu.make_async_copy(hid_h.at[rows_of(i), :], hid, hid_sem.at[i])

    def out_store(i, s):
        return pltpu.make_async_copy(
            out.at[i % 2, s], out_o.at[pl.ds(pl.multiple_of(i * half, half), half), pl.ds(s * width, width)],
            store_sem.at[0, i, s],
        )

    def tg_store(i, s):
        return pltpu.make_async_copy(
            tg.at[i, s], tg_o.at[pl.ds(pl.multiple_of(i * half, half), half), pl.ds(s * width, width)],
            store_sem.at[1, i, s],
        )

    def attend_back(i):
        rows = rows_of(i)
        go = lax.dot_general(unit[rows, :], wo[...], NT_DIMS, preferred_element_type=F32).astype(BF16)
        inner = (go.astype(F32) * mixf[rows, :]).T
        go_t = go.T
        row_ids = lax.broadcasted_iota(jnp.int32, (128, chunk), 0)
        lane_ids = lax.broadcasted_iota(jnp.int32, (chunk, 128), 1)
        heads = width // HEAD_DIM
        queries, grads, query_rows, grad_rows, deltas, logs = [], [], [], [], [], []
        for h in range(heads):
            lanes = slice(h // 2 * 128, h // 2 * 128 + 128)
            pick = row_ids // HEAD_DIM == h % 2
            value = qt[i, lanes, :]
            queries.append(jnp.where(pick, value, jnp.zeros_like(value)))
            value = go_t[lanes, :]
            grads.append(jnp.where(pick, value, jnp.zeros_like(value)))
            pick = lane_ids // HEAD_DIM == h % 2
            value = q[rows, lanes]
            query_rows.append(jnp.where(pick, value, jnp.zeros_like(value)))
            value = go[:, lanes]
            grad_rows.append(jnp.where(pick, value, jnp.zeros_like(value)))
            deltas.append(jnp.sum(inner[h * HEAD_DIM : (h + 1) * HEAD_DIM, :], axis=0, keepdims=True))
            logs.append(lse[i, h : h + 1, :])

        parts = [jnp.zeros((HEAD_DIM, chunk), F32)] * heads
        for j in range(CHUNKS):
            keys = pl.ds(j * chunk, chunk)
            probs, grad_scores = [], []
            for h in range(heads):
                lanes = slice(h // 2 * 128, h // 2 * 128 + 128)
                block = jnp.dot(k[keys, lanes], queries[h], preferred_element_type=F32)
                grad_probs = jnp.dot(v[keys, lanes], grads[h], preferred_element_type=F32)
                prob = jnp.exp2(block * scale - logs[h])
                probs.append(prob.astype(BF16))
                grad_scores.append((prob * (grad_probs - deltas[h])).astype(BF16))
            for pair in range(heads // 2):
                lanes = slice(pair * 128, pair * 128 + 128)
                h = 2 * pair
                dv[keys, lanes] += jnp.dot(
                    probs[h], grad_rows[h], preferred_element_type=F32
                ) + jnp.dot(probs[h + 1], grad_rows[h + 1], preferred_element_type=F32)
                dk[keys, lanes] += jnp.dot(
                    grad_scores[h], query_rows[h], preferred_element_type=F32
                ) + jnp.dot(grad_scores[h + 1], query_rows[h + 1], preferred_element_type=F32)
            for h in range(heads):
                rows_h = slice(h * HEAD_DIM, (h + 1) * HEAD_DIM)
                parts[h] = parts[h] + jnp.dot(kt[j, rows_h, :], grad_scores[h], preferred_element_type=F32)
        flat[rows, 0:width] = (jnp.concatenate(parts, axis=0).T * HEAD_DIM ** (-0.5)).astype(BF16)

    def finish_out(i):
        @pl.when(i >= 2)
        def _():
            for s in range(2):
                out_store(i - 2, s).wait()

        hid_load(i).start()
        h2o(i).wait()
        hid_load(i).wait()
        total = rb_o[i, xx].astype(F32) + xr_o[i].astype(F32)
        value = (hid[...] + total + vecs[5:6, own]).astype(BF16)
        for s in range(2):
            out[i % 2, s] = value[s * half : (s + 1) * half, :]
        for s in range(2):
            out_store(i, s).start()

    def second_norm_back(i):
        for x in range(2):
            h3g(i, x, core).wait_send()
            h3g(i, x, 1 - core).wait_recv()
        step_rows = chunk // 7
        for part in range(7):
            rows = pl.ds(pl.multiple_of(i * chunk + part * step_rows, step_rows), step_rows)
            span = slice(part * step_rows, (part + 1) * step_rows)
            incoming = grad[i % 4, span, :]
            units = unit[rows, :].astype(F32)
            scaled = incoming * vecs[3:4, :]
            plain = jnp.mean(scaled, axis=1, keepdims=True)
            cross = jnp.mean(scaled * units, axis=1, keepdims=True)
            total = cot[rows, :].astype(F32) + inv[rows, 0:1] * (scaled - plain - units * cross)
            mine = grad[i % 4, span, own]
            col_sums[1:2, 0:width] += jnp.sum(mine * unit[rows, own].astype(F32), axis=0, keepdims=True)
            col_sums[2:3, 0:width] += jnp.sum(mine, axis=0, keepdims=True)
            unit[rows, :] = total.astype(BF16)
            grad[i % 4, span, :] = total
        for s in range(2):
            tg[i, s] = grad[i % 4, s * half : (s + 1) * half, own]

    @pl.loop(-1, CHUNKS)
    def _(i):
        @pl.when(i + 1 < CHUNKS)
        def _():
            second_norm_back(i + 1)

        @pl.when((i >= 0) & (i + 2 < CHUNKS))
        def _():
            spread_grad(i + 2)

        @pl.when(i == CHUNKS - 2)
        def _():
            for s in range(4):
                grad_block(1, s, mixf[...].astype(BF16), unit)
                gy(1, s).start()

        @pl.when(i == CHUNKS - 1)
        def _():
            loads["stat"].start()

        @pl.when(i >= 0)
        def _():
            attend_back(i)

        @pl.when(i == -1)
        def _():
            pass_on(3, 2)
            gy(2, 1).start()

        @pl.when(i == 0)
        def _():
            pass_on(2, 0)
            gy(2, 2).start()

        @pl.when(i == 1)
        def _():
            pass_on(2, 1)
            gy(3, 3).start()

        @pl.when(i == 2)
        def _():
            pass_on(2, 2)
            gy(2, 3).start()

        @pl.when(i == CHUNKS - 2)
        def _():
            finish_grad(3, gred)

        @pl.when(i == CHUNKS - 1)
        def _():
            for s in range(3):
                pass_on(1, s)

        @pl.when(i >= 3)
        def _():
            @pl.loop(2 * (i - 3), jnp.minimum(2 * (i - 3) + 2, CHUNKS))
            def _(n):
                h2o(n).start()

        @pl.when(i >= 5)
        def _():
            @pl.loop(2 * (i - 5), 2 * (i - 5) + 2)
            def _(n):
                finish_out(n)

    for i in range(CHUNKS):
        rows = pl.ds(i * chunk, chunk)
        flat[rows, width : 2 * width] = (dk[rows, :] * HEAD_DIM ** (-0.5)).astype(BF16)
        flat[rows, 2 * width : 3 * width] = dv[rows, :].astype(BF16)
    for name in late[2:]:
        loads[name].wait()

    def inward_block(s):
        zt = (z + 1 + s) % 4
        left = one[:, aligned(zt, 256)]
        block = lax.dot_general(left, flat[...], TN_DIMS, preferred_element_type=F32).astype(BF16)
        for n in range(3):
            lanes = slice(n * width, (n + 1) * width)

            @pl.when(y == 0)
            def _():
                oh_in[s, n] = block[0:128, lanes]
                ys_in[s, n] = block[128:256, lanes]

            @pl.when(y == 1)
            def _():
                oh_in[s, n] = block[128:256, lanes]
                ys_in[s, n] = block[0:128, lanes]

        gy(0, s).start()

    def stat_copy(i, slot, target):
        return remote(st.at[i], st_in.at[i, slot], st_send.at[i, slot], st_recv.at[i, slot], r, target)

    lane_ids = lax.broadcasted_iota(jnp.int32, (chunk, 128), 1)
    gain = vecs[0:1, :]

    @pl.loop(0, CHUNKS + 3)
    def _(i):
        @pl.when(i < CHUNKS)
        def _():
            rows = rows_of(i)
            partial = lax.dot_general(flat[rows, :], win[...], NT_DIMS, preferred_element_type=F32)
            fill(sb_g, i, partial)
            h1t(i).start()
            units = (tok[rows, :].astype(F32) - stat[rows, 0:1]) * stat[rows, 64:65]
            scaled = partial * gain
            plain = jnp.sum(scaled, axis=1, keepdims=True)
            cross = jnp.sum(scaled * units, axis=1, keepdims=True)
            both = jnp.where(lane_ids == 0, plain, jnp.where(lane_ids == 1, cross, 0.0))
            st[i] = both.T[0:8, :]
            for slot, target in enumerate((c_x, c_core, c_far)):
                stat_copy(i, slot, target).start()

        for at, s in ((0, 1), (2, 0), (3, 2), (4, 3)):
            @pl.when(i == at)
            def _():
                inward_block(s)

        @pl.when((i >= 4) & (i <= 6))
        def _():
            finish_out(i)

        @pl.when((i >= 1) & (i <= CHUNKS))
        def _():
            h1t(i - 1).wait()
            merge(sb_g, rb_g, i - 1)
            h2t(i - 1).start()

        for at, s in ((3, 1), (5, 0), (6, 2)):
            @pl.when(i == at)
            def _():
                pass_on(0, s)

        @pl.when(i == 5)
        def _():
            packet[7:8, :] = column_sums(cot[:, own])
            packet[4:5, :] = column_sums(unit[:, own])

        @pl.when(i == 6)
        def _():
            packet[2:3, :] = column_sums(flat[:, 0:width])
            packet[3:4, :] = column_sums(flat[:, 2 * width : 3 * width])
            finish_grad(2, gexp)

        @pl.when(i == 7)
        def _():
            finish_grad(1, gout)

        @pl.when(i >= 3)
        def _():
            t = i - 3
            rows = rows_of(t)
            h2t(t).wait()
            total = st[t]
            for slot, target in enumerate((c_x, c_core, c_far)):
                stat_copy(t, slot, target).wait()
                total = total + st_in[t, slot]
            columns = jnp.concatenate([total, jnp.zeros((120, chunk), F32)], axis=0).T
            plain = columns[:, 0:1] / full
            cross = columns[:, 1:2] / full
            incoming = rb_g[t, xx].astype(F32) + xr_1[t].astype(F32)
            inverse = stat[rows, 64:65]
            units = (tok[rows, own].astype(F32) - stat[rows, 0:1]) * inverse
            back = inverse * (incoming * vecs[0:1, own] - plain - units * cross)
            for s in range(2):
                tg[t, s] = tg[t, s] + back[s * half : (s + 1) * half, :]
            for s in range(2):
                tg_store(t, s).start()
            col_sums[6:7, 0:width] += jnp.sum(incoming * units, axis=0, keepdims=True)
            col_sums[7:8, 0:width] += jnp.sum(incoming, axis=0, keepdims=True)

    packet[0:1, :] = col_sums[6:7, 0:width]
    packet[1:2, :] = col_sums[7:8, 0:width]
    packet[5:7, :] = col_sums[1:3, 0:width]

    def packet_copy(step):
        return remote(packet, packets.at[step], pk_send.at[step], pk_recv.at[step], others[step], c)

    for step in range(7):
        packet_copy(step).start()
    finish_grad(0, gin)
    stores = [
        pltpu.make_async_copy(src, dst, store_sem.at[2, n, 0])
        for n, (src, dst) in enumerate(((gin, gin_o), (gout, gout_o), (gexp, gexp_o), (gred, gred_o)))
    ]
    for copy in stores:
        copy.start()
    total = packet[...]
    for step in range(7):
        packet_copy(step).wait()
        total = total + packets[step]
    packet[...] = total
    copy = pltpu.make_async_copy(packet, sums_o, store_sem.at[2, 4, 0])
    copy.start()
    copy.wait()
    for copy in stores:
        copy.wait()
    for i in range(CHUNKS - 2, CHUNKS):
        for s in range(2):
            out_store(i, s).wait()

    @pl.loop(0, CHUNKS)
    def _(i):
        for s in range(2):
            tg_store(i, s).wait()


def backward_call(*arrays):
    (tok, cot, q, qt, k, kt, v, mixf, lse, hid, unit, inv, normed, act, slope, win, wo, we, wr, vec, one, stat) = arrays
    rows, width = q.shape
    full, hidden = we.shape
    n, chunk = CHUNKS, rows // CHUNKS
    half = chunk // 2
    pairs = rows // 2

    def sd(shape, dtype):
        return jax.ShapeDtypeStruct(shape, dtype)

    outs = [
        sd((pairs, 2 * width), BF16), sd((pairs, 2 * width), F32), sd((16, width), F32),
        sd((3, 128, width), F32), sd((width, 128), F32), sd((128, hidden), F32), sd((hidden, 128), F32),
    ]
    vm = pltpu.VMEM
    dma = pltpu.SemaphoreType.DMA

    def shapes(lead):
        return [
            vm((lead, 3, 128, width), BF16), vm((lead, width, 128), BF16),
            vm((lead, 128, hidden), BF16), vm((lead, hidden, 128), BF16),
        ]

    def like(array):
        return vm(array.shape, array.dtype)

    scratch = [
        vm((rows, full), BF16), like(q), like(qt), like(k), like(kt), like(v), like(mixf), like(lse),
        vm((chunk, width), F32),
        like(unit), like(inv), like(normed), like(act), like(slope),
        vm((full, 3 * width), BF16), like(wo), like(we), like(wr), like(vec),
        vm((4, chunk, full), F32), vm((rows, 3 * width), BF16), vm((rows, width), F32), vm((rows, width), F32),
        vm((n, 2, half, width), F32), vm((2, 2, half, width), BF16),
        vm((2, 2, 2, chunk, width), BF16), vm((2, 2, 2, chunk, width), BF16),
        vm((n, 2, chunk, width), BF16), vm((n, 2, chunk, width), BF16),
        vm((n, 2, chunk, width), BF16), vm((n, chunk, width), BF16), vm((n, chunk, width), BF16),
        vm((n, 8, chunk), F32), vm((n, 3, 8, chunk), F32),
        vm((8, full), F32), vm((16, width), F32), vm((7, 16, width), F32),
        *shapes(4), *shapes(4), *shapes(4), *shapes(3),
        vm((3, 128, width), F32), vm((width, 128), F32), vm((128, hidden), F32), vm((hidden, 128), F32),
        dma((23,)), dma((3, n)), dma((3, n, 2)), dma((n,)), dma((4, 4)), dma((4, 4)), dma((4, 3)), dma((4, 3)),
        dma((n,)), dma((n,)), dma((n,)), dma((n,)), dma((n, 2)), dma((n, 2)),
        dma((n,)), dma((n,)), dma((n,)), dma((n,)), dma((n,)), dma((n,)), dma((n,)), dma((n,)),
        dma((n, 3)), dma((n, 3)), dma((7,)), dma((7,)),
    ]
    return pl.pallas_call(
        backward_kernel,
        out_shape=outs,
        in_specs=[pl.BlockSpec(memory_space=pl.ANY)] * len(arrays),
        out_specs=[pl.BlockSpec(memory_space=pl.ANY)] * len(outs),
        scratch_shapes=scratch,
        compiler_params=pltpu.CompilerParams(
            collective_id=1, has_side_effects=True, vmem_limit_bytes=63 << 20
        ),
    )(*arrays)


def finish_kernel(out_i, tg_i, sums_i, gin_i, gout_i, gexp_i, gred_i, *refs):
    outs, vector_o, buffers = refs[:6], refs[6:14], refs[14:20]
    load_sem, store_sem = refs[20:]
    ins = (out_i, tg_i, gin_i, gout_i, gexp_i, gred_i)
    loads = [pltpu.make_async_copy(a, b, load_sem.at[n]) for n, (a, b) in enumerate(zip(ins, buffers))]
    stores = [pltpu.make_async_copy(a, b, store_sem.at[n]) for n, (a, b) in enumerate(zip(buffers, outs))]
    order = (0, 2, 3, 4, 5, 1)
    for n in order:
        loads[n].start()
    first_gain, first_shift, attn, b_out, g_two, s_two, b_red, b_exp = vector_o
    first_gain[...] = sums_i[0:1, :]
    first_shift[...] = sums_i[1:2, :]
    attn[...] = sums_i[2:4, :]
    b_out[...] = sums_i[4:5, :]
    g_two[...] = sums_i[5:6, :]
    s_two[...] = sums_i[6:7, :]
    b_red[...] = sums_i[7:8, :]
    for n in range(4):
        width = sums_i.shape[1]
        b_exp[:, n * width : (n + 1) * width] = sums_i[8 + n : 9 + n, :]
    for n in order:
        loads[n].wait()
        stores[n].start()
    for n in order:
        stores[n].wait()


def finish_call(out, tg, sums, gin, gout, gexp, gred):
    width = sums.shape[1]
    big = [jax.ShapeDtypeStruct(a.shape, a.dtype) for a in (out, tg, gin, gout, gexp, gred)]
    small = [jax.ShapeDtypeStruct((n, m), F32) for n, m in ((1, width),) * 2 + ((2, width),) + ((1, width),) * 4 + ((1, 4 * width),)]
    hbm, vm = pl.BlockSpec(memory_space=pl.ANY), pl.BlockSpec(memory_space=pltpu.VMEM)
    return pl.pallas_call(
        finish_kernel,
        out_shape=big + small,
        in_specs=[hbm, hbm, vm, hbm, hbm, hbm, hbm],
        out_specs=[hbm] * 6 + [vm] * 8,
        scratch_shapes=[pltpu.VMEM(a.shape, a.dtype) for a in big] + [pltpu.SemaphoreType.DMA((6,))] * 2,
    )(out, tg, sums, gin, gout, gexp, gred)


CONTRACT_ROWS = (((0,), (0,)), ((), ()))
CONTRACT_COLS = (((1,), (1,)), ((), ()))


def norm_forward(values, gain, shift, full_width):
    row_total = lax.psum(jnp.sum(values, axis=1), "col")
    centred = values - (row_total / full_width)[:, None]
    row_square = lax.psum(jnp.sum(centred * centred, axis=1), "col")
    inverse = lax.rsqrt(row_square / full_width + EPSILON)
    unit_rows = centred * inverse[:, None]
    return (unit_rows, inverse, unit_rows * gain + shift)


def norm_backward(incoming, unit_rows, inverse, gain, full_width):
    scaled = incoming * gain
    plain_sum, cross_sum = lax.psum(
        (jnp.sum(scaled, axis=1), jnp.sum(scaled * unit_rows, axis=1)), "col"
    )
    result = inverse[:, None] * (
        scaled - (plain_sum / full_width)[:, None] - unit_rows * (cross_sum / full_width)[:, None]
    )
    return (result, jnp.sum(incoming * unit_rows, axis=0), jnp.sum(incoming, axis=0))


def spread_features(values):
    return lax.all_gather(values, "col", axis=1, tiled=True)


def sum_partials(values):
    return lax.psum_scatter(values, "col", scatter_dimension=1, tiled=True)


def spread_grads(values):
    return lax.all_gather(values, "col", axis=1, tiled=True)


def sum_grad_partials(values):
    return lax.psum_scatter(values, "col", scatter_dimension=1, tiled=True)


def fetch_weights(inward_weight, output_weight, expand_weight, reduce_weight):
    return (
        lax.all_gather(inward_weight, "row", axis=0, tiled=True),
        lax.all_gather(output_weight, "row", axis=1, tiled=True),
        lax.all_gather(expand_weight, "row", axis=0, tiled=True),
        lax.all_gather(reduce_weight, "row", axis=1, tiled=True),
    )


def attend_clip(queries, key_rows, value_rows, score_scale):
    seq_len = queries.shape[0]
    blocks = queries.reshape((2, seq_len // 2) + queries.shape[1:])

    def one_block(query_part):
        scores = (
            jnp.einsum("qhd,khd->hqk", query_part, key_rows, preferred_element_type=jnp.float32)
            * score_scale
        )
        row_peak = jnp.max(scores, axis=-1, keepdims=True)
        exponent = jnp.exp(scores - row_peak)
        row_sum = jnp.sum(exponent, axis=-1, keepdims=True)
        prob_low = (exponent / row_sum).astype(jnp.bfloat16)
        mixed_rows = jnp.einsum(
            "hqk,khd->qhd", prob_low, value_rows, preferred_element_type=jnp.float32
        )
        return (mixed_rows, (row_peak + jnp.log(row_sum))[..., 0])

    mixed_rows, logsum = lax.map(one_block, blocks)
    return (mixed_rows.reshape(queries.shape), logsum)


def attend_clip_back(queries, key_rows, value_rows, logsum, grad_out, score_scale):
    seq_len = queries.shape[0]
    block_shape = (2, seq_len // 2) + queries.shape[1:]

    def step_block(carry, pieces):
        key_acc, value_acc = carry
        query_part, grad_part, log_part = pieces
        scores = (
            jnp.einsum("qhd,khd->hqk", query_part, key_rows, preferred_element_type=jnp.float32)
            * score_scale
        )
        probs = jnp.exp(scores - log_part[..., None])
        grad_probs = jnp.einsum(
            "qhd,khd->hqk", grad_part, value_rows, preferred_element_type=jnp.float32
        )
        inner_sum = jnp.sum(probs * grad_probs, axis=-1, keepdims=True)
        grad_scores = (probs * (grad_probs - inner_sum)).astype(jnp.bfloat16)
        query_grad = (
            jnp.einsum("hqk,khd->qhd", grad_scores, key_rows, preferred_element_type=jnp.float32)
            * score_scale
        )
        key_acc = key_acc + jnp.einsum(
            "hqk,qhd->khd", grad_scores, query_part, preferred_element_type=jnp.float32
        )
        value_acc = value_acc + jnp.einsum(
            "hqk,qhd->khd",
            probs.astype(jnp.bfloat16),
            grad_part,
            preferred_element_type=jnp.float32,
        )
        return ((key_acc, value_acc), query_grad)

    zero_acc = jnp.zeros(key_rows.shape, jnp.float32)
    (key_acc, value_acc), query_grads = lax.scan(
        step_block,
        (zero_acc, zero_acc),
        (queries.reshape(block_shape), grad_out.reshape(block_shape), logsum),
    )
    return (query_grads.reshape(queries.shape), key_acc * score_scale, value_acc)


def forward_pass(
    tokens,
    first_gain,
    first_shift,
    attention_bias,
    output_bias,
    second_gain,
    second_shift,
    expand_bias,
    reduce_bias,
    gathered,
):
    inward_all, output_rows, expand_all, reduce_rows = gathered
    full_width = inward_all.shape[0]
    local_width = inward_all.shape[2]
    row_count = tokens.shape[0]
    clip_shape = (row_count // SEQ, SEQ, local_width // HEAD_DIM, HEAD_DIM)
    score_scale = HEAD_DIM ** (-0.5)
    source = tokens.astype(jnp.float32)
    unit_one, inverse_one, normed_one = norm_forward(source, first_gain, first_shift, full_width)
    normed_all = spread_features(normed_one.astype(jnp.bfloat16))
    projected = jnp.dot(
        normed_all,
        inward_all.reshape(full_width, 3 * local_width),
        preferred_element_type=jnp.float32,
    )
    projected = projected.reshape(row_count, 3, local_width)
    queries = (projected[:, 0] + attention_bias[0]).astype(jnp.bfloat16)
    key_rows = projected[:, 1].astype(jnp.bfloat16)
    value_rows = (projected[:, 2] + attention_bias[1]).astype(jnp.bfloat16)
    mixed_rows, logsum = lax.map(
        lambda clip_parts: attend_clip(clip_parts[0], clip_parts[1], clip_parts[2], score_scale),
        (queries.reshape(clip_shape), key_rows.reshape(clip_shape), value_rows.reshape(clip_shape)),
    )
    mixed_low = mixed_rows.reshape(row_count, local_width).astype(jnp.bfloat16)
    hidden_state = (
        source
        + sum_partials(jnp.dot(mixed_low, output_rows, preferred_element_type=jnp.float32))
        + output_bias
    )
    unit_two, inverse_two, normed_two = norm_forward(
        hidden_state, second_gain, second_shift, full_width
    )
    normed_all_two = spread_features(normed_two.astype(jnp.bfloat16))
    expanded = jnp.dot(normed_all_two, expand_all, preferred_element_type=jnp.float32) + expand_bias
    activated = jax.nn.gelu(expanded, approximate=False).astype(jnp.bfloat16)
    output_value = (
        hidden_state
        + sum_partials(jnp.dot(activated, reduce_rows, preferred_element_type=jnp.float32))
        + reduce_bias
    )
    saved_state = (
        unit_one,
        inverse_one,
        normed_all,
        queries,
        key_rows,
        value_rows,
        logsum,
        mixed_low,
        unit_two,
        inverse_two,
        normed_all_two,
        expanded,
        activated,
    )
    return (output_value, saved_state)


def plain_device(
    tokens,
    first_gain,
    first_shift,
    inward_weight,
    attention_bias,
    output_weight,
    output_bias,
    second_gain,
    second_shift,
    expand_weight,
    expand_bias,
    reduce_weight,
    reduce_bias,
    cotangent,
):
    packed_width = tokens.shape[1]
    tokens = tokens.reshape(-1, packed_width // 2)
    cotangent = cotangent.reshape(-1, packed_width // 2)
    gathered = fetch_weights(inward_weight, output_weight, expand_weight, reduce_weight)
    output_value, saved_state = forward_pass(
        tokens,
        first_gain,
        first_shift,
        attention_bias,
        output_bias,
        second_gain,
        second_shift,
        expand_bias,
        reduce_bias,
        gathered,
    )
    gathered = fetch_weights(inward_weight, output_weight, expand_weight, reduce_weight)
    unused_value, saved_state = forward_pass(
        tokens,
        first_gain,
        first_shift,
        attention_bias,
        output_bias,
        second_gain,
        second_shift,
        expand_bias,
        reduce_bias,
        gathered,
    )
    inward_all, output_rows, expand_all, reduce_rows = gathered
    (
        unit_one,
        inverse_one,
        normed_all,
        queries,
        key_rows,
        value_rows,
        logsum,
        mixed_low,
        unit_two,
        inverse_two,
        normed_all_two,
        expanded,
        activated,
    ) = saved_state
    full_width = inward_all.shape[0]
    local_width = inward_all.shape[2]
    row_count = tokens.shape[0]
    clip_shape = (row_count // SEQ, SEQ, local_width // HEAD_DIM, HEAD_DIM)
    score_scale = HEAD_DIM ** (-0.5)
    grad_rows = cotangent.astype(jnp.float32)
    grad_all = spread_grads(cotangent)
    grad_act = lax.dot_general(
        grad_all, reduce_rows, CONTRACT_COLS, preferred_element_type=jnp.float32
    )
    reduce_grad = lax.dot_general(
        activated, grad_all, CONTRACT_ROWS, preferred_element_type=jnp.float32
    )
    reduce_bias_grad = jnp.sum(grad_rows, axis=0)
    gelu_value, gelu_back = jax.vjp(
        lambda inner_value: jax.nn.gelu(inner_value, approximate=False), expanded
    )
    grad_expanded = gelu_back(grad_act)[0].astype(jnp.bfloat16)
    expand_grad = lax.dot_general(
        normed_all_two, grad_expanded, CONTRACT_ROWS, preferred_element_type=jnp.float32
    )
    expand_bias_grad = jnp.sum(grad_expanded.astype(jnp.float32), axis=0)
    grad_normed_two = sum_grad_partials(
        lax.dot_general(
            grad_expanded, expand_all, CONTRACT_COLS, preferred_element_type=jnp.float32
        )
    )
    back_two, second_gain_grad, second_shift_grad = norm_backward(
        grad_normed_two, unit_two, inverse_two, second_gain, full_width
    )
    grad_hidden = grad_rows + back_two
    grad_hidden_low = grad_hidden.astype(jnp.bfloat16)
    grad_hidden_all = spread_grads(grad_hidden_low)
    output_grad = lax.dot_general(
        mixed_low, grad_hidden_all, CONTRACT_ROWS, preferred_element_type=jnp.float32
    )
    output_bias_grad = jnp.sum(grad_hidden_low.astype(jnp.float32), axis=0)
    grad_mixed = lax.dot_general(
        grad_hidden_all, output_rows, CONTRACT_COLS, preferred_element_type=jnp.float32
    ).astype(jnp.bfloat16)
    query_grads, key_grads, value_grads = lax.map(
        lambda clip_parts: attend_clip_back(
            clip_parts[0], clip_parts[1], clip_parts[2], clip_parts[3], clip_parts[4], score_scale
        ),
        (
            queries.reshape(clip_shape),
            key_rows.reshape(clip_shape),
            value_rows.reshape(clip_shape),
            logsum,
            grad_mixed.reshape(clip_shape),
        ),
    )
    stacked = jnp.stack(
        [
            query_grads.reshape(row_count, local_width),
            key_grads.reshape(row_count, local_width),
            value_grads.reshape(row_count, local_width),
        ],
        axis=1,
    ).astype(jnp.bfloat16)
    attention_bias_grad = jnp.stack(
        [
            jnp.sum(stacked[:, 0].astype(jnp.float32), axis=0),
            jnp.sum(stacked[:, 2].astype(jnp.float32), axis=0),
        ]
    )
    flat_grads = stacked.reshape(row_count, 3 * local_width)
    inward_grad = lax.dot_general(
        normed_all, flat_grads, CONTRACT_ROWS, preferred_element_type=jnp.float32
    ).reshape(full_width, 3, local_width)
    grad_normed_one = sum_grad_partials(
        lax.dot_general(
            flat_grads,
            inward_all.reshape(full_width, 3 * local_width),
            CONTRACT_COLS,
            preferred_element_type=jnp.float32,
        )
    )
    back_one, first_gain_grad, first_shift_grad = norm_backward(
        grad_normed_one, unit_one, inverse_one, first_gain, full_width
    )
    tokens_grad = grad_hidden + back_one
    inward_grad, output_grad, expand_grad, reduce_grad = (
        lax.psum_scatter(
            inward_grad.astype(jnp.bfloat16), "row", scatter_dimension=0, tiled=True
        ).astype(jnp.float32),
        lax.psum_scatter(
            output_grad.astype(jnp.bfloat16), "row", scatter_dimension=1, tiled=True
        ).astype(jnp.float32),
        lax.psum_scatter(
            expand_grad.astype(jnp.bfloat16), "row", scatter_dimension=0, tiled=True
        ).astype(jnp.float32),
        lax.psum_scatter(
            reduce_grad.astype(jnp.bfloat16), "row", scatter_dimension=1, tiled=True
        ).astype(jnp.float32),
    )
    (
        first_gain_grad,
        first_shift_grad,
        attention_bias_grad,
        output_bias_grad,
        second_gain_grad,
        second_shift_grad,
        expand_bias_grad,
        reduce_bias_grad,
    ) = lax.psum(
        (
            first_gain_grad,
            first_shift_grad,
            attention_bias_grad,
            output_bias_grad,
            second_gain_grad,
            second_shift_grad,
            expand_bias_grad,
            reduce_bias_grad,
        ),
        "row",
    )
    return (
        output_value.astype(jnp.bfloat16).reshape(-1, packed_width),
        tokens_grad.reshape(-1, packed_width),
        first_gain_grad,
        first_shift_grad,
        inward_grad,
        attention_bias_grad,
        output_grad,
        output_bias_grad,
        second_gain_grad,
        second_shift_grad,
        expand_grad,
        expand_bias_grad,
        reduce_grad,
        reduce_bias_grad,
    )


def fused_device(
    tokens,
    first_gain,
    first_shift,
    inward_weight,
    attention_bias,
    output_weight,
    output_bias,
    second_gain,
    second_shift,
    expand_weight,
    expand_bias,
    reduce_weight,
    reduce_bias,
    cotangent,
):
    kept = forward_call(
        tokens,
        cotangent,
        first_gain[None],
        first_shift[None],
        output_bias[None],
        second_gain[None],
        second_shift[None],
        reduce_bias[None],
        attention_bias,
        expand_bias[None],
        inward_weight.transpose(1, 0, 2),
        output_weight,
        expand_weight,
        reduce_weight,
    )
    (tok, cot, q, qt, k, kt, v, mixf, lse, hid, unit, inv, normed, act, slope, win, wo, we, wr, vec, one, stat) = kept

    def flat(array):
        return array.reshape(-1, array.shape[-1])

    outs = backward_call(
        flat(tok), flat(cot), flat(q), qt, flat(k), kt, flat(v), flat(mixf), lse, flat(hid), flat(unit),
        flat(inv), flat(normed), flat(act), flat(slope), win, wo, we, wr, vec, flat(one), flat(stat),
    )
    outs = finish_call(*outs)
    layer_output, tokens_grad, inward_grad, output_grad, expand_grad, reduce_grad = outs[:6]
    first_gain_grad, first_shift_grad, attention_grad, out_grad, gain_grad, shift_grad, red_grad, exp_grad = outs[6:]
    return (
        layer_output,
        tokens_grad,
        first_gain_grad[0],
        first_shift_grad[0],
        inward_grad.transpose(1, 0, 2),
        attention_grad,
        output_grad,
        out_grad[0],
        gain_grad[0],
        shift_grad[0],
        expand_grad,
        exp_grad[0],
        reduce_grad,
        red_grad[0],
    )


def per_device(rows, cols, *arrays):
    tokens, inward_weight, expand_weight = arrays[0], arrays[3], arrays[9]
    fits = (
        (rows, cols) == (8, 4)
        and tokens.shape == (SEQ // 2, 512)
        and inward_weight.shape == (128, 3, 256)
        and expand_weight.shape == (128, 1024)
    )
    return fused_device(*arrays) if fits else plain_device(*arrays)


def solution(mesh):
    in_specs = (
        P("row", "col"),
        P("col"),
        P("col"),
        P("row", None, "col"),
        P(None, "col"),
        P("col", "row"),
        P("col"),
        P("col"),
        P("col"),
        P("row", "col"),
        P("col"),
        P("col", "row"),
        P("col"),
        P("row", "col"),
    )
    out_specs = (
        P("row", "col"),
        P("row", "col"),
        P("col"),
        P("col"),
        P("row", None, "col"),
        P(None, "col"),
        P("col", "row"),
        P("col"),
        P("col"),
        P("col"),
        P("row", "col"),
        P("col"),
        P("col", "row"),
        P("col"),
    )
    return jax.shard_map(
        functools.partial(per_device, mesh.shape["row"], mesh.shape["col"]),
        mesh=mesh, in_specs=in_specs, out_specs=out_specs, check_vma=False
    )
```

```python
import functools
import jax
import jax.numpy as jnp
from jax import lax
from jax.experimental import pallas as pl
from jax.experimental.pallas import tpu as pltpu
from jax.sharding import PartitionSpec as P

HEAD_DIM = 64
SEQ = 1568
EPSILON = 1e-06
CHUNKS = 7
WINDOW = 2
F32 = jnp.float32
BF16 = jnp.bfloat16
MESH = pl.DeviceIdType.MESH
LOG2E = 1.4426950408889634
NT_DIMS = (((1,), (1,)), ((), ()))
TN_DIMS = (((0,), (0,)), ((), ()))


def remote(src, dst, send, recv, row, col):
    return pltpu.make_async_remote_copy(
        src_ref=src, dst_ref=dst, send_sem=send, recv_sem=recv,
        device_id=(row, col), device_id_type=MESH,
    )


def aligned(index, size):
    return pl.ds(pl.multiple_of(index * size, size), size)


def row_norm(values):
    mean = jnp.mean(values, axis=1, keepdims=True)
    centred = values - mean
    inverse = lax.rsqrt(jnp.mean(centred * centred, axis=1, keepdims=True) + EPSILON)
    return centred * inverse, mean, inverse


def weight_blocks(ref, kind, row):
    if kind == "three":
        return ref.at[:, aligned(row, 128), :]
    if kind == "rows":
        return ref.at[aligned(row, 128), :]
    return ref.at[:, aligned(row, 128)]


WEIGHT_KINDS = ("three", "cols", "rows", "cols")


def forward_kernel(
    tok, cot, g_one, s_one, b_out, g_two, s_two, b_red, attn_bias, exp_bias, win_s, wo_s, we_s, wr_s,
    tok_o, cot_o, q_o, qt_o, k_o, kt_o, v_o, mixf_o, lse_o, hid_o, unit_o, inv_o,
    norm_o, act_o, slope_o, win_o, wo_o, we_o, wr_o, vec_o, one_o, stat_o,
    tok_all, cot_all, norm_one, q, qt, k, kt, v, vt, mixed, mixf, lse, hid, unit, inv, norm_two, act, slope,
    win, wo, we, wr, vecs, stat, scores,
    local_sem, shard_sem, tok_sem, cot_sem, wz_send, wz_recv, wy_send, wy_recv, vec_send, vec_recv,
    tx_send, tx_recv, tc_send, tc_recv, tp_send, tp_recv, cx_send, cx_recv, cc_send, cc_recv, cp_send, cp_recv,
    wx_send, wx_recv, wc_send, wc_recv, mx_send, mx_recv, mc_send, mc_recv,
):
    r, c = lax.axis_index("row"), lax.axis_index("col")
    z, y = r // 2, r % 2
    xx, core = c // 2, c % 2
    c_x, c_core, c_far = (c + 2) % 4, c + 1 - 2 * core, (c + 2) % 4 + 1 - 2 * core
    r_y = r + 1 - 2 * y
    half = tok.shape[0] // CHUNKS
    chunk = 2 * half
    width = g_one.shape[1]
    scale = LOG2E * HEAD_DIM ** (-0.5)

    barrier = pltpu.get_barrier_semaphore()
    for col in (c_x, c_core, c_far):
        pl.semaphore_signal(barrier, inc=1, device_id=(r, col), device_id_type=MESH)
    pl.semaphore_signal(barrier, inc=1, device_id=(r_y, c), device_id_type=MESH)

    @pl.when(z >= 1)
    def _():
        pl.semaphore_signal(barrier, inc=1, device_id=(r - 2, c), device_id_type=MESH)

    @pl.when(z <= 2)
    def _():
        pl.semaphore_signal(barrier, inc=1, device_id=(r + 2, c), device_id_type=MESH)


    own = aligned(c, width)
    shards = (win_s, wo_s, we_s, wr_s)
    fulls = (win, wo, we, wr)
    shard_loads = [
        pltpu.make_async_copy(
            shards[w],
            wo.at[aligned(core * 2 + xx, width), aligned(r, 128)] if w == 1
            else weight_blocks(fulls[w], WEIGHT_KINDS[w], r),
            shard_sem.at[w],
        )
        for w in range(4)
    ]
    for copy in shard_loads:
        copy.start()

    def half_source(ref, i, s):
        return ref.at[pl.ds(pl.multiple_of(i * half, half), half), pl.ds(s * width, width)]

    def half_load(ref, full_ref, sem, i, s):
        return pltpu.make_async_copy(
            half_source(ref, i, s), full_ref.at[i, pl.ds(s * half, half), own], sem.at[i, s]
        )

    for i in range(CHUNKS):
        for s in range(2):
            half_load(tok, tok_all, tok_sem, i, s).start()
            half_load(cot, cot_all, cot_sem, i, s).start()
    for n, vector in enumerate((g_one, s_one, b_out, g_two, s_two, b_red, b_red, b_red)):
        vecs[n : n + 1, own] = vector[...]
    pl.semaphore_wait(barrier, 4 + jnp.where(z >= 1, 1, 0) + jnp.where(z <= 2, 1, 0))

    slab = core * 2 + xx

    def out_x(order):
        block = wo.at[aligned(order, width), :]
        return remote(block, block, wx_send.at[0], wx_recv.at[0], r, c_x)

    def out_core(side):
        block = wo.at[aligned(side, 2 * width), :]
        return remote(block, block, wc_send.at[0], wc_recv.at[0], r, c_core)

    def weight_ref(w, zb, side):
        if w == 1:
            return wo.at[aligned(slab, width), aligned(zb * 2 + side, 128)]
        return weight_blocks(fulls[w], WEIGHT_KINDS[w], zb * 2 + side)

    def line_copy(w, up, hop):
        zb = z - hop if up else z + hop
        block = weight_ref(w, zb, y)
        target = (z + 1 if up else z - 1) * 2 + y
        source = shards[w] if hop == 0 else block
        return remote(source, block, wz_send.at[w, up, hop], wz_recv.at[w, up, hop], target, c)

    def line_sends(up, hop):
        return (z >= hop) & (z <= 2) if up else (z <= 3 - hop) & (z >= 1)

    def line_receives(up, hop):
        return z >= hop + 1 if up else z <= 2 - hop

    def y_copy(w, zb, side):
        block = weight_ref(w, zb, side)
        return remote(block, block, wy_send.at[w, zb], wy_recv.at[w, zb], r_y, c)

    def start_weight(w):
        for up in (0, 1):
            @pl.when(line_sends(up, 0))
            def _():
                line_copy(w, up, 0).start()

    def own_to_y(w):
        return remote(shards[w], weight_ref(w, z, y), wy_send.at[w, z], wy_recv.at[w, z], r_y, c)

    def forward_weight(w, hop):
        for up in (0, 1):
            @pl.when(line_receives(up, hop))
            def _():
                zb = z - 1 - hop if up else z + 1 + hop
                block = weight_ref(w, zb, y)
                remote(block, block, wz_send.at[w, up, hop], wz_recv.at[w, up, hop], r_y, c).wait_recv()
                y_copy(w, zb, y).start()

            if hop < 2:
                @pl.when(line_receives(up, hop) & line_sends(up, hop + 1))
                def _():
                    line_copy(w, up, hop + 1).start()

    def finish_weight(w):
        for up in (0, 1):
            for hop in range(3):
                @pl.when(line_sends(up, hop))
                def _():
                    line_copy(w, up, hop).wait_send()
        for zb in range(4):
            y_copy(w, zb, y).wait_send()
            y_copy(w, zb, 1 - y).wait_recv()

    def vec_copy(slot, target, col):
        block = vecs.at[:, aligned(col, width)]
        return remote(block, block, vec_send.at[slot], vec_recv.at[slot], r, target)

    def half_x(ref, full_ref, send, recv, i, s, col):
        block = full_ref.at[i, pl.ds(s * half, half), aligned(col, width)]
        return remote(half_source(ref, i, s), block, send.at[i, s], recv.at[i, s], r, c_x)

    def half_core(ref, full_ref, send, recv, i, s, col):
        block = full_ref.at[i, pl.ds(s * half, half), aligned(col, width)]
        return remote(half_source(ref, i, s), block, send.at[i, s], recv.at[i, s], r, c_core)

    def tok_x(i, s, col):
        return half_x(tok, tok_all, tx_send, tx_recv, i, s, col)

    def tok_core(i, s, col):
        return half_core(tok, tok_all, tc_send, tc_recv, i, s, col)

    def cot_x(i, s, col):
        return half_x(cot, cot_all, cx_send, cx_recv, i, s, col)

    def cot_core(i, s, col):
        return half_core(cot, cot_all, cc_send, cc_recv, i, s, col)

    def pass_core(full_ref, send, recv, i, col):
        block = full_ref.at[i, :, aligned(col, width)]
        return remote(block, block, send.at[i], recv.at[i], r, c_core)

    def tok_pass(i, col):
        return pass_core(tok_all, tp_send, tp_recv, i, col)

    def cot_pass(i, col):
        return pass_core(cot_all, cp_send, cp_recv, i, col)

    def send_cot(i):
        for s in range(2):
            cot_x(i, s, c).start()
            cot_core(i, s, c).start()

    def send_tok(i):
        for s in range(2):
            tok_x(i, s, c).start()
            tok_core(i, s, c).start()

    start_weight(0)
    own_to_y(0).start()
    for i in range(WINDOW):
        send_tok(i)
    for slot, target in enumerate((c_x, c_core, c_far)):
        vec_copy(slot, target, c).start()

    def keep(index, i, src, dst):
        return pltpu.make_async_copy(src, dst, local_sem.at[index, i])

    def kept(i, stage):
        if stage == 0:
            pairs = ((tok_all, tok_o), (q, q_o), (qt, qt_o), (k, k_o), (kt, kt_o), (v, v_o), (norm_one, one_o), (stat, stat_o))
            base = 0
        elif stage == 1:
            pairs = ((mixf, mixf_o), (lse, lse_o))
            base = 8
        elif stage == 2:
            pairs = ((unit, unit_o), (inv, inv_o), (norm_two, norm_o))
            base = 10
        elif stage == 4:
            pairs = ((act, act_o), (slope, slope_o))
            base = 13
        else:
            pairs = ((cot_all, cot_o),)
            base = 15
        return [keep(base + n, i, a.at[i], b.at[i]) for n, (a, b) in enumerate(pairs)]

    last = [
        keep(17, n, a, b)
        for n, (a, b) in enumerate(
            ((win, win_o), (wo.at[aligned(slab, width), :], wo_o), (we, we_o), (wr, wr_o), (vecs, vec_o))
        )
    ]

    def keep_hid(i):
        return keep(16, i, hid.at[i % 2, :, own], hid_o.at[i])

    lane_ids = lax.broadcasted_iota(jnp.int32, (chunk // 7, 128), 1)

    def first_norm(i):
        for s in range(2):
            half_load(tok, tok_all, tok_sem, i, s).wait()
            tok_core(i, s, c_core).wait_recv()
        tok_pass(i, c_far).wait_recv()
        for part in range(7):
            rows = pl.ds(part * (chunk // 7), chunk // 7)
            units, mean, inverse = row_norm(tok_all[i, rows, :].astype(F32))
            stat[i, rows, :] = jnp.where(lane_ids < 64, mean, inverse)
            norm_one[i, rows, :] = (units * vecs[0:1, :] + vecs[1:2, :]).astype(BF16)

    @pl.loop(0, CHUNKS // 2 + 1)
    def _(g):
        @pl.loop(2 * g, jnp.minimum(2 * g + 2, CHUNKS))
        def _(i):
            for s in range(2):
                tok_x(i, s, c_x).wait_recv()

            @pl.when(i + WINDOW < CHUNKS)
            def _():
                send_tok(i + WINDOW)

            tok_pass(i, c_x).start()

        @pl.when(g == 0)
        def _():
            for slot, target in enumerate((c_x, c_core, c_far)):
                vec_copy(slot, target, c).wait_send()
                vec_copy(slot, target, target).wait_recv()

        for hop in range(3):
            @pl.when(g == hop)
            def _():
                forward_weight(0, hop)

        @pl.when(g == 0)
        def _():
            start_weight(1)
            own_to_y(1).start()

        @pl.when(g == 1)
        def _():
            forward_weight(1, 0)

        @pl.when(g == 3)
        def _():
            forward_weight(1, 1)
            send_cot(0)
            send_cot(1)

        @pl.loop(2 * g, jnp.minimum(2 * g + 2, CHUNKS))
        def _(i):
            first_norm(i)

    for w in range(4):
        shard_loads[w].wait()
    forward_weight(1, 2)
    start_weight(2)
    finish_weight(0)
    last[0].start()
    last[4].start()

    @pl.loop(0, CHUNKS)
    def _(i):
        part = jnp.dot(norm_one[i], win[0], preferred_element_type=F32)
        part = (part + attn_bias[0:1, :]).astype(BF16)
        q[i] = part
        qt[i] = part.T
        part = jnp.dot(norm_one[i], win[1], preferred_element_type=F32).astype(BF16)
        k[i] = part
        kt[i] = part.T
        part = jnp.dot(norm_one[i], win[2], preferred_element_type=F32)
        part = (part + attn_bias[1:2, :]).astype(BF16)
        v[i] = part
        vt[i] = part.T
        for copy in kept(i, 0):
            copy.start()

        @pl.when(i == 0)
        def _():
            own_to_y(2).start()
            finish_weight(1)
            out_x(slab).start()

        @pl.when(i == 2)
        def _():
            own_to_y(3).start()

        @pl.when(i == 4)
        def _():
            forward_weight(2, 0)

        @pl.when(i == 6)
        def _():
            forward_weight(2, 1)

    def attend(i):
        row_ids = lax.broadcasted_iota(jnp.int32, (128, chunk), 0)
        heads = width // HEAD_DIM

        def score(h):
            lanes = slice(h // 2 * 128, h // 2 * 128 + 128)
            query = qt[i, lanes, :]
            query = jnp.where(row_ids // HEAD_DIM == h % 2, query, jnp.zeros_like(query))
            peak = jnp.full((1, chunk), -jnp.inf, F32)
            for j in range(CHUNKS):
                block = jnp.dot(k[j, :, lanes], query, preferred_element_type=F32)
                scores[h % 2, j] = block
                peak = jnp.maximum(peak, jnp.max(block, axis=0, keepdims=True))
            return peak * scale

        def mix(h, peak):
            total = jnp.zeros((1, chunk), F32)
            acc = jnp.zeros((HEAD_DIM, chunk), F32)
            for j in range(CHUNKS):
                weights = jnp.exp2(scores[h % 2, j] * scale - peak)
                total = total + jnp.sum(weights, axis=0, keepdims=True)
                rows = slice(h * HEAD_DIM, (h + 1) * HEAD_DIM)
                acc = acc + jnp.dot(vt[j, rows, :], weights.astype(BF16), preferred_element_type=F32)
            lse[i, h : h + 1, :] = peak + jnp.log2(total)
            return acc / total

        outs = []
        peak = score(0)
        for h in range(heads):
            following = score(h + 1) if h + 1 < heads else None
            outs.append(mix(h, peak))
            peak = following
        out = jnp.concatenate(outs, axis=0).T
        mixf[i] = out
        mixed[i, :, aligned(slab, width)] = out.astype(BF16)

    def mixed_block(i, order):
        return mixed.at[i, :, aligned(order, width)]

    def mixed_x(i, order):
        block = mixed_block(i, order)
        return remote(block, block, mx_send.at[i], mx_recv.at[i], r, c_x)

    def mixed_core(i, slot, order):
        block = mixed_block(i, order)
        return remote(block, block, mc_send.at[i, slot], mc_recv.at[i, slot], r, c_core)

    def second_norm(t):
        mixed_core(t, 0, (1 - core) * 2 + xx).wait_recv()
        mixed_core(t, 1, (1 - core) * 2 + 1 - xx).wait_recv()

        @pl.when(t >= 2)
        def _():
            keep_hid(t - 2).wait()

        hid[t % 2] = tok_all[t].astype(F32) + (
            jnp.dot(mixed[t], wo[...], preferred_element_type=F32) + vecs[2:3, :]
        )
        for part in range(7):
            rows = pl.ds(part * (chunk // 7), chunk // 7)
            units, _, inverse = row_norm(hid[t % 2, rows, :])
            unit[t, rows, :] = units.astype(BF16)
            inv[t, rows, :] = jnp.broadcast_to(inverse, (chunk // 7, 128))
            norm_two[t, rows, :] = (units * vecs[3:4, :] + vecs[4:5, :]).astype(BF16)
        for copy in kept(t, 2):
            copy.start()
        keep_hid(t).start()

    def expand(t):
        for n in range(we.shape[1] // 256):
            lanes = slice(n * 256, (n + 1) * 256)
            expanded = jnp.dot(norm_two[t], we[:, lanes], preferred_element_type=F32) + exp_bias[:, lanes]
            gate = 0.5 + 0.5 * lax.erf(expanded * (0.5 ** 0.5))
            act[t, :, lanes] = (expanded * gate).astype(BF16)
            bell = jnp.exp2(expanded * expanded * (-0.5 * LOG2E)) * 0.3989422804014327
            slope[t, :, lanes] = (gate + expanded * bell).astype(BF16)
        for copy in kept(t, 4):
            copy.start()

    def pass_mixed(t):
        mixed_x(t, core * 2 + 1 - xx).wait_recv()
        mixed_core(t, 1, core * 2 + 1 - xx).start()

    def pass_on_cot(t):
        for s in range(2):
            cot_x(t, s, c_x).wait_recv()
            half_load(cot, cot_all, cot_sem, t, s).wait()
        cot_pass(t, c_x).start()

    @pl.loop(0, CHUNKS)
    def _(i):
        attend(i)
        mixed_x(i, slab).start()
        mixed_core(i, 0, slab).start()
        for copy in kept(i, 1):
            copy.start()

        @pl.when(i == 0)
        def _():
            start_weight(3)

        @pl.when(i == 2)
        def _():
            forward_weight(2, 2)

        @pl.when(i == 3)
        def _():
            out_x(slab).wait_send()
            out_x(core * 2 + 1 - xx).wait_recv()
            out_core(core).start()

        @pl.when(i == 4)
        def _():
            forward_weight(3, 0)
            send_cot(2)
            pass_mixed(0)
            pass_mixed(1)
            out_core(core).wait_send()
            out_core(1 - core).wait_recv()

        @pl.when(i == 6)
        def _():
            forward_weight(3, 1)
            send_cot(3)

        @pl.when(i >= 5)
        def _():
            @pl.loop(2 * (i - 5), i - 3)
            def _(t):
                second_norm(t)

        @pl.when(i == 5)
        def _():
            pass_mixed(2)

    finish_weight(2)
    last[1].start()
    last[2].start()

    @pl.loop(0, CHUNKS)
    def _(t):
        expand(t)

        @pl.when(t == 0)
        def _():
            send_cot(4)

        @pl.when(t == 1)
        def _():
            send_cot(5)
            send_cot(6)

        @pl.when(t == 3)
        def _():
            forward_weight(3, 2)

        @pl.when((t >= 2) & (t <= 5))
        def _():
            second_norm(t + 1)

        @pl.when((t >= 1) & (t <= 4))
        def _():
            pass_mixed(t + 2)

        @pl.when(t >= 3)
        def _():
            pass_on_cot(t - 3)

    for n in range(4, CHUNKS):
        pass_on_cot(n)

    @pl.loop(0, CHUNKS)
    def _(i):
        mixed_x(i, slab).wait_send()
        mixed_core(i, 0, slab).wait_send()
        mixed_core(i, 1, core * 2 + 1 - xx).wait_send()
        for s in range(2):
            cot_x(i, s, c).wait_send()
            cot_core(i, s, c).wait_send()
            cot_core(i, s, c_core).wait_recv()
        cot_pass(i, c_x).wait_send()
        cot_pass(i, c_far).wait_recv()
        for copy in kept(i, 3):
            copy.start()

    @pl.loop(0, CHUNKS)
    def _(i):
        for s in range(2):
            tok_x(i, s, c).wait_send()
            tok_core(i, s, c).wait_send()
        tok_pass(i, c_x).wait_send()

    finish_weight(3)
    last[3].start()

    @pl.loop(0, CHUNKS)
    def _(i):
        for stage in range(5):
            for copy in kept(i, stage):
                copy.wait()

    for t in (CHUNKS - 2, CHUNKS - 1):
        keep_hid(t).wait()

    for copy in last:
        copy.wait()


def forward_call(*arrays):
    tok, we_s = arrays[0], arrays[-2]
    pairs, width = tok.shape[0], tok.shape[1] // 2
    chunk = 2 * pairs // CHUNKS
    full = 4 * width
    hidden = we_s.shape[1]
    n = CHUNKS

    def sd(shape, dtype):
        return jax.ShapeDtypeStruct(shape, dtype)

    outs = [
        sd((n, chunk, full), BF16),
        sd((n, chunk, full), BF16),
        sd((n, chunk, width), BF16),
        sd((n, width, chunk), BF16),
        sd((n, chunk, width), BF16),
        sd((n, width, chunk), BF16),
        sd((n, chunk, width), BF16),
        sd((n, chunk, width), F32),
        sd((n, 8, chunk), F32),
        sd((n, chunk, width), F32),
        sd((n, chunk, full), BF16),
        sd((n, chunk, 128), F32),
        sd((n, chunk, full), BF16),
        sd((n, chunk, hidden), BF16),
        sd((n, chunk, hidden), BF16),
        sd((3, full, width), BF16),
        sd((width, full), BF16),
        sd((full, hidden), BF16),
        sd((hidden, full), BF16),
        sd((8, full), F32),
        sd((n, chunk, full), BF16),
        sd((n, chunk, 128), F32),
    ]
    vm = pltpu.VMEM
    dma = pltpu.SemaphoreType.DMA
    scratch = [
        vm((n, chunk, full), BF16), vm((n, chunk, full), BF16), vm((n, chunk, full), BF16),
        vm((n, chunk, width), BF16), vm((n, width, chunk), BF16),
        vm((n, chunk, width), BF16), vm((n, width, chunk), BF16),
        vm((n, chunk, width), BF16), vm((n, width, chunk), BF16),
        vm((n, chunk, full), BF16), vm((n, chunk, width), F32), vm((n, 8, chunk), F32),
        vm((2, chunk, full), F32), vm((n, chunk, full), BF16), vm((n, chunk, 128), F32),
        vm((n, chunk, full), BF16), vm((n, chunk, hidden), BF16), vm((n, chunk, hidden), BF16),
        vm((3, full, width), BF16), vm((full, full), BF16), vm((full, hidden), BF16), vm((hidden, full), BF16),
        vm((8, full), F32), vm((n, chunk, 128), F32),
        vm((2, n, chunk, chunk), F32),
        dma((18, n)), dma((4,)), dma((n, 2)), dma((n, 2)), dma((4, 2, 3)), dma((4, 2, 3)), dma((4, 4)), dma((4, 4)), dma((3,)), dma((3,)),
        dma((n, 2)), dma((n, 2)), dma((n, 2)), dma((n, 2)), dma((n,)), dma((n,)),
        dma((n, 2)), dma((n, 2)), dma((n, 2)), dma((n, 2)), dma((n,)), dma((n,)),
        dma((1,)), dma((1,)), dma((1,)), dma((1,)), dma((n,)), dma((n,)), dma((n, 2)), dma((n, 2)),
    ]
    return pl.pallas_call(
        forward_kernel,
        out_shape=outs,
        in_specs=[pl.BlockSpec(memory_space=pl.ANY if n in (0, 1, 10, 11, 12, 13) else pltpu.VMEM) for n in range(len(arrays))],
        out_specs=[pl.BlockSpec(memory_space=pl.ANY)] * len(outs),
        scratch_shapes=scratch,
        compiler_params=pltpu.CompilerParams(
            collective_id=0, has_side_effects=True, vmem_limit_bytes=63 << 20
        ),
    )(*arrays)


GRAD_KINDS = ("three", "cols", "rows", "cols")


def backward_kernel(
    tok_h, cot_h, q_h, qt_h, k_h, kt_h, v_h, mixf_h, lse_h, hid_h, unit_h, inv_h,
    normed_h, act_h, slope_h, win_h, wo_h, we_h, wr_h, vec_h, one_h, stat_h,
    out_o, tg_o, sums_o, gin_o, gout_o, gexp_o, gred_o,
    cot, q, qt, k, kt, v, mixf, lse, hid, unit, inv, normed, act, slope, win, wo, we, wr, vecs,
    grad, flat, dk, dv, tg, out, sb_g, sb_o, rb_g, xr_g, rb_o, xr_o, xr_1, st, st_in,
    col_sums, packet, packets,
    ys_in, ys_out, ys_exp, ys_red, oh_in, oh_out, oh_exp, oh_red,
    yr_in, yr_out, yr_exp, yr_red, zr_in, zr_out, zr_exp, zr_red,
    gin, gout, gexp, gred,
    load_sem, chunk_sem, store_sem, hid_sem, gy_send, gy_recv, gz_send, gz_recv,
    h1g_send, h1g_recv, h2g_send, h2g_recv, h3g_send, h3g_recv,
    h1o_send, h1o_recv, h2o_send, h2o_recv, h1t_send, h1t_recv, h2t_send, h2t_recv,
    st_send, st_recv, pk_send, pk_recv,
):
    r, c = lax.axis_index("row"), lax.axis_index("col")
    z, y = r // 2, r % 2
    xx, core = c // 2, c % 2
    c_x, c_core, c_far = (c + 2) % 4, c + 1 - 2 * core, (c + 2) % 4 + 1 - 2 * core
    r_y = r + 1 - 2 * y
    tok, one, stat = act, normed, inv
    chunk = q.shape[0] // CHUNKS
    half = chunk // 2
    width = q.shape[1]
    full = cot.shape[1]
    scale = LOG2E * HEAD_DIM ** (-0.5)
    own = aligned(c, width)
    others = [(r + step) % 8 for step in range(1, 8)]

    barrier = pltpu.get_barrier_semaphore()
    for col in (c_x, c_core, c_far):
        pl.semaphore_signal(barrier, inc=1, device_id=(r, col), device_id_type=MESH)
    for row in others:
        pl.semaphore_signal(barrier, inc=1, device_id=(row, c), device_id_type=MESH)

    def rows_of(i):
        return pl.ds(pl.multiple_of(i * chunk, chunk), chunk)

    loads = {}
    order = (
        ("wr", wr_h, wr), ("we", we_h, we),
        ("vec", vec_h, vecs), ("unit", unit_h, unit), ("inv", inv_h, inv), ("wo", wo_h, wo),
        ("normed", normed_h, normed), ("mixf", mixf_h, mixf), ("lse", lse_h, lse), ("qt", qt_h, qt), ("q", q_h, q),
        ("k", k_h, k), ("v", v_h, v), ("kt", kt_h, kt), ("stat", stat_h, stat),
        ("tok", tok_h, tok), ("one", one_h, one),
    )
    for n, (name, src, dst) in enumerate(order):
        loads[name] = pltpu.make_async_copy(src, dst, load_sem.at[n])
    for n in range(3):
        loads["win" + str(n)] = pltpu.make_async_copy(
            win_h.at[n], win.at[:, pl.ds(n * width, width)], load_sem.at[len(order) + n]
        )
    def chunk_loads(i):
        rows = rows_of(i)
        return [
            pltpu.make_async_copy(a.at[rows, :], b.at[rows, :], chunk_sem.at[n, i])
            for n, (a, b) in enumerate(((cot_h, cot), (slope_h, slope), (act_h, act)))
        ]

    loads["wr"].start()
    loads["we"].start()
    for i in range(CHUNKS):
        for copy in chunk_loads(i):
            copy.start()
    late = ("wr", "we", "tok", "one", "stat", "win0", "win1", "win2")
    for name in loads:
        if name not in late:
            loads[name].start()
    dk[...] = jnp.zeros_like(dk)
    dv[...] = jnp.zeros_like(dv)
    col_sums[...] = jnp.zeros_like(col_sums)
    pl.semaphore_wait(barrier, 10)

    def h1(sb, rb, send, recv, i):
        return remote(sb.at[i % 2, 1 - core], rb.at[i], send.at[i], recv.at[i], r, c_core)

    def fill(sb, i, partial):
        for x in range(2):
            for side in range(2):
                block = x * 2 + side
                sb[i % 2, side, x] = partial[:, block * width : (block + 1) * width].astype(BF16)

    def merge(sb, rb, i):
        for x in range(2):
            rb[i, x] = (sb[i % 2, core, x].astype(F32) + rb[i, x].astype(F32)).astype(BF16)

    def h1g(i):
        return h1(sb_g, rb_g, h1g_send, h1g_recv, i)

    def h1o(i):
        return h1(sb_o, rb_o, h1o_send, h1o_recv, i)

    def h1t(i):
        return h1(sb_g, rb_g, h1t_send, h1t_recv, i)

    def h2g(i):
        return remote(rb_g.at[i], xr_g.at[i], h2g_send.at[i], h2g_recv.at[i], r, c_x)

    def h2o(i):
        return remote(rb_o.at[i, 1 - xx], xr_o.at[i], h2o_send.at[i], h2o_recv.at[i], r, c_x)

    def h2t(i):
        return remote(rb_g.at[i, 1 - xx], xr_1.at[i], h2t_send.at[i], h2t_recv.at[i], r, c_x)

    def h3g(i, x, side):
        block = grad.at[i % 4, :, aligned(x * 2 + side, width)]
        return remote(block, block, h3g_send.at[i, x], h3g_recv.at[i, x], r, c_core)

    def spread_grad(i):
        h2g(i).wait()
        if isinstance(i, int):
            h2g(i + 4).start()
        else:
            @pl.when(i + 4 < CHUNKS)
            def _():
                h2g(i + 4).start()

        for x in range(2):
            grad[i % 4, :, aligned(x * 2 + core, width)] = rb_g[i, x].astype(F32) + xr_g[i, x].astype(F32)
        for x in range(2):
            h3g(i, x, core).start()

    def column_sums(values):
        ones = jnp.ones((8, values.shape[0]), BF16)
        return jnp.dot(ones, values, preferred_element_type=F32)[0:1, :]

    ys = (ys_in, ys_out, ys_exp, ys_red)
    oh = (oh_in, oh_out, oh_exp, oh_red)
    yr = (yr_in, yr_out, yr_exp, yr_red)
    zr = (zr_in, zr_out, zr_exp, zr_red)

    def gy(w, s):
        return remote(ys[w].at[s], yr[w].at[s], gy_send.at[w, s], gy_recv.at[w, s], r_y, c)

    def gz(w, s):
        target = ((z + 1 + s) % 4) * 2 + y
        return remote(oh[w].at[s], zr[w].at[s], gz_send.at[w, s], gz_recv.at[w, s], target, c)

    def grad_block(w, s, left, right):
        zt = (z + 1 + s) % 4
        lanes = aligned(zt, 256)
        if GRAD_KINDS[w] == "rows":
            block = lax.dot_general(left[:, lanes], right, TN_DIMS, preferred_element_type=F32).astype(BF16)
            low, high = block[0:128, :], block[128:256, :]
        else:
            block = lax.dot_general(left, right[:, lanes], TN_DIMS, preferred_element_type=F32).astype(BF16)
            low, high = block[:, 0:128], block[:, 128:256]

        @pl.when(y == 0)
        def _():
            oh[w][s] = low
            ys[w][s] = high

        @pl.when(y == 1)
        def _():
            oh[w][s] = high
            ys[w][s] = low

    def pass_on(w, s):
        gy(w, s).wait()
        oh[w][s] = (oh[w][s].astype(F32) + yr[w][s].astype(F32)).astype(BF16)
        gz(w, s).start()

    stores = [
        pltpu.make_async_copy(src, dst, store_sem.at[2, n, 0])
        for n, (src, dst) in enumerate(((gin, gin_o), (gout, gout_o), (gexp, gexp_o), (gred, gred_o)))
    ]

    def finish_grad(w, dst):
        gy(w, 3).wait()
        total = oh[w][3].astype(F32) + yr[w][3].astype(F32)
        for s in range(3):
            gz(w, s).wait()
            total = total + zr[w][s].astype(F32)
        dst[...] = total
        stores[w].start()

    loads["wr"].wait()
    loads["we"].wait()

    @pl.loop(0, CHUNKS + 1)
    def _(i):
        @pl.when(i < CHUNKS)
        def _():
            @pl.when(i < 3)
            def _():
                for copy in chunk_loads(i):
                    copy.wait()

            @pl.when(i == 3)
            def _():
                for n in range(3, CHUNKS):
                    for copy in chunk_loads(n):
                        copy.wait()

            rows = rows_of(i)
            for n in range(slope.shape[1] // 256):
                lanes = slice(n * 256, (n + 1) * 256)
                grad_act = lax.dot_general(cot[rows, :], wr[lanes, :], NT_DIMS, preferred_element_type=F32)
                low = (slope[rows, lanes].astype(F32) * grad_act).astype(BF16)
                slope[rows, lanes] = low
            fill(sb_g, i, lax.dot_general(slope[rows, :], we[...], NT_DIMS, preferred_element_type=F32))
            h1g(i).start()

        @pl.when(i >= 1)
        def _():
            h1o(i - 1).wait()
            merge(sb_o, rb_o, i - 1)
            h1g(i - 1).wait()
            merge(sb_g, rb_g, i - 1)

        for at, n in ((1, 0), (2, 1), (4, 2), (6, 3)):
            @pl.when(i == at)
            def _():
                h2g(n).start()

        @pl.when(i == 3)
        def _():
            grad_block(3, 0, act[...], cot)
            gy(3, 0).start()

        @pl.when(i == 5)
        def _():
            grad_block(3, 1, act[...], cot)
            gy(3, 1).start()

        @pl.when(i < CHUNKS)
        def _():
            fill(sb_o, i, jnp.dot(act[rows_of(i), :], wr[...], preferred_element_type=F32))
            h1o(i).start()

    for n in range(4):
        packet[8 + n : 9 + n, :] = column_sums(slope[:, n * width : (n + 1) * width])
    loads["normed"].wait()
    spread_grad(0)
    pass_on(3, 0)
    grad_block(3, 2, act[...], cot)
    gy(3, 2).start()
    grad_block(3, 3, act[...], cot)
    spread_grad(1)
    grad_block(2, 0, normed, slope[...])
    pass_on(3, 1)
    gy(2, 0).start()
    for s in range(1, 4):
        grad_block(2, s, normed, slope[...])
    for name in late[2:]:
        if name != "stat":
            loads[name].start()
    for name in ("unit", "inv", "vec", "wo", "mixf", "lse", "qt", "q", "k", "v", "kt"):
        loads[name].wait()

    def hid_load(i):
        return pltpu.make_async_copy(hid_h.at[rows_of(i), :], hid, hid_sem.at[i])

    def out_store(i, s):
        return pltpu.make_async_copy(
            out.at[i % 2, s], out_o.at[pl.ds(pl.multiple_of(i * half, half), half), pl.ds(s * width, width)],
            store_sem.at[0, i, s],
        )

    def tg_store(i, s):
        return pltpu.make_async_copy(
            tg.at[i, s], tg_o.at[pl.ds(pl.multiple_of(i * half, half), half), pl.ds(s * width, width)],
            store_sem.at[1, i, s],
        )

    def attend_back(i):
        rows = rows_of(i)
        go = lax.dot_general(unit[rows, :], wo[...], NT_DIMS, preferred_element_type=F32).astype(BF16)
        inner = (go.astype(F32) * mixf[rows, :]).T
        go_t = go.T
        row_ids = lax.broadcasted_iota(jnp.int32, (128, chunk), 0)
        lane_ids = lax.broadcasted_iota(jnp.int32, (chunk, 128), 1)
        heads = width // HEAD_DIM
        queries, grads, query_rows, grad_rows, deltas, logs = [], [], [], [], [], []
        for h in range(heads):
            lanes = slice(h // 2 * 128, h // 2 * 128 + 128)
            pick = row_ids // HEAD_DIM == h % 2
            value = qt[i, lanes, :]
            queries.append(jnp.where(pick, value, jnp.zeros_like(value)))
            value = go_t[lanes, :]
            grads.append(jnp.where(pick, value, jnp.zeros_like(value)))
            pick = lane_ids // HEAD_DIM == h % 2
            value = q[rows, lanes]
            query_rows.append(jnp.where(pick, value, jnp.zeros_like(value)))
            value = go[:, lanes]
            grad_rows.append(jnp.where(pick, value, jnp.zeros_like(value)))
            deltas.append(jnp.sum(inner[h * HEAD_DIM : (h + 1) * HEAD_DIM, :], axis=0, keepdims=True))
            logs.append(lse[i, h : h + 1, :])

        parts = [jnp.zeros((HEAD_DIM, chunk), F32)] * heads
        for j in range(CHUNKS):
            keys = pl.ds(j * chunk, chunk)
            probs, grad_scores = [], []
            for h in range(heads):
                lanes = slice(h // 2 * 128, h // 2 * 128 + 128)
                block = jnp.dot(k[keys, lanes], queries[h], preferred_element_type=F32)
                grad_probs = jnp.dot(v[keys, lanes], grads[h], preferred_element_type=F32)
                prob = jnp.exp2(block * scale - logs[h])
                probs.append(prob.astype(BF16))
                grad_scores.append((prob * (grad_probs - deltas[h])).astype(BF16))
            for pair in range(heads // 2):
                lanes = slice(pair * 128, pair * 128 + 128)
                h = 2 * pair
                dv[keys, lanes] += jnp.dot(
                    probs[h], grad_rows[h], preferred_element_type=F32
                ) + jnp.dot(probs[h + 1], grad_rows[h + 1], preferred_element_type=F32)
                dk[keys, lanes] += jnp.dot(
                    grad_scores[h], query_rows[h], preferred_element_type=F32
                ) + jnp.dot(grad_scores[h + 1], query_rows[h + 1], preferred_element_type=F32)
            for h in range(heads):
                rows_h = slice(h * HEAD_DIM, (h + 1) * HEAD_DIM)
                parts[h] = parts[h] + jnp.dot(kt[j, rows_h, :], grad_scores[h], preferred_element_type=F32)
        flat[rows, 0:width] = (jnp.concatenate(parts, axis=0).T * HEAD_DIM ** (-0.5)).astype(BF16)

    def finish_out(i):
        @pl.when(i >= 2)
        def _():
            for s in range(2):
                out_store(i - 2, s).wait()

        hid_load(i).start()
        h2o(i).wait()
        hid_load(i).wait()
        total = rb_o[i, xx].astype(F32) + xr_o[i].astype(F32)
        value = (hid[...] + total + vecs[5:6, own]).astype(BF16)
        for s in range(2):
            out[i % 2, s] = value[s * half : (s + 1) * half, :]
        for s in range(2):
            out_store(i, s).start()

    def second_norm_back(i):
        for x in range(2):
            h3g(i, x, core).wait_send()
            h3g(i, x, 1 - core).wait_recv()
        step_rows = chunk // 7
        for part in range(7):
            rows = pl.ds(pl.multiple_of(i * chunk + part * step_rows, step_rows), step_rows)
            span = slice(part * step_rows, (part + 1) * step_rows)
            incoming = grad[i % 4, span, :]
            units = unit[rows, :].astype(F32)
            scaled = incoming * vecs[3:4, :]
            plain = jnp.mean(scaled, axis=1, keepdims=True)
            cross = jnp.mean(scaled * units, axis=1, keepdims=True)
            total = cot[rows, :].astype(F32) + inv[rows, 0:1] * (scaled - plain - units * cross)
            mine = grad[i % 4, span, own]
            col_sums[1:2, 0:width] += jnp.sum(mine * unit[rows, own].astype(F32), axis=0, keepdims=True)
            col_sums[2:3, 0:width] += jnp.sum(mine, axis=0, keepdims=True)
            unit[rows, :] = total.astype(BF16)
            grad[i % 4, span, :] = total
        for s in range(2):
            tg[i, s] = grad[i % 4, s * half : (s + 1) * half, own]

    @pl.loop(-1, CHUNKS)
    def _(i):
        @pl.when(i + 1 < CHUNKS)
        def _():
            second_norm_back(i + 1)

        @pl.when((i >= 0) & (i + 2 < CHUNKS))
        def _():
            spread_grad(i + 2)

        @pl.when(i == CHUNKS - 2)
        def _():
            for s in range(4):
                grad_block(1, s, mixf[...].astype(BF16), unit)
                gy(1, s).start()

        @pl.when(i == CHUNKS - 1)
        def _():
            loads["stat"].start()

        @pl.when(i >= 0)
        def _():
            attend_back(i)

        @pl.when(i == -1)
        def _():
            pass_on(3, 2)
            gy(2, 1).start()

        @pl.when(i == 0)
        def _():
            pass_on(2, 0)
            gy(2, 2).start()

        @pl.when(i == 1)
        def _():
            pass_on(2, 1)
            gy(3, 3).start()

        @pl.when(i == 2)
        def _():
            pass_on(2, 2)
            gy(2, 3).start()

        @pl.when(i == CHUNKS - 2)
        def _():
            finish_grad(3, gred)

        @pl.when(i == CHUNKS - 1)
        def _():
            for s in range(3):
                pass_on(1, s)

        @pl.when(i >= 3)
        def _():
            @pl.loop(2 * (i - 3), jnp.minimum(2 * (i - 3) + 2, CHUNKS))
            def _(n):
                h2o(n).start()

        @pl.when(i >= 5)
        def _():
            @pl.loop(2 * (i - 5), 2 * (i - 5) + 2)
            def _(n):
                finish_out(n)

    for i in range(CHUNKS):
        rows = pl.ds(i * chunk, chunk)
        flat[rows, width : 2 * width] = (dk[rows, :] * HEAD_DIM ** (-0.5)).astype(BF16)
        flat[rows, 2 * width : 3 * width] = dv[rows, :].astype(BF16)
    for name in late[2:]:
        loads[name].wait()

    def inward_block(s):
        zt = (z + 1 + s) % 4
        left = one[:, aligned(zt, 256)]
        block = lax.dot_general(left, flat[...], TN_DIMS, preferred_element_type=F32).astype(BF16)
        for n in range(3):
            lanes = slice(n * width, (n + 1) * width)

            @pl.when(y == 0)
            def _():
                oh_in[s, n] = block[0:128, lanes]
                ys_in[s, n] = block[128:256, lanes]

            @pl.when(y == 1)
            def _():
                oh_in[s, n] = block[128:256, lanes]
                ys_in[s, n] = block[0:128, lanes]

        gy(0, s).start()

    def stat_copy(i, slot, target):
        return remote(st.at[i], st_in.at[i, slot], st_send.at[i, slot], st_recv.at[i, slot], r, target)

    lane_ids = lax.broadcasted_iota(jnp.int32, (chunk, 128), 1)
    gain = vecs[0:1, :]

    @pl.loop(0, CHUNKS + 3)
    def _(i):
        @pl.when(i < CHUNKS)
        def _():
            rows = rows_of(i)
            partial = lax.dot_general(flat[rows, :], win[...], NT_DIMS, preferred_element_type=F32)
            fill(sb_g, i, partial)
            h1t(i).start()
            units = (tok[rows, :].astype(F32) - stat[rows, 0:1]) * stat[rows, 64:65]
            scaled = partial * gain
            plain = jnp.sum(scaled, axis=1, keepdims=True)
            cross = jnp.sum(scaled * units, axis=1, keepdims=True)
            both = jnp.where(lane_ids == 0, plain, jnp.where(lane_ids == 1, cross, 0.0))
            st[i] = both.T[0:8, :]
            for slot, target in enumerate((c_x, c_core, c_far)):
                stat_copy(i, slot, target).start()

        for at, s in ((0, 1), (2, 0), (3, 2), (4, 3)):
            @pl.when(i == at)
            def _():
                inward_block(s)

        @pl.when((i >= 4) & (i <= 6))
        def _():
            finish_out(i)

        @pl.when((i >= 1) & (i <= CHUNKS))
        def _():
            h1t(i - 1).wait()
            merge(sb_g, rb_g, i - 1)
            h2t(i - 1).start()

        for at, s in ((3, 1), (5, 0), (6, 2)):
            @pl.when(i == at)
            def _():
                pass_on(0, s)

        @pl.when(i == 5)
        def _():
            packet[7:8, :] = column_sums(cot[:, own])
            packet[4:5, :] = column_sums(unit[:, own])

        @pl.when(i == 6)
        def _():
            packet[2:3, :] = column_sums(flat[:, 0:width])
            packet[3:4, :] = column_sums(flat[:, 2 * width : 3 * width])
            finish_grad(2, gexp)

        @pl.when(i == 7)
        def _():
            finish_grad(1, gout)

        @pl.when(i >= 3)
        def _():
            t = i - 3
            rows = rows_of(t)
            h2t(t).wait()
            total = st[t]
            for slot, target in enumerate((c_x, c_core, c_far)):
                stat_copy(t, slot, target).wait()
                total = total + st_in[t, slot]
            columns = jnp.concatenate([total, jnp.zeros((120, chunk), F32)], axis=0).T
            plain = columns[:, 0:1] / full
            cross = columns[:, 1:2] / full
            incoming = rb_g[t, xx].astype(F32) + xr_1[t].astype(F32)
            inverse = stat[rows, 64:65]
            units = (tok[rows, own].astype(F32) - stat[rows, 0:1]) * inverse
            back = inverse * (incoming * vecs[0:1, own] - plain - units * cross)
            for s in range(2):
                tg[t, s] = tg[t, s] + back[s * half : (s + 1) * half, :]
            for s in range(2):
                tg_store(t, s).start()
            col_sums[6:7, 0:width] += jnp.sum(incoming * units, axis=0, keepdims=True)
            col_sums[7:8, 0:width] += jnp.sum(incoming, axis=0, keepdims=True)

    packet[0:1, :] = col_sums[6:7, 0:width]
    packet[1:2, :] = col_sums[7:8, 0:width]
    packet[5:7, :] = col_sums[1:3, 0:width]

    def packet_copy(step):
        return remote(packet, packets.at[step], pk_send.at[step], pk_recv.at[step], others[step], c)

    for step in range(7):
        packet_copy(step).start()
    finish_grad(0, gin)
    total = packet[...]
    for step in range(7):
        packet_copy(step).wait()
        total = total + packets[step]
    packet[...] = total
    copy = pltpu.make_async_copy(packet, sums_o, store_sem.at[2, 4, 0])
    copy.start()
    copy.wait()
    for copy in stores:
        copy.wait()
    for i in range(CHUNKS - 2, CHUNKS):
        for s in range(2):
            out_store(i, s).wait()

    @pl.loop(0, CHUNKS)
    def _(i):
        for s in range(2):
            tg_store(i, s).wait()


def backward_call(*arrays):
    (tok, cot, q, qt, k, kt, v, mixf, lse, hid, unit, inv, normed, act, slope, win, wo, we, wr, vec, one, stat) = arrays
    rows, width = q.shape
    full, hidden = we.shape
    n, chunk = CHUNKS, rows // CHUNKS
    half = chunk // 2
    pairs = rows // 2

    def sd(shape, dtype):
        return jax.ShapeDtypeStruct(shape, dtype)

    outs = [
        sd((pairs, 2 * width), BF16), sd((pairs, 2 * width), F32), sd((16, width), F32),
        sd((3, 128, width), F32), sd((width, 128), F32), sd((128, hidden), F32), sd((hidden, 128), F32),
    ]
    vm = pltpu.VMEM
    dma = pltpu.SemaphoreType.DMA

    def shapes(lead):
        return [
            vm((lead, 3, 128, width), BF16), vm((lead, width, 128), BF16),
            vm((lead, 128, hidden), BF16), vm((lead, hidden, 128), BF16),
        ]

    def like(array):
        return vm(array.shape, array.dtype)

    scratch = [
        vm((rows, full), BF16), like(q), like(qt), like(k), like(kt), like(v), like(mixf), like(lse),
        vm((chunk, width), F32),
        like(unit), like(inv), like(normed), like(act), like(slope),
        vm((full, 3 * width), BF16), like(wo), like(we), like(wr), like(vec),
        vm((4, chunk, full), F32), vm((rows, 3 * width), BF16), vm((rows, width), F32), vm((rows, width), F32),
        vm((n, 2, half, width), F32), vm((2, 2, half, width), BF16),
        vm((2, 2, 2, chunk, width), BF16), vm((2, 2, 2, chunk, width), BF16),
        vm((n, 2, chunk, width), BF16), vm((n, 2, chunk, width), BF16),
        vm((n, 2, chunk, width), BF16), vm((n, chunk, width), BF16), vm((n, chunk, width), BF16),
        vm((n, 8, chunk), F32), vm((n, 3, 8, chunk), F32),
        vm((8, full), F32), vm((16, width), F32), vm((7, 16, width), F32),
        *shapes(4), *shapes(4), *shapes(4), *shapes(3),
        vm((3, 128, width), F32), vm((width, 128), F32), vm((128, hidden), F32), vm((hidden, 128), F32),
        dma((23,)), dma((3, n)), dma((3, n, 2)), dma((n,)), dma((4, 4)), dma((4, 4)), dma((4, 3)), dma((4, 3)),
        dma((n,)), dma((n,)), dma((n,)), dma((n,)), dma((n, 2)), dma((n, 2)),
        dma((n,)), dma((n,)), dma((n,)), dma((n,)), dma((n,)), dma((n,)), dma((n,)), dma((n,)),
        dma((n, 3)), dma((n, 3)), dma((7,)), dma((7,)),
    ]
    return pl.pallas_call(
        backward_kernel,
        out_shape=outs,
        in_specs=[pl.BlockSpec(memory_space=pl.ANY)] * len(arrays),
        out_specs=[pl.BlockSpec(memory_space=pl.ANY)] * len(outs),
        scratch_shapes=scratch,
        compiler_params=pltpu.CompilerParams(
            collective_id=1, has_side_effects=True, vmem_limit_bytes=63 << 20
        ),
    )(*arrays)


def finish_kernel(out_i, tg_i, sums_i, gin_i, gout_i, gexp_i, gred_i, *refs):
    outs, vector_o, buffers = refs[:6], refs[6:14], refs[14:20]
    load_sem, store_sem = refs[20:]
    ins = (out_i, tg_i, gin_i, gout_i, gexp_i, gred_i)
    loads, stores = [], []
    for n, parts in ((1, 2), (0, 1), (4, 1), (5, 1), (2, 1), (3, 1)):
        size = ins[n].shape[0] // parts
        for part in range(parts):
            span = pl.ds(part * size, size)
            slot = len(loads)
            loads.append(pltpu.make_async_copy(ins[n].at[span], buffers[n].at[span], load_sem.at[slot]))
            stores.append(pltpu.make_async_copy(buffers[n].at[span], outs[n].at[span], store_sem.at[slot]))
    for copy in loads:
        copy.start()
    first_gain, first_shift, attn, b_out, g_two, s_two, b_red, b_exp = vector_o
    first_gain[...] = sums_i[0:1, :]
    first_shift[...] = sums_i[1:2, :]
    attn[...] = sums_i[2:4, :]
    b_out[...] = sums_i[4:5, :]
    g_two[...] = sums_i[5:6, :]
    s_two[...] = sums_i[6:7, :]
    b_red[...] = sums_i[7:8, :]
    for n in range(4):
        width = sums_i.shape[1]
        b_exp[:, n * width : (n + 1) * width] = sums_i[8 + n : 9 + n, :]
    for load, store in zip(loads, stores):
        load.wait()
        store.start()
    for store in stores:
        store.wait()


def finish_call(out, tg, sums, gin, gout, gexp, gred):
    width = sums.shape[1]
    big = [jax.ShapeDtypeStruct(a.shape, a.dtype) for a in (out, tg, gin, gout, gexp, gred)]
    small = [jax.ShapeDtypeStruct((n, m), F32) for n, m in ((1, width),) * 2 + ((2, width),) + ((1, width),) * 4 + ((1, 4 * width),)]
    hbm, vm = pl.BlockSpec(memory_space=pl.ANY), pl.BlockSpec(memory_space=pltpu.VMEM)
    return pl.pallas_call(
        finish_kernel,
        out_shape=big + small,
        in_specs=[hbm, hbm, vm, hbm, hbm, hbm, hbm],
        out_specs=[hbm] * 6 + [vm] * 8,
        scratch_shapes=[pltpu.VMEM(a.shape, a.dtype) for a in big] + [pltpu.SemaphoreType.DMA((7,))] * 2,
    )(out, tg, sums, gin, gout, gexp, gred)


CONTRACT_ROWS = (((0,), (0,)), ((), ()))
CONTRACT_COLS = (((1,), (1,)), ((), ()))


def norm_forward(values, gain, shift, full_width):
    row_total = lax.psum(jnp.sum(values, axis=1), "col")
    centred = values - (row_total / full_width)[:, None]
    row_square = lax.psum(jnp.sum(centred * centred, axis=1), "col")
    inverse = lax.rsqrt(row_square / full_width + EPSILON)
    unit_rows = centred * inverse[:, None]
    return (unit_rows, inverse, unit_rows * gain + shift)


def norm_backward(incoming, unit_rows, inverse, gain, full_width):
    scaled = incoming * gain
    plain_sum, cross_sum = lax.psum(
        (jnp.sum(scaled, axis=1), jnp.sum(scaled * unit_rows, axis=1)), "col"
    )
    result = inverse[:, None] * (
        scaled - (plain_sum / full_width)[:, None] - unit_rows * (cross_sum / full_width)[:, None]
    )
    return (result, jnp.sum(incoming * unit_rows, axis=0), jnp.sum(incoming, axis=0))


def spread_features(values):
    return lax.all_gather(values, "col", axis=1, tiled=True)


def sum_partials(values):
    return lax.psum_scatter(values, "col", scatter_dimension=1, tiled=True)


def spread_grads(values):
    return lax.all_gather(values, "col", axis=1, tiled=True)


def sum_grad_partials(values):
    return lax.psum_scatter(values, "col", scatter_dimension=1, tiled=True)


def fetch_weights(inward_weight, output_weight, expand_weight, reduce_weight):
    return (
        lax.all_gather(inward_weight, "row", axis=0, tiled=True),
        lax.all_gather(output_weight, "row", axis=1, tiled=True),
        lax.all_gather(expand_weight, "row", axis=0, tiled=True),
        lax.all_gather(reduce_weight, "row", axis=1, tiled=True),
    )


def attend_clip(queries, key_rows, value_rows, score_scale):
    seq_len = queries.shape[0]
    blocks = queries.reshape((2, seq_len // 2) + queries.shape[1:])

    def one_block(query_part):
        scores = (
            jnp.einsum("qhd,khd->hqk", query_part, key_rows, preferred_element_type=jnp.float32)
            * score_scale
        )
        row_peak = jnp.max(scores, axis=-1, keepdims=True)
        exponent = jnp.exp(scores - row_peak)
        row_sum = jnp.sum(exponent, axis=-1, keepdims=True)
        prob_low = (exponent / row_sum).astype(jnp.bfloat16)
        mixed_rows = jnp.einsum(
            "hqk,khd->qhd", prob_low, value_rows, preferred_element_type=jnp.float32
        )
        return (mixed_rows, (row_peak + jnp.log(row_sum))[..., 0])

    mixed_rows, logsum = lax.map(one_block, blocks)
    return (mixed_rows.reshape(queries.shape), logsum)


def attend_clip_back(queries, key_rows, value_rows, logsum, grad_out, score_scale):
    seq_len = queries.shape[0]
    block_shape = (2, seq_len // 2) + queries.shape[1:]

    def step_block(carry, pieces):
        key_acc, value_acc = carry
        query_part, grad_part, log_part = pieces
        scores = (
            jnp.einsum("qhd,khd->hqk", query_part, key_rows, preferred_element_type=jnp.float32)
            * score_scale
        )
        probs = jnp.exp(scores - log_part[..., None])
        grad_probs = jnp.einsum(
            "qhd,khd->hqk", grad_part, value_rows, preferred_element_type=jnp.float32
        )
        inner_sum = jnp.sum(probs * grad_probs, axis=-1, keepdims=True)
        grad_scores = (probs * (grad_probs - inner_sum)).astype(jnp.bfloat16)
        query_grad = (
            jnp.einsum("hqk,khd->qhd", grad_scores, key_rows, preferred_element_type=jnp.float32)
            * score_scale
        )
        key_acc = key_acc + jnp.einsum(
            "hqk,qhd->khd", grad_scores, query_part, preferred_element_type=jnp.float32
        )
        value_acc = value_acc + jnp.einsum(
            "hqk,qhd->khd",
            probs.astype(jnp.bfloat16),
            grad_part,
            preferred_element_type=jnp.float32,
        )
        return ((key_acc, value_acc), query_grad)

    zero_acc = jnp.zeros(key_rows.shape, jnp.float32)
    (key_acc, value_acc), query_grads = lax.scan(
        step_block,
        (zero_acc, zero_acc),
        (queries.reshape(block_shape), grad_out.reshape(block_shape), logsum),
    )
    return (query_grads.reshape(queries.shape), key_acc * score_scale, value_acc)


def forward_pass(
    tokens,
    first_gain,
    first_shift,
    attention_bias,
    output_bias,
    second_gain,
    second_shift,
    expand_bias,
    reduce_bias,
    gathered,
):
    inward_all, output_rows, expand_all, reduce_rows = gathered
    full_width = inward_all.shape[0]
    local_width = inward_all.shape[2]
    row_count = tokens.shape[0]
    clip_shape = (row_count // SEQ, SEQ, local_width // HEAD_DIM, HEAD_DIM)
    score_scale = HEAD_DIM ** (-0.5)
    source = tokens.astype(jnp.float32)
    unit_one, inverse_one, normed_one = norm_forward(source, first_gain, first_shift, full_width)
    normed_all = spread_features(normed_one.astype(jnp.bfloat16))
    projected = jnp.dot(
        normed_all,
        inward_all.reshape(full_width, 3 * local_width),
        preferred_element_type=jnp.float32,
    )
    projected = projected.reshape(row_count, 3, local_width)
    queries = (projected[:, 0] + attention_bias[0]).astype(jnp.bfloat16)
    key_rows = projected[:, 1].astype(jnp.bfloat16)
    value_rows = (projected[:, 2] + attention_bias[1]).astype(jnp.bfloat16)
    mixed_rows, logsum = lax.map(
        lambda clip_parts: attend_clip(clip_parts[0], clip_parts[1], clip_parts[2], score_scale),
        (queries.reshape(clip_shape), key_rows.reshape(clip_shape), value_rows.reshape(clip_shape)),
    )
    mixed_low = mixed_rows.reshape(row_count, local_width).astype(jnp.bfloat16)
    hidden_state = (
        source
        + sum_partials(jnp.dot(mixed_low, output_rows, preferred_element_type=jnp.float32))
        + output_bias
    )
    unit_two, inverse_two, normed_two = norm_forward(
        hidden_state, second_gain, second_shift, full_width
    )
    normed_all_two = spread_features(normed_two.astype(jnp.bfloat16))
    expanded = jnp.dot(normed_all_two, expand_all, preferred_element_type=jnp.float32) + expand_bias
    activated = jax.nn.gelu(expanded, approximate=False).astype(jnp.bfloat16)
    output_value = (
        hidden_state
        + sum_partials(jnp.dot(activated, reduce_rows, preferred_element_type=jnp.float32))
        + reduce_bias
    )
    saved_state = (
        unit_one,
        inverse_one,
        normed_all,
        queries,
        key_rows,
        value_rows,
        logsum,
        mixed_low,
        unit_two,
        inverse_two,
        normed_all_two,
        expanded,
        activated,
    )
    return (output_value, saved_state)


def plain_device(
    tokens,
    first_gain,
    first_shift,
    inward_weight,
    attention_bias,
    output_weight,
    output_bias,
    second_gain,
    second_shift,
    expand_weight,
    expand_bias,
    reduce_weight,
    reduce_bias,
    cotangent,
):
    packed_width = tokens.shape[1]
    tokens = tokens.reshape(-1, packed_width // 2)
    cotangent = cotangent.reshape(-1, packed_width // 2)
    gathered = fetch_weights(inward_weight, output_weight, expand_weight, reduce_weight)
    output_value, saved_state = forward_pass(
        tokens,
        first_gain,
        first_shift,
        attention_bias,
        output_bias,
        second_gain,
        second_shift,
        expand_bias,
        reduce_bias,
        gathered,
    )
    gathered = fetch_weights(inward_weight, output_weight, expand_weight, reduce_weight)
    unused_value, saved_state = forward_pass(
        tokens,
        first_gain,
        first_shift,
        attention_bias,
        output_bias,
        second_gain,
        second_shift,
        expand_bias,
        reduce_bias,
        gathered,
    )
    inward_all, output_rows, expand_all, reduce_rows = gathered
    (
        unit_one,
        inverse_one,
        normed_all,
        queries,
        key_rows,
        value_rows,
        logsum,
        mixed_low,
        unit_two,
        inverse_two,
        normed_all_two,
        expanded,
        activated,
    ) = saved_state
    full_width = inward_all.shape[0]
    local_width = inward_all.shape[2]
    row_count = tokens.shape[0]
    clip_shape = (row_count // SEQ, SEQ, local_width // HEAD_DIM, HEAD_DIM)
    score_scale = HEAD_DIM ** (-0.5)
    grad_rows = cotangent.astype(jnp.float32)
    grad_all = spread_grads(cotangent)
    grad_act = lax.dot_general(
        grad_all, reduce_rows, CONTRACT_COLS, preferred_element_type=jnp.float32
    )
    reduce_grad = lax.dot_general(
        activated, grad_all, CONTRACT_ROWS, preferred_element_type=jnp.float32
    )
    reduce_bias_grad = jnp.sum(grad_rows, axis=0)
    gelu_value, gelu_back = jax.vjp(
        lambda inner_value: jax.nn.gelu(inner_value, approximate=False), expanded
    )
    grad_expanded = gelu_back(grad_act)[0].astype(jnp.bfloat16)
    expand_grad = lax.dot_general(
        normed_all_two, grad_expanded, CONTRACT_ROWS, preferred_element_type=jnp.float32
    )
    expand_bias_grad = jnp.sum(grad_expanded.astype(jnp.float32), axis=0)
    grad_normed_two = sum_grad_partials(
        lax.dot_general(
            grad_expanded, expand_all, CONTRACT_COLS, preferred_element_type=jnp.float32
        )
    )
    back_two, second_gain_grad, second_shift_grad = norm_backward(
        grad_normed_two, unit_two, inverse_two, second_gain, full_width
    )
    grad_hidden = grad_rows + back_two
    grad_hidden_low = grad_hidden.astype(jnp.bfloat16)
    grad_hidden_all = spread_grads(grad_hidden_low)
    output_grad = lax.dot_general(
        mixed_low, grad_hidden_all, CONTRACT_ROWS, preferred_element_type=jnp.float32
    )
    output_bias_grad = jnp.sum(grad_hidden_low.astype(jnp.float32), axis=0)
    grad_mixed = lax.dot_general(
        grad_hidden_all, output_rows, CONTRACT_COLS, preferred_element_type=jnp.float32
    ).astype(jnp.bfloat16)
    query_grads, key_grads, value_grads = lax.map(
        lambda clip_parts: attend_clip_back(
            clip_parts[0], clip_parts[1], clip_parts[2], clip_parts[3], clip_parts[4], score_scale
        ),
        (
            queries.reshape(clip_shape),
            key_rows.reshape(clip_shape),
            value_rows.reshape(clip_shape),
            logsum,
            grad_mixed.reshape(clip_shape),
        ),
    )
    stacked = jnp.stack(
        [
            query_grads.reshape(row_count, local_width),
            key_grads.reshape(row_count, local_width),
            value_grads.reshape(row_count, local_width),
        ],
        axis=1,
    ).astype(jnp.bfloat16)
    attention_bias_grad = jnp.stack(
        [
            jnp.sum(stacked[:, 0].astype(jnp.float32), axis=0),
            jnp.sum(stacked[:, 2].astype(jnp.float32), axis=0),
        ]
    )
    flat_grads = stacked.reshape(row_count, 3 * local_width)
    inward_grad = lax.dot_general(
        normed_all, flat_grads, CONTRACT_ROWS, preferred_element_type=jnp.float32
    ).reshape(full_width, 3, local_width)
    grad_normed_one = sum_grad_partials(
        lax.dot_general(
            flat_grads,
            inward_all.reshape(full_width, 3 * local_width),
            CONTRACT_COLS,
            preferred_element_type=jnp.float32,
        )
    )
    back_one, first_gain_grad, first_shift_grad = norm_backward(
        grad_normed_one, unit_one, inverse_one, first_gain, full_width
    )
    tokens_grad = grad_hidden + back_one
    inward_grad, output_grad, expand_grad, reduce_grad = (
        lax.psum_scatter(
            inward_grad.astype(jnp.bfloat16), "row", scatter_dimension=0, tiled=True
        ).astype(jnp.float32),
        lax.psum_scatter(
            output_grad.astype(jnp.bfloat16), "row", scatter_dimension=1, tiled=True
        ).astype(jnp.float32),
        lax.psum_scatter(
            expand_grad.astype(jnp.bfloat16), "row", scatter_dimension=0, tiled=True
        ).astype(jnp.float32),
        lax.psum_scatter(
            reduce_grad.astype(jnp.bfloat16), "row", scatter_dimension=1, tiled=True
        ).astype(jnp.float32),
    )
    (
        first_gain_grad,
        first_shift_grad,
        attention_bias_grad,
        output_bias_grad,
        second_gain_grad,
        second_shift_grad,
        expand_bias_grad,
        reduce_bias_grad,
    ) = lax.psum(
        (
            first_gain_grad,
            first_shift_grad,
            attention_bias_grad,
            output_bias_grad,
            second_gain_grad,
            second_shift_grad,
            expand_bias_grad,
            reduce_bias_grad,
        ),
        "row",
    )
    return (
        output_value.astype(jnp.bfloat16).reshape(-1, packed_width),
        tokens_grad.reshape(-1, packed_width),
        first_gain_grad,
        first_shift_grad,
        inward_grad,
        attention_bias_grad,
        output_grad,
        output_bias_grad,
        second_gain_grad,
        second_shift_grad,
        expand_grad,
        expand_bias_grad,
        reduce_grad,
        reduce_bias_grad,
    )


def fused_device(
    tokens,
    first_gain,
    first_shift,
    inward_weight,
    attention_bias,
    output_weight,
    output_bias,
    second_gain,
    second_shift,
    expand_weight,
    expand_bias,
    reduce_weight,
    reduce_bias,
    cotangent,
):
    kept = forward_call(
        tokens,
        cotangent,
        first_gain[None],
        first_shift[None],
        output_bias[None],
        second_gain[None],
        second_shift[None],
        reduce_bias[None],
        attention_bias,
        expand_bias[None],
        inward_weight.transpose(1, 0, 2),
        output_weight,
        expand_weight,
        reduce_weight,
    )
    (tok, cot, q, qt, k, kt, v, mixf, lse, hid, unit, inv, normed, act, slope, win, wo, we, wr, vec, one, stat) = kept

    def flat(array):
        return array.reshape(-1, array.shape[-1])

    outs = backward_call(
        flat(tok), flat(cot), flat(q), qt, flat(k), kt, flat(v), flat(mixf), lse, flat(hid), flat(unit),
        flat(inv), flat(normed), flat(act), flat(slope), win, wo, we, wr, vec, flat(one), flat(stat),
    )
    outs = finish_call(*outs)
    layer_output, tokens_grad, inward_grad, output_grad, expand_grad, reduce_grad = outs[:6]
    first_gain_grad, first_shift_grad, attention_grad, out_grad, gain_grad, shift_grad, red_grad, exp_grad = outs[6:]
    return (
        layer_output,
        tokens_grad,
        first_gain_grad[0],
        first_shift_grad[0],
        inward_grad.transpose(1, 0, 2),
        attention_grad,
        output_grad,
        out_grad[0],
        gain_grad[0],
        shift_grad[0],
        expand_grad,
        exp_grad[0],
        reduce_grad,
        red_grad[0],
    )


def per_device(rows, cols, *arrays):
    tokens, inward_weight, expand_weight = arrays[0], arrays[3], arrays[9]
    fits = (
        (rows, cols) == (8, 4)
        and tokens.shape == (SEQ // 2, 512)
        and inward_weight.shape == (128, 3, 256)
        and expand_weight.shape == (128, 1024)
    )
    return fused_device(*arrays) if fits else plain_device(*arrays)


def solution(mesh):
    in_specs = (
        P("row", "col"),
        P("col"),
        P("col"),
        P("row", None, "col"),
        P(None, "col"),
        P("col", "row"),
        P("col"),
        P("col"),
        P("col"),
        P("row", "col"),
        P("col"),
        P("col", "row"),
        P("col"),
        P("row", "col"),
    )
    out_specs = (
        P("row", "col"),
        P("row", "col"),
        P("col"),
        P("col"),
        P("row", None, "col"),
        P(None, "col"),
        P("col", "row"),
        P("col"),
        P("col"),
        P("col"),
        P("row", "col"),
        P("col"),
        P("col", "row"),
        P("col"),
    )
    return jax.shard_map(
        functools.partial(per_device, mesh.shape["row"], mesh.shape["col"]),
        mesh=mesh, in_specs=in_specs, out_specs=out_specs, check_vma=False
    )
```
